32 devices in a mesh: row: 8 (over z, x), col: 4 (over y, core).
Axes of the slice: x: 2, y: 2, z: 4, core: 2. Of those that a mesh axis runs over, the one named last changes fastest.
Arguments:
- tokens: bfloat16 [2, 8192, 768], P(None, ('row', 'col')), may hold values from -6 to 6
- segments: int32 [2, 8192], P(None, ('row', 'col')), may hold values from 0 to 17, as said below
- positions: int32 [2, 8192], P(None, ('row', 'col')), may hold values from 0 to 799, as said below
- w_qkv: bfloat16 [768, 3, 768], P('row', None, 'col'), may hold values from -0.21875 to 0.21875
- w_out: bfloat16 [768, 768], P('col', 'row'), may hold values from -0.875 to 0.875
- w_gate_up: bfloat16 [768, 2, 3072], P('row', None, 'col'), may hold values from -0.21875 to 0.21875
- w_down: bfloat16 [3072, 768], P('col', 'row'), may hold values from -0.109375 to 0.109375
- norm_gain: bfloat16 [768, 2], P('row'), may hold values from 0.5 to 1.5
- norm_bias: bfloat16 [768, 2], P('row'), may hold values from -1.1953125 to 1.1953125
- cotangent: float32 [2, 8192, 768], P(None, ('row', 'col')), may hold values from -6 to 6
Outputs:
- layer_out: bfloat16 [2, 8192, 768], P(None, ('row', 'col'))
- input_grad: float32 [2, 8192, 768], P(None, ('row', 'col'))
- grad_qkv: float32 [768, 3, 768], P('row', None, 'col')
- grad_out: float32 [768, 768], P('col', 'row')
- grad_gate_up: float32 [768, 2, 3072], P('row', None, 'col')
- grad_down: float32 [3072, 768], P('col', 'row')
- grad_gain: float32 [768, 2], P('row')
- grad_bias: float32 [768, 2], P('row')
The draws below stay inside these ranges and needn't reach their ends.
Inputs may be any that keep to these rules, and one draw needn't show every extreme that they name: `segments`: within each sequence documents are numbered from 0 upward and never fall; a document has at most 800 tokens and at least 60 unless it is the last of its sequence; some document has exactly 800 tokens, and in some sequence every document but the last has exactly 60 tokens. `positions`: the place of each token within its document, counted from 0.
All inputs are finite; a program needn't handle non-finite values.
Results may differ from the reference program's by a relative error of at most 0.017.
Values may be sent and summed in bfloat16 or wider, within the bound.
No kernel may reach another device: no remote copies, remote signals or barrier semaphores. Data moves between devices by JAX's collectives and lax.ppermute only.
A program may use at most 192 MiB of HBM per device.

```python
import math
import jax
import jax.numpy as jnp
from jax import lax

D = 768
H = 12
HD = 64
FF = 3072
LEN = 1024
DOC_MAX = 800
DOC_MIN = 60
MB = 2
ROWS_MB = 8192


def doc_layout(key):
    seq_count = MB * (ROWS_MB // LEN)
    most_docs = LEN // DOC_MIN + 1
    key_len = jax.random.fold_in(key, 11)
    key_pick = jax.random.fold_in(key, 12)
    lengths = jax.random.randint(key_len, (seq_count, most_docs), DOC_MIN, DOC_MAX + 1, dtype=jnp.int32)
    chosen = jax.random.randint(key_pick, (), 0, seq_count, dtype=jnp.int32)
    seq_index = jnp.arange(seq_count, dtype=jnp.int32)
    short_row = (seq_index == (chosen + 1) % seq_count)[:, None]
    lengths = jnp.where(short_row, DOC_MIN, lengths).astype(jnp.int32)
    forced = (seq_index == chosen)[:, None] & (jnp.arange(most_docs, dtype=jnp.int32) == 0)[None, :]
    lengths = jnp.where(forced, DOC_MAX, lengths).astype(jnp.int32)
    doc_ends = jnp.cumsum(lengths, axis=1).astype(jnp.int32)
    places = jnp.arange(LEN, dtype=jnp.int32)
    passed = (doc_ends[:, None, :] <= places[None, :, None]).astype(jnp.int32)
    segment = jnp.sum(passed, axis=2).astype(jnp.int32)
    doc_start = jnp.sum(passed * lengths[:, None, :], axis=2).astype(jnp.int32)
    inside = (places[None, :] - doc_start).astype(jnp.int32)
    return (segment.reshape(MB, ROWS_MB), inside.reshape(MB, ROWS_MB))


def draw_segments(key, part):
    return doc_layout(key)[0]


def draw_positions(key, part):
    return doc_layout(key)[1]


def block_scale(stream_key, extent, pieces, smallest, high):
    level, own = 1.0, jax.random.fold_in(stream_key, 6)
    for dim, blocks in pieces:
        steps = jnp.exp(jax.random.uniform(jax.random.fold_in(own, dim), (blocks,), jnp.float32, smallest / len(pieces), high / len(pieces)))
        level = level * jnp.repeat(steps, extent[dim] // blocks).reshape([-1 if axis == dim else 1 for axis in range(len(extent))])
    return level


def normal_values(rng, dims, spread, reach, pieces=(), held_as=jnp.bfloat16):
    values = jax.random.normal(rng, dims, jnp.float32) * spread
    if len(pieces) > 0:
        values = block_scale(rng, dims, pieces, -0.22, 0.18) * values
    return jnp.clip(values, min=-reach, max=reach).astype(held_as)


def setup_inputs(seed: int = 0) -> dict:
    key_of = jax.random.split(jax.random.key(seed), 11)
    tokens = normal_values(key_of[0], (MB, ROWS_MB, D), 1.0, 6.0, ((1, 32),))
    segments = draw_segments(jax.random.fold_in(key_of[10], 71), 0)
    positions = draw_positions(jax.random.fold_in(key_of[10], 71), 0)
    w_qkv = normal_values(key_of[3], (D, 3, D), D ** -0.5, 0.21875, ((0, 8), (2, 4)))
    w_out = normal_values(key_of[4], (D, D), (D // 16) ** -0.5, 0.875, ((0, 4), (1, 8)))
    w_gate_up = normal_values(key_of[5], (D, 2, FF), D ** -0.5, 0.21875, ((0, 8), (2, 4)))
    w_down = normal_values(key_of[6], (FF, D), FF ** -0.5, 0.109375, ((0, 4), (1, 8)))
    norm_gain = jnp.clip(1.0 + 0.1 * jax.random.normal(key_of[7], (D, 2), jnp.float32), 0.5, 1.5).astype(jnp.bfloat16)
    norm_bias = normal_values(key_of[8], (D, 2), 0.2, 1.1953125, ((0, 8),))
    cotangent = normal_values(key_of[9], (MB, ROWS_MB, D), 1.0, 6.0, ((1, 32),), jnp.float32)
    return dict(tokens=tokens, segments=segments, positions=positions, w_qkv=w_qkv, w_out=w_out, w_gate_up=w_gate_up, w_down=w_down, norm_gain=norm_gain, norm_bias=norm_bias, cotangent=cotangent)


@jax.custom_vjp
def low(v):
    return lax.optimization_barrier(v.astype(jnp.bfloat16)).astype(jnp.float32)

@jax.custom_vjp
def low_back(v):
    return v

def low_keep(v):
    return (low(v), None)

def low_pass(kept, grad):
    return (grad,)

def back_keep(v):
    return (v, None)

def back_low(kept, grad):
    return (low(grad),)
low.defvjp(low_keep, low_pass)
low_back.defvjp(back_keep, back_low)
epsilon = 1e-12
rope_base = 1000.0
masked_score = -1e+30
highest = lax.Precision.HIGHEST

def rope_tables(positions):
    half_dim = HD // 2
    freq = rope_base ** (-jnp.arange(half_dim, dtype=jnp.float32) / half_dim)
    angles = positions.astype(jnp.float32)[:, None] * freq[None, :]
    return (jnp.cos(angles), jnp.sin(angles))

def rotate(values, cosine, sine):
    half_dim = HD // 2
    first = values[..., :half_dim]
    second = values[..., half_dim:]
    cosine = cosine[:, None, :]
    sine = sine[:, None, :]
    return jnp.concatenate([first * cosine - second * sine, second * cosine + first * sine], axis=-1)

def normalize(hidden, gain_col, bias_col):
    centred = hidden - lax.optimization_barrier(jnp.mean(hidden, axis=-1, keepdims=True))
    variance = lax.optimization_barrier(jnp.mean(centred * centred, axis=-1, keepdims=True))
    return centred * lax.rsqrt(variance + epsilon) * gain_col + bias_col

def layer_forward(inputs, w_qkv, w_out, w_gate_up, w_down, norm_gain, norm_bias, segment, position):
    seq_len = inputs.shape[0]
    proj = low_back(jnp.dot(inputs, w_qkv.reshape(D, 3 * D), precision=highest)).reshape(seq_len, 3, H, HD)
    cosine, sine = rope_tables(position)
    queries = low(rotate(proj[:, 0], cosine, sine))
    keys = low(rotate(proj[:, 1], cosine, sine))
    values = low(proj[:, 2])
    scale = 1.0 / math.sqrt(HD)
    scores = low_back(jnp.einsum('qhd,khd->hqk', queries, keys, precision=highest) * scale)
    same_doc = segment[:, None] == segment[None, :]
    scores = jnp.where(same_doc[None], scores, masked_score)
    probs = low(jax.nn.softmax(scores, axis=-1))
    attended = jnp.einsum('hqk,khd->qhd', probs, values, precision=highest)
    attended = low(low_back(attended)).reshape(seq_len, D)
    branch = low_back(jnp.dot(attended, w_out, precision=highest))
    first_norm = normalize(inputs + branch, norm_gain[:, 0], norm_bias[:, 0])
    gate_up = low_back(jnp.dot(low(first_norm), w_gate_up.reshape(D, 2 * FF), precision=highest)).reshape(seq_len, 2, FF)
    hidden = low(jax.nn.silu(gate_up[:, 0]) * gate_up[:, 1])
    feed = low_back(jnp.dot(hidden, w_down, precision=highest))
    return normalize(first_norm + feed, norm_gain[:, 1], norm_bias[:, 1])

def reference(tokens, segments, positions, w_qkv, w_out, w_gate_up, w_down, norm_gain, norm_bias, cotangent):
    weights = (w_qkv.astype(jnp.float32), w_out.astype(jnp.float32), w_gate_up.astype(jnp.float32), w_down.astype(jnp.float32), norm_gain.astype(jnp.float32), norm_bias.astype(jnp.float32))
    seq_total = MB * (ROWS_MB // LEN)
    inputs = tokens.astype(jnp.float32).reshape(seq_total, LEN, D)
    seg_rows = segments.reshape(seq_total, LEN)
    pos_rows = positions.reshape(seq_total, LEN)
    cot_rows = cotangent.astype(jnp.float32).reshape(seq_total, LEN, D)

    def sequence_step(totals, items):
        inputs_seq, seg_seq, pos_seq, cot_seq = items

        def forward(inputs_arg, p_qkv, p_out, p_gate_up, p_down, p_gain, p_bias):
            return layer_forward(inputs_arg, p_qkv, p_out, p_gate_up, p_down, p_gain, p_bias, seg_seq, pos_seq)
        outputs, pullback = jax.vjp(forward, inputs_seq, weights[0], weights[1], weights[2], weights[3], weights[4], weights[5])
        gradients = pullback(cot_seq)
        totals = tuple((total + grad_part for total, grad_part in zip(totals, gradients[1:])))
        return (totals, (outputs.astype(jnp.bfloat16), gradients[0]))
    zero_sums = tuple((jnp.zeros(weight.shape, jnp.float32) for weight in weights))
    totals, (outputs, input_grads) = lax.scan(sequence_step, zero_sums, (inputs, seg_rows, pos_rows, cot_rows))
    return (outputs.reshape(MB, ROWS_MB, D), input_grads.reshape(MB, ROWS_MB, D), totals[0], totals[1], totals[2], totals[3], totals[4], totals[5])
```

```python
import functools
import math

import jax
import jax.numpy as jnp
from jax import lax
from jax.experimental import pallas as pl
from jax.experimental.pallas import tpu as pltpu
from jax.sharding import PartitionSpec as P

HD = 64
PAIR = 2 * HD
QROWS = 256
epsilon = 1e-12
rope_base = 1000.0
masked_score = -1e30
f32 = jnp.float32
bf16 = jnp.bfloat16

NN = (((1,), (0,)), ((), ()))
NT = (((1,), (1,)), ((), ()))
TN = (((0,), (0,)), ((), ()))


def dot(a, b, dims=NN):
    return lax.dot_general(a, b, dims, preferred_element_type=f32)


def rope_tables(positions, heads):
    half_dim = HD // 2
    freq = rope_base ** (-jnp.arange(half_dim, dtype=f32) / half_dim)
    angles = positions.astype(f32)[:, None] * freq[None, :]
    cosine, sine = jnp.cos(angles), jnp.sin(angles)
    return (
        jnp.concatenate([cosine, cosine], axis=1)[:, None, :],
        jnp.concatenate([-sine, sine], axis=1)[:, None, :],
    )


def rotate(values, cosine, sine):
    rows, width = values.shape
    heads = values.reshape(rows, width // HD, HD)
    swapped = jnp.concatenate([heads[..., HD // 2 :], heads[..., : HD // 2]], axis=-1)
    return (heads * cosine + swapped * sine).reshape(rows, width)


def normalize(hidden):
    centred = hidden - jnp.mean(hidden, axis=-1, keepdims=True)
    variance = jnp.mean(centred * centred, axis=-1, keepdims=True)
    inv_std = lax.rsqrt(variance + epsilon)
    return (centred * inv_std, inv_std)


def norm_back(grad_norm, normed, inv_std):
    return inv_std * (
        grad_norm
        - jnp.mean(grad_norm, axis=-1, keepdims=True)
        - normed * jnp.mean(grad_norm * normed, axis=-1, keepdims=True)
    )


def attend_kernel(q_ref, k_ref, v_ref, segq_ref, segk_ref, out_ref, log_ref):
    rows = q_ref.shape[0]
    low_half = lax.broadcasted_iota(jnp.int32, (QROWS, PAIR), 1) < HD
    keys = k_ref[...]
    values = v_ref[...]
    for block in range(rows // QROWS):
        span = slice(block * QROWS, (block + 1) * QROWS)
        q = q_ref[span, :]
        same = segq_ref[span, :] == segk_ref[...]
        bias = jnp.where(same, 0.0, masked_score)
        parts = []
        logs = []
        for head in range(2):
            mine = low_half if head == 0 else jnp.logical_not(low_half)
            scores = dot(jnp.where(mine, q, jnp.zeros_like(q)), keys, NT) + bias
            top = jnp.max(scores, axis=1, keepdims=True)
            expo = jnp.exp(scores - top)
            total = jnp.sum(expo, axis=1, keepdims=True)
            parts.append(dot(expo.astype(bf16), values) / total)
            logs.append(top + jnp.log(total))
        out_ref[span, :] = jnp.where(low_half, parts[0], parts[1]).astype(bf16)
        log_ref[0, span, :] = jnp.concatenate(logs, axis=1)


def attend(q, k, v, seg_q, seg_k):
    rows, width = q.shape
    keys = k.shape[0]
    pairs = width // PAIR
    return pl.pallas_call(
        attend_kernel,
        grid=(pairs,),
        in_specs=[
            pl.BlockSpec((rows, PAIR), lambda j: (0, j)),
            pl.BlockSpec((keys, PAIR), lambda j: (0, j)),
            pl.BlockSpec((keys, PAIR), lambda j: (0, j)),
            pl.BlockSpec((rows, 1), lambda j: (0, 0)),
            pl.BlockSpec((1, keys), lambda j: (0, 0)),
        ],
        out_specs=[
            pl.BlockSpec((rows, PAIR), lambda j: (0, j)),
            pl.BlockSpec((1, rows, 2), lambda j: (j, 0, 0)),
        ],
        out_shape=[
            jax.ShapeDtypeStruct((rows, width), bf16),
            jax.ShapeDtypeStruct((pairs, rows, 2), f32),
        ],
        cost_estimate=pl.CostEstimate(
            flops=16 * rows * keys * width, bytes_accessed=8 * keys * width, transcendentals=rows * keys * width // HD
        ),
        name="attend",
    )(q, k, v, seg_q[:, None], seg_k[None, :])


def attend_back_kernel(
    q_ref, k_ref, v_ref, do_ref, log_ref, delta_ref, segq_ref, segk_ref, dq_ref, dk_ref, dv_ref
):
    rows = q_ref.shape[0]
    low_half = lax.broadcasted_iota(jnp.int32, (QROWS, PAIR), 1) < HD
    low_out = lax.broadcasted_iota(jnp.int32, (k_ref.shape[0], PAIR), 1) < HD
    low_rows = lax.broadcasted_iota(jnp.int32, (PAIR, QROWS), 0) < HD
    keys = k_ref[...]
    values = v_ref[...]
    keys_t = keys.T
    for block in range(rows // QROWS):
        span = slice(block * QROWS, (block + 1) * QROWS)
        q = q_ref[span, :]
        do = do_ref[span, :]
        same = segk_ref[...] == segq_ref[:, span]
        bias = jnp.where(same, 0.0, masked_score)
        dq = []
        dk = []
        dv = []
        for head in range(2):
            mine = low_half if head == 0 else jnp.logical_not(low_half)
            scores = dot(keys, jnp.where(mine, q, jnp.zeros_like(q)), NT) + bias
            probs = jnp.exp(scores - log_ref[0, head : head + 1, span])
            dprobs = dot(values, jnp.where(mine, do, jnp.zeros_like(do)), NT)
            dscores = (probs * (dprobs - delta_ref[0, head : head + 1, span])).astype(bf16)
            dv.append(dot(probs.astype(bf16), do))
            dk.append(dot(dscores, q))
            dq.append(dot(keys_t, dscores))
        dq_ref[span, :] = (jnp.where(low_rows, dq[0], dq[1]) * (1.0 / math.sqrt(HD))).T
        dk_part = jnp.where(low_out, dk[0], dk[1])
        dv_part = jnp.where(low_out, dv[0], dv[1])
        if block == 0:
            dk_ref[...] = dk_part
            dv_ref[...] = dv_part
        else:
            dk_ref[...] += dk_part
            dv_ref[...] += dv_part


def attend_back(q, k, v, do, logs, delta, seg_q, seg_k):
    rows, width = q.shape
    keys = k.shape[0]
    pairs = width // PAIR
    by_pair = lambda j: (0, j)
    return pl.pallas_call(
        attend_back_kernel,
        grid=(pairs,),
        in_specs=[
            pl.BlockSpec((rows, PAIR), by_pair),
            pl.BlockSpec((keys, PAIR), by_pair),
            pl.BlockSpec((keys, PAIR), by_pair),
            pl.BlockSpec((rows, PAIR), by_pair),
            pl.BlockSpec((1, 2, rows), lambda j: (j, 0, 0)),
            pl.BlockSpec((1, 2, rows), lambda j: (j, 0, 0)),
            pl.BlockSpec((1, rows), lambda j: (0, 0)),
            pl.BlockSpec((keys, 1), lambda j: (0, 0)),
        ],
        out_specs=[
            pl.BlockSpec((rows, PAIR), by_pair),
            pl.BlockSpec((keys, PAIR), by_pair),
            pl.BlockSpec((keys, PAIR), by_pair),
        ],
        out_shape=[
            jax.ShapeDtypeStruct((rows, width), f32),
            jax.ShapeDtypeStruct((keys, width), f32),
            jax.ShapeDtypeStruct((keys, width), f32),
        ],
        cost_estimate=pl.CostEstimate(
            flops=40 * rows * keys * width, bytes_accessed=20 * keys * width, transcendentals=rows * keys * width // HD
        ),
        name="attend_back",
    )(q, k, v, do, logs, delta, seg_q[None, :], seg_k[:, None])


def on_device(
    tokens, segments, positions, w_qkv, w_out, w_gate_up, w_down, norm_gain, norm_bias, cotangent
):
    peers = lax.axis_size("col")
    rings = lax.axis_size("row")
    half = tokens.shape[0]
    side = lax.axis_index("col") // (peers // half)
    scale = 1.0 / math.sqrt(HD)

    def across(v):
        return lax.ppermute(v, "col", [(i, (i + peers // 2) % peers) for i in range(peers)])

    def beside(v):
        return lax.ppermute(v, "col", [(i, i ^ 1) for i in range(peers)])

    def to_sequence(v):
        own = lax.dynamic_index_in_dim(v, side, 0, keepdims=False)
        other = lax.dynamic_index_in_dim(v, 1 - side, 0, keepdims=False)
        return jnp.concatenate([own, across(other)], axis=0)

    def from_sequence(v):
        rows = v.shape[0] // 2
        came = across(v[rows:])
        own = v[:rows]
        first = side == 0
        return jnp.stack([jnp.where(first, own, came), jnp.where(first, came, own)], axis=0)

    depth = w_qkv.shape[0]
    width = tokens.shape[2]
    head_cols = w_qkv.shape[2]
    hid = w_gate_up.shape[2]

    norms = jnp.concatenate([norm_gain, norm_bias], axis=1)
    norms = jnp.pad(norms, ((0, 0), (0, 128 - norms.shape[1])))
    pack_a = jnp.concatenate([w_qkv.reshape(depth, -1), w_out.T, norms], axis=1)
    pack_b = jnp.concatenate([w_gate_up.reshape(depth, -1), w_down.T], axis=1)

    def gathered(v):
        return lax.all_gather(v, ("col", "row"), axis=0, tiled=True).reshape(peers, width, -1)

    full_a = gathered(pack_a)
    full_b = gathered(pack_b)

    x = to_sequence(tokens)
    seg_pos = to_sequence(jnp.stack([segments, positions], axis=2))
    seg = seg_pos[:, 0]
    seg_all = jnp.concatenate([seg, beside(seg)], axis=0)
    cosine, sine = rope_tables(seg_pos[:, 1], width // HD)
    dy = to_sequence(cotangent)

    def columns(lo):
        return jnp.concatenate(
            [full_a[c, :, lo : lo + head_cols] for c in range(peers)], axis=1
        )

    wq, wk, wv = columns(0), columns(head_cols), columns(2 * head_cols)
    wo_t = columns(3 * head_cols)
    gains = full_a[0, :, 4 * head_cols : 4 * head_cols + 2].astype(f32)
    biases = full_a[0, :, 4 * head_cols + 2 : 4 * head_cols + 4].astype(f32)

    q = (rotate(dot(x, wq), cosine, sine)).astype(bf16)
    k = rotate(dot(x, wk), cosine, sine).astype(bf16)
    v = dot(x, wv).astype(bf16)
    kv = jnp.concatenate([k, v], axis=1)
    kv_all = jnp.concatenate([kv, beside(kv)], axis=0)
    k_all = kv_all[:, :width]
    v_all = kv_all[:, width:]
    q_small = q * jnp.asarray(scale, bf16)
    attended, logs = attend(q_small, k_all, v_all, seg, seg_all)
    branch = dot(attended, wo_t, NT)
    n1, s1 = normalize(x.astype(f32) + branch)
    first = n1 * gains[:, 0] + biases[:, 0]
    first_low = first.astype(bf16)
    gates = []
    ups = []
    feed = jnp.zeros(first.shape, f32)
    for c in range(peers):
        gates.append(dot(first_low, full_b[c, :, :hid]))
        ups.append(dot(first_low, full_b[c, :, hid : 2 * hid]))
        hidden = (jax.nn.silu(gates[c]) * ups[c]).astype(bf16)
        feed = feed + dot(hidden, full_b[c, :, 2 * hid :], NT)
    n2, s2 = normalize(first + feed)
    layer_out = (n2 * gains[:, 1] + biases[:, 1]).astype(bf16)

    gain_two = jnp.sum(dy * n2, axis=0)
    bias_two = jnp.sum(dy, axis=0)
    dh2 = norm_back(dy * gains[:, 1], n2, s2)
    dfeed = dh2.astype(bf16)
    dfirst = dh2
    grads_b = []
    for c in range(peers):
        dhidden = dot(dfeed, full_b[c, :, 2 * hid :])
        sg = jax.nn.sigmoid(gates[c])
        silu = gates[c] * sg
        dgate = (dhidden * ups[c] * sg * (1.0 + gates[c] * (1.0 - sg))).astype(bf16)
        dup = (dhidden * silu).astype(bf16)
        hidden = (silu * ups[c]).astype(bf16)
        grads_b.append(
            jnp.concatenate(
                [
                    dot(first_low, dgate, TN).astype(bf16),
                    dot(first_low, dup, TN).astype(bf16),
                    dot(dfeed, hidden, TN).astype(bf16),
                ],
                axis=1,
            )
        )
        dfirst = (
            dfirst
            + dot(dgate, full_b[c, :, :hid], NT)
            + dot(dup, full_b[c, :, hid : 2 * hid], NT)
        )

    def scattered(grads):
        both = jnp.stack(grads, axis=0).reshape(peers * width, -1)
        return lax.psum_scatter(both, ("col", "row"), scatter_dimension=0, tiled=True).astype(f32)

    own_b = scattered(grads_b)

    gain_one = jnp.sum(dfirst * n1, axis=0)
    bias_one = jnp.sum(dfirst, axis=0)
    dh1 = norm_back(dfirst * gains[:, 0], n1, s1)
    dbranch = dh1.astype(bf16)
    do = dot(dbranch, wo_t).astype(bf16)
    delta = jnp.sum(
        (do.astype(f32) * attended.astype(f32)).reshape(do.shape[0], -1, 2, HD), axis=3
    )
    dq, dk, dv = attend_back(
        q_small,
        k_all,
        v_all,
        do,
        logs.transpose(0, 2, 1),
        delta.transpose(1, 2, 0),
        seg,
        seg_all,
    )
    rows = x.shape[0]
    dkv = jnp.concatenate([dk, dv], axis=1)
    dkv_sum = dkv[:rows] + beside(dkv[rows:].astype(bf16)).astype(f32)
    dproj = jnp.concatenate(
        [rotate(dq, cosine, -sine), rotate(dkv_sum[:, :width], cosine, -sine), dkv_sum[:, width:]],
        axis=1,
    ).astype(bf16)
    d_qkv = dot(x, dproj, TN).astype(bf16)
    d_out = dot(dbranch, attended, TN).astype(bf16)
    grads_a = []
    for c in range(peers):
        lo = c * head_cols
        grads_a.append(
            jnp.concatenate(
                [d_qkv[:, p * width + lo : p * width + lo + head_cols] for p in range(3)]
                + [d_out[:, lo : lo + head_cols]],
                axis=1,
            )
        )
    own_a = scattered(grads_a)
    w_all = jnp.concatenate([wq, wk, wv], axis=1)
    input_grad = from_sequence(dh1 + dot(dproj, w_all, NT))
    layer_out = from_sequence(layer_out)

    small = lax.psum(
        jnp.stack([gain_one, gain_two, bias_one, bias_two], axis=1), ("row", "col")
    )
    small = lax.dynamic_slice_in_dim(small, lax.axis_index("row") * depth, depth, axis=0)
    return (
        layer_out,
        input_grad,
        own_a[:, : 3 * head_cols].reshape(depth, 3, head_cols),
        own_a[:, 3 * head_cols :].T,
        own_b[:, : 2 * hid].reshape(depth, 2, hid),
        own_b[:, 2 * hid :].T,
        small[:, :2],
        small[:, 2:],
    )


def solution(mesh):
    in_specs = (
        P(None, ("row", "col"), None),
        P(None, ("row", "col")),
        P(None, ("row", "col")),
        P("row", None, "col"),
        P("col", "row"),
        P("row", None, "col"),
        P("col", "row"),
        P("row", None),
        P("row", None),
        P(None, ("row", "col"), None),
    )
    out_specs = (
        P(None, ("row", "col"), None),
        P(None, ("row", "col"), None),
        P("row", None, "col"),
        P("col", "row"),
        P("row", None, "col"),
        P("col", "row"),
        P("row", None),
        P("row", None),
    )
    return jax.shard_map(
        on_device, mesh=mesh, in_specs=in_specs, out_specs=out_specs, check_vma=False
    )
```

```python
import functools
import math

import jax
import jax.numpy as jnp
from jax import lax
from jax.experimental import pallas as pl
from jax.experimental.pallas import tpu as pltpu
from jax.sharding import PartitionSpec as P

HD = 64
PAIR = 2 * HD
QROWS = 256
epsilon = 1e-12
rope_base = 1000.0
masked_score = -1e30
f32 = jnp.float32
bf16 = jnp.bfloat16

NN = (((1,), (0,)), ((), ()))
NT = (((1,), (1,)), ((), ()))
TN = (((0,), (0,)), ((), ()))


def dot(a, b, dims=NN):
    return lax.dot_general(a, b, dims, preferred_element_type=f32)


def rope_tables(positions, heads):
    half_dim = HD // 2
    freq = rope_base ** (-jnp.arange(half_dim, dtype=f32) / half_dim)
    angles = positions.astype(f32)[:, None] * freq[None, :]
    cosine, sine = jnp.cos(angles), jnp.sin(angles)
    return (
        jnp.concatenate([cosine, cosine], axis=1)[:, None, :],
        jnp.concatenate([-sine, sine], axis=1)[:, None, :],
    )


def rotate(values, cosine, sine):
    rows, width = values.shape
    heads = values.reshape(rows, width // HD, HD)
    swapped = jnp.concatenate([heads[..., HD // 2 :], heads[..., : HD // 2]], axis=-1)
    return (heads * cosine + swapped * sine).reshape(rows, width)


def normalize(hidden):
    centred = hidden - jnp.mean(hidden, axis=-1, keepdims=True)
    variance = jnp.mean(centred * centred, axis=-1, keepdims=True)
    inv_std = lax.rsqrt(variance + epsilon)
    return (centred * inv_std, inv_std)


def norm_back(grad_norm, normed, inv_std):
    return inv_std * (
        grad_norm
        - jnp.mean(grad_norm, axis=-1, keepdims=True)
        - normed * jnp.mean(grad_norm * normed, axis=-1, keepdims=True)
    )


def attend_kernel(q_ref, k_ref, v_ref, segq_ref, segk_ref, out_ref, log_ref):
    rows = q_ref.shape[0]
    low_half = lax.broadcasted_iota(jnp.int32, (QROWS, PAIR), 1) < HD
    keys = k_ref[...]
    values = v_ref[...]
    for block in range(rows // QROWS):
        span = slice(block * QROWS, (block + 1) * QROWS)
        q = q_ref[span, :]
        same = segq_ref[span, :] == segk_ref[...]
        bias = jnp.where(same, 0.0, masked_score)
        parts = []
        logs = []
        for head in range(2):
            mine = low_half if head == 0 else jnp.logical_not(low_half)
            scores = dot(jnp.where(mine, q, jnp.zeros_like(q)), keys, NT) + bias
            top = jnp.max(scores, axis=1, keepdims=True)
            expo = jnp.exp(scores - top)
            total = jnp.sum(expo, axis=1, keepdims=True)
            parts.append(dot(expo.astype(bf16), values) / total)
            logs.append(top + jnp.log(total))
        out_ref[span, :] = jnp.where(low_half, parts[0], parts[1]).astype(bf16)
        log_ref[0, span, :] = jnp.concatenate(logs, axis=1)


def attend(q, k, v, seg_q, seg_k):
    rows, width = q.shape
    keys = k.shape[0]
    pairs = width // PAIR
    return pl.pallas_call(
        attend_kernel,
        grid=(pairs,),
        in_specs=[
            pl.BlockSpec((rows, PAIR), lambda j: (0, j)),
            pl.BlockSpec((keys, PAIR), lambda j: (0, j)),
            pl.BlockSpec((keys, PAIR), lambda j: (0, j)),
            pl.BlockSpec((rows, 1), lambda j: (0, 0)),
            pl.BlockSpec((1, keys), lambda j: (0, 0)),
        ],
        out_specs=[
            pl.BlockSpec((rows, PAIR), lambda j: (0, j)),
            pl.BlockSpec((1, rows, 2), lambda j: (j, 0, 0)),
        ],
        out_shape=[
            jax.ShapeDtypeStruct((rows, width), bf16),
            jax.ShapeDtypeStruct((pairs, rows, 2), f32),
        ],
        cost_estimate=pl.CostEstimate(
            flops=16 * rows * keys * width, bytes_accessed=8 * keys * width, transcendentals=rows * keys * width // HD
        ),
        name="attend",
    )(q, k, v, seg_q[:, None], seg_k[None, :])


def attend_back_kernel(
    q_ref, k_ref, v_ref, do_ref, log_ref, delta_ref, segq_ref, segk_ref, dq_ref, dk_ref, dv_ref
):
    rows = q_ref.shape[0]
    low_half = lax.broadcasted_iota(jnp.int32, (QROWS, PAIR), 1) < HD
    low_out = lax.broadcasted_iota(jnp.int32, (k_ref.shape[0], PAIR), 1) < HD
    low_rows = lax.broadcasted_iota(jnp.int32, (PAIR, QROWS), 0) < HD
    keys = k_ref[...]
    values = v_ref[...]
    keys_t = keys.T
    for block in range(rows // QROWS):
        span = slice(block * QROWS, (block + 1) * QROWS)
        q = q_ref[span, :]
        do = do_ref[span, :]
        same = segk_ref[...] == segq_ref[:, span]
        bias = jnp.where(same, 0.0, masked_score)
        dq = []
        dk = []
        dv = []
        for head in range(2):
            mine = low_half if head == 0 else jnp.logical_not(low_half)
            scores = dot(keys, jnp.where(mine, q, jnp.zeros_like(q)), NT) + bias
            probs = jnp.exp(scores - log_ref[0, head : head + 1, span])
            dprobs = dot(values, jnp.where(mine, do, jnp.zeros_like(do)), NT)
            dscores = (probs * (dprobs - delta_ref[0, head : head + 1, span])).astype(bf16)
            dv.append(dot(probs.astype(bf16), do))
            dk.append(dot(dscores, q))
            dq.append(dot(keys_t, dscores))
        dq_ref[span, :] = (jnp.where(low_rows, dq[0], dq[1]) * (1.0 / math.sqrt(HD))).T
        dk_part = jnp.where(low_out, dk[0], dk[1])
        dv_part = jnp.where(low_out, dv[0], dv[1])
        if block == 0:
            dk_ref[...] = dk_part
            dv_ref[...] = dv_part
        else:
            dk_ref[...] += dk_part
            dv_ref[...] += dv_part


def attend_back(q, k, v, do, logs, delta, seg_q, seg_k):
    rows, width = q.shape
    keys = k.shape[0]
    pairs = width // PAIR
    by_pair = lambda j: (0, j)
    return pl.pallas_call(
        attend_back_kernel,
        grid=(pairs,),
        in_specs=[
            pl.BlockSpec((rows, PAIR), by_pair),
            pl.BlockSpec((keys, PAIR), by_pair),
            pl.BlockSpec((keys, PAIR), by_pair),
            pl.BlockSpec((rows, PAIR), by_pair),
            pl.BlockSpec((1, 2, rows), lambda j: (j, 0, 0)),
            pl.BlockSpec((1, 2, rows), lambda j: (j, 0, 0)),
            pl.BlockSpec((1, rows), lambda j: (0, 0)),
            pl.BlockSpec((keys, 1), lambda j: (0, 0)),
        ],
        out_specs=[
            pl.BlockSpec((rows, PAIR), by_pair),
            pl.BlockSpec((keys, PAIR), by_pair),
            pl.BlockSpec((keys, PAIR), by_pair),
        ],
        out_shape=[
            jax.ShapeDtypeStruct((rows, width), f32),
            jax.ShapeDtypeStruct((keys, width), f32),
            jax.ShapeDtypeStruct((keys, width), f32),
        ],
        cost_estimate=pl.CostEstimate(
            flops=40 * rows * keys * width, bytes_accessed=20 * keys * width, transcendentals=rows * keys * width // HD
        ),
        name="attend_back",
    )(q, k, v, do, logs, delta, seg_q[None, :], seg_k[:, None])


def factors_of(n):
    out = []
    while n > 1:
        step = 4 if n % 4 == 0 else (2 if n % 2 == 0 else n)
        out.append(step)
        n //= step
    return out


class Links:
    def __init__(self, mesh):
        self.rows = mesh.shape["row"]
        self.cols = mesh.shape["col"]
        self.digits = factors_of(self.rows // 2)

    def locate(self):
        row = lax.axis_index("row")
        col = lax.axis_index("col")
        x = row % 2
        place = row // 2
        ring = []
        for size in reversed(self.digits):
            ring.insert(0, place % size)
            place = place // size
        return ring, x, col // (self.cols // 2), col % 2

    def send(self, v, move):
        pairs = []
        for row in range(self.rows):
            for col in range(self.cols):
                place, ring = row // 2, []
                for size in reversed(self.digits):
                    ring.insert(0, place % size)
                    place //= size
                ring, x, y, k = move(ring, row % 2, col // (self.cols // 2), col % 2)
                place = 0
                for size, digit in zip(self.digits, ring):
                    place = place * size + digit % size
                pairs.append(
                    (row * self.cols + col, (place * 2 + x) * self.cols + y * (self.cols // 2) + k)
                )
        return lax.ppermute(v, ("row", "col"), pairs)

    def across(self, v):
        return self.send(v, lambda ring, x, y, k: (ring, x, 1 - y, k))

    def beside(self, v):
        return self.send(v, lambda ring, x, y, k: (ring, x, y, 1 - k))

    def near(self, v):
        return self.send(
            v, lambda ring, x, y, k: (ring, x, 1 - y, k) if k else (ring, 1 - x, y, k)
        )

    def far(self, v):
        return self.send(
            v, lambda ring, x, y, k: (ring, 1 - x, y, k) if k else (ring, x, 1 - y, k)
        )

    def shift(self, v, axis, step):
        def move(ring, x, y, k):
            moved = list(ring)
            moved[axis] = ring[axis] + step
            return moved, x, y, k

        return self.send(v, move)

    def gather(self, shard, odd):
        block = shard
        for axis in reversed(range(len(self.digits))):
            block = jnp.concatenate(
                [block] + [self.shift(block, axis, -d) for d in range(1, self.digits[axis])], axis=0
            )
        b = self.near(block)
        c = self.far(block)
        d = self.far(b)
        mine = [block, b, c, d]
        theirs = [self.beside(v) for v in mine]
        out = {}
        for k, (a, b, c, d), flip in ((0, mine, odd), (1, theirs, jnp.logical_not(odd))):
            out[0, k] = jnp.concatenate([a, jnp.where(flip, c, b)], axis=0)
            out[1, k] = jnp.concatenate([jnp.where(flip, b, c), d], axis=0)
        return out

    def scatter(self, parts, odd):
        came = [self.beside(parts[y, 1]) for y in range(2)]
        cut = parts[0, 0].shape[0] // 2

        def total(y, x):
            rows = slice(x * cut, (x + 1) * cut)
            return parts[y, 0][rows].astype(f32) + came[y][rows].astype(f32)

        first = jnp.where(odd, total(0, 1), total(1, 0)).astype(bf16)
        second = total(1, 1).astype(bf16)
        got_first, got_second = self.far(first), self.far(second)
        third = (jnp.where(odd, total(1, 0), total(0, 1)) + got_second.astype(f32)).astype(bf16)
        block = total(0, 0) + got_first.astype(f32) + self.near(third).astype(f32)
        for axis in range(len(self.digits)):
            size = self.digits[axis]
            pieces = jnp.split(block, size, axis=0)
            block = pieces[0]
            for d in range(1, size):
                block = block + self.shift(pieces[d].astype(bf16), axis, d).astype(f32)
        return block


def relative_order(links, depth):
    ring, x, _, _ = links.locate()
    where = lax.broadcasted_iota(jnp.int32, (1, links.rows * depth), 1)
    block, inside = where // depth, where % depth
    steps = links.rows // 2
    place = block % steps
    parts = []
    for axis in reversed(range(len(links.digits))):
        size = links.digits[axis]
        parts.insert(0, (place % size + ring[axis]) % size)
        place = place // size
    row = jnp.zeros_like(block)
    for size, part in zip(links.digits, parts):
        row = row * size + part
    row = row * 2 + jnp.bitwise_xor(x, block // steps)
    return row * depth + inside


def on_device(
    links, tokens, segments, positions, w_qkv, w_out, w_gate_up, w_down, norm_gain, norm_bias, cotangent
):
    ring, x_place, side, core = links.locate()
    odd = core == 1
    scale = 1.0 / math.sqrt(HD)
    depth = w_qkv.shape[0]
    width = tokens.shape[2]
    head_cols = w_qkv.shape[2]
    hid = w_gate_up.shape[2]
    rows = 2 * tokens.shape[1]
    quarters = [(0, 0), (0, 1), (1, 0), (1, 1)]

    source = relative_order(links, depth)
    swap = (lax.broadcasted_iota(jnp.int32, (width, width), 0) == source).astype(bf16)

    def to_relative(v):
        if v.dtype == bf16:
            return dot(v, swap)
        high = v.astype(bf16)
        low = (v - high.astype(f32)).astype(bf16)
        return dot(high, swap) + dot(low, swap)

    def from_relative(v):
        if v.dtype == bf16:
            return dot(v, swap, NT)
        high = v.astype(bf16)
        low = (v - high.astype(f32)).astype(bf16)
        return dot(high, swap, NT) + dot(low, swap, NT)

    def own_and_other(v):
        own = lax.dynamic_index_in_dim(v, side, 0, keepdims=False)
        return own, lax.dynamic_index_in_dim(v, 1 - side, 0, keepdims=False)

    def from_sequence(own, came):
        first = side == 0
        return jnp.stack([jnp.where(first, own, came), jnp.where(first, came, own)], axis=0)

    norms = jnp.concatenate([norm_gain, norm_bias], axis=1)
    norms = jnp.pad(norms, ((0, 0), (0, 64 - norms.shape[1])))
    half = hid // 2
    shards = [jnp.concatenate([w_qkv.reshape(depth, -1), norms], axis=1)]
    down_t = w_down.T
    for h in range(2):
        cols = slice(h * half, (h + 1) * half)
        shards.append(
            jnp.concatenate(
                ([w_out.T] if h == 0 else [])
                + [down_t[:, cols], w_gate_up[:, 0, cols], w_gate_up[:, 1, cols]],
                axis=1,
            )
        )
    tokens_own, tokens_other = own_and_other(tokens)
    tokens_came = links.across(tokens_other)
    small_own, small_other = own_and_other(jnp.stack([segments, positions], axis=1))
    small_came = links.across(small_other)
    full = [links.gather(s, odd) for s in shards]

    x = to_relative(jnp.concatenate([tokens_own, tokens_came], axis=0)).astype(bf16)
    small = jnp.concatenate([small_own, small_came], axis=1)
    seg = small[0]
    seg_all = jnp.concatenate([seg, links.beside(seg)], axis=0)
    cosine, sine = rope_tables(small[1], width // HD)
    dy_own, dy_other = own_and_other(cotangent)
    dy_came = links.across(dy_other.astype(bf16))
    dy = jnp.concatenate([to_relative(dy_own), to_relative(dy_came)], axis=0)

    def columns(which, lo, size):
        return jnp.concatenate([full[which][c][:, lo : lo + size] for c in quarters], axis=1)

    wq, wk, wv = (columns(0, p * head_cols, head_cols) for p in range(3))
    wo_t = columns(1, 0, head_cols)
    norm_cols = full[0][0, 0][:, 3 * head_cols : 3 * head_cols + 4].astype(f32).T
    gains, biases = norm_cols[:2], norm_cols[2:]

    q = rotate(dot(x, wq), cosine, sine)
    k = rotate(dot(x, wk), cosine, sine).astype(bf16)
    v = dot(x, wv).astype(bf16)

    def swapped_heads(v):
        parts = jnp.split(v, 4, axis=1)
        return [parts[1], parts[0], parts[3], parts[2]]

    kv_came = links.beside(jnp.concatenate(swapped_heads(k) + swapped_heads(v), axis=1))
    k_all = jnp.concatenate([k, kv_came[:, :width]], axis=0)
    v_all = jnp.concatenate([v, kv_came[:, width:]], axis=0)
    q_small = (q.astype(bf16) * jnp.asarray(scale, bf16)).astype(bf16)
    attended, logs = attend(q_small, k_all, v_all, seg, seg_all)
    branch = dot(attended, wo_t, NT)
    n1, s1 = normalize(x.astype(f32) + branch)
    first = n1 * gains[0] + biases[0]
    first_low = first.astype(bf16)
    gates, ups, hiddens, downs, gate_ups = {}, {}, {}, {}, {}
    feed = jnp.zeros(first.shape, f32)
    for h in range(2):
        base = head_cols if h == 0 else 0
        for c in quarters:
            w = full[1 + h][c]
            downs[h, c] = w[:, base : base + half]
            gate_ups[h, c] = w[:, base + half : base + 3 * half]
            both = dot(first_low, gate_ups[h, c])
            gates[h, c], ups[h, c] = both[:, :half], both[:, half:]
            hiddens[h, c] = (jax.nn.silu(gates[h, c]) * ups[h, c]).astype(bf16)
            feed = feed + dot(hiddens[h, c], downs[h, c], NT)
    n2, s2 = normalize(first + feed)
    layer_out = (n2 * gains[1] + biases[1]).astype(bf16)

    gain_two = jnp.sum(dy * n2, axis=0)
    bias_two = jnp.sum(dy, axis=0)
    dh2 = norm_back(dy * gains[1], n2, s2)
    dfeed = dh2.astype(bf16)
    grads = {}
    for c in quarters:
        grads[c] = jnp.concatenate(
            [dot(dfeed, hiddens[h, c], TN).astype(bf16) for h in range(2)], axis=1
        )
    own_down = links.scatter(grads, odd)
    dfirst = dh2
    own_gate_up = []
    for h in range(2):
        grads = {}
        for c in quarters:
            dhidden = dot(dfeed, downs[h, c])
            gate, up = gates[h, c], ups[h, c]
            sg = jax.nn.sigmoid(gate)
            dgate = dhidden * up * sg * (1.0 + gate * (1.0 - sg))
            dup = dhidden * (gate * sg)
            dgate_up = jnp.concatenate([dgate, dup], axis=1).astype(bf16)
            grads[c] = dot(first_low, dgate_up, TN).astype(bf16)
            dfirst = dfirst + dot(dgate_up, gate_ups[h, c], NT)
        own_gate_up.append(links.scatter(grads, odd))

    gain_one = jnp.sum(dfirst * n1, axis=0)
    bias_one = jnp.sum(dfirst, axis=0)
    dh1 = norm_back(dfirst * gains[0], n1, s1)
    dbranch = dh1.astype(bf16)
    do = dot(dbranch, wo_t).astype(bf16)
    delta = jnp.sum(
        (do.astype(f32) * attended.astype(f32)).reshape(do.shape[0], -1, 2, HD), axis=3
    )
    dq, dk, dv = attend_back(
        q_small,
        k_all,
        v_all,
        do,
        logs.transpose(0, 2, 1),
        delta.transpose(1, 2, 0),
        seg,
        seg_all,
    )
    dkv_came = links.beside(
        jnp.concatenate(swapped_heads(dk[rows:]) + swapped_heads(dv[rows:]), axis=1).astype(bf16)
    ).astype(f32)
    dk = dk[:rows] + dkv_came[:, :width]
    dv = (dv[:rows] + dkv_came[:, width:]).astype(bf16)
    dq = rotate(dq, cosine, -sine).astype(bf16)
    dk = rotate(dk, cosine, -sine).astype(bf16)
    small_grads = jnp.stack([gain_one, gain_two, bias_one, bias_two], axis=1).astype(bf16)
    small_grads = jnp.pad(small_grads, ((0, 0), (0, 124)))
    grads = {}
    for i, c in enumerate(quarters):
        cols = slice(i * head_cols, (i + 1) * head_cols)
        grads[c] = jnp.concatenate(
            [dot(x, d[:, cols], TN).astype(bf16) for d in (dq, dk, dv)]
            + [dot(dbranch, attended[:, cols], TN).astype(bf16), small_grads],
            axis=1,
        )
    own_attn = links.scatter(grads, odd)
    input_grad = from_relative(dh1 + dot(dq, wq, NT) + dot(dk, wk, NT) + dot(dv, wv, NT))
    mine = rows // 2
    input_grad = from_sequence(
        input_grad[:mine], links.across(input_grad[mine:].astype(bf16)).astype(f32)
    )
    layer_out = from_relative(layer_out).astype(bf16)
    layer_out = from_sequence(layer_out[:mine], links.across(layer_out[mine:]))

    gate_up_grad = jnp.stack(
        [
            jnp.concatenate([own_gate_up[h][:, p * half : (p + 1) * half] for h in range(2)], axis=1)
            for p in range(2)
        ],
        axis=1,
    )
    edge = 4 * head_cols
    return (
        layer_out,
        input_grad,
        own_attn[:, : 3 * head_cols].reshape(depth, 3, head_cols),
        own_attn[:, 3 * head_cols : edge].T,
        gate_up_grad,
        own_down.T,
        own_attn[:, edge : edge + 2],
        own_attn[:, edge + 2 : edge + 4],
    )


def solution(mesh):
    in_specs = (
        P(None, ("row", "col"), None),
        P(None, ("row", "col")),
        P(None, ("row", "col")),
        P("row", None, "col"),
        P("col", "row"),
        P("row", None, "col"),
        P("col", "row"),
        P("row", None),
        P("row", None),
        P(None, ("row", "col"), None),
    )
    out_specs = (
        P(None, ("row", "col"), None),
        P(None, ("row", "col"), None),
        P("row", None, "col"),
        P("col", "row"),
        P("row", None, "col"),
        P("col", "row"),
        P("row", None),
        P("row", None),
    )
    return jax.shard_map(
        functools.partial(on_device, Links(mesh)), mesh=mesh, in_specs=in_specs, out_specs=out_specs, check_vma=False
    )
```

```python
import functools
import math

import jax
import jax.numpy as jnp
from jax import lax
from jax.experimental import pallas as pl
from jax.experimental.pallas import tpu as pltpu
from jax.sharding import PartitionSpec as P

HD = 64
PAIR = 2 * HD
QROWS = 256
epsilon = 1e-12
rope_base = 1000.0
masked_score = -1e30
f32 = jnp.float32
bf16 = jnp.bfloat16

NN = (((1,), (0,)), ((), ()))
NT = (((1,), (1,)), ((), ()))
TN = (((0,), (0,)), ((), ()))


def dot(a, b, dims=NN):
    return lax.dot_general(a, b, dims, preferred_element_type=f32)


def rope_tables(positions, width):
    half_dim = HD // 2
    freq = rope_base ** (-jnp.arange(half_dim, dtype=f32) / half_dim)
    angles = positions.astype(f32)[:, None] * freq[None, :]
    cosine, sine = jnp.cos(angles), jnp.sin(angles)
    times = width // HD
    return (
        jnp.tile(jnp.concatenate([cosine, cosine], axis=1), (1, times)),
        jnp.tile(jnp.concatenate([-sine, sine], axis=1), (1, times)),
    )


def rotated(values, cosine, sine):
    width = values.shape[1]
    lane = lax.broadcasted_iota(jnp.int32, values.shape, 1)
    up = pltpu.roll(values, width - HD // 2, 1)
    down = pltpu.roll(values, HD // 2, 1)
    return values * cosine + jnp.where(lane % HD < HD // 2, up, down) * sine


def normalize(hidden):
    centred = hidden - jnp.mean(hidden, axis=-1, keepdims=True)
    variance = jnp.mean(centred * centred, axis=-1, keepdims=True)
    inv_std = lax.rsqrt(variance + epsilon)
    return (centred * inv_std, inv_std)


def norm_back(grad_norm, normed, inv_std):
    return inv_std * (
        grad_norm
        - jnp.mean(grad_norm, axis=-1, keepdims=True)
        - normed * jnp.mean(grad_norm * normed, axis=-1, keepdims=True)
    )


BLOCKS = 10


def block_starts(width):
    half, quarter = width // 2, width // 4
    return [(0, 0), (0, half), (1, 0), (1, half), (1, half + quarter)]


def weight_copies(blocks, w_ref, sems, core):
    copies = []
    for k in range(2):
        for block, (y, row) in zip(blocks[5 * k : 5 * k + 5], block_starts(w_ref.shape[1])):
            slot = 2 * y + jnp.bitwise_xor(core, k)
            copies.append(
                pltpu.make_async_copy(
                    block, w_ref.at[slot, pl.ds(row, block.shape[0])], sems.at[slot]
                )
            )
    return copies


def start_weights(blocks, w_ref, sems, core):
    @pl.when(pl.program_id(0) == 0)
    def _():
        for copy in weight_copies(blocks, w_ref, sems, core):
            copy.start()


def wait_weights(w_ref, sems, slot):
    pltpu.make_async_copy(w_ref.at[slot], w_ref.at[slot], sems.at[slot]).wait()


def weight_scratch(blocks):
    width = 2 * blocks[0].shape[0]
    return [
        pltpu.VMEM((4, width, blocks[0].shape[1]), bf16),
        pltpu.SemaphoreType.DMA((4,)),
    ]


ANY = pl.BlockSpec(memory_space=pl.ANY)


def cost(flops, nbytes, exps=0):
    return pl.CostEstimate(flops=int(flops), bytes_accessed=int(nbytes), transcendentals=int(exps))


def whole(shape):
    return pl.BlockSpec(shape, lambda *_: (0,) * len(shape))


def qkv_kernel(core_ref, x_ref, cos_ref, sin_ref, *rest):
    blocks, (q_ref, kv_ref, wo_ref, w_ref, sems) = rest[:BLOCKS], rest[BLOCKS:]
    slot = pl.program_id(0)
    start_weights(blocks, w_ref, sems, core_ref[0])
    wait_weights(w_ref, sems, slot)
    lane = lax.broadcasted_iota(jnp.int32, (w_ref.shape[1], 4 * HD), 1)
    cosine, sine = cos_ref[...], sin_ref[...]
    part = w_ref.shape[2] // 3
    x = x_ref[...]
    q = dot(x, w_ref[slot, :, :part])
    q_ref[...] = (rotated(q, cosine, sine) * (1.0 / math.sqrt(HD))).astype(bf16)
    k = dot(x, w_ref[slot, :, part : 2 * part])
    kv_ref[:, :part] = rotated(k, cosine, sine).astype(bf16)
    kv_ref[:, part:] = dot(x, w_ref[slot, :, 2 * part :]).astype(bf16)
    out = jnp.zeros(lane.shape, f32)
    for h in range(3):
        piece = w_ref[slot, :, h * part : (h + 1) * part].astype(f32)
        piece = pltpu.roll(piece, (h + 1) * HD, 1)
        out = jnp.where(lane // HD == h, piece, out)
    wo_ref[...] = out.astype(bf16)


def qkv(core, x, cosine, sine, blocks):
    rows, width = x.shape
    part = blocks[0].shape[1] // 3
    grid_spec = pltpu.PrefetchScalarGridSpec(
        num_scalar_prefetch=1,
        grid=(4,),
        in_specs=[whole((rows, width)), whole((rows, part)), whole((rows, part))] + [ANY] * BLOCKS,
        out_specs=[
            pl.BlockSpec((rows, part), lambda i, core: (0, i)),
            pl.BlockSpec((rows, 2 * part), lambda i, core: (0, i)),
            pl.BlockSpec((width, part), lambda i, core: (0, i)),
        ],
        scratch_shapes=weight_scratch(blocks),
    )
    return pl.pallas_call(
        qkv_kernel,
        grid_spec=grid_spec,
        out_shape=[
            jax.ShapeDtypeStruct((rows, 4 * part), bf16),
            jax.ShapeDtypeStruct((rows, 8 * part), bf16),
            jax.ShapeDtypeStruct((width, 4 * part), bf16),
        ],
        cost_estimate=cost(24 * rows * width * part, 40 * width * part),
        name="qkv",
    )(core, x, cosine, sine, *blocks)


def attend_kernel(q_ref, own_ref, other_ref, segq_ref, segk_ref, out_ref, log_ref):
    rows, part = q_ref.shape
    low_half = lax.broadcasted_iota(jnp.int32, (QROWS, PAIR), 1) < HD
    keys = jnp.concatenate([own_ref[:, :part], other_ref[:, :part]], axis=0)
    values = jnp.concatenate([own_ref[:, part:], other_ref[:, part:]], axis=0)
    values_t = values.T
    for block in range(rows // QROWS):
        span = slice(block * QROWS, (block + 1) * QROWS)
        q = q_ref[span, :]
        bias = jnp.where(segk_ref[...] == segq_ref[:, span], 0.0, masked_score)
        parts = []
        for h in range(3):
            pair = slice(h // 2 * PAIR, (h // 2 + 1) * PAIR)
            mine = low_half if h % 2 == 0 else jnp.logical_not(low_half)
            masked = jnp.where(mine, q[:, pair], jnp.zeros((QROWS, PAIR), bf16))
            scores = dot(keys[:, pair], masked, NT) + bias
            top = jnp.max(scores, axis=0, keepdims=True)
            expo = jnp.exp(scores - top)
            total = jnp.sum(expo, axis=0, keepdims=True)
            out = dot(values_t[h * HD : (h + 1) * HD, :], expo.astype(bf16))
            parts.append(out / total)
            log_ref[0, h : h + 1, span] = top + jnp.log(total)
        parts.append(jnp.zeros((HD, QROWS), f32))
        out_ref[span, :] = jnp.concatenate(parts, axis=0).T.astype(bf16)


def attend(q, kv_own, kv_other, seg_q, seg_k):
    rows, width = q.shape
    part = width // 4
    keys = seg_k.shape[0]
    by_part = lambda j: (0, j)
    return pl.pallas_call(
        attend_kernel,
        grid=(4,),
        in_specs=[
            pl.BlockSpec((rows, part), by_part),
            pl.BlockSpec((rows, 2 * part), by_part),
            pl.BlockSpec((rows, 2 * part), by_part),
            whole((1, rows)),
            whole((keys, 1)),
        ],
        out_specs=[
            pl.BlockSpec((rows, part), by_part),
            pl.BlockSpec((1, 8, rows), lambda j: (j, 0, 0)),
        ],
        out_shape=[
            jax.ShapeDtypeStruct((rows, width), bf16),
            jax.ShapeDtypeStruct((4, 8, rows), f32),
        ],
        cost_estimate=cost(16 * rows * keys * width, 12 * keys * width, rows * keys * 12),
        name="attend",
    )(q, kv_own, kv_other, seg_q, seg_k)


def attend_back_kernel(
    q_ref, own_ref, other_ref, do_ref, log_ref, delta_ref, segq_ref, segk_ref, cos_ref, sin_ref,
    dq_ref, dkv_own_ref, dkv_other_ref,
):
    rows, part = q_ref.shape
    low_half = lax.broadcasted_iota(jnp.int32, (QROWS, PAIR), 1) < HD
    keys = jnp.concatenate([own_ref[:, :part], other_ref[:, :part]], axis=0)
    values = jnp.concatenate([own_ref[:, part:], other_ref[:, part:]], axis=0)
    keys_t = keys.T
    dk = [0.0, 0.0]
    dv = [0.0, 0.0]
    for block in range(rows // QROWS):
        span = slice(block * QROWS, (block + 1) * QROWS)
        q = q_ref[span, :]
        do = do_ref[span, :]
        bias = jnp.where(segk_ref[...] == segq_ref[:, span], 0.0, masked_score)
        dq = []
        for h in range(3):
            pair = slice(h // 2 * PAIR, (h // 2 + 1) * PAIR)
            mine = low_half if h % 2 == 0 else jnp.logical_not(low_half)
            zero = jnp.zeros((QROWS, PAIR), bf16)
            q_head = jnp.where(mine, q[:, pair], zero)
            do_head = jnp.where(mine, do[:, pair], zero)
            scores = dot(keys[:, pair], q_head, NT) + bias
            probs = jnp.exp(scores - log_ref[0, h : h + 1, span])
            dprobs = dot(values[:, pair], do_head, NT)
            dscores = (probs * (dprobs - delta_ref[0, h : h + 1, span])).astype(bf16)
            dv[h // 2] = dv[h // 2] + dot(probs.astype(bf16), do_head)
            dk[h // 2] = dk[h // 2] + dot(dscores, q_head)
            dq.append(dot(keys_t[h * HD : (h + 1) * HD, :], dscores))
        dq.append(jnp.zeros((HD, QROWS), f32))
        dq = (jnp.concatenate(dq, axis=0) * (1.0 / math.sqrt(HD))).T
        dq_ref[span, :] = rotated(dq, cos_ref[span, :], -sin_ref[span, :]).astype(bf16)
    for i, pieces in enumerate((dk, dv)):
        for p in range(2):
            lanes = slice(i * part + p * PAIR, i * part + (p + 1) * PAIR)
            dkv_own_ref[:, lanes] = pieces[p][:rows]
            dkv_other_ref[:, lanes] = pieces[p][rows:].astype(bf16)


def attend_back(q, kv_own, kv_other, do, logs, delta, seg_q, seg_k, cosine, sine):
    rows, width = q.shape
    part = width // 4
    keys = seg_k.shape[0]
    by_part = lambda j: (0, j)
    stat = pl.BlockSpec((1, 8, rows), lambda j: (j, 0, 0))
    return pl.pallas_call(
        attend_back_kernel,
        grid=(4,),
        in_specs=[
            pl.BlockSpec((rows, part), by_part),
            pl.BlockSpec((rows, 2 * part), by_part),
            pl.BlockSpec((rows, 2 * part), by_part),
            pl.BlockSpec((rows, part), by_part),
            stat,
            stat,
            whole((1, rows)),
            whole((keys, 1)),
            whole((rows, part)),
            whole((rows, part)),
        ],
        out_specs=[
            pl.BlockSpec((rows, part), by_part),
            pl.BlockSpec((rows, 2 * part), by_part),
            pl.BlockSpec((rows, 2 * part), by_part),
        ],
        out_shape=[
            jax.ShapeDtypeStruct((rows, width), bf16),
            jax.ShapeDtypeStruct((rows, 2 * width), f32),
            jax.ShapeDtypeStruct((rows, 2 * width), bf16),
        ],
        cost_estimate=cost(40 * rows * keys * width, 30 * keys * width, rows * keys * 12),
        name="attend_back",
    )(q, kv_own, kv_other, do, logs, delta, seg_q, seg_k, cosine, sine)


def first_kernel(x_ref, att_ref, wo_ref, norm_a_ref, norm_b_ref, n_ref, s_ref, low_ref, low_t_ref, gains_ref):
    norms = jnp.concatenate([norm_a_ref[...], norm_b_ref[...]], axis=0).astype(f32).T
    gains_ref[...] = norms[:8]
    branch = dot(att_ref[...], wo_ref[...], NT)
    normed, inv = normalize(x_ref[...].astype(f32) + branch)
    n_ref[...] = normed
    s_ref[...] = jnp.broadcast_to(inv, s_ref.shape)
    first = normed * norms[0:1] + norms[2:3]
    low_ref[...] = first.astype(bf16)
    low_t_ref[...] = first.T.astype(bf16)


def first_norm(x, attended, wo, norm_a, norm_b):
    rows, width = x.shape
    at = norm_a.shape[1] // 128 - 1
    strip = pl.BlockSpec((width // 2, 128), lambda i: (0, at))
    return pl.pallas_call(
        first_kernel,
        grid=(1,),
        in_specs=[whole(x.shape), whole(attended.shape), whole(wo.shape), strip, strip],
        out_specs=[
            whole((rows, width)), whole((rows, 128)), whole((rows, width)), whole((width, rows)), whole((8, width)),
        ],
        out_shape=[
            jax.ShapeDtypeStruct((rows, width), f32),
            jax.ShapeDtypeStruct((rows, 128), f32),
            jax.ShapeDtypeStruct((rows, width), bf16),
            jax.ShapeDtypeStruct((width, rows), bf16),
            jax.ShapeDtypeStruct((8, width), f32),
        ],
        cost_estimate=cost(2 * rows * width * wo.shape[1], 16 * rows * width),
        name="first_norm",
    )(x, attended, wo, norm_a, norm_b)


def mlp_kernel(has_base, core_ref, low_ref, *rest):
    if has_base:
        base_ref, rest = rest[0], rest[1:]
    blocks, (act_ref, feed_ref, w_ref, sems) = rest[:BLOCKS], rest[BLOCKS:]
    slot = pl.program_id(0)
    half = act_ref.shape[3]
    start_weights(blocks, w_ref, sems, core_ref[0])

    @pl.when(slot == 0)
    def _():
        feed_ref[...] = base_ref[...] if has_base else jnp.zeros_like(feed_ref)

    wait_weights(w_ref, sems, slot)

    def body(i, _):
        span = pl.ds(pl.multiple_of(i * QROWS, QROWS), QROWS)
        low = low_ref[span, :]
        gate = dot(low, w_ref[slot, :, half : 2 * half])
        up = dot(low, w_ref[slot, :, 2 * half : 3 * half])
        hidden = (gate / (1.0 + jnp.exp(-gate)) * up).astype(bf16)
        act_ref[0, 0, span, :] = gate.astype(bf16)
        act_ref[0, 1, span, :] = up.astype(bf16)
        act_ref[0, 2, span, :] = hidden
        feed_ref[span, :] += dot(hidden, w_ref[slot, :, :half], NT)
        return 0

    lax.fori_loop(0, low_ref.shape[0] // QROWS, body, 0)


def mlp(core, low, base, blocks, half):
    rows, width = low.shape
    has_base = base is not None
    extra = [base] if has_base else []
    grid_spec = pltpu.PrefetchScalarGridSpec(
        num_scalar_prefetch=1,
        grid=(4,),
        in_specs=[whole((rows, width))] + [whole((rows, width))] * has_base + [ANY] * BLOCKS,
        out_specs=[
            pl.BlockSpec((1, 3, rows, half), lambda i, core: (i, 0, 0, 0)),
            whole((rows, width)),
        ],
        scratch_shapes=weight_scratch(blocks),
    )
    return pl.pallas_call(
        functools.partial(mlp_kernel, has_base),
        grid_spec=grid_spec,
        out_shape=[
            jax.ShapeDtypeStruct((4, 3, rows, half), bf16),
            jax.ShapeDtypeStruct((rows, width), f32),
        ],
        cost_estimate=cost(24 * rows * width * half, 60 * half * width, 4 * rows * half),
        name="mlp",
    )(core, low, *extra, *blocks)


def second_kernel(n_ref, gains_ref, feed_ref, dy_ref, out_ref, dh_ref, low_ref, low_t_ref, sums_ref):
    first = n_ref[...] * gains_ref[0:1] + gains_ref[2:3]
    normed, inv = normalize(first + feed_ref[...])
    out_ref[...] = (normed * gains_ref[1:2] + gains_ref[3:4]).astype(bf16)
    dy = dy_ref[...]
    sums_ref[...] = jnp.zeros_like(sums_ref)
    sums_ref[1:2] = jnp.sum(dy * normed, axis=0, keepdims=True)
    sums_ref[3:4] = jnp.sum(dy, axis=0, keepdims=True)
    dh = norm_back(dy * gains_ref[1:2], normed, inv)
    dh_ref[...] = dh
    low_ref[...] = dh.astype(bf16)
    low_t_ref[...] = dh.T.astype(bf16)


def second_norm(n1, gains, feed, dy):
    rows, width = n1.shape
    full = whole((rows, width))
    return pl.pallas_call(
        second_kernel,
        grid=(1,),
        in_specs=[full, whole((8, width)), full, full],
        out_specs=[full, full, full, whole((width, rows)), whole((8, width))],
        out_shape=[
            jax.ShapeDtypeStruct((rows, width), bf16),
            jax.ShapeDtypeStruct((rows, width), f32),
            jax.ShapeDtypeStruct((rows, width), bf16),
            jax.ShapeDtypeStruct((width, rows), bf16),
            jax.ShapeDtypeStruct((8, width), f32),
        ],
        cost_estimate=cost(40 * rows * width, 22 * rows * width),
        name="second_norm",
    )(n1, gains, feed, dy)


def for_slot(i, core):
    return 2 * (i % 2) + jnp.bitwise_xor(core[0], 1 - i // 2)


def to_other(i, core):
    return jnp.minimum(i, 1)


def to_own(i, core):
    return jnp.maximum(i - 2, 0)


def mlp_back_kernel(core_ref, base_ref, dfeed_ref, dfeed_t_ref, low_t_ref, act_ref, *rest):
    blocks, (dfirst_ref, send_ref, keep_ref, w_ref, sems, part_ref) = rest[:BLOCKS], rest[BLOCKS:]
    step = pl.program_id(0)
    slot = for_slot(step, core_ref)
    half = act_ref.shape[3]
    start_weights(blocks, w_ref, sems, core_ref[0])

    @pl.when(step == 0)
    def _():
        dfirst_ref[...] = base_ref[...]

    wait_weights(w_ref, sems, slot)

    def body(i, _):
        span = pl.ds(pl.multiple_of(i * QROWS, QROWS), QROWS)
        dhidden = dot(dfeed_ref[span, :], w_ref[slot, :, :half])
        gate = act_ref[0, 0, span, :].astype(f32)
        up = act_ref[0, 1, span, :].astype(f32)
        sg = 1.0 / (1.0 + jnp.exp(-gate))
        dgate = dhidden * up * sg * (1.0 + gate * (1.0 - sg))
        dup = dhidden * (gate * sg)
        part_ref[span, :half] = dgate.astype(bf16)
        part_ref[span, half:] = dup.astype(bf16)
        dfirst_ref[span, :] += dot(part_ref[span, :], w_ref[slot, :, half : 3 * half], NT)
        return 0

    lax.fori_loop(0, dfeed_ref.shape[0] // QROWS, body, 0)

    def emit(out_ref):
        out_ref[0, :, half:] = dot(low_t_ref[...], part_ref[...]).astype(bf16)
        out_ref[0, :, :half] = dot(dfeed_t_ref[...], act_ref[0, 2]).astype(bf16)

    @pl.when(step < 2)
    def _():
        emit(send_ref)

    @pl.when(step >= 2)
    def _():
        emit(keep_ref)


def mlp_back(core, base, dfeed, dfeed_t, low_t, act, blocks):
    rows, width = dfeed.shape
    half = act.shape[3]
    full = whole((rows, width))
    grid_spec = pltpu.PrefetchScalarGridSpec(
        num_scalar_prefetch=1,
        grid=(4,),
        in_specs=[
            full,
            full,
            whole((width, rows)),
            whole((width, rows)),
            pl.BlockSpec((1, 3, rows, half), lambda i, core: (for_slot(i, core), 0, 0, 0)),
        ]
        + [ANY] * BLOCKS,
        out_specs=[
            full,
            pl.BlockSpec((1, width, 3 * half), lambda i, core: (to_other(i, core), 0, 0)),
            pl.BlockSpec((1, width, 3 * half), lambda i, core: (to_own(i, core), 0, 0)),
        ],
        scratch_shapes=weight_scratch(blocks) + [pltpu.VMEM((rows, 2 * half), bf16)],
    )
    return pl.pallas_call(
        mlp_back_kernel,
        grid_spec=grid_spec,
        out_shape=[
            jax.ShapeDtypeStruct((rows, width), f32),
            jax.ShapeDtypeStruct((2, width, 3 * half), bf16),
            jax.ShapeDtypeStruct((2, width, 3 * half), bf16),
        ],
        cost_estimate=cost(48 * rows * width * half, 100 * half * width, 4 * rows * half),
        name="mlp_back",
    )(core, base, dfeed, dfeed_t, low_t, act, *blocks)


def first_back_kernel(
    dfirst_ref, n_ref, s_ref, gains_ref, sums_ref, wo_ref, att_ref, dh_ref, low_t_ref, do_ref, delta_ref, cols_ref
):
    dfirst, normed = dfirst_ref[...], n_ref[...]
    rows, width = dfirst.shape
    lanes = att_ref.shape[1]
    gain_sum = jnp.sum(dfirst * normed, axis=0, keepdims=True)
    bias_sum = jnp.sum(dfirst, axis=0, keepdims=True)
    sums = sums_ref[...]
    stacked = jnp.concatenate(
        [gain_sum, sums[1:2], bias_sum, sums[3:4], jnp.zeros((124, width), f32)], axis=0
    )
    cols_ref[...] = stacked.T.astype(bf16)
    dh = norm_back(dfirst * gains_ref[0:1], normed, s_ref[:, 0:1])
    dh_ref[...] = dh
    low = dh.astype(bf16)
    low_t_ref[...] = dh.T.astype(bf16)
    do = dot(low, wo_ref[...]).astype(bf16)
    do_ref[...] = do
    prod = do.astype(f32) * att_ref[...].astype(f32)
    high = prod.astype(bf16)
    rest = (prod - high.astype(f32)).astype(bf16)
    row = lax.broadcasted_iota(jnp.int32, (32, lanes), 0)
    lane = lax.broadcasted_iota(jnp.int32, (32, lanes), 1) // HD
    pick = jnp.where(row // 8 * 4 + row % 8 == lane, 1.0, 0.0)
    pick = jnp.where(row % 8 < 4, pick, 0.0).astype(bf16)
    delta = dot(pick, high, NT) + dot(pick, rest, NT)
    for j in range(4):
        delta_ref[j] = delta[8 * j : 8 * j + 8]


def first_back(dfirst, n1, s1, gains, sums, wo, attended):
    rows, width = n1.shape
    full = whole((rows, width))
    lanes = attended.shape[1]
    return pl.pallas_call(
        first_back_kernel,
        grid=(1,),
        in_specs=[
            full, full, whole((rows, 128)), whole((8, width)), whole((8, width)), whole(wo.shape), whole(attended.shape),
        ],
        out_specs=[full, whole((width, rows)), whole((rows, lanes)), whole((4, 8, rows)), whole((width, 128))],
        out_shape=[
            jax.ShapeDtypeStruct((rows, width), f32),
            jax.ShapeDtypeStruct((width, rows), bf16),
            jax.ShapeDtypeStruct((rows, lanes), bf16),
            jax.ShapeDtypeStruct((4, 8, rows), f32),
            jax.ShapeDtypeStruct((width, 128), bf16),
        ],
        cost_estimate=cost(2 * rows * width * lanes, 20 * rows * width),
        name="first_back",
    )(dfirst, n1, s1, gains, sums, wo, attended)


def qkv_back_kernel(core_ref, dh_ref, dq_ref, own_ref, came_ref, cos_ref, sin_ref, x_t_ref, low_t_ref, att_ref, cols_ref, *rest):
    blocks, (grad_ref, send_ref, keep_ref, w_ref, sems, part_ref) = rest[:BLOCKS], rest[BLOCKS:]
    step = pl.program_id(0)
    slot = for_slot(step, core_ref)
    part = dq_ref.shape[1]
    start_weights(blocks, w_ref, sems, core_ref[0])

    @pl.when(step == 0)
    def _():
        grad_ref[...] = dh_ref[...]

    part_ref[:, :part] = dq_ref[...]
    dk = own_ref[:, :part] + came_ref[:, :part].astype(f32)
    part_ref[:, part : 2 * part] = rotated(dk, cos_ref[...], -sin_ref[...]).astype(bf16)
    dv = own_ref[:, part:] + came_ref[:, part:].astype(f32)
    part_ref[:, 2 * part :] = dv.astype(bf16)
    wait_weights(w_ref, sems, slot)
    grad_ref[...] += dot(part_ref[...], w_ref[slot], NT)
    d_out = dot(low_t_ref[...], att_ref[...])
    lane = lax.broadcasted_iota(jnp.int32, d_out.shape, 1)

    def emit(out_ref):
        for h in range(3):
            lanes = slice(h * part, (h + 1) * part)
            piece = dot(x_t_ref[...], part_ref[:, lanes])
            moved = pltpu.roll(d_out, (3 - h) * HD, 1)
            out_ref[0, :, lanes] = jnp.where(lane < 3 * HD, piece, moved).astype(bf16)
        out_ref[0, :, 3 * part :] = cols_ref[...]

    @pl.when(step < 2)
    def _():
        emit(send_ref)

    @pl.when(step >= 2)
    def _():
        emit(keep_ref)


def qkv_back(core, dh, dq, own, came, cosine, sine, x_t, low_t, attended, cols, blocks):
    rows, width = dh.shape
    part = dq.shape[1] // 4
    full = whole((rows, width))
    grid_spec = pltpu.PrefetchScalarGridSpec(
        num_scalar_prefetch=1,
        grid=(4,),
        in_specs=[
            full,
            pl.BlockSpec((rows, part), lambda i, core: (0, for_slot(i, core))),
            pl.BlockSpec((rows, 2 * part), lambda i, core: (0, for_slot(i, core))),
            pl.BlockSpec((rows, 2 * part), lambda i, core: (0, for_slot(i, core))),
            whole((rows, part)),
            whole((rows, part)),
            whole((width, rows)),
            whole((width, rows)),
            pl.BlockSpec((rows, part), lambda i, core: (0, for_slot(i, core))),
            whole((width, 128)),
        ]
        + [ANY] * BLOCKS,
        out_specs=[
            full,
            pl.BlockSpec((1, width, 3 * part + 128), lambda i, core: (to_other(i, core), 0, 0)),
            pl.BlockSpec((1, width, 3 * part + 128), lambda i, core: (to_own(i, core), 0, 0)),
        ],
        scratch_shapes=weight_scratch(blocks) + [pltpu.VMEM((rows, 3 * part), bf16)],
    )
    return pl.pallas_call(
        qkv_back_kernel,
        grid_spec=grid_spec,
        out_shape=[
            jax.ShapeDtypeStruct((rows, width), f32),
            jax.ShapeDtypeStruct((2, width, 3 * part + 128), bf16),
            jax.ShapeDtypeStruct((2, width, 3 * part + 128), bf16),
        ],
        cost_estimate=cost(52 * rows * width * part, 80 * width * part),
        name="qkv_back",
    )(core, dh, dq, own, came, cosine, sine, x_t, low_t, attended, cols, *blocks)


def factors_of(n):
    out = []
    while n > 1:
        step = 4 if n % 4 == 0 else (2 if n % 2 == 0 else n)
        out.append(step)
        n //= step
    return out


class Links:
    def __init__(self, mesh):
        self.rows = mesh.shape["row"]
        self.cols = mesh.shape["col"]
        self.digits = factors_of(self.rows // 2)

    def locate(self):
        row = lax.axis_index("row")
        col = lax.axis_index("col")
        x = row % 2
        place = row // 2
        ring = []
        for size in reversed(self.digits):
            ring.insert(0, place % size)
            place = place // size
        return ring, x, col // (self.cols // 2), col % 2

    def send(self, v, move):
        pairs = []
        for row in range(self.rows):
            for col in range(self.cols):
                place, ring = row // 2, []
                for size in reversed(self.digits):
                    ring.insert(0, place % size)
                    place //= size
                ring, x, y, k = move(ring, row % 2, col // (self.cols // 2), col % 2)
                place = 0
                for size, digit in zip(self.digits, ring):
                    place = place * size + digit % size
                pairs.append(
                    (row * self.cols + col, (place * 2 + x) * self.cols + y * (self.cols // 2) + k)
                )
        return lax.ppermute(v, ("row", "col"), pairs)

    def across(self, v):
        return self.send(v, lambda ring, x, y, k: (ring, x, 1 - y, k))

    def beside(self, v):
        return self.send(v, lambda ring, x, y, k: (ring, x, y, 1 - k))

    def along(self, v):
        return self.send(v, lambda ring, x, y, k: (ring, 1 - x, y, k))

    def shift(self, v, axis, step):
        def move(ring, x, y, k):
            moved = list(ring)
            moved[axis] = ring[axis] + step
            return moved, x, y, k

        return self.send(v, move)

    def gather(self, shard):
        block = shard
        for axis in reversed(range(len(self.digits))):
            block = jnp.concatenate(
                [block] + [self.shift(block, axis, -d) for d in range(1, self.digits[axis])], axis=0
            )
        cut = block.shape[0] // 2
        by_x, by_y = self.along(block), self.across(block)
        mine = [block, by_x, by_y, self.across(by_x[:cut]), self.along(by_y[cut:])]
        return mine + [self.beside(v) for v in mine]

    def scatter(self, send, keep):
        came = self.beside(send)
        shape = (2, 2, 2, keep.shape[1] // 4, keep.shape[2])
        keep, came = keep.reshape(shape), came.reshape(shape)

        def total(*at):
            return keep[at].astype(f32) + came[at].astype(f32)

        every = slice(None)
        by_x = self.along(total(every, 1, 1).astype(bf16))
        by_y = self.across(total(1, every, 0).astype(bf16))
        late_x = self.along((total(0, 1, 0) + by_y[1].astype(f32)).astype(bf16))
        late_y = self.across((total(1, 0, 1) + by_x[1].astype(f32)).astype(bf16))
        low = total(0, 0, 0) + by_y[0].astype(f32) + late_x.astype(f32)
        high = total(0, 0, 1) + by_x[0].astype(f32) + late_y.astype(f32)
        block = jnp.concatenate([low, high], axis=0)
        for axis in range(len(self.digits)):
            size = self.digits[axis]
            pieces = jnp.split(block, size, axis=0)
            block = pieces[0]
            for d in range(1, size):
                block = block + self.shift(pieces[d].astype(bf16), axis, d).astype(f32)
        return block


def relative_order(links, depth):
    ring, x, _, _ = links.locate()
    where = lax.broadcasted_iota(jnp.int32, (1, links.rows * depth), 1)
    block, inside = where // depth, where % depth
    steps = links.rows // 2
    place = block % steps
    parts = []
    for axis in reversed(range(len(links.digits))):
        size = links.digits[axis]
        parts.insert(0, (place % size + ring[axis]) % size)
        place = place // size
    row = jnp.zeros_like(block)
    for size, part in zip(links.digits, parts):
        row = row * size + part
    row = row * 2 + jnp.bitwise_xor(x, block // steps)
    return row * depth + inside


def on_device(
    links, tokens, segments, positions, w_qkv, w_out, w_gate_up, w_down, norm_gain, norm_bias, cotangent
):
    ring, x_place, side, core = links.locate()
    core = core.astype(jnp.int32)[None]
    depth = w_qkv.shape[0]
    width = tokens.shape[2]
    head_cols = w_qkv.shape[2]
    hid = w_gate_up.shape[2]
    half = hid // 2
    rows = 2 * tokens.shape[1]
    mine = rows // 2
    part = head_cols + HD

    source = relative_order(links, depth)
    swap = (lax.broadcasted_iota(jnp.int32, (width, width), 0) == source).astype(bf16)

    def split(v):
        high = v.astype(bf16)
        return high, (v - high.astype(f32)).astype(bf16)

    def own_and_other(v):
        own = lax.dynamic_index_in_dim(v, side, 0, keepdims=False)
        return own, lax.dynamic_index_in_dim(v, 1 - side, 0, keepdims=False)

    def from_sequence(own, came):
        first = side == 0
        return jnp.stack([jnp.where(first, own, came), jnp.where(first, came, own)], axis=0)

    out_t = w_out.T
    attn_shard = jnp.concatenate(
        sum(
            [[w_qkv[:, p], out_t[:, p * HD : (p + 1) * HD]] for p in range(3)],
            [],
        ),
        axis=1,
    )
    norms = jnp.concatenate([norm_gain, norm_bias], axis=1)
    norms = jnp.pad(norms, ((0, 0), (0, 128 - norms.shape[1])))
    down_t = w_down.T
    mlp_shards = []
    for h in range(2):
        cols = slice(h * half, (h + 1) * half)
        pieces = [down_t[:, cols], w_gate_up[:, 0, cols], w_gate_up[:, 1, cols]]
        mlp_shards.append(jnp.concatenate(pieces + ([norms] if h == 0 else []), axis=1))

    tokens_own, tokens_other = own_and_other(tokens)
    tokens_came = links.across(tokens_other)
    small_own, small_other = own_and_other(jnp.stack([segments, positions], axis=1))
    small_came = links.across(small_other)
    attn_w = links.gather(attn_shard)
    mlp_w = [links.gather(s) for s in mlp_shards]

    x_abs = jnp.concatenate([tokens_own, tokens_came], axis=0)
    x = dot(x_abs, swap).astype(bf16)
    x_t = lax.dot_general(swap, x_abs, (((0,), (1,)), ((), ())), preferred_element_type=f32).astype(bf16)
    small = jnp.concatenate([small_own, small_came], axis=1)
    seg = small[0]
    seg_all = jnp.concatenate([seg, links.beside(seg)], axis=0)[:, None]
    seg = seg[None, :]
    cosine, sine = rope_tables(small[1], part)
    dy_own, dy_other = own_and_other(cotangent)
    dy_came = links.across(dy_other.astype(bf16))
    high, low = split(dy_own)
    dy = jnp.concatenate([dot(high, swap) + dot(low, swap), dot(dy_came, swap)], axis=0)

    q, kv, wo = qkv(core, x, cosine, sine, attn_w)
    kv_came = links.beside(kv)
    attended, logs = attend(q, kv, kv_came, seg, seg_all)
    n1, s1, low1, low1_t, gains = first_norm(x, attended, wo, mlp_w[0][0], mlp_w[0][1])
    act_a, feed = mlp(core, low1, None, mlp_w[0], half)
    act_b, feed = mlp(core, low1, feed, mlp_w[1], half)
    layer_out, dh2, dfeed, dfeed_t, sums = second_norm(n1, gains, feed, dy)
    layer_out = dot(layer_out, swap, NT).astype(bf16)
    layer_out = from_sequence(layer_out[:mine], links.across(layer_out[mine:]))

    dfirst, send, keep = mlp_back(core, dh2, dfeed, dfeed_t, low1_t, act_a, mlp_w[0])
    own_mlp = [links.scatter(send, keep)]
    dfirst, send, keep = mlp_back(core, dfirst, dfeed, dfeed_t, low1_t, act_b, mlp_w[1])
    own_mlp.append(links.scatter(send, keep))
    dh1, low_t, do, delta, cols = first_back(dfirst, n1, s1, gains, sums, wo, attended)
    dq, dkv_own, dkv_other = attend_back(q, kv, kv_came, do, logs, delta, seg, seg_all, cosine, sine)
    dkv_came = links.beside(dkv_other)
    grad, send, keep = qkv_back(
        core, dh1, dq, dkv_own, dkv_came, cosine, sine, x_t, low_t, attended, cols, attn_w
    )
    own_attn = links.scatter(send, keep)
    high, low = split(grad)
    grad = dot(high, swap, NT) + dot(low, swap, NT)
    input_grad = from_sequence(grad[:mine], links.across(grad[mine:].astype(bf16)).astype(f32))

    grad_down = jnp.concatenate([v[:, :half] for v in own_mlp], axis=1).T
    grad_gate_up = jnp.stack(
        [
            jnp.concatenate([v[:, (p + 1) * half : (p + 2) * half] for v in own_mlp], axis=1)
            for p in range(2)
        ],
        axis=1,
    )
    thirds = [own_attn[:, p * part : (p + 1) * part] for p in range(3)]
    edge = 3 * part
    return (
        layer_out,
        input_grad,
        jnp.stack([v[:, :head_cols] for v in thirds], axis=1),
        jnp.concatenate([v[:, head_cols:] for v in thirds], axis=1).T,
        grad_gate_up,
        grad_down,
        own_attn[:, edge : edge + 2],
        own_attn[:, edge + 2 : edge + 4],
    )


def solution(mesh):
    in_specs = (
        P(None, ("row", "col"), None),
        P(None, ("row", "col")),
        P(None, ("row", "col")),
        P("row", None, "col"),
        P("col", "row"),
        P("row", None, "col"),
        P("col", "row"),
        P("row", None),
        P("row", None),
        P(None, ("row", "col"), None),
    )
    out_specs = (
        P(None, ("row", "col"), None),
        P(None, ("row", "col"), None),
        P("row", None, "col"),
        P("col", "row"),
        P("row", None, "col"),
        P("col", "row"),
        P("row", None),
        P("row", None),
    )
    return jax.shard_map(
        functools.partial(on_device, Links(mesh)), mesh=mesh, in_specs=in_specs, out_specs=out_specs, check_vma=False
    )
```

```python
import functools
import math

import jax
import jax.numpy as jnp
from jax import lax
from jax.experimental import pallas as pl
from jax.experimental.pallas import tpu as pltpu
from jax.sharding import PartitionSpec as P

HD = 64
PAIR = 2 * HD
QROWS = 256
epsilon = 1e-12
rope_base = 1000.0
masked_score = -1e30
f32 = jnp.float32
bf16 = jnp.bfloat16

NN = (((1,), (0,)), ((), ()))
NT = (((1,), (1,)), ((), ()))
TN = (((0,), (0,)), ((), ()))


def dot(a, b, dims=NN):
    return lax.dot_general(a, b, dims, preferred_element_type=f32)


def rope_tables(positions, width):
    half_dim = HD // 2
    freq = rope_base ** (-jnp.arange(half_dim, dtype=f32) / half_dim)
    angles = positions.astype(f32)[:, None] * freq[None, :]
    cosine, sine = jnp.cos(angles), jnp.sin(angles)
    times = width // HD
    return (
        jnp.tile(jnp.concatenate([cosine, cosine], axis=1), (1, times)),
        jnp.tile(jnp.concatenate([-sine, sine], axis=1), (1, times)),
    )


def rotated(values, cosine, sine):
    width = values.shape[1]
    lane = lax.broadcasted_iota(jnp.int32, values.shape, 1)
    up = pltpu.roll(values, width - HD // 2, 1)
    down = pltpu.roll(values, HD // 2, 1)
    return values * cosine + jnp.where(lane % HD < HD // 2, up, down) * sine


def normalize(hidden):
    centred = hidden - jnp.mean(hidden, axis=-1, keepdims=True)
    variance = jnp.mean(centred * centred, axis=-1, keepdims=True)
    inv_std = lax.rsqrt(variance + epsilon)
    return (centred * inv_std, inv_std)


def norm_back(grad_norm, normed, inv_std):
    return inv_std * (
        grad_norm
        - jnp.mean(grad_norm, axis=-1, keepdims=True)
        - normed * jnp.mean(grad_norm * normed, axis=-1, keepdims=True)
    )


BLOCKS = 5


def block_starts(width):
    half, quarter = width // 2, width // 4
    return [(0, 0), (0, half), (1, 0), (1, half), (1, half + quarter)]


def start_weights(blocks, w_ref, sems):
    @pl.when(pl.program_id(0) == 0)
    def _():
        for i, block in enumerate(blocks):
            y, row = block_starts(w_ref.shape[1])[i % BLOCKS]
            slot = i // BLOCKS * 2 + y
            pltpu.make_async_copy(
                block, w_ref.at[slot, pl.ds(row, block.shape[0])], sems.at[slot]
            ).start()


def wait_weights(w_ref, sems, slot):
    pltpu.make_async_copy(w_ref.at[slot], w_ref.at[slot], sems.at[slot]).wait()


def weight_scratch(blocks):
    width = 2 * blocks[0].shape[0]
    slots = 2 * len(blocks) // BLOCKS
    return [
        pltpu.VMEM((slots, width, blocks[0].shape[1]), bf16),
        pltpu.SemaphoreType.DMA((slots,)),
    ]


ANY = pl.BlockSpec(memory_space=pl.ANY)


def cost(flops, nbytes, exps=0):
    return pl.CostEstimate(flops=int(flops), bytes_accessed=int(nbytes), transcendentals=int(exps))


def whole(shape):
    return pl.BlockSpec(shape, lambda *_: (0,) * len(shape))


def qkv_kernel(x_ref, cos_ref, sin_ref, *rest):
    blocks, (q_ref, kv_ref, wo_ref, w_ref, sems) = rest[: 2 * BLOCKS], rest[2 * BLOCKS :]
    slot = pl.program_id(0)
    start_weights(blocks, w_ref, sems)
    wait_weights(w_ref, sems, slot)
    lane = lax.broadcasted_iota(jnp.int32, (w_ref.shape[1], 4 * HD), 1)
    cosine, sine = cos_ref[...], sin_ref[...]
    part = w_ref.shape[2] // 3
    x = x_ref[...]
    q = dot(x, w_ref[slot, :, :part])
    q_ref[...] = (rotated(q, cosine, sine) * (1.0 / math.sqrt(HD))).astype(bf16)
    k = dot(x, w_ref[slot, :, part : 2 * part])
    kv_ref[:, :part] = rotated(k, cosine, sine).astype(bf16)
    kv_ref[:, part:] = dot(x, w_ref[slot, :, 2 * part :]).astype(bf16)
    out = jnp.zeros(lane.shape, f32)
    for h in range(3):
        piece = w_ref[slot, :, h * part : (h + 1) * part].astype(f32)
        piece = pltpu.roll(piece, (h + 1) * HD, 1)
        out = jnp.where(lane // HD == h, piece, out)
    wo_ref[...] = out.astype(bf16)


def qkv(x, cosine, sine, blocks):
    rows, width = x.shape
    part = blocks[0].shape[1] // 3
    return pl.pallas_call(
        qkv_kernel,
        grid=(4,),
        in_specs=[whole((rows, width)), whole((rows, part)), whole((rows, part))] + [ANY] * len(blocks),
        out_specs=[
            pl.BlockSpec((rows, part), lambda i: (0, i)),
            pl.BlockSpec((rows, 2 * part), lambda i: (0, i)),
            pl.BlockSpec((width, part), lambda i: (0, i)),
        ],
        scratch_shapes=weight_scratch(blocks),
        out_shape=[
            jax.ShapeDtypeStruct((rows, 4 * part), bf16),
            jax.ShapeDtypeStruct((rows, 8 * part), bf16),
            jax.ShapeDtypeStruct((width, 4 * part), bf16),
        ],
        cost_estimate=cost(24 * rows * width * part, 40 * width * part),
        name="qkv",
    )(x, cosine, sine, *blocks)


def attend_kernel(q_ref, own_ref, other_ref, segq_ref, segk_ref, out_ref, log_ref):
    rows, part = q_ref.shape
    low_half = lax.broadcasted_iota(jnp.int32, (QROWS, PAIR), 1) < HD
    keys = jnp.concatenate([own_ref[:, :part], other_ref[:, :part]], axis=0)
    values = jnp.concatenate([own_ref[:, part:], other_ref[:, part:]], axis=0)
    values_t = values.T
    for block in range(rows // QROWS):
        span = slice(block * QROWS, (block + 1) * QROWS)
        q = q_ref[span, :]
        bias = jnp.where(segk_ref[...] == segq_ref[:, span], 0.0, masked_score)
        parts = []
        for h in range(3):
            pair = slice(h // 2 * PAIR, (h // 2 + 1) * PAIR)
            mine = low_half if h % 2 == 0 else jnp.logical_not(low_half)
            masked = jnp.where(mine, q[:, pair], jnp.zeros((QROWS, PAIR), bf16))
            scores = dot(keys[:, pair], masked, NT) + bias
            top = jnp.max(scores, axis=0, keepdims=True)
            expo = jnp.exp(scores - top)
            total = jnp.sum(expo, axis=0, keepdims=True)
            out = dot(values_t[h * HD : (h + 1) * HD, :], expo.astype(bf16))
            parts.append(out / total)
            log_ref[0, h : h + 1, span] = top + jnp.log(total)
        parts.append(jnp.zeros((HD, QROWS), f32))
        out_ref[span, :] = jnp.concatenate(parts, axis=0).T.astype(bf16)


def attend(which, q, kv_own, kv_other, seg_q, seg_k):
    rows, width = q.shape
    part = width // 4
    width = width // 2
    keys = seg_k.shape[0]
    by_part = lambda j: (0, 2 * which + j)
    flipped = lambda j: (0, 2 * (1 - which) + j)
    out_part = lambda j: (0, j)
    return pl.pallas_call(
        attend_kernel,
        grid=(2,),
        in_specs=[
            pl.BlockSpec((rows, part), by_part),
            pl.BlockSpec((rows, 2 * part), by_part),
            pl.BlockSpec((rows, 2 * part), flipped),
            whole((1, rows)),
            whole((keys, 1)),
        ],
        out_specs=[
            pl.BlockSpec((rows, part), out_part),
            pl.BlockSpec((1, 8, rows), lambda j: (j, 0, 0)),
        ],
        out_shape=[
            jax.ShapeDtypeStruct((rows, width), bf16),
            jax.ShapeDtypeStruct((2, 8, rows), f32),
        ],
        cost_estimate=cost(16 * rows * keys * width, 12 * keys * width, rows * keys * 6),
        name="attend",
    )(q, kv_own, kv_other, seg_q, seg_k)


def attend_back_kernel(
    q_ref, own_ref, other_ref, do_ref, log_ref, delta_ref, segq_ref, segk_ref, cos_ref, sin_ref,
    dq_ref, dkv_own_ref, dkv_other_ref,
):
    rows, part = q_ref.shape
    low_half = lax.broadcasted_iota(jnp.int32, (QROWS, PAIR), 1) < HD
    keys = jnp.concatenate([own_ref[:, :part], other_ref[:, :part]], axis=0)
    values = jnp.concatenate([own_ref[:, part:], other_ref[:, part:]], axis=0)
    keys_t = keys.T
    dk = [0.0, 0.0]
    dv = [0.0, 0.0]
    for block in range(rows // QROWS):
        span = slice(block * QROWS, (block + 1) * QROWS)
        q = q_ref[span, :]
        do = do_ref[span, :]
        bias = jnp.where(segk_ref[...] == segq_ref[:, span], 0.0, masked_score)
        dq = []
        for h in range(3):
            pair = slice(h // 2 * PAIR, (h // 2 + 1) * PAIR)
            mine = low_half if h % 2 == 0 else jnp.logical_not(low_half)
            zero = jnp.zeros((QROWS, PAIR), bf16)
            q_head = jnp.where(mine, q[:, pair], zero)
            do_head = jnp.where(mine, do[:, pair], zero)
            scores = dot(keys[:, pair], q_head, NT) + bias
            probs = jnp.exp(scores - log_ref[0, h : h + 1, span])
            dprobs = dot(values[:, pair], do_head, NT)
            dscores = (probs * (dprobs - delta_ref[0, h : h + 1, span])).astype(bf16)
            dv[h // 2] = dv[h // 2] + dot(probs.astype(bf16), do_head)
            dk[h // 2] = dk[h // 2] + dot(dscores, q_head)
            dq.append(dot(keys_t[h * HD : (h + 1) * HD, :], dscores))
        dq.append(jnp.zeros((HD, QROWS), f32))
        dq = (jnp.concatenate(dq, axis=0) * (1.0 / math.sqrt(HD))).T
        dq_ref[span, :] = rotated(dq, cos_ref[span, :], -sin_ref[span, :]).astype(bf16)
    for i, pieces in enumerate((dk, dv)):
        for p in range(2):
            lanes = slice(i * part + p * PAIR, i * part + (p + 1) * PAIR)
            dkv_own_ref[:, lanes] = pieces[p][:rows]
            dkv_other_ref[:, lanes] = pieces[p][rows:].astype(bf16)


def attend_back(which, q, kv_own, kv_other, do, logs, delta, seg_q, seg_k, cosine, sine):
    rows, width = q.shape
    part = width // 4
    width = width // 2
    keys = seg_k.shape[0]
    by_part = lambda j: (0, 2 * which + j)
    flipped = lambda j: (0, 2 * (1 - which) + j)
    out_part = lambda j: (0, j)
    return pl.pallas_call(
        attend_back_kernel,
        grid=(2,),
        in_specs=[
            pl.BlockSpec((rows, part), by_part),
            pl.BlockSpec((rows, 2 * part), by_part),
            pl.BlockSpec((rows, 2 * part), flipped),
            pl.BlockSpec((rows, part), by_part),
            pl.BlockSpec((1, 8, rows), lambda j: (j, 0, 0)),
            pl.BlockSpec((1, 8, rows), lambda j: (2 * which + j, 0, 0)),
            whole((1, rows)),
            whole((keys, 1)),
            whole((rows, part)),
            whole((rows, part)),
        ],
        out_specs=[
            pl.BlockSpec((rows, part), out_part),
            pl.BlockSpec((rows, 2 * part), out_part),
            pl.BlockSpec((rows, 2 * part), out_part),
        ],
        out_shape=[
            jax.ShapeDtypeStruct((rows, width), bf16),
            jax.ShapeDtypeStruct((rows, 2 * width), f32),
            jax.ShapeDtypeStruct((rows, 2 * width), bf16),
        ],
        cost_estimate=cost(40 * rows * keys * width, 30 * keys * width, rows * keys * 6),
        name="attend_back",
    )(q, kv_own, kv_other, do, logs, delta, seg_q, seg_k, cosine, sine)


def first_kernel(x_ref, att_own_ref, att_other_ref, wo_ref, norm_a_ref, norm_b_ref, n_ref, s_ref, low_ref, low_t_ref, gains_ref):
    norms = jnp.concatenate([norm_a_ref[...], norm_b_ref[...]], axis=0).astype(f32).T
    gains_ref[...] = norms[:8]
    lanes = att_own_ref.shape[1]
    branch = dot(att_own_ref[...], wo_ref[:, :lanes], NT) + dot(att_other_ref[...], wo_ref[:, lanes:], NT)
    normed, inv = normalize(x_ref[...].astype(f32) + branch)
    n_ref[...] = normed
    s_ref[...] = jnp.broadcast_to(inv, s_ref.shape)
    first = normed * norms[0:1] + norms[2:3]
    low_ref[...] = first.astype(bf16)
    low_t_ref[...] = first.T.astype(bf16)


def first_norm(x, att_own, att_other, wo, norm_a, norm_b):
    rows, width = x.shape
    at = norm_a.shape[1] // 128 - 1
    strip = pl.BlockSpec((width // 2, 128), lambda i: (0, at))
    return pl.pallas_call(
        first_kernel,
        grid=(1,),
        in_specs=[
            whole(x.shape), whole(att_own.shape), whole(att_own.shape), whole(wo.shape), strip, strip,
        ],
        out_specs=[
            whole((rows, width)), whole((rows, 128)), whole((rows, width)), whole((width, rows)), whole((8, width)),
        ],
        out_shape=[
            jax.ShapeDtypeStruct((rows, width), f32),
            jax.ShapeDtypeStruct((rows, 128), f32),
            jax.ShapeDtypeStruct((rows, width), bf16),
            jax.ShapeDtypeStruct((width, rows), bf16),
            jax.ShapeDtypeStruct((8, width), f32),
        ],
        cost_estimate=cost(2 * rows * width * wo.shape[1], 16 * rows * width),
        name="first_norm",
    )(x, att_own, att_other, wo, norm_a, norm_b)


def mlp_kernel(has_base, low_ref, *rest):
    if has_base:
        base_ref, rest = rest[0], rest[1:]
    blocks, (act_ref, feed_ref, w_ref, sems) = rest[: 2 * BLOCKS], rest[2 * BLOCKS :]
    slot = pl.program_id(0)
    half = act_ref.shape[3]
    start_weights(blocks, w_ref, sems)

    @pl.when(slot == 0)
    def _():
        feed_ref[...] = base_ref[...] if has_base else jnp.zeros_like(feed_ref)

    wait_weights(w_ref, sems, slot)

    def body(i, _):
        span = pl.ds(pl.multiple_of(i * QROWS, QROWS), QROWS)
        low = low_ref[span, :]
        gate = dot(low, w_ref[slot, :, half : 2 * half])
        up = dot(low, w_ref[slot, :, 2 * half : 3 * half])
        hidden = (gate / (1.0 + jnp.exp(-gate)) * up).astype(bf16)
        act_ref[0, 0, span, :] = gate.astype(bf16)
        act_ref[0, 1, span, :] = up.astype(bf16)
        act_ref[0, 2, span, :] = hidden
        feed_ref[span, :] += dot(hidden, w_ref[slot, :, :half], NT)
        return 0

    lax.fori_loop(0, low_ref.shape[0] // QROWS, body, 0)


def mlp(low, base, blocks, half):
    rows, width = low.shape
    has_base = base is not None
    extra = [base] if has_base else []
    return pl.pallas_call(
        functools.partial(mlp_kernel, has_base),
        grid=(4,),
        in_specs=[whole((rows, width))] * (1 + has_base) + [ANY] * len(blocks),
        out_specs=[
            pl.BlockSpec((1, 3, rows, half), lambda i: (i, 0, 0, 0)),
            whole((rows, width)),
        ],
        scratch_shapes=weight_scratch(blocks),
        out_shape=[
            jax.ShapeDtypeStruct((4, 3, rows, half), bf16),
            jax.ShapeDtypeStruct((rows, width), f32),
        ],
        cost_estimate=cost(24 * rows * width * half, 60 * half * width, 4 * rows * half),
        name="mlp",
    )(low, *extra, *blocks)


def second_kernel(n_ref, gains_ref, feed_ref, dy_ref, out_ref, dh_ref, low_ref, low_t_ref, sums_ref):
    first = n_ref[...] * gains_ref[0:1] + gains_ref[2:3]
    normed, inv = normalize(first + feed_ref[...])
    out_ref[...] = (normed * gains_ref[1:2] + gains_ref[3:4]).astype(bf16)
    dy = dy_ref[...]
    sums_ref[...] = jnp.zeros_like(sums_ref)
    sums_ref[1:2] = jnp.sum(dy * normed, axis=0, keepdims=True)
    sums_ref[3:4] = jnp.sum(dy, axis=0, keepdims=True)
    dh = norm_back(dy * gains_ref[1:2], normed, inv)
    dh_ref[...] = dh
    low_ref[...] = dh.astype(bf16)
    low_t_ref[...] = dh.T.astype(bf16)


def second_norm(n1, gains, feed, dy):
    rows, width = n1.shape
    full = whole((rows, width))
    return pl.pallas_call(
        second_kernel,
        grid=(1,),
        in_specs=[full, whole((8, width)), full, full],
        out_specs=[full, full, full, whole((width, rows)), whole((8, width))],
        out_shape=[
            jax.ShapeDtypeStruct((rows, width), bf16),
            jax.ShapeDtypeStruct((rows, width), f32),
            jax.ShapeDtypeStruct((rows, width), bf16),
            jax.ShapeDtypeStruct((width, rows), bf16),
            jax.ShapeDtypeStruct((8, width), f32),
        ],
        cost_estimate=cost(40 * rows * width, 22 * rows * width),
        name="second_norm",
    )(n1, gains, feed, dy)


def mlp_back_kernel(base_ref, dfeed_ref, dfeed_t_ref, low_t_ref, act_ref, *rest):
    blocks, (dfirst_ref, grad_ref, w_ref, sems, part_ref) = rest[:BLOCKS], rest[BLOCKS:]
    slot = pl.program_id(0)
    half = act_ref.shape[3]
    start_weights(blocks, w_ref, sems)

    @pl.when(slot == 0)
    def _():
        dfirst_ref[...] = base_ref[...]

    wait_weights(w_ref, sems, slot)

    def body(i, _):
        span = pl.ds(pl.multiple_of(i * QROWS, QROWS), QROWS)
        dhidden = dot(dfeed_ref[span, :], w_ref[slot, :, :half])
        gate = act_ref[0, 0, span, :].astype(f32)
        up = act_ref[0, 1, span, :].astype(f32)
        sg = 1.0 / (1.0 + jnp.exp(-gate))
        dgate = dhidden * up * sg * (1.0 + gate * (1.0 - sg))
        dup = dhidden * (gate * sg)
        part_ref[span, :half] = dgate.astype(bf16)
        part_ref[span, half:] = dup.astype(bf16)
        dfirst_ref[span, :] += dot(part_ref[span, :], w_ref[slot, :, half : 3 * half], NT)
        return 0

    lax.fori_loop(0, dfeed_ref.shape[0] // QROWS, body, 0)
    grad_ref[0, :, half:] = dot(low_t_ref[...], part_ref[...]).astype(bf16)
    grad_ref[0, :, :half] = dot(dfeed_t_ref[...], act_ref[0, 2]).astype(bf16)


def mlp_back(which, base, dfeed, dfeed_t, low_t, act, blocks):
    rows, width = dfeed.shape
    half = act.shape[3]
    blocks = blocks[which * BLOCKS : (which + 1) * BLOCKS]
    full = whole((rows, width))
    return pl.pallas_call(
        mlp_back_kernel,
        grid=(2,),
        in_specs=[
            full,
            full,
            whole((width, rows)),
            whole((width, rows)),
            pl.BlockSpec((1, 3, rows, half), lambda i: (2 * which + i, 0, 0, 0)),
        ]
        + [ANY] * BLOCKS,
        out_specs=[full, pl.BlockSpec((1, width, 3 * half), lambda i: (i, 0, 0))],
        scratch_shapes=weight_scratch(blocks) + [pltpu.VMEM((rows, 2 * half), bf16)],
        out_shape=[
            jax.ShapeDtypeStruct((rows, width), f32),
            jax.ShapeDtypeStruct((2, width, 3 * half), bf16),
        ],
        cost_estimate=cost(24 * rows * width * half, 50 * half * width, 2 * rows * half),
        name="mlp_back",
    )(base, dfeed, dfeed_t, low_t, act, *blocks)


def first_back_kernel(
    dfirst_ref, n_ref, s_ref, gains_ref, sums_ref, wo_ref, att_own_ref, att_other_ref,
    dh_ref, low_t_ref, do_ref, delta_ref, cols_ref,
):
    dfirst, normed = dfirst_ref[...], n_ref[...]
    rows, width = dfirst.shape
    lanes = wo_ref.shape[1]
    gain_sum = jnp.sum(dfirst * normed, axis=0, keepdims=True)
    bias_sum = jnp.sum(dfirst, axis=0, keepdims=True)
    sums = sums_ref[...]
    stacked = jnp.concatenate(
        [gain_sum, sums[1:2], bias_sum, sums[3:4], jnp.zeros((124, width), f32)], axis=0
    )
    cols_ref[...] = stacked.T.astype(bf16)
    dh = norm_back(dfirst * gains_ref[0:1], normed, s_ref[:, 0:1])
    dh_ref[...] = dh
    low = dh.astype(bf16)
    low_t_ref[...] = dh.T.astype(bf16)
    do = dot(low, wo_ref[...]).astype(bf16)
    do_ref[...] = do
    attended = jnp.concatenate([att_own_ref[...], att_other_ref[...]], axis=1)
    prod = do.astype(f32) * attended.astype(f32)
    high = prod.astype(bf16)
    rest = (prod - high.astype(f32)).astype(bf16)
    row = lax.broadcasted_iota(jnp.int32, (32, lanes), 0)
    lane = lax.broadcasted_iota(jnp.int32, (32, lanes), 1) // HD
    pick = jnp.where(row // 8 * 4 + row % 8 == lane, 1.0, 0.0)
    pick = jnp.where(row % 8 < 4, pick, 0.0).astype(bf16)
    delta = dot(pick, high, NT) + dot(pick, rest, NT)
    for j in range(4):
        delta_ref[j] = delta[8 * j : 8 * j + 8]


def first_back(dfirst, n1, s1, gains, sums, wo, att_own, att_other):
    rows, width = n1.shape
    full = whole((rows, width))
    lanes = wo.shape[1]
    return pl.pallas_call(
        first_back_kernel,
        grid=(1,),
        in_specs=[
            full, full, whole((rows, 128)), whole((8, width)), whole((8, width)),
            whole(wo.shape), whole(att_own.shape), whole(att_own.shape),
        ],
        out_specs=[full, whole((width, rows)), whole((rows, lanes)), whole((4, 8, rows)), whole((width, 128))],
        out_shape=[
            jax.ShapeDtypeStruct((rows, width), f32),
            jax.ShapeDtypeStruct((width, rows), bf16),
            jax.ShapeDtypeStruct((rows, lanes), bf16),
            jax.ShapeDtypeStruct((4, 8, rows), f32),
            jax.ShapeDtypeStruct((width, 128), bf16),
        ],
        cost_estimate=cost(2 * rows * width * lanes, 20 * rows * width),
        name="first_back",
    )(dfirst, n1, s1, gains, sums, wo, att_own, att_other)


def qkv_back_kernel(
    base_ref, dq_ref, own_ref, came_ref, cos_ref, sin_ref, x_t_ref, low_t_ref, att_ref, cols_ref, *rest
):
    blocks, (sum_ref, grad_ref, w_ref, sems, part_ref) = rest[:BLOCKS], rest[BLOCKS:]
    slot = pl.program_id(0)
    part = dq_ref.shape[1]
    start_weights(blocks, w_ref, sems)

    @pl.when(slot == 0)
    def _():
        sum_ref[...] = base_ref[...]

    part_ref[:, :part] = dq_ref[...]
    dk = own_ref[:, :part] + came_ref[:, :part].astype(f32)
    part_ref[:, part : 2 * part] = rotated(dk, cos_ref[...], -sin_ref[...]).astype(bf16)
    dv = own_ref[:, part:] + came_ref[:, part:].astype(f32)
    part_ref[:, 2 * part :] = dv.astype(bf16)
    wait_weights(w_ref, sems, slot)
    sum_ref[...] += dot(part_ref[...], w_ref[slot], NT)
    d_out = dot(low_t_ref[...], att_ref[...])
    lane = lax.broadcasted_iota(jnp.int32, d_out.shape, 1)
    for h in range(3):
        lanes = slice(h * part, (h + 1) * part)
        piece = dot(x_t_ref[...], part_ref[:, lanes])
        moved = pltpu.roll(d_out, (3 - h) * HD, 1)
        grad_ref[0, :, lanes] = jnp.where(lane < 3 * HD, piece, moved).astype(bf16)
    grad_ref[0, :, 3 * part :] = cols_ref[...]


def qkv_back(which, base, dq, own, came, cosine, sine, x_t, low_t, attended, cols, blocks):
    rows, width = base.shape
    part = dq.shape[1] // 2
    blocks = blocks[which * BLOCKS : (which + 1) * BLOCKS]
    full = whole((rows, width))
    by_part = lambda i: (0, i)
    return pl.pallas_call(
        qkv_back_kernel,
        grid=(2,),
        in_specs=[
            full,
            pl.BlockSpec((rows, part), by_part),
            pl.BlockSpec((rows, 2 * part), by_part),
            pl.BlockSpec((rows, 2 * part), by_part),
            whole((rows, part)),
            whole((rows, part)),
            whole((width, rows)),
            whole((width, rows)),
            pl.BlockSpec((rows, part), by_part),
            whole((width, 128)),
        ]
        + [ANY] * BLOCKS,
        out_specs=[full, pl.BlockSpec((1, width, 3 * part + 128), lambda i: (i, 0, 0))],
        scratch_shapes=weight_scratch(blocks) + [pltpu.VMEM((rows, 3 * part), bf16)],
        out_shape=[
            jax.ShapeDtypeStruct((rows, width), f32),
            jax.ShapeDtypeStruct((2, width, 3 * part + 128), bf16),
        ],
        cost_estimate=cost(26 * rows * width * part, 40 * width * part),
        name="qkv_back",
    )(base, dq, own, came, cosine, sine, x_t, low_t, attended, cols, *blocks)


def factors_of(n):
    out = []
    while n > 1:
        step = 4 if n % 4 == 0 else (2 if n % 2 == 0 else n)
        out.append(step)
        n //= step
    return out


class Links:
    def __init__(self, mesh):
        self.rows = mesh.shape["row"]
        self.cols = mesh.shape["col"]
        self.digits = factors_of(self.rows // 2)

    def locate(self):
        row = lax.axis_index("row")
        col = lax.axis_index("col")
        x = row % 2
        place = row // 2
        ring = []
        for size in reversed(self.digits):
            ring.insert(0, place % size)
            place = place // size
        return ring, x, col // (self.cols // 2), col % 2

    def send(self, v, move):
        pairs = []
        for row in range(self.rows):
            for col in range(self.cols):
                place, ring = row // 2, []
                for size in reversed(self.digits):
                    ring.insert(0, place % size)
                    place //= size
                ring, x, y, k = move(ring, row % 2, col // (self.cols // 2), col % 2)
                place = 0
                for size, digit in zip(self.digits, ring):
                    place = place * size + digit % size
                pairs.append(
                    (row * self.cols + col, (place * 2 + x) * self.cols + y * (self.cols // 2) + k)
                )
        return lax.ppermute(v, ("row", "col"), pairs)

    def across(self, v):
        return self.send(v, lambda ring, x, y, k: (ring, x, 1 - y, k))

    def beside(self, v):
        return self.send(v, lambda ring, x, y, k: (ring, x, y, 1 - k))

    def along(self, v):
        return self.send(v, lambda ring, x, y, k: (ring, 1 - x, y, k))

    def shift(self, v, axis, step):
        def move(ring, x, y, k):
            moved = list(ring)
            moved[axis] = ring[axis] + step
            return moved, x, y, k

        return self.send(v, move)

    def ring_gather(self, block):
        for axis in reversed(range(len(self.digits))):
            block = jnp.concatenate(
                [block] + [self.shift(block, axis, -d) for d in range(1, self.digits[axis])], axis=0
            )
        return block

    def ring_scatter(self, block):
        for axis in range(len(self.digits)):
            size = self.digits[axis]
            pieces = jnp.split(block, size, axis=0)
            low = [p.astype(bf16) for p in pieces[1:]]
            block = pieces[0]
            for d in range(1, size):
                block = block + self.shift(low[d - 1], axis, d).astype(f32)
        return block


def tie(value, *others):
    return lax.optimization_barrier((value, *others))[0]


class Scatter:
    def __init__(self, links, send):
        self.links = links
        self.came = links.beside(send)

    def total(self, *at):
        return self.keep[at].astype(f32) + self.came[at].astype(f32)

    def first(self, keep):
        shape = (2, 2, 2, keep.shape[1] // 4, keep.shape[2])
        self.keep, self.came = keep.reshape(shape), self.came.reshape(shape)
        every = slice(None)
        to_x = self.total(every, 1, 1).astype(bf16)
        to_y = self.total(1, every, 0).astype(bf16)
        self.by_x, self.by_y = self.links.along(to_x), self.links.across(to_y)
        return to_x, to_y

    def second(self):
        to_x = (self.total(0, 1, 0) + self.by_y[1].astype(f32)).astype(bf16)
        to_y = (self.total(1, 0, 1) + self.by_x[1].astype(f32)).astype(bf16)
        self.late_x, self.late_y = self.links.along(to_x), self.links.across(to_y)
        return to_x, to_y

    def third(self):
        low = self.total(0, 0, 0) + self.by_y[0].astype(f32) + self.late_x.astype(f32)
        high = self.total(0, 0, 1) + self.by_x[0].astype(f32) + self.late_y.astype(f32)
        self.block = jnp.concatenate([low, high], axis=0)
        return self.block

    def last(self):
        return self.links.ring_scatter(self.block)


def relative_order(links, depth):
    ring, x, _, _ = links.locate()
    where = lax.broadcasted_iota(jnp.int32, (1, links.rows * depth), 1)
    block, inside = where // depth, where % depth
    steps = links.rows // 2
    place = block % steps
    parts = []
    for axis in reversed(range(len(links.digits))):
        size = links.digits[axis]
        parts.insert(0, (place % size + ring[axis]) % size)
        place = place // size
    row = jnp.zeros_like(block)
    for size, part in zip(links.digits, parts):
        row = row * size + part
    row = row * 2 + jnp.bitwise_xor(x, block // steps)
    return row * depth + inside


def on_device(
    links, tokens, segments, positions, w_qkv, w_out, w_gate_up, w_down, norm_gain, norm_bias, cotangent
):
    ring, x_place, side, core = links.locate()
    depth = w_qkv.shape[0]
    width = tokens.shape[2]
    head_cols = w_qkv.shape[2]
    hid = w_gate_up.shape[2]
    half = hid // 2
    rows = 2 * tokens.shape[1]
    mine = rows // 2
    part = head_cols + HD

    source = relative_order(links, depth)
    swap = (lax.broadcasted_iota(jnp.int32, (width, width), 0) == source).astype(bf16)

    def split(v):
        high = v.astype(bf16)
        return high, (v - high.astype(f32)).astype(bf16)

    def own_and_other(v):
        own = lax.dynamic_index_in_dim(v, side, 0, keepdims=False)
        return own, lax.dynamic_index_in_dim(v, 1 - side, 0, keepdims=False)

    def from_sequence(own, came):
        first = side == 0
        return jnp.stack([jnp.where(first, own, came), jnp.where(first, came, own)], axis=0)

    out_t = w_out.T
    attn_shard = jnp.concatenate(
        sum(
            [[w_qkv[:, p], out_t[:, p * HD : (p + 1) * HD]] for p in range(3)],
            [],
        ),
        axis=1,
    )
    norms = jnp.concatenate([norm_gain, norm_bias], axis=1)
    norms = jnp.pad(norms, ((0, 0), (0, 128 - norms.shape[1])))
    down_t = w_down.T
    mlp_shards = []
    for h in range(2):
        cols = slice(h * half, (h + 1) * half)
        pieces = [down_t[:, cols], w_gate_up[:, 0, cols], w_gate_up[:, 1, cols]]
        mlp_shards.append(jnp.concatenate(pieces + ([norms] if h == 0 else []), axis=1))

    tokens_own, tokens_other = own_and_other(tokens)
    tokens_came = links.across(tokens_other)
    small_own, small_other = own_and_other(jnp.stack([segments, positions], axis=1))
    small_came = links.across(small_other)
    dy_own, dy_other = own_and_other(cotangent)

    ring_a = links.ring_gather(attn_shard)
    cut = ring_a.shape[0] // 2
    x_a, y_a = links.along(ring_a), links.across(ring_a)
    ring_b = links.ring_gather(tie(mlp_shards[0], ring_a))
    ends_a = links.across(x_a[:cut]), links.along(y_a[cut:])
    attn_w = [ring_a, x_a, y_a, *ends_a]
    attn_w += [links.beside(v) for v in attn_w]

    x_abs = jnp.concatenate([tokens_own, tokens_came], axis=0)
    x = dot(x_abs, swap).astype(bf16)
    x_t = lax.dot_general(swap, x_abs, (((0,), (1,)), ((), ())), preferred_element_type=f32).astype(bf16)
    small = jnp.concatenate([small_own, small_came], axis=1)
    seg = small[0]
    seg_all = jnp.concatenate([seg, links.beside(seg)], axis=0)[:, None]
    seg = seg[None, :]
    cosine, sine = rope_tables(small[1], part)

    ring_b = tie(ring_b, x_a, y_a)
    x_b, y_b = links.along(ring_b), links.across(ring_b)
    q, kv, wo = qkv(tie(x, ring_b), cosine, sine, attn_w)
    ring_c = links.ring_gather(tie(mlp_shards[1], ring_b))
    kv_came = links.beside(kv)
    att_own, logs_own = attend(0, q, kv, kv_came, seg, seg_all)
    ring_c = tie(ring_c, x_b, y_b)
    x_c, y_c = links.along(ring_c), links.across(ring_c)
    ends_b = links.across(x_b[:cut]), links.along(y_b[cut:])
    mlp_b = [ring_b, x_b, y_b, *ends_b]
    mlp_b += [links.beside(v) for v in mlp_b]
    att_other, logs_other = attend(1, tie(q, ring_c, x_b, y_b), kv, kv_came, seg, seg_all)
    n1, s1, low1, low1_t, gains = first_norm(x, att_own, att_other, wo, ring_b, x_b)
    act_b, feed = mlp(tie(low1, x_c, y_c), None, mlp_b, half)
    ends_c = links.across(x_c[:cut]), links.along(y_c[cut:])
    mlp_c = [ring_c, x_c, y_c, *ends_c]
    mlp_c += [links.beside(v) for v in mlp_c]
    act_c, feed = mlp(low1, feed, mlp_c, half)
    dy_came = links.across(tie(dy_other.astype(bf16), y_c))
    high, low = split(dy_own)
    dy = jnp.concatenate([dot(high, swap) + dot(low, swap), dot(dy_came, swap)], axis=0)
    layer_out, dh2, dfeed, dfeed_t, sums = second_norm(n1, gains, feed, dy)

    back = functools.partial(mlp_back, dfeed=dfeed, dfeed_t=dfeed_t, low_t=low1_t)
    dfirst, send = back(1, dh2, act=act_c, blocks=mlp_c)
    sum_c = Scatter(links, send)
    dfirst, keep = back(0, dfirst, act=act_c, blocks=mlp_c)
    ops_c = sum_c.first(keep)
    dfirst, send = back(1, tie(dfirst, *ops_c), act=act_b, blocks=mlp_b)
    sum_b = Scatter(links, send)
    dfirst, keep = back(0, dfirst, act=act_b, blocks=mlp_b)
    ops_b = sum_b.first(keep)
    ops_c = sum_c.second()
    layer_out = dot(layer_out, swap, NT).astype(bf16)
    layer_out = from_sequence(layer_out[:mine], links.across(layer_out[mine:]))
    dh1, low_t, do, delta, cols = first_back(
        tie(dfirst, *ops_b, *ops_c), n1, s1, gains, sums, wo, att_own, att_other
    )
    attend_back_ = functools.partial(
        attend_back, q=q, kv_own=kv, kv_other=kv_came, delta=delta, seg_q=seg, seg_k=seg_all, cosine=cosine, sine=sine
    )
    dq_own, dkv_a, dkv_send = attend_back_(0, do=do, logs=logs_own)
    dkv_came_other = links.beside(dkv_send)
    block_c = sum_c.third()
    dq_other, dkv_b, dkv_send = attend_back_(1, do=tie(do, dq_own, block_c), logs=logs_other)
    dkv_came_own = links.beside(dkv_send)
    own_c = sum_c.last()
    ops_b = sum_b.second()
    grad, send = qkv_back(
        1, tie(dh1, *ops_b), dq_other, dkv_b, dkv_came_other, cosine, sine, x_t, low_t, att_other, cols, attn_w
    )
    sum_a = Scatter(links, send)
    block_b = sum_b.third()
    grad, keep = qkv_back(
        0, tie(grad, block_b), dq_own, dkv_a, dkv_came_own, cosine, sine, x_t, low_t, att_own, cols, attn_w
    )
    own_b = sum_b.last()
    ops_a = sum_a.first(keep)
    high, low = split(tie(grad, *ops_a))
    grad = dot(high, swap, NT) + dot(low, swap, NT)
    ops_a = sum_a.second()
    other = tie(grad[mine:].astype(bf16), *ops_a)
    input_grad = from_sequence(grad[:mine], links.across(other).astype(f32))
    sum_a.third()
    own_attn = sum_a.last()
    own_mlp = [own_b, own_c]

    grad_down = jnp.concatenate([v[:, :half] for v in own_mlp], axis=1).T
    grad_gate_up = jnp.stack(
        [
            jnp.concatenate([v[:, (p + 1) * half : (p + 2) * half] for v in own_mlp], axis=1)
            for p in range(2)
        ],
        axis=1,
    )
    thirds = [own_attn[:, p * part : (p + 1) * part] for p in range(3)]
    edge = 3 * part
    return (
        layer_out,
        input_grad,
        jnp.stack([v[:, :head_cols] for v in thirds], axis=1),
        jnp.concatenate([v[:, head_cols:] for v in thirds], axis=1).T,
        grad_gate_up,
        grad_down,
        own_attn[:, edge : edge + 2],
        own_attn[:, edge + 2 : edge + 4],
    )


def solution(mesh):
    in_specs = (
        P(None, ("row", "col"), None),
        P(None, ("row", "col")),
        P(None, ("row", "col")),
        P("row", None, "col"),
        P("col", "row"),
        P("row", None, "col"),
        P("col", "row"),
        P("row", None),
        P("row", None),
        P(None, ("row", "col"), None),
    )
    out_specs = (
        P(None, ("row", "col"), None),
        P(None, ("row", "col"), None),
        P("row", None, "col"),
        P("col", "row"),
        P("row", None, "col"),
        P("col", "row"),
        P("row", None),
        P("row", None),
    )
    return jax.shard_map(
        functools.partial(on_device, Links(mesh)), mesh=mesh, in_specs=in_specs, out_specs=out_specs, check_vma=False
    )
```

```python
import functools
import math

import jax
import jax.numpy as jnp
from jax import lax
from jax.experimental import pallas as pl
from jax.experimental.pallas import tpu as pltpu
from jax.sharding import PartitionSpec as P

HD = 64
PAIR = 2 * HD
QROWS = 256
epsilon = 1e-12
rope_base = 1000.0
masked_score = -1e30
f32 = jnp.float32
bf16 = jnp.bfloat16

NN = (((1,), (0,)), ((), ()))
NT = (((1,), (1,)), ((), ()))
TN = (((0,), (0,)), ((), ()))


def dot(a, b, dims=NN):
    return lax.dot_general(a, b, dims, preferred_element_type=f32)


def rope_tables(positions, width):
    half_dim = HD // 2
    freq = rope_base ** (-jnp.arange(half_dim, dtype=f32) / half_dim)
    angles = positions.astype(f32)[:, None] * freq[None, :]
    cosine, sine = jnp.cos(angles), jnp.sin(angles)
    times = width // HD
    return (
        jnp.tile(jnp.concatenate([cosine, cosine], axis=1), (1, times)),
        jnp.tile(jnp.concatenate([-sine, sine], axis=1), (1, times)),
    )


def rotated(values, cosine, sine):
    width = values.shape[1]
    lane = lax.broadcasted_iota(jnp.int32, values.shape, 1)
    up = pltpu.roll(values, width - HD // 2, 1)
    down = pltpu.roll(values, HD // 2, 1)
    return values * cosine + jnp.where(lane % HD < HD // 2, up, down) * sine


def normalize(hidden):
    centred = hidden - jnp.mean(hidden, axis=-1, keepdims=True)
    variance = jnp.mean(centred * centred, axis=-1, keepdims=True)
    inv_std = lax.rsqrt(variance + epsilon)
    return (centred * inv_std, inv_std)


def norm_back(grad_norm, normed, inv_std):
    return inv_std * (
        grad_norm
        - jnp.mean(grad_norm, axis=-1, keepdims=True)
        - normed * jnp.mean(grad_norm * normed, axis=-1, keepdims=True)
    )


BLOCKS = 5


def block_starts(width):
    half, quarter = width // 2, width // 4
    return [(0, 0), (0, half), (1, 0), (1, half), (1, half + quarter)]


def start_weights(blocks, w_ref, sems):
    @pl.when(pl.program_id(0) == 0)
    def _():
        for block, (slot, row) in zip(blocks, block_starts(w_ref.shape[1])):
            pltpu.make_async_copy(
                block, w_ref.at[slot, pl.ds(row, block.shape[0])], sems.at[slot]
            ).start()


def wait_weights(w_ref, sems, slot):
    pltpu.make_async_copy(w_ref.at[slot], w_ref.at[slot], sems.at[slot]).wait()


def weight_scratch(blocks):
    width = 2 * blocks[0].shape[0]
    return [
        pltpu.VMEM((2, width, blocks[0].shape[1]), bf16),
        pltpu.SemaphoreType.DMA((2,)),
    ]


ANY = pl.BlockSpec(memory_space=pl.ANY)


def cost(flops, nbytes, exps=0):
    return pl.CostEstimate(flops=int(flops), bytes_accessed=int(nbytes), transcendentals=int(exps))


def whole(shape):
    return pl.BlockSpec(shape, lambda *_: (0,) * len(shape))


def qkv_kernel(own_ref, other_ref, cos_ref, sin_ref, *rest):
    blocks, (q_ref, kv_ref, wo_ref, w_ref, sems) = rest[:BLOCKS], rest[BLOCKS:]
    slot = pl.program_id(0)
    start_weights(blocks, w_ref, sems)
    wait_weights(w_ref, sems, slot)
    part = w_ref.shape[2] // 3
    rows = own_ref.shape[0]
    for i, x_ref in enumerate((own_ref, other_ref)):
        span = slice(i * rows, (i + 1) * rows)
        cosine, sine = cos_ref[span, :], sin_ref[span, :]
        x = x_ref[...]
        q = dot(x, w_ref[slot, :, :part])
        q_ref[span, :] = (rotated(q, cosine, sine) * (1.0 / math.sqrt(HD))).astype(bf16)
        k = dot(x, w_ref[slot, :, part : 2 * part])
        kv_ref[span, :part] = rotated(k, cosine, sine).astype(bf16)
        kv_ref[span, part:] = dot(x, w_ref[slot, :, 2 * part :]).astype(bf16)
    lane = lax.broadcasted_iota(jnp.int32, (w_ref.shape[1], part), 1)
    out = jnp.zeros(lane.shape, f32)
    for h in range(3):
        piece = w_ref[slot, :, h * part : (h + 1) * part].astype(f32)
        piece = pltpu.roll(piece, (h + 1) * HD, 1)
        out = jnp.where(lane // HD == h, piece, out)
    wo_ref[...] = out.astype(bf16)


def qkv(own, other, cosine, sine, blocks):
    rows, width = own.shape
    part = blocks[0].shape[1] // 3
    table = whole((2 * rows, part))
    return pl.pallas_call(
        qkv_kernel,
        grid=(2,),
        in_specs=[whole((rows, width))] * 2 + [table] * 2 + [ANY] * BLOCKS,
        out_specs=[
            pl.BlockSpec((2 * rows, part), lambda i: (0, i)),
            pl.BlockSpec((2 * rows, 2 * part), lambda i: (0, i)),
            pl.BlockSpec((width, part), lambda i: (0, i)),
        ],
        scratch_shapes=weight_scratch(blocks),
        out_shape=[
            jax.ShapeDtypeStruct((2 * rows, 2 * part), bf16),
            jax.ShapeDtypeStruct((2 * rows, 4 * part), bf16),
            jax.ShapeDtypeStruct((width, 2 * part), bf16),
        ],
        cost_estimate=cost(24 * rows * width * part, 40 * width * part),
        name="qkv",
    )(own, other, cosine, sine, *blocks)


def attend_kernel(q_ref, kv_ref, segq_ref, segk_ref, out_ref, log_ref, vt_ref):
    block, part = q_ref.shape
    low_half = lax.broadcasted_iota(jnp.int32, (block, PAIR), 1) < HD

    @pl.when(pl.program_id(0) == 0)
    def _():
        vt_ref[...] = kv_ref[:, part:].T

    q = q_ref[...]
    bias = jnp.where(segk_ref[...] == segq_ref[...], 0.0, masked_score)
    parts = []
    for h in range(3):
        pair = slice(h // 2 * PAIR, (h // 2 + 1) * PAIR)
        mine = low_half if h % 2 == 0 else jnp.logical_not(low_half)
        masked = jnp.where(mine, q[:, pair], jnp.zeros((block, PAIR), bf16))
        scores = dot(kv_ref[:, pair], masked, NT) + bias
        top = jnp.max(scores, axis=0, keepdims=True)
        expo = jnp.exp(scores - top)
        total = jnp.sum(expo, axis=0, keepdims=True)
        out = dot(vt_ref[h * HD : (h + 1) * HD, :], expo.astype(bf16))
        parts.append(out / total)
        log_ref[h : h + 1, :] = top + jnp.log(total)
    parts.append(jnp.zeros((HD, block), f32))
    out_ref[...] = jnp.concatenate(parts, axis=0).T.astype(bf16)


def attend(quarter, q, kv, seg_row, seg_col):
    rows = q.shape[0]
    part = q.shape[1] // 2
    return pl.pallas_call(
        attend_kernel,
        grid=(rows // QROWS,),
        in_specs=[
            pl.BlockSpec((QROWS, part), lambda i: (i, quarter)),
            pl.BlockSpec((rows, 2 * part), lambda i: (0, quarter)),
            pl.BlockSpec((1, QROWS), lambda i: (0, i)),
            whole((rows, 1)),
        ],
        out_specs=[
            pl.BlockSpec((QROWS, part), lambda i: (i, 0)),
            pl.BlockSpec((8, QROWS), lambda i: (0, i)),
        ],
        out_shape=[
            jax.ShapeDtypeStruct((rows, part), bf16),
            jax.ShapeDtypeStruct((8, rows), f32),
        ],
        scratch_shapes=[pltpu.VMEM((part, rows), bf16)],
        cost_estimate=cost(16 * rows * rows * part, 12 * rows * part, rows * rows * 3),
        name="attend",
    )(q, kv, seg_row, seg_col)


def attend_back_kernel(
    q_ref, kv_ref, own_ref, other_ref, wo_ref, att_ref, log_ref, segq_ref, segk_ref, cos_ref, sin_ref,
    dq_ref, dkv_ref, kt_ref, dk_ref, dv_ref,
):
    step = pl.program_id(0)
    block, part = q_ref.shape
    low_half = lax.broadcasted_iota(jnp.int32, (block, PAIR), 1) < HD

    @pl.when(step == 0)
    def _():
        kt_ref[...] = kv_ref[:, :part].T
        dk_ref[...] = jnp.zeros_like(dk_ref)
        dv_ref[...] = jnp.zeros_like(dv_ref)

    low = jnp.where(step < pl.num_programs(0) // 2, own_ref[...], other_ref[...])
    do = dot(low, wo_ref[...]).astype(bf16)
    prod = do.astype(f32) * att_ref[...].astype(f32)
    high = prod.astype(bf16)
    rest = (prod - high.astype(f32)).astype(bf16)
    row = lax.broadcasted_iota(jnp.int32, (8, part), 0)
    lane = lax.broadcasted_iota(jnp.int32, (8, part), 1) // HD
    pick = jnp.where(row == lane, 1.0, 0.0).astype(bf16)
    delta = dot(pick, high, NT) + dot(pick, rest, NT)

    q = q_ref[...]
    bias = jnp.where(segk_ref[...] == segq_ref[...], 0.0, masked_score)
    zero = jnp.zeros((block, PAIR), bf16)
    dq = []
    for h in range(3):
        pair = slice(h // 2 * PAIR, (h // 2 + 1) * PAIR)
        values = slice(part + h // 2 * PAIR, part + (h // 2 + 1) * PAIR)
        mine = low_half if h % 2 == 0 else jnp.logical_not(low_half)
        q_head = jnp.where(mine, q[:, pair], zero)
        do_head = jnp.where(mine, do[:, pair], zero)
        scores = dot(kv_ref[:, pair], q_head, NT) + bias
        probs = jnp.exp(scores - log_ref[h : h + 1, :])
        dprobs = dot(kv_ref[:, values], do_head, NT)
        dscores = (probs * (dprobs - delta[h : h + 1, :])).astype(bf16)
        dv_ref[:, pair] += dot(probs.astype(bf16), do_head)
        dk_ref[:, pair] += dot(dscores, q_head)
        dq.append(dot(kt_ref[h * HD : (h + 1) * HD, :], dscores))
    dq.append(jnp.zeros((HD, block), f32))
    dq = (jnp.concatenate(dq, axis=0) * (1.0 / math.sqrt(HD))).T
    span = pl.ds(pl.multiple_of(step * block, block), block)
    dq_ref[...] = rotated(dq, cos_ref[span, :], -sin_ref[span, :]).astype(bf16)

    @pl.when(step == pl.num_programs(0) - 1)
    def _():
        dkv_ref[:, :part] = rotated(dk_ref[...], cos_ref[...], -sin_ref[...]).astype(bf16)
        dkv_ref[:, part:] = dv_ref[...].astype(bf16)


def attend_back(quarter, q, kv, own, other, wo, att, logs, seg_row, seg_col, cosine, sine):
    rows = q.shape[0]
    width = own.shape[1]
    part = q.shape[1] // 2
    steps = rows // QROWS
    return pl.pallas_call(
        attend_back_kernel,
        grid=(steps,),
        in_specs=[
            pl.BlockSpec((QROWS, part), lambda i: (i, quarter)),
            pl.BlockSpec((rows, 2 * part), lambda i: (0, quarter)),
            pl.BlockSpec((QROWS, width), lambda i: (jnp.minimum(i, steps // 2 - 1), 0)),
            pl.BlockSpec((QROWS, width), lambda i: (jnp.maximum(i - steps // 2, 0), 0)),
            pl.BlockSpec((width, part), lambda i: (0, quarter)),
            pl.BlockSpec((QROWS, part), lambda i: (i, 0)),
            pl.BlockSpec((8, QROWS), lambda i: (0, i)),
            pl.BlockSpec((1, QROWS), lambda i: (0, i)),
            whole((rows, 1)),
            whole((rows, part)),
            whole((rows, part)),
        ],
        out_specs=[
            pl.BlockSpec((QROWS, part), lambda i: (i, 0)),
            whole((rows, 2 * part)),
        ],
        out_shape=[
            jax.ShapeDtypeStruct((rows, part), bf16),
            jax.ShapeDtypeStruct((rows, 2 * part), bf16),
        ],
        scratch_shapes=[
            pltpu.VMEM((part, rows), bf16),
            pltpu.VMEM((rows, part), f32),
            pltpu.VMEM((rows, part), f32),
        ],
        cost_estimate=cost(40 * rows * rows * part, 30 * rows * part, rows * rows * 3),
        name="attend_back",
    )(q, kv, own, other, wo, att, logs, seg_row, seg_col, cosine, sine)


def project_kernel(att_a_ref, att_b_ref, wo_ref, own_ref, send_ref):
    part = att_a_ref.shape[1]
    rows = own_ref.shape[0]
    for out_ref, span in ((send_ref, slice(rows, 2 * rows)), (own_ref, slice(0, rows))):
        out = dot(att_a_ref[span, :], wo_ref[:, :part], NT) + dot(att_b_ref[span, :], wo_ref[:, part:], NT)
        out_ref[...] = out.astype(out_ref.dtype)


def project(att_a, att_b, wo):
    rows, part = att_a.shape
    rows = rows // 2
    width = wo.shape[0]
    return pl.pallas_call(
        project_kernel,
        grid=(1,),
        in_specs=[whole(att_a.shape)] * 2 + [whole(wo.shape)],
        out_specs=[whole((rows, width))] * 2,
        out_shape=[
            jax.ShapeDtypeStruct((rows, width), f32),
            jax.ShapeDtypeStruct((rows, width), bf16),
        ],
        cost_estimate=cost(8 * rows * width * part, 16 * rows * width),
        name="project",
    )(att_a, att_b, wo)


def first_kernel(
    x_ref, own_ref, came_ref, norm_a_ref, norm_b_ref, n_ref, s_ref, low_ref, low_t_ref, gains_ref
):
    norms = jnp.concatenate([norm_a_ref[...], norm_b_ref[...]], axis=0).astype(f32).T
    gains_ref[...] = norms[:8]
    branch = own_ref[...] + came_ref[...].astype(f32)
    normed, inv = normalize(x_ref[...].astype(f32) + branch)
    n_ref[...] = normed
    s_ref[...] = jnp.broadcast_to(inv, s_ref.shape)
    first = normed * norms[0:1] + norms[2:3]
    low_ref[...] = first.astype(bf16)
    low_t_ref[...] = first.T.astype(bf16)


def first_norm(x, own, came, norm_a, norm_b):
    rows, width = x.shape
    at = norm_a.shape[1] // 128 - 1
    strip = pl.BlockSpec((width // 2, 128), lambda i: (0, at))
    return pl.pallas_call(
        first_kernel,
        grid=(1,),
        in_specs=[whole(x.shape)] * 3 + [strip] * 2,
        out_specs=[
            whole((rows, width)), whole((rows, 128)), whole((rows, width)), whole((width, rows)), whole((8, width)),
        ],
        out_shape=[
            jax.ShapeDtypeStruct((rows, width), f32),
            jax.ShapeDtypeStruct((rows, 128), f32),
            jax.ShapeDtypeStruct((rows, width), bf16),
            jax.ShapeDtypeStruct((width, rows), bf16),
            jax.ShapeDtypeStruct((8, width), f32),
        ],
        cost_estimate=cost(20 * rows * width, 16 * rows * width),
        name="first_norm",
    )(x, own, came, norm_a, norm_b)


def mlp_kernel(has_base, low_ref, *rest):
    if has_base:
        base_ref, rest = rest[0], rest[1:]
    blocks, (act_ref, feed_ref, w_ref, sems, sum_ref) = rest[:BLOCKS], rest[BLOCKS:]
    slot = pl.program_id(0)
    half = act_ref.shape[3]
    start_weights(blocks, w_ref, sems)

    @pl.when(slot == 0)
    def _():
        sum_ref[...] = base_ref[...] if has_base else jnp.zeros_like(sum_ref)

    wait_weights(w_ref, sems, slot)

    def body(i, _):
        span = pl.ds(pl.multiple_of(i * QROWS, QROWS), QROWS)
        low = low_ref[span, :]
        gate = dot(low, w_ref[slot, :, half : 2 * half])
        up = dot(low, w_ref[slot, :, 2 * half : 3 * half])
        hidden = (gate / (1.0 + jnp.exp(-gate)) * up).astype(bf16)
        act_ref[0, 0, span, :] = gate.astype(bf16)
        act_ref[0, 1, span, :] = up.astype(bf16)
        act_ref[0, 2, span, :] = hidden
        sum_ref[span, :] += dot(hidden, w_ref[slot, :, :half], NT)
        return 0

    lax.fori_loop(0, low_ref.shape[0] // QROWS, body, 0)

    @pl.when(slot == 1)
    def _():
        feed_ref[...] = sum_ref[...].astype(feed_ref.dtype)


def mlp(low, base, blocks, half, dtype):
    rows, width = low.shape
    has_base = base is not None
    extra = [base] if has_base else []
    return pl.pallas_call(
        functools.partial(mlp_kernel, has_base),
        grid=(2,),
        in_specs=[whole((rows, width))] * (1 + has_base) + [ANY] * BLOCKS,
        out_specs=[
            pl.BlockSpec((1, 3, rows, half), lambda i: (i, 0, 0, 0)),
            whole((rows, width)),
        ],
        scratch_shapes=weight_scratch(blocks) + [pltpu.VMEM((rows, width), f32)],
        out_shape=[
            jax.ShapeDtypeStruct((2, 3, rows, half), bf16),
            jax.ShapeDtypeStruct((rows, width), dtype),
        ],
        cost_estimate=cost(12 * rows * width * half, 30 * half * width, 2 * rows * half),
        name="mlp",
    )(low, *extra, *blocks)


def second_kernel(
    n_ref, gains_ref, feed_ref, came_ref, dy_ref, out_ref, dh_ref, low_ref, low_t_ref, sums_ref
):
    first = n_ref[...] * gains_ref[0:1] + gains_ref[2:3]
    normed, inv = normalize(first + feed_ref[...] + came_ref[...].astype(f32))
    out_ref[...] = (normed * gains_ref[1:2] + gains_ref[3:4]).astype(bf16)
    dy = dy_ref[...]
    sums_ref[...] = jnp.zeros_like(sums_ref)
    sums_ref[1:2] = jnp.sum(dy * normed, axis=0, keepdims=True)
    sums_ref[3:4] = jnp.sum(dy, axis=0, keepdims=True)
    dh = norm_back(dy * gains_ref[1:2], normed, inv)
    dh_ref[...] = dh
    low_ref[...] = dh.astype(bf16)
    low_t_ref[...] = dh.T.astype(bf16)


def second_norm(n1, gains, feed, came, dy):
    rows, width = n1.shape
    full = whole((rows, width))
    return pl.pallas_call(
        second_kernel,
        grid=(1,),
        in_specs=[full, whole((8, width)), full, full, full],
        out_specs=[full, full, full, whole((width, rows)), whole((8, width))],
        out_shape=[
            jax.ShapeDtypeStruct((rows, width), bf16),
            jax.ShapeDtypeStruct((rows, width), f32),
            jax.ShapeDtypeStruct((rows, width), bf16),
            jax.ShapeDtypeStruct((width, rows), bf16),
            jax.ShapeDtypeStruct((8, width), f32),
        ],
        cost_estimate=cost(40 * rows * width, 22 * rows * width),
        name="second_norm",
    )(n1, gains, feed, came, dy)


def mlp_back_kernel(has_base, *rest):
    dfeeds, dfeeds_t, lows_t, acts = rest[:2], rest[2:4], rest[4:6], rest[6:8]
    rest = rest[8:]
    if has_base:
        bases, rest = rest[:2], rest[2:]
    blocks, rest = rest[:BLOCKS], rest[BLOCKS:]
    own_ref, other_ref, to_x_ref, to_y_ref, keep_ref, w_ref, sems, part_ref, sum_ref = rest
    slot = pl.program_id(0)
    rows = own_ref.shape[0]
    half = acts[0].shape[3]
    start_weights(blocks, w_ref, sems)

    @pl.when(slot == 0)
    def _():
        for i in range(2):
            sum_ref[i * rows : (i + 1) * rows, :] = (
                bases[i][...] if has_base else jnp.zeros((rows, sum_ref.shape[1]), f32)
            )

    wait_weights(w_ref, sems, slot)

    for i in range(2):

        def body(j, _):
            span = pl.ds(pl.multiple_of(j * QROWS, QROWS), QROWS)
            both = pl.ds(pl.multiple_of(i * rows + j * QROWS, QROWS), QROWS)
            dhidden = dot(dfeeds[i][span, :], w_ref[slot, :, :half])
            gate = acts[i][0, 0, span, :].astype(f32)
            up = acts[i][0, 1, span, :].astype(f32)
            sg = 1.0 / (1.0 + jnp.exp(-gate))
            dgate = dhidden * up * sg * (1.0 + gate * (1.0 - sg))
            dup = dhidden * (gate * sg)
            part_ref[both, :half] = dgate.astype(bf16)
            part_ref[both, half:] = dup.astype(bf16)
            sum_ref[both, :] += dot(part_ref[both, :], w_ref[slot, :, half : 3 * half], NT)
            return 0

        lax.fori_loop(0, rows // QROWS, body, 0)
    gate_up = (
        dot(lows_t[0][...], part_ref[:rows, :]) + dot(lows_t[1][...], part_ref[rows:, :])
    ).astype(bf16)
    down = (
        dot(dfeeds_t[0][...], acts[0][0, 2]) + dot(dfeeds_t[1][...], acts[1][0, 2])
    ).astype(bf16)
    cut = keep_ref.shape[1]

    def emit(out_ref, at, block):
        span = slice(block * cut, (block + 1) * cut)
        out_ref[at, :, :half] = down[span]
        out_ref[at, :, half:] = gate_up[span]

    emit(to_x_ref, 0, 3)

    @pl.when(slot == 0)
    def _():
        for block in range(3):
            emit(keep_ref, block, block)

    @pl.when(slot == 1)
    def _():
        emit(to_y_ref, 0, 0)
        emit(to_y_ref, 1, 2)
        emit(keep_ref, 3, 1)
        own_ref[...] = sum_ref[:rows, :]
        other_ref[...] = sum_ref[rows:, :].astype(other_ref.dtype)


def mlp_back(bases, dfeeds, dfeeds_t, lows_t, acts, blocks):
    rows, width = dfeeds[0].shape
    half = acts[0].shape[3]
    has_base = bases is not None
    full = whole((rows, width))
    return pl.pallas_call(
        functools.partial(mlp_back_kernel, has_base),
        grid=(2,),
        in_specs=[full] * 2
        + [whole((width, rows))] * 4
        + [pl.BlockSpec((1, 3, rows, half), lambda i: (i, 0, 0, 0))] * 2
        + [full] * (2 * has_base)
        + [ANY] * BLOCKS,
        out_specs=[
            full,
            full,
            pl.BlockSpec((1, width // 4, 3 * half), lambda i: (i, 0, 0)),
            whole((2, width // 4, 3 * half)),
            whole((4, width // 4, 3 * half)),
        ],
        scratch_shapes=weight_scratch(blocks)
        + [pltpu.VMEM((2 * rows, 2 * half), bf16), pltpu.VMEM((2 * rows, width), f32)],
        out_shape=[
            jax.ShapeDtypeStruct((rows, width), f32),
            jax.ShapeDtypeStruct((rows, width), bf16 if has_base else f32),
            jax.ShapeDtypeStruct((2, width // 4, 3 * half), bf16),
            jax.ShapeDtypeStruct((2, width // 4, 3 * half), bf16),
            jax.ShapeDtypeStruct((4, width // 4, 3 * half), bf16),
        ],
        cost_estimate=cost(48 * rows * width * half, 100 * half * width, 4 * rows * half),
        name="mlp_back",
    )(*dfeeds, *dfeeds_t, *lows_t, *acts, *(bases if has_base else ()), *blocks)


def first_back_kernel(
    base_ref, own_ref, came_ref, n_ref, s_ref, gains_ref, sums_ref, dh_ref, low_ref, low_t_ref, cols_ref
):
    dfirst = base_ref[...] + own_ref[...] + came_ref[...].astype(f32)
    normed = n_ref[...]
    width = dfirst.shape[1]
    gain_sum = jnp.sum(dfirst * normed, axis=0, keepdims=True)
    bias_sum = jnp.sum(dfirst, axis=0, keepdims=True)
    sums = sums_ref[...]
    stacked = jnp.concatenate(
        [gain_sum, sums[1:2], bias_sum, sums[3:4], jnp.zeros((124, width), f32)], axis=0
    )
    cols_ref[...] = stacked.T.astype(bf16)
    dh = norm_back(dfirst * gains_ref[0:1], normed, s_ref[:, 0:1])
    dh_ref[...] = dh
    low_ref[...] = dh.astype(bf16)
    low_t_ref[...] = dh.T.astype(bf16)


def first_back(base, own, came, n1, s1, gains, sums):
    rows, width = n1.shape
    full = whole((rows, width))
    return pl.pallas_call(
        first_back_kernel,
        grid=(1,),
        in_specs=[full] * 4 + [whole((rows, 128)), whole((8, width)), whole((8, width))],
        out_specs=[full, full, whole((width, rows)), whole((width, 128))],
        out_shape=[
            jax.ShapeDtypeStruct((rows, width), f32),
            jax.ShapeDtypeStruct((rows, width), bf16),
            jax.ShapeDtypeStruct((width, rows), bf16),
            jax.ShapeDtypeStruct((width, 128), bf16),
        ],
        cost_estimate=cost(40 * rows * width, 20 * rows * width),
        name="first_back",
    )(base, own, came, n1, s1, gains, sums)


def qkv_back_kernel(
    quarter, has_base, dq_ref, dkv_ref, x_a_ref, x_b_ref, low_a_ref, low_b_ref, att_ref, cols_ref, *rest
):
    if has_base:
        bases, rest = rest[:2], rest[2:]
    blocks, (own_ref, other_ref, send_ref, keep_ref, w_ref, sem) = rest[:3], rest[3:]
    rows = own_ref.shape[0]
    part = dq_ref.shape[1]
    starts = [row for slot, row in block_starts(w_ref.shape[0]) if slot == quarter]
    for block, row in zip(blocks, starts):
        pltpu.make_async_copy(block, w_ref.at[pl.ds(row, block.shape[0])], sem).start()
    d_out = dot(low_a_ref[...], att_ref[:rows, :]) + dot(low_b_ref[...], att_ref[rows:, :])
    lane = lax.broadcasted_iota(jnp.int32, d_out.shape, 1)
    cut = keep_ref.shape[1]
    if quarter == 0:
        places = [(keep_ref, 0), (keep_ref, 1), (keep_ref, 2), (send_ref, 0)]
    else:
        places = [(send_ref, 0), (keep_ref, 0), (send_ref, 1), (send_ref, 2)]

    def emit(value, lanes):
        for block, (out_ref, at) in enumerate(places):
            out_ref[at, :, lanes] = value[block * cut : (block + 1) * cut]

    for h in range(3):
        source, at = (dq_ref, 0) if h == 0 else (dkv_ref, (h - 1) * part)
        piece = dot(x_a_ref[...], source[:rows, at : at + part]) + dot(x_b_ref[...], source[rows:, at : at + part])
        moved = pltpu.roll(d_out, (3 - h) * HD, 1)
        emit(jnp.where(lane < 3 * HD, piece, moved).astype(bf16), slice(h * part, (h + 1) * part))
    emit(cols_ref[...], slice(3 * part, 3 * part + 128))
    pltpu.make_async_copy(w_ref, w_ref, sem).wait()
    for i, out_ref in enumerate((own_ref, other_ref)):
        span = slice(i * rows, (i + 1) * rows)
        total = dot(dq_ref[span, :], w_ref[:, :part], NT) + dot(dkv_ref[span, :], w_ref[:, part:], NT)
        if has_base:
            total = total + bases[i][...]
        out_ref[...] = total.astype(out_ref.dtype)


def qkv_back(quarter, bases, dq, dkv, x_t, low_t, att, cols, blocks):
    rows = dq.shape[0] // 2
    width = cols.shape[0]
    part = dq.shape[1]
    has_base = bases is not None
    full = whole((rows, width))
    turned = whole((width, rows))
    blocks = [b for b, (slot, _) in zip(blocks, block_starts(width)) if slot == quarter]
    blocks += [blocks[0]] * (3 - len(blocks))
    counts = (1, 3) if quarter == 0 else (3, 1)
    pieces = [(n, width // 4, 3 * part + 128) for n in counts]
    return pl.pallas_call(
        functools.partial(qkv_back_kernel, quarter, has_base),
        grid=(1,),
        in_specs=[whole(dq.shape), whole(dkv.shape)]
        + [turned] * 4
        + [whole(att.shape), whole((width, 128))]
        + [full] * (2 * has_base)
        + [ANY] * 3,
        out_specs=[full, full] + [whole(p) for p in pieces],
        scratch_shapes=[pltpu.VMEM((width, 3 * part), bf16), pltpu.SemaphoreType.DMA],
        out_shape=[
            jax.ShapeDtypeStruct((rows, width), f32),
            jax.ShapeDtypeStruct((rows, width), bf16 if has_base else f32),
        ]
        + [jax.ShapeDtypeStruct(p, bf16) for p in pieces],
        cost_estimate=cost(26 * rows * width * part, 40 * width * part),
        name="qkv_back",
    )(dq, dkv, *x_t, *low_t, att, cols, *(bases if has_base else ()), *blocks)


def factors_of(n):
    out = []
    while n > 1:
        step = 4 if n % 4 == 0 else (2 if n % 2 == 0 else n)
        out.append(step)
        n //= step
    return out


class Links:
    def __init__(self, mesh):
        self.rows = mesh.shape["row"]
        self.cols = mesh.shape["col"]
        self.digits = factors_of(self.rows // 2)

    def locate(self):
        row = lax.axis_index("row")
        col = lax.axis_index("col")
        x = row % 2
        place = row // 2
        ring = []
        for size in reversed(self.digits):
            ring.insert(0, place % size)
            place = place // size
        return ring, x, col // (self.cols // 2), col % 2

    def send(self, v, move):
        pairs = []
        for row in range(self.rows):
            for col in range(self.cols):
                place, ring = row // 2, []
                for size in reversed(self.digits):
                    ring.insert(0, place % size)
                    place //= size
                ring, x, y, k = move(ring, row % 2, col // (self.cols // 2), col % 2)
                place = 0
                for size, digit in zip(self.digits, ring):
                    place = place * size + digit % size
                pairs.append(
                    (row * self.cols + col, (place * 2 + x) * self.cols + y * (self.cols // 2) + k)
                )
        return lax.ppermute(v, ("row", "col"), pairs)

    def across(self, v):
        return self.send(v, lambda ring, x, y, k: (ring, x, 1 - y, k))

    def beside(self, v):
        return self.send(v, lambda ring, x, y, k: (ring, x, y, 1 - k))

    def along(self, v):
        return self.send(v, lambda ring, x, y, k: (ring, 1 - x, y, k))

    def shift(self, v, axis, step):
        def move(ring, x, y, k):
            moved = list(ring)
            moved[axis] = ring[axis] + step
            return moved, x, y, k

        return self.send(v, move)

    def ring_gather(self, block):
        for axis in reversed(range(len(self.digits))):
            block = jnp.concatenate(
                [block] + [self.shift(block, axis, -d) for d in range(1, self.digits[axis])], axis=0
            )
        return block

    def ring_scatter(self, block):
        for axis in range(len(self.digits)):
            size = self.digits[axis]
            pieces = jnp.split(block, size, axis=0)
            low = [p.astype(bf16) for p in pieces[1:]]
            block = pieces[0]
            for d in range(1, size):
                block = block + self.shift(low[d - 1], axis, d).astype(f32)
        return block


def tie(value, *others):
    return lax.optimization_barrier((value, *others))[0]


class Scatter:
    def __init__(self, links, to_x, to_y, keep):
        self.links, self.keep = links, keep
        self.by_x = [links.along(v) for v in to_x]
        self.by_y = links.across(to_y)

    def second(self):
        by_x = self.by_x[0][1] if len(self.by_x) == 1 else self.by_x[1][0]
        to_x = (self.keep[2].astype(f32) + self.by_y[1].astype(f32)).astype(bf16)
        to_y = (self.keep[3].astype(f32) + by_x.astype(f32)).astype(bf16)
        self.late_x, self.late_y = self.links.along(to_x), self.links.across(to_y)
        return to_x, to_y

    def third(self):
        low = self.keep[0].astype(f32) + self.by_y[0].astype(f32) + self.late_x.astype(f32)
        high = self.keep[1].astype(f32) + self.by_x[0][0].astype(f32) + self.late_y.astype(f32)
        self.block = jnp.concatenate([low, high], axis=0)
        return self.block

    def last(self):
        return self.links.ring_scatter(self.block)


def relative_order(links, depth):
    ring, x, _, _ = links.locate()
    where = lax.broadcasted_iota(jnp.int32, (1, links.rows * depth), 1)
    block, inside = where // depth, where % depth
    steps = links.rows // 2
    place = block % steps
    parts = []
    for axis in reversed(range(len(links.digits))):
        size = links.digits[axis]
        parts.insert(0, (place % size + ring[axis]) % size)
        place = place // size
    row = jnp.zeros_like(block)
    for size, part in zip(links.digits, parts):
        row = row * size + part
    row = row * 2 + jnp.bitwise_xor(x, block // steps)
    return row * depth + inside


def on_device(
    links, tokens, segments, positions, w_qkv, w_out, w_gate_up, w_down, norm_gain, norm_bias, cotangent
):
    ring, x_place, side, core = links.locate()
    depth = w_qkv.shape[0]
    width = tokens.shape[2]
    head_cols = w_qkv.shape[2]
    hid = w_gate_up.shape[2]
    half = hid // 2
    rows = 2 * tokens.shape[1]
    mine = rows // 2
    part = head_cols + HD

    source = relative_order(links, depth)
    swap = (lax.broadcasted_iota(jnp.int32, (width, width), 0) == source).astype(bf16)

    def split(v):
        high = v.astype(bf16)
        return high, (v - high.astype(f32)).astype(bf16)

    def own_and_other(v):
        own = lax.dynamic_index_in_dim(v, side, 0, keepdims=False)
        return own, lax.dynamic_index_in_dim(v, 1 - side, 0, keepdims=False)

    def from_sequence(own, came):
        first = side == 0
        return jnp.stack([jnp.where(first, own, came), jnp.where(first, came, own)], axis=0)

    out_t = w_out.T
    attn_shard = jnp.concatenate(
        sum(
            [[w_qkv[:, p], out_t[:, p * HD : (p + 1) * HD]] for p in range(3)],
            [],
        ),
        axis=1,
    )
    norms = jnp.concatenate([norm_gain, norm_bias], axis=1)
    norms = jnp.pad(norms, ((0, 0), (0, 128 - norms.shape[1])))
    down_t = w_down.T
    mlp_shards = []
    for h in range(2):
        cols = slice(h * half, (h + 1) * half)
        pieces = [down_t[:, cols], w_gate_up[:, 0, cols], w_gate_up[:, 1, cols]]
        mlp_shards.append(jnp.concatenate(pieces + ([norms] if h == 0 else []), axis=1))

    tokens_own, tokens_other = own_and_other(tokens)
    tokens_came = links.across(tokens_other)
    small_own, small_other = own_and_other(jnp.stack([segments, positions], axis=1))
    small_came = links.across(small_other)
    dy_own, dy_other = own_and_other(cotangent)

    ring_a = links.ring_gather(attn_shard)
    cut = ring_a.shape[0] // 2
    x_a, y_a = links.along(ring_a), links.across(ring_a)
    ring_b = links.ring_gather(tie(mlp_shards[0], ring_a))
    attn_w = [ring_a, x_a, y_a, links.across(x_a[:cut]), links.along(y_a[cut:])]

    x_abs = jnp.concatenate([tokens_own, tokens_came], axis=0)
    x = dot(x_abs, swap).astype(bf16)
    x_other = links.beside(x)
    x_t = lax.dot_general(swap, x_abs, (((0,), (1,)), ((), ())), preferred_element_type=f32).astype(bf16)
    x_t = [x_t, links.beside(x_t)]
    small = jnp.concatenate([small_own, small_came], axis=1)
    small = jnp.concatenate([small, links.beside(small)], axis=1)
    seg_row, seg_col = small[0][None, :], small[0][:, None]
    cosine, sine = rope_tables(small[1], part)

    ring_b = tie(ring_b, x_a, y_a)
    x_b, y_b = links.along(ring_b), links.across(ring_b)
    q, kv, wo = qkv(tie(x, ring_b), x_other, cosine, sine, attn_w)
    ring_c = links.ring_gather(tie(mlp_shards[1], ring_b))
    att_0, logs_0 = attend(0, q, kv, seg_row, seg_col)
    ring_c = tie(ring_c, x_b, y_b)
    x_c, y_c = links.along(ring_c), links.across(ring_c)
    mlp_b = [ring_b, x_b, y_b, links.across(x_b[:cut]), links.along(y_b[cut:])]
    att_1, logs_1 = attend(1, tie(q, ring_c, x_b, y_b), kv, seg_row, seg_col)
    own, send = project(att_0, att_1, wo)
    n1, s1, low, low_t, gains = first_norm(x, own, links.beside(send), ring_b, x_b)
    low_other = links.beside(low)
    low1_t = [low_t, links.beside(low_t)]
    act_b_own, feed = mlp(low, None, mlp_b, half, f32)
    act_b_other, feed_other = mlp(tie(low_other, x_c, y_c), None, mlp_b, half, f32)
    mlp_c = [ring_c, x_c, y_c, links.across(x_c[:cut]), links.along(y_c[cut:])]
    act_c_other, send = mlp(low_other, feed_other, mlp_c, half, bf16)
    came = links.beside(send)
    act_c_own, feed = mlp(tie(low, send), feed, mlp_c, half, f32)
    dy_came = links.across(tie(dy_other.astype(bf16), y_c))
    high, low = split(dy_own)
    dy = jnp.concatenate([dot(high, swap) + dot(low, swap), dot(dy_came, swap)], axis=0)
    layer_out, dh2, dfeed, dfeed_t, sums = second_norm(n1, gains, feed, came, dy)
    dfeeds = [dfeed, links.beside(dfeed)]
    dfeeds_t = [dfeed_t, links.beside(dfeed_t)]

    own, other, to_x, to_y, keep = mlp_back(None, dfeeds, dfeeds_t, low1_t, (act_c_own, act_c_other), mlp_c)
    sum_c = Scatter(links, [to_x], to_y, keep)
    own, other, to_x, to_y, keep = mlp_back(
        (own, other), dfeeds, dfeeds_t, low1_t, (act_b_own, act_b_other), mlp_b
    )
    came = links.beside(other)
    sum_b = Scatter(links, [to_x], to_y, keep)
    ops_c = sum_c.second()
    dh1, low, low_t, cols = first_back(tie(dh2, *ops_c), own, came, n1, s1, gains, sums)
    lows = [low, links.beside(low)]
    low_t = [low_t, links.beside(low_t)]
    cols = (cols.astype(f32) + links.beside(cols).astype(f32)).astype(bf16)
    layer_out = dot(layer_out, swap, NT).astype(bf16)
    layer_out = from_sequence(layer_out[:mine], links.across(layer_out[mine:]))

    dq, dkv = attend_back(1, q, kv, *lows, wo, att_1, logs_1, seg_row, seg_col, cosine, sine)
    block_c = sum_c.third()
    own, other, send, keep_1 = qkv_back(1, None, tie(dq, block_c), dkv, x_t, low_t, att_1, cols, attn_w)
    own_c = sum_c.last()
    ops_b = sum_b.second()
    dq, dkv = attend_back(
        0, tie(q, own, *ops_b), kv, *lows, wo, att_0, logs_0, seg_row, seg_col, cosine, sine
    )
    block_b = sum_b.third()
    to_y, to_x = send[:2], [send[2:]]
    own, other, send, keep_0 = qkv_back(0, (own, other), tie(dq, block_b), dkv, x_t, low_t, att_0, cols, attn_w)
    own_b = sum_b.last()
    sum_a = Scatter(links, [send] + to_x, to_y, jnp.concatenate([keep_0, keep_1], axis=0))
    grad = dh1 + own + links.beside(other).astype(f32)
    high, low = split(grad)
    grad = dot(high, swap, NT) + dot(low, swap, NT)
    ops_a = sum_a.second()
    other = tie(grad[mine:].astype(bf16), *ops_a)
    input_grad = from_sequence(grad[:mine], links.across(other).astype(f32))
    sum_a.third()
    own_attn = sum_a.last()
    own_mlp = [own_b, own_c]

    grad_down = jnp.concatenate([v[:, :half] for v in own_mlp], axis=1).T
    grad_gate_up = jnp.stack(
        [
            jnp.concatenate([v[:, (p + 1) * half : (p + 2) * half] for v in own_mlp], axis=1)
            for p in range(2)
        ],
        axis=1,
    )
    thirds = [own_attn[:, p * part : (p + 1) * part] for p in range(3)]
    edge = 3 * part
    return (
        layer_out,
        input_grad,
        jnp.stack([v[:, :head_cols] for v in thirds], axis=1),
        jnp.concatenate([v[:, head_cols:] for v in thirds], axis=1).T,
        grad_gate_up,
        grad_down,
        own_attn[:, edge : edge + 2],
        own_attn[:, edge + 2 : edge + 4],
    )


def solution(mesh):
    in_specs = (
        P(None, ("row", "col"), None),
        P(None, ("row", "col")),
        P(None, ("row", "col")),
        P("row", None, "col"),
        P("col", "row"),
        P("row", None, "col"),
        P("col", "row"),
        P("row", None),
        P("row", None),
        P(None, ("row", "col"), None),
    )
    out_specs = (
        P(None, ("row", "col"), None),
        P(None, ("row", "col"), None),
        P("row", None, "col"),
        P("col", "row"),
        P("row", None, "col"),
        P("col", "row"),
        P("row", None),
        P("row", None),
    )
    return jax.shard_map(
        functools.partial(on_device, Links(mesh)), mesh=mesh, in_specs=in_specs, out_specs=out_specs, check_vma=False
    )
```

```python
import functools
import math

import jax
import jax.numpy as jnp
from jax import lax
from jax.experimental import pallas as pl
from jax.experimental.pallas import tpu as pltpu
from jax.sharding import PartitionSpec as P

HD = 64
PAIR = 2 * HD
QROWS = 256
epsilon = 1e-12
rope_base = 1000.0
masked_score = -1e30
f32 = jnp.float32
bf16 = jnp.bfloat16

NN = (((1,), (0,)), ((), ()))
NT = (((1,), (1,)), ((), ()))
TN = (((0,), (0,)), ((), ()))


def dot(a, b, dims=NN):
    return lax.dot_general(a, b, dims, preferred_element_type=f32)


def rope_tables(positions, width):
    half_dim = HD // 2
    freq = rope_base ** (-jnp.arange(half_dim, dtype=f32) / half_dim)
    angles = positions.astype(f32)[:, None] * freq[None, :]
    cosine, sine = jnp.cos(angles), jnp.sin(angles)
    times = width // HD
    return (
        jnp.tile(jnp.concatenate([cosine, cosine], axis=1), (1, times)),
        jnp.tile(jnp.concatenate([-sine, sine], axis=1), (1, times)),
    )


def rotated(values, cosine, sine):
    width = values.shape[1]
    lane = lax.broadcasted_iota(jnp.int32, values.shape, 1)
    up = pltpu.roll(values, width - HD // 2, 1)
    down = pltpu.roll(values, HD // 2, 1)
    return values * cosine + jnp.where(lane % HD < HD // 2, up, down) * sine


def normalize(hidden):
    centred = hidden - jnp.mean(hidden, axis=-1, keepdims=True)
    variance = jnp.mean(centred * centred, axis=-1, keepdims=True)
    inv_std = lax.rsqrt(variance + epsilon)
    return (centred * inv_std, inv_std)


def norm_back(grad_norm, normed, inv_std):
    return inv_std * (
        grad_norm
        - jnp.mean(grad_norm, axis=-1, keepdims=True)
        - normed * jnp.mean(grad_norm * normed, axis=-1, keepdims=True)
    )


BLOCKS = 5


def block_starts(width):
    half, quarter = width // 2, width // 4
    return [(0, 0), (0, half), (1, 0), (1, half), (1, half + quarter)]


def start_weights(blocks, w_ref, sems):
    @pl.when(pl.program_id(0) == 0)
    def _():
        for block, (slot, row) in zip(blocks, block_starts(w_ref.shape[1])):
            pltpu.make_async_copy(
                block, w_ref.at[slot, pl.ds(row, block.shape[0])], sems.at[slot]
            ).start()


def wait_weights(w_ref, sems, slot):
    pltpu.make_async_copy(w_ref.at[slot], w_ref.at[slot], sems.at[slot]).wait()


def weight_scratch(blocks):
    width = 2 * blocks[0].shape[0]
    return [
        pltpu.VMEM((2, width, blocks[0].shape[1]), bf16),
        pltpu.SemaphoreType.DMA((2,)),
    ]


ANY = pl.BlockSpec(memory_space=pl.ANY)


def cost(flops, nbytes, exps=0):
    return pl.CostEstimate(flops=int(flops), bytes_accessed=int(nbytes), transcendentals=int(exps))


def whole(shape):
    return pl.BlockSpec(shape, lambda *_: (0,) * len(shape))


def qkv_kernel(own_ref, other_ref, cos_ref, sin_ref, *rest):
    blocks, (q_ref, kv_ref, wo_ref, w_ref, sems) = rest[:BLOCKS], rest[BLOCKS:]
    slot = pl.program_id(0)
    start_weights(blocks, w_ref, sems)
    wait_weights(w_ref, sems, slot)
    part = w_ref.shape[2] // 3
    rows = own_ref.shape[0]
    for i, x_ref in enumerate((own_ref, other_ref)):
        span = slice(i * rows, (i + 1) * rows)
        cosine, sine = cos_ref[span, :], sin_ref[span, :]
        x = x_ref[...]
        q = dot(x, w_ref[slot, :, :part])
        q_ref[span, :] = (rotated(q, cosine, sine) * (1.0 / math.sqrt(HD))).astype(bf16)
        k = dot(x, w_ref[slot, :, part : 2 * part])
        kv_ref[span, :part] = rotated(k, cosine, sine).astype(bf16)
        kv_ref[span, part:] = dot(x, w_ref[slot, :, 2 * part :]).astype(bf16)
    lane = lax.broadcasted_iota(jnp.int32, (w_ref.shape[1], part), 1)
    out = jnp.zeros(lane.shape, f32)
    for h in range(3):
        piece = w_ref[slot, :, h * part : (h + 1) * part].astype(f32)
        piece = pltpu.roll(piece, (h + 1) * HD, 1)
        out = jnp.where(lane // HD == h, piece, out)
    wo_ref[...] = out.astype(bf16)


def qkv(own, other, cosine, sine, blocks):
    rows, width = own.shape
    part = blocks[0].shape[1] // 3
    table = whole((2 * rows, part))
    return pl.pallas_call(
        qkv_kernel,
        grid=(2,),
        in_specs=[whole((rows, width))] * 2 + [table] * 2 + [ANY] * BLOCKS,
        out_specs=[
            pl.BlockSpec((2 * rows, part), lambda i: (0, i)),
            pl.BlockSpec((2 * rows, 2 * part), lambda i: (0, i)),
            pl.BlockSpec((width, part), lambda i: (0, i)),
        ],
        scratch_shapes=weight_scratch(blocks),
        out_shape=[
            jax.ShapeDtypeStruct((2 * rows, 2 * part), bf16),
            jax.ShapeDtypeStruct((2 * rows, 4 * part), bf16),
            jax.ShapeDtypeStruct((width, 2 * part), bf16),
        ],
        cost_estimate=cost(24 * rows * width * part, 40 * width * part),
        name="qkv",
    )(own, other, cosine, sine, *blocks)


def attend_kernel(q_ref, kv_ref, segq_ref, segk_ref, out_ref, log_ref, vt_ref):
    block, part = q_ref.shape
    low_half = lax.broadcasted_iota(jnp.int32, (block, PAIR), 1) < HD

    @pl.when(pl.program_id(0) == 0)
    def _():
        vt_ref[...] = kv_ref[:, part:].T

    q = q_ref[...]
    bias = jnp.where(segk_ref[...] == segq_ref[...], 0.0, masked_score)
    parts = []
    for h in range(3):
        pair = slice(h // 2 * PAIR, (h // 2 + 1) * PAIR)
        mine = low_half if h % 2 == 0 else jnp.logical_not(low_half)
        masked = jnp.where(mine, q[:, pair], jnp.zeros((block, PAIR), bf16))
        scores = dot(kv_ref[:, pair], masked, NT) + bias
        top = jnp.max(scores, axis=0, keepdims=True)
        expo = jnp.exp(scores - top)
        total = jnp.sum(expo, axis=0, keepdims=True)
        out = dot(vt_ref[h * HD : (h + 1) * HD, :], expo.astype(bf16))
        parts.append(out / total)
        log_ref[h : h + 1, :] = top + jnp.log(total)
    parts.append(jnp.zeros((HD, block), f32))
    out_ref[...] = jnp.concatenate(parts, axis=0).T.astype(bf16)


def attend(quarter, q, kv, seg_row, seg_col):
    rows = q.shape[0]
    part = q.shape[1] // 2
    return pl.pallas_call(
        attend_kernel,
        grid=(rows // QROWS,),
        in_specs=[
            pl.BlockSpec((QROWS, part), lambda i: (i, quarter)),
            pl.BlockSpec((rows, 2 * part), lambda i: (0, quarter)),
            pl.BlockSpec((1, QROWS), lambda i: (0, i)),
            whole((rows, 1)),
        ],
        out_specs=[
            pl.BlockSpec((QROWS, part), lambda i: (i, 0)),
            pl.BlockSpec((8, QROWS), lambda i: (0, i)),
        ],
        out_shape=[
            jax.ShapeDtypeStruct((rows, part), bf16),
            jax.ShapeDtypeStruct((8, rows), f32),
        ],
        scratch_shapes=[pltpu.VMEM((part, rows), bf16)],
        cost_estimate=cost(16 * rows * rows * part, 12 * rows * part, rows * rows * 3),
        name="attend",
    )(q, kv, seg_row, seg_col)


def attend_back_kernel(
    q_ref, kv_ref, own_ref, other_ref, wo_ref, att_ref, log_ref, segq_ref, segk_ref, cos_ref, sin_ref,
    dq_ref, dkv_ref, kt_ref, dk_ref, dv_ref,
):
    step = pl.program_id(0)
    block, part = q_ref.shape
    low_half = lax.broadcasted_iota(jnp.int32, (block, PAIR), 1) < HD

    @pl.when(step == 0)
    def _():
        kt_ref[...] = kv_ref[:, :part].T
        dk_ref[...] = jnp.zeros_like(dk_ref)
        dv_ref[...] = jnp.zeros_like(dv_ref)

    low = jnp.where(step < pl.num_programs(0) // 2, own_ref[...], other_ref[...])
    do = dot(low, wo_ref[...]).astype(bf16)
    prod = do.astype(f32) * att_ref[...].astype(f32)
    high = prod.astype(bf16)
    rest = (prod - high.astype(f32)).astype(bf16)
    row = lax.broadcasted_iota(jnp.int32, (8, part), 0)
    lane = lax.broadcasted_iota(jnp.int32, (8, part), 1) // HD
    pick = jnp.where(row == lane, 1.0, 0.0).astype(bf16)
    delta = dot(pick, high, NT) + dot(pick, rest, NT)

    q = q_ref[...]
    bias = jnp.where(segk_ref[...] == segq_ref[...], 0.0, masked_score)
    zero = jnp.zeros((block, PAIR), bf16)
    dq = []
    for h in range(3):
        pair = slice(h // 2 * PAIR, (h // 2 + 1) * PAIR)
        values = slice(part + h // 2 * PAIR, part + (h // 2 + 1) * PAIR)
        mine = low_half if h % 2 == 0 else jnp.logical_not(low_half)
        q_head = jnp.where(mine, q[:, pair], zero)
        do_head = jnp.where(mine, do[:, pair], zero)
        scores = dot(kv_ref[:, pair], q_head, NT) + bias
        probs = jnp.exp(scores - log_ref[h : h + 1, :])
        dprobs = dot(kv_ref[:, values], do_head, NT)
        dscores = (probs * (dprobs - delta[h : h + 1, :])).astype(bf16)
        dv_ref[:, pair] += dot(probs.astype(bf16), do_head)
        dk_ref[:, pair] += dot(dscores, q_head)
        dq.append(dot(kt_ref[h * HD : (h + 1) * HD, :], dscores))
    dq.append(jnp.zeros((HD, block), f32))
    dq = (jnp.concatenate(dq, axis=0) * (1.0 / math.sqrt(HD))).T
    span = pl.ds(pl.multiple_of(step * block, block), block)
    dq_ref[...] = rotated(dq, cos_ref[span, :], -sin_ref[span, :]).astype(bf16)

    @pl.when(step == pl.num_programs(0) - 1)
    def _():
        dkv_ref[:, :part] = rotated(dk_ref[...], cos_ref[...], -sin_ref[...]).astype(bf16)
        dkv_ref[:, part:] = dv_ref[...].astype(bf16)


def attend_back(quarter, q, kv, own, other, wo, att, logs, seg_row, seg_col, cosine, sine):
    rows = q.shape[0]
    width = own.shape[1]
    part = q.shape[1] // 2
    steps = rows // QROWS
    return pl.pallas_call(
        attend_back_kernel,
        grid=(steps,),
        in_specs=[
            pl.BlockSpec((QROWS, part), lambda i: (i, quarter)),
            pl.BlockSpec((rows, 2 * part), lambda i: (0, quarter)),
            pl.BlockSpec((QROWS, width), lambda i: (jnp.minimum(i, steps // 2 - 1), 0)),
            pl.BlockSpec((QROWS, width), lambda i: (jnp.maximum(i - steps // 2, 0), 0)),
            pl.BlockSpec((width, part), lambda i: (0, quarter)),
            pl.BlockSpec((QROWS, part), lambda i: (i, 0)),
            pl.BlockSpec((8, QROWS), lambda i: (0, i)),
            pl.BlockSpec((1, QROWS), lambda i: (0, i)),
            whole((rows, 1)),
            whole((rows, part)),
            whole((rows, part)),
        ],
        out_specs=[
            pl.BlockSpec((QROWS, part), lambda i: (i, 0)),
            whole((rows, 2 * part)),
        ],
        out_shape=[
            jax.ShapeDtypeStruct((rows, part), bf16),
            jax.ShapeDtypeStruct((rows, 2 * part), bf16),
        ],
        scratch_shapes=[
            pltpu.VMEM((part, rows), bf16),
            pltpu.VMEM((rows, part), f32),
            pltpu.VMEM((rows, part), f32),
        ],
        cost_estimate=cost(40 * rows * rows * part, 30 * rows * part, rows * rows * 3),
        name="attend_back",
    )(q, kv, own, other, wo, att, logs, seg_row, seg_col, cosine, sine)


def project_kernel(att_a_ref, att_b_ref, wo_ref, own_ref, send_ref):
    part = att_a_ref.shape[1]
    rows = own_ref.shape[0]
    for out_ref, span in ((send_ref, slice(rows, 2 * rows)), (own_ref, slice(0, rows))):
        out = dot(att_a_ref[span, :], wo_ref[:, :part], NT) + dot(att_b_ref[span, :], wo_ref[:, part:], NT)
        out_ref[...] = out.astype(out_ref.dtype)


def project(att_a, att_b, wo):
    rows, part = att_a.shape
    rows = rows // 2
    width = wo.shape[0]
    return pl.pallas_call(
        project_kernel,
        grid=(1,),
        in_specs=[whole(att_a.shape)] * 2 + [whole(wo.shape)],
        out_specs=[whole((rows, width))] * 2,
        out_shape=[
            jax.ShapeDtypeStruct((rows, width), f32),
            jax.ShapeDtypeStruct((rows, width), bf16),
        ],
        cost_estimate=cost(8 * rows * width * part, 16 * rows * width),
        name="project",
    )(att_a, att_b, wo)


def first_kernel(
    x_ref, own_ref, came_ref, norm_a_ref, norm_b_ref, n_ref, s_ref, low_ref, low_t_ref, gains_ref
):
    norms = jnp.concatenate([norm_a_ref[...], norm_b_ref[...]], axis=0).astype(f32).T
    gains_ref[...] = norms[:8]
    branch = own_ref[...] + came_ref[...].astype(f32)
    normed, inv = normalize(x_ref[...].astype(f32) + branch)
    n_ref[...] = normed
    s_ref[...] = jnp.broadcast_to(inv, s_ref.shape)
    first = normed * norms[0:1] + norms[2:3]
    low_ref[...] = first.astype(bf16)
    low_t_ref[...] = first.T.astype(bf16)


def first_norm(x, own, came, norm_a, norm_b):
    rows, width = x.shape
    at = norm_a.shape[1] // 128 - 1
    strip = pl.BlockSpec((width // 2, 128), lambda i: (0, at))
    return pl.pallas_call(
        first_kernel,
        grid=(1,),
        in_specs=[whole(x.shape)] * 3 + [strip] * 2,
        out_specs=[
            whole((rows, width)), whole((rows, 128)), whole((rows, width)), whole((width, rows)), whole((8, width)),
        ],
        out_shape=[
            jax.ShapeDtypeStruct((rows, width), f32),
            jax.ShapeDtypeStruct((rows, 128), f32),
            jax.ShapeDtypeStruct((rows, width), bf16),
            jax.ShapeDtypeStruct((width, rows), bf16),
            jax.ShapeDtypeStruct((8, width), f32),
        ],
        cost_estimate=cost(20 * rows * width, 16 * rows * width),
        name="first_norm",
    )(x, own, came, norm_a, norm_b)


def mlp_kernel(has_base, low_ref, *rest):
    if has_base:
        base_ref, rest = rest[0], rest[1:]
    blocks, (act_ref, feed_ref, w_ref, sems, sum_ref) = rest[:BLOCKS], rest[BLOCKS:]
    slot = pl.program_id(0)
    half = act_ref.shape[3]
    start_weights(blocks, w_ref, sems)

    @pl.when(slot == 0)
    def _():
        sum_ref[...] = base_ref[...] if has_base else jnp.zeros_like(sum_ref)

    wait_weights(w_ref, sems, slot)

    def body(i, _):
        span = pl.ds(pl.multiple_of(i * QROWS, QROWS), QROWS)
        low = low_ref[span, :]
        gate = dot(low, w_ref[slot, :, half : 2 * half])
        up = dot(low, w_ref[slot, :, 2 * half : 3 * half])
        hidden = (gate / (1.0 + jnp.exp(-gate)) * up).astype(bf16)
        act_ref[0, 0, span, :] = gate.astype(bf16)
        act_ref[0, 1, span, :] = up.astype(bf16)
        act_ref[0, 2, span, :] = hidden
        sum_ref[span, :] += dot(hidden, w_ref[slot, :, :half], NT)
        return 0

    lax.fori_loop(0, low_ref.shape[0] // QROWS, body, 0)

    @pl.when(slot == 1)
    def _():
        feed_ref[...] = sum_ref[...].astype(feed_ref.dtype)


def mlp(low, base, blocks, half, dtype):
    rows, width = low.shape
    has_base = base is not None
    extra = [base] if has_base else []
    return pl.pallas_call(
        functools.partial(mlp_kernel, has_base),
        grid=(2,),
        in_specs=[whole((rows, width))] * (1 + has_base) + [ANY] * BLOCKS,
        out_specs=[
            pl.BlockSpec((1, 3, rows, half), lambda i: (i, 0, 0, 0)),
            whole((rows, width)),
        ],
        scratch_shapes=weight_scratch(blocks) + [pltpu.VMEM((rows, width), f32)],
        out_shape=[
            jax.ShapeDtypeStruct((2, 3, rows, half), bf16),
            jax.ShapeDtypeStruct((rows, width), dtype),
        ],
        cost_estimate=cost(12 * rows * width * half, 30 * half * width, 2 * rows * half),
        name="mlp",
    )(low, *extra, *blocks)


def second_kernel(
    n_ref, gains_ref, feed_ref, came_ref, dy_ref, out_ref, dh_ref, low_ref, low_t_ref, sums_ref
):
    first = n_ref[...] * gains_ref[0:1] + gains_ref[2:3]
    normed, inv = normalize(first + feed_ref[...] + came_ref[...].astype(f32))
    out_ref[...] = (normed * gains_ref[1:2] + gains_ref[3:4]).astype(bf16)
    dy = dy_ref[...]
    sums_ref[...] = jnp.zeros_like(sums_ref)
    sums_ref[1:2] = jnp.sum(dy * normed, axis=0, keepdims=True)
    sums_ref[3:4] = jnp.sum(dy, axis=0, keepdims=True)
    dh = norm_back(dy * gains_ref[1:2], normed, inv)
    dh_ref[...] = dh
    low_ref[...] = dh.astype(bf16)
    low_t_ref[...] = dh.T.astype(bf16)


def second_norm(n1, gains, feed, came, dy):
    rows, width = n1.shape
    full = whole((rows, width))
    return pl.pallas_call(
        second_kernel,
        grid=(1,),
        in_specs=[full, whole((8, width)), full, full, full],
        out_specs=[full, full, full, whole((width, rows)), whole((8, width))],
        out_shape=[
            jax.ShapeDtypeStruct((rows, width), bf16),
            jax.ShapeDtypeStruct((rows, width), f32),
            jax.ShapeDtypeStruct((rows, width), bf16),
            jax.ShapeDtypeStruct((width, rows), bf16),
            jax.ShapeDtypeStruct((8, width), f32),
        ],
        cost_estimate=cost(40 * rows * width, 22 * rows * width),
        name="second_norm",
    )(n1, gains, feed, came, dy)


def mlp_back_kernel(has_base, *rest):
    dfeeds, dfeeds_t, lows_t, acts = rest[:2], rest[2:4], rest[4:6], rest[6:8]
    rest = rest[8:]
    if has_base:
        bases, rest = rest[:2], rest[2:]
    blocks, rest = rest[:BLOCKS], rest[BLOCKS:]
    own_ref, other_ref, to_x_ref, to_y_ref, keep_ref, w_ref, sems, part_ref, sum_ref = rest
    slot = pl.program_id(0)
    rows = own_ref.shape[0]
    half = acts[0].shape[3]
    start_weights(blocks, w_ref, sems)

    @pl.when(slot == 0)
    def _():
        for i in range(2):
            sum_ref[i * rows : (i + 1) * rows, :] = (
                bases[i][...] if has_base else jnp.zeros((rows, sum_ref.shape[1]), f32)
            )

    wait_weights(w_ref, sems, slot)

    for i in range(2):

        def body(j, _):
            span = pl.ds(pl.multiple_of(j * QROWS, QROWS), QROWS)
            both = pl.ds(pl.multiple_of(i * rows + j * QROWS, QROWS), QROWS)
            dhidden = dot(dfeeds[i][span, :], w_ref[slot, :, :half])
            gate = acts[i][0, 0, span, :].astype(f32)
            up = acts[i][0, 1, span, :].astype(f32)
            sg = 1.0 / (1.0 + jnp.exp(-gate))
            dgate = dhidden * up * sg * (1.0 + gate * (1.0 - sg))
            dup = dhidden * (gate * sg)
            part_ref[both, :half] = dgate.astype(bf16)
            part_ref[both, half:] = dup.astype(bf16)
            sum_ref[both, :] += dot(part_ref[both, :], w_ref[slot, :, half : 3 * half], NT)
            return 0

        lax.fori_loop(0, rows // QROWS, body, 0)
    gate_up = (
        dot(lows_t[0][...], part_ref[:rows, :]) + dot(lows_t[1][...], part_ref[rows:, :])
    ).astype(bf16)
    down = (
        dot(dfeeds_t[0][...], acts[0][0, 2]) + dot(dfeeds_t[1][...], acts[1][0, 2])
    ).astype(bf16)
    cut = keep_ref.shape[1]

    def emit(out_ref, at, block):
        span = slice(block * cut, (block + 1) * cut)
        out_ref[at, :, :half] = down[span]
        out_ref[at, :, half:] = gate_up[span]

    emit(to_x_ref, 0, 3)

    @pl.when(slot == 0)
    def _():
        for block in range(3):
            emit(keep_ref, block, block)

    @pl.when(slot == 1)
    def _():
        emit(to_y_ref, 0, 0)
        emit(to_y_ref, 1, 2)
        emit(keep_ref, 3, 1)
        own_ref[...] = sum_ref[:rows, :]
        other_ref[...] = sum_ref[rows:, :].astype(other_ref.dtype)


def mlp_back(bases, dfeeds, dfeeds_t, lows_t, acts, blocks):
    rows, width = dfeeds[0].shape
    half = acts[0].shape[3]
    has_base = bases is not None
    full = whole((rows, width))
    return pl.pallas_call(
        functools.partial(mlp_back_kernel, has_base),
        grid=(2,),
        in_specs=[full] * 2
        + [whole((width, rows))] * 4
        + [pl.BlockSpec((1, 3, rows, half), lambda i: (i, 0, 0, 0))] * 2
        + [full] * (2 * has_base)
        + [ANY] * BLOCKS,
        out_specs=[
            full,
            full,
            pl.BlockSpec((1, width // 4, 3 * half), lambda i: (i, 0, 0)),
            whole((2, width // 4, 3 * half)),
            whole((4, width // 4, 3 * half)),
        ],
        scratch_shapes=weight_scratch(blocks)
        + [pltpu.VMEM((2 * rows, 2 * half), bf16), pltpu.VMEM((2 * rows, width), f32)],
        out_shape=[
            jax.ShapeDtypeStruct((rows, width), f32),
            jax.ShapeDtypeStruct((rows, width), bf16 if has_base else f32),
            jax.ShapeDtypeStruct((2, width // 4, 3 * half), bf16),
            jax.ShapeDtypeStruct((2, width // 4, 3 * half), bf16),
            jax.ShapeDtypeStruct((4, width // 4, 3 * half), bf16),
        ],
        cost_estimate=cost(48 * rows * width * half, 100 * half * width, 4 * rows * half),
        name="mlp_back",
    )(*dfeeds, *dfeeds_t, *lows_t, *acts, *(bases if has_base else ()), *blocks)


def first_back_kernel(
    base_ref, own_ref, came_ref, n_ref, s_ref, gains_ref, sums_ref, dh_ref, low_ref, low_t_ref
):
    dfirst = base_ref[...] + own_ref[...] + came_ref[...].astype(f32)
    normed = n_ref[...]
    width = dfirst.shape[1]
    gain_sum = jnp.sum(dfirst * normed, axis=0, keepdims=True)
    bias_sum = jnp.sum(dfirst, axis=0, keepdims=True)
    sums = sums_ref[...]
    stacked = jnp.concatenate(
        [gain_sum, sums[1:2], bias_sum, sums[3:4], jnp.zeros((124, width), f32)], axis=0
    )
    rows = dfirst.shape[0]
    low_t_ref[:, rows:] = stacked.T.astype(bf16)
    dh = norm_back(dfirst * gains_ref[0:1], normed, s_ref[:, 0:1])
    dh_ref[...] = dh
    low_ref[...] = dh.astype(bf16)
    low_t_ref[:, :rows] = dh.T.astype(bf16)


def first_back(base, own, came, n1, s1, gains, sums):
    rows, width = n1.shape
    full = whole((rows, width))
    return pl.pallas_call(
        first_back_kernel,
        grid=(1,),
        in_specs=[full] * 4 + [whole((rows, 128)), whole((8, width)), whole((8, width))],
        out_specs=[full, full, whole((width, rows + 128))],
        out_shape=[
            jax.ShapeDtypeStruct((rows, width), f32),
            jax.ShapeDtypeStruct((rows, width), bf16),
            jax.ShapeDtypeStruct((width, rows + 128), bf16),
        ],
        cost_estimate=cost(40 * rows * width, 20 * rows * width),
        name="first_back",
    )(base, own, came, n1, s1, gains, sums)


def qkv_back_kernel(
    quarter, has_base, dq_ref, dkv_ref, x_a_ref, x_b_ref, low_a_ref, low_b_ref, cols_a_ref, cols_b_ref, att_ref, *rest
):
    if has_base:
        bases, rest = rest[:2], rest[2:]
    blocks, (own_ref, other_ref, send_ref, keep_ref, w_ref, sem) = rest[:3], rest[3:]
    rows = own_ref.shape[0]
    part = dq_ref.shape[1]
    starts = [row for slot, row in block_starts(w_ref.shape[0]) if slot == quarter]
    for block, row in zip(blocks, starts):
        pltpu.make_async_copy(block, w_ref.at[pl.ds(row, block.shape[0])], sem).start()
    d_out = dot(low_a_ref[...], att_ref[:rows, :]) + dot(low_b_ref[...], att_ref[rows:, :])
    lane = lax.broadcasted_iota(jnp.int32, d_out.shape, 1)
    cut = keep_ref.shape[1]
    if quarter == 0:
        places = [(keep_ref, 0), (keep_ref, 1), (keep_ref, 2), (send_ref, 0)]
    else:
        places = [(send_ref, 0), (keep_ref, 0), (send_ref, 1), (send_ref, 2)]

    def emit(value, lanes):
        for block, (out_ref, at) in enumerate(places):
            out_ref[at, :, lanes] = value[block * cut : (block + 1) * cut]

    for h in range(3):
        source, at = (dq_ref, 0) if h == 0 else (dkv_ref, (h - 1) * part)
        piece = dot(x_a_ref[...], source[:rows, at : at + part]) + dot(x_b_ref[...], source[rows:, at : at + part])
        moved = pltpu.roll(d_out, (3 - h) * HD, 1)
        emit(jnp.where(lane < 3 * HD, piece, moved).astype(bf16), slice(h * part, (h + 1) * part))
    cols = cols_a_ref[...].astype(f32) + cols_b_ref[...].astype(f32)
    emit(cols.astype(bf16), slice(3 * part, 3 * part + 128))
    pltpu.make_async_copy(w_ref, w_ref, sem).wait()
    for i, out_ref in enumerate((own_ref, other_ref)):
        span = slice(i * rows, (i + 1) * rows)
        total = dot(dq_ref[span, :], w_ref[:, :part], NT) + dot(dkv_ref[span, :], w_ref[:, part:], NT)
        if has_base:
            total = total + bases[i][...]
        out_ref[...] = total.astype(out_ref.dtype)


def qkv_back(quarter, bases, dq, dkv, x_t, low_t, att, blocks):
    rows = dq.shape[0] // 2
    width = low_t[0].shape[0]
    part = dq.shape[1]
    has_base = bases is not None
    full = whole((rows, width))
    turned = whole((width, rows))
    blocks = [b for b, (slot, _) in zip(blocks, block_starts(width)) if slot == quarter]
    blocks += [blocks[0]] * (3 - len(blocks))
    counts = (1, 3) if quarter == 0 else (3, 1)
    pieces = [(n, width // 4, 3 * part + 128) for n in counts]
    return pl.pallas_call(
        functools.partial(qkv_back_kernel, quarter, has_base),
        grid=(1,),
        in_specs=[whole(dq.shape), whole(dkv.shape)]
        + [turned] * 4
        + [pl.BlockSpec((width, 128), lambda i: (0, rows // 128))] * 2
        + [whole(att.shape)]
        + [full] * (2 * has_base)
        + [ANY] * 3,
        out_specs=[full, full] + [whole(p) for p in pieces],
        scratch_shapes=[pltpu.VMEM((width, 3 * part), bf16), pltpu.SemaphoreType.DMA],
        out_shape=[
            jax.ShapeDtypeStruct((rows, width), f32),
            jax.ShapeDtypeStruct((rows, width), bf16 if has_base else f32),
        ]
        + [jax.ShapeDtypeStruct(p, bf16) for p in pieces],
        cost_estimate=cost(26 * rows * width * part, 40 * width * part),
        name="qkv_back",
    )(dq, dkv, *x_t, *low_t, *low_t, att, *(bases if has_base else ()), *blocks)


def factors_of(n):
    out = []
    while n > 1:
        step = 4 if n % 4 == 0 else (2 if n % 2 == 0 else n)
        out.append(step)
        n //= step
    return out


class Links:
    def __init__(self, mesh):
        self.rows = mesh.shape["row"]
        self.cols = mesh.shape["col"]
        self.digits = factors_of(self.rows // 2)

    def locate(self):
        row = lax.axis_index("row")
        col = lax.axis_index("col")
        x = row % 2
        place = row // 2
        ring = []
        for size in reversed(self.digits):
            ring.insert(0, place % size)
            place = place // size
        return ring, x, col // (self.cols // 2), col % 2

    def send(self, v, move):
        pairs = []
        for row in range(self.rows):
            for col in range(self.cols):
                place, ring = row // 2, []
                for size in reversed(self.digits):
                    ring.insert(0, place % size)
                    place //= size
                ring, x, y, k = move(ring, row % 2, col // (self.cols // 2), col % 2)
                place = 0
                for size, digit in zip(self.digits, ring):
                    place = place * size + digit % size
                pairs.append(
                    (row * self.cols + col, (place * 2 + x) * self.cols + y * (self.cols // 2) + k)
                )
        return lax.ppermute(v, ("row", "col"), pairs)

    def across(self, v):
        return self.send(v, lambda ring, x, y, k: (ring, x, 1 - y, k))

    def beside(self, v):
        return self.send(v, lambda ring, x, y, k: (ring, x, y, 1 - k))

    def along(self, v):
        return self.send(v, lambda ring, x, y, k: (ring, 1 - x, y, k))

    def shift(self, v, axis, step):
        def move(ring, x, y, k):
            moved = list(ring)
            moved[axis] = ring[axis] + step
            return moved, x, y, k

        return self.send(v, move)

    def ring_gather(self, block):
        for axis in reversed(range(len(self.digits))):
            block = jnp.concatenate(
                [block] + [self.shift(block, axis, -d) for d in range(1, self.digits[axis])], axis=0
            )
        return block

    def ring_pieces(self, block, axis):
        pieces = jnp.split(block, self.digits[axis], axis=0)
        return pieces[0], [p.astype(bf16) for p in pieces[1:]]

    def ring_scatter(self, own, low):
        for axis in range(len(self.digits)):
            if axis > 0:
                own, low = self.ring_pieces(own, axis)
            for d, piece in enumerate(low, 1):
                own = own + self.shift(piece, axis, d).astype(f32)
        return own


def tie(value, *others):
    return lax.optimization_barrier((value, *others))[0]


class Scatter:
    def __init__(self, links, to_x, to_y, keep):
        self.links, self.keep = links, keep
        self.by_x = [links.along(v) for v in to_x]
        self.by_y = links.across(to_y)

    def second(self):
        by_x = self.by_x[0][1] if len(self.by_x) == 1 else self.by_x[1][0]
        to_x = (self.keep[2].astype(f32) + self.by_y[1].astype(f32)).astype(bf16)
        to_y = (self.keep[3].astype(f32) + by_x.astype(f32)).astype(bf16)
        self.late_x, self.late_y = self.links.along(to_x), self.links.across(to_y)
        return to_x, to_y

    def third(self):
        low = self.keep[0].astype(f32) + self.by_y[0].astype(f32) + self.late_x.astype(f32)
        high = self.keep[1].astype(f32) + self.by_x[0][0].astype(f32) + self.late_y.astype(f32)
        self.own, self.low = self.links.ring_pieces(jnp.concatenate([low, high], axis=0), 0)
        return self.low

    def last(self):
        return self.links.ring_scatter(self.own, self.low)


def relative_order(links, depth):
    ring, x, _, _ = links.locate()
    where = lax.broadcasted_iota(jnp.int32, (1, links.rows * depth), 1)
    block, inside = where // depth, where % depth
    steps = links.rows // 2
    place = block % steps
    parts = []
    for axis in reversed(range(len(links.digits))):
        size = links.digits[axis]
        parts.insert(0, (place % size + ring[axis]) % size)
        place = place // size
    row = jnp.zeros_like(block)
    for size, part in zip(links.digits, parts):
        row = row * size + part
    row = row * 2 + jnp.bitwise_xor(x, block // steps)
    return row * depth + inside


def on_device(
    links, tokens, segments, positions, w_qkv, w_out, w_gate_up, w_down, norm_gain, norm_bias, cotangent
):
    ring, x_place, side, core = links.locate()
    depth = w_qkv.shape[0]
    width = tokens.shape[2]
    head_cols = w_qkv.shape[2]
    hid = w_gate_up.shape[2]
    half = hid // 2
    rows = 2 * tokens.shape[1]
    mine = rows // 2
    part = head_cols + HD

    source = relative_order(links, depth)
    swap = (lax.broadcasted_iota(jnp.int32, (width, width), 0) == source).astype(bf16)

    def split(v):
        high = v.astype(bf16)
        return high, (v - high.astype(f32)).astype(bf16)

    def own_and_other(v):
        own = lax.dynamic_index_in_dim(v, side, 0, keepdims=False)
        return own, lax.dynamic_index_in_dim(v, 1 - side, 0, keepdims=False)

    def from_sequence(own, came):
        first = side == 0
        return jnp.stack([jnp.where(first, own, came), jnp.where(first, came, own)], axis=0)

    out_t = w_out.T
    attn_shard = jnp.concatenate(
        sum(
            [[w_qkv[:, p], out_t[:, p * HD : (p + 1) * HD]] for p in range(3)],
            [],
        ),
        axis=1,
    )
    norms = jnp.concatenate([norm_gain, norm_bias], axis=1)
    norms = jnp.pad(norms, ((0, 0), (0, 128 - norms.shape[1])))
    down_t = w_down.T
    mlp_shards = []
    for h in range(2):
        cols = slice(h * half, (h + 1) * half)
        pieces = [down_t[:, cols], w_gate_up[:, 0, cols], w_gate_up[:, 1, cols]]
        mlp_shards.append(jnp.concatenate(pieces + ([norms] if h == 0 else []), axis=1))

    tokens_own, tokens_other = own_and_other(tokens)
    tokens_came = links.across(tokens_other)
    small_own, small_other = own_and_other(jnp.stack([segments, positions], axis=1))
    small_came = links.across(small_other)
    dy_own, dy_other = own_and_other(cotangent)

    ring_a = links.ring_gather(attn_shard)
    cut = ring_a.shape[0] // 2
    x_a, y_a = links.along(ring_a), links.across(ring_a)
    ring_b = links.ring_gather(tie(mlp_shards[0], ring_a))
    ends_a = links.across(x_a[:cut]), links.along(y_a[cut:])
    attn_w = [ring_a, x_a, y_a, *ends_a]

    x_abs = jnp.concatenate([tokens_own, tokens_came], axis=0)
    x = dot(x_abs, swap).astype(bf16)
    x_other = links.beside(x)
    x_t = lax.dot_general(swap, x_abs, (((0,), (1,)), ((), ())), preferred_element_type=f32).astype(bf16)
    x_t = [x_t, links.beside(x_t)]
    small = jnp.concatenate([small_own, small_came], axis=1)
    small = jnp.concatenate([small, links.beside(small)], axis=1)
    seg_row, seg_col = small[0][None, :], small[0][:, None]
    cosine, sine = rope_tables(small[1], part)

    ring_b = tie(ring_b, x_a, y_a)
    x_b, y_b = links.along(ring_b), links.across(ring_b)
    q, kv, wo = qkv(tie(x, ring_b, *x_t), x_other, cosine, sine, attn_w)
    ring_c = links.ring_gather(tie(mlp_shards[1], *ends_a))
    att_0, logs_0 = attend(0, q, kv, seg_row, seg_col)
    ends_b = links.across(x_b[:cut]), links.along(y_b[cut:])
    mlp_b = [ring_b, x_b, y_b, *ends_b]
    att_1, logs_1 = attend(1, tie(q, ring_c, x_b, y_b), kv, seg_row, seg_col)
    ring_c = tie(ring_c, att_1)
    x_c, y_c = links.along(ring_c), links.across(ring_c)
    own, send = project(att_0, tie(att_1, *ends_b), wo)
    n1, s1, low, low_t, gains = first_norm(x, own, links.beside(send), ring_b, x_b)
    low_other = links.beside(low)
    low1_t = [low_t, links.beside(low_t)]
    act_b_own, feed = mlp(low, None, mlp_b, half, f32)
    held_x, held_y = lax.optimization_barrier((x_c, y_c, feed))[:2]
    held_x, held_y = held_x[:cut], held_y[cut:]
    ends_c = links.across(held_x), links.along(held_y)
    act_b_other, feed_other = mlp(tie(low_other, held_x, held_y), None, mlp_b, half, f32)
    mlp_c = [ring_c, x_c, y_c, *ends_c]
    act_c_other, send = mlp(low_other, feed_other, mlp_c, half, bf16)
    came = links.beside(send)
    act_c_own, feed = mlp(tie(low, send), feed, mlp_c, half, f32)
    dy_came = links.across(tie(dy_other.astype(bf16), feed_other))
    high, low = split(dy_own)
    dy = jnp.concatenate([dot(high, swap) + dot(low, swap), dot(dy_came, swap)], axis=0)
    layer_out, dh2, dfeed, dfeed_t, sums = second_norm(n1, gains, feed, came, dy)
    dfeeds = [dfeed, links.beside(dfeed)]
    dfeeds_t = [dfeed_t, links.beside(dfeed_t)]

    own, other, to_x, to_y, keep = mlp_back(None, dfeeds, dfeeds_t, low1_t, (act_c_own, act_c_other), mlp_c)
    sum_c = Scatter(links, [to_x], to_y, keep)
    own, other, to_x, to_y, keep = mlp_back(
        (own, other), dfeeds, dfeeds_t, low1_t, (act_b_own, act_b_other), mlp_b
    )
    came = links.beside(other)
    sum_b = Scatter(links, [to_x], to_y, keep)
    sum_c.keep = tie(sum_c.keep, own)
    ops_c = sum_c.second()
    dh1, low, low_t = first_back(tie(dh2, *ops_c), own, came, n1, s1, gains, sums)
    lows = [low, links.beside(low)]
    low_t = [low_t, links.beside(low_t)]
    dq, dkv = attend_back(1, q, kv, *lows, wo, att_1, logs_1, seg_row, seg_col, cosine, sine)
    sum_c.keep = tie(sum_c.keep, dq)
    block_c = sum_c.third()
    sum_b.keep = tie(sum_b.keep, dq)
    ops_b = sum_b.second()
    own, other, send, keep_1 = qkv_back(
        1, None, tie(dq, *block_c, *ops_b), dkv, x_t, low_t, att_1, attn_w
    )
    own_c = sum_c.last()
    dq, dkv = attend_back(0, tie(q, own), kv, *lows, wo, att_0, logs_0, seg_row, seg_col, cosine, sine)
    sum_b.keep = tie(sum_b.keep, dq)
    block_b = sum_b.third()
    to_y, to_x = send[:2], [send[2:]]
    own, other, send, keep_0 = qkv_back(
        0, (own, other), tie(dq, *block_b, own_c), dkv, x_t, low_t, att_0, attn_w
    )
    own_b = sum_b.last()
    sum_a = Scatter(links, [send] + to_x, to_y, jnp.concatenate([keep_0, keep_1], axis=0))
    layer_out = dot(layer_out, swap, NT).astype(bf16)
    layer_out = from_sequence(layer_out[:mine], links.across(tie(layer_out[mine:], dq)))
    grad = dh1 + own + links.beside(other).astype(f32)
    high, low = split(grad)
    grad = dot(high, swap, NT) + dot(low, swap, NT)
    ops_a = sum_a.second()
    other = tie(grad[mine:].astype(bf16), *ops_a)
    input_grad = from_sequence(grad[:mine], links.across(other).astype(f32))
    sum_a.third()
    own_attn = sum_a.last()
    own_mlp = [own_b, own_c]

    grad_down = jnp.concatenate([v[:, :half] for v in own_mlp], axis=1).T
    grad_gate_up = jnp.stack(
        [
            jnp.concatenate([v[:, (p + 1) * half : (p + 2) * half] for v in own_mlp], axis=1)
            for p in range(2)
        ],
        axis=1,
    )
    thirds = [own_attn[:, p * part : (p + 1) * part] for p in range(3)]
    edge = 3 * part
    return (
        layer_out,
        input_grad,
        jnp.stack([v[:, :head_cols] for v in thirds], axis=1),
        jnp.concatenate([v[:, head_cols:] for v in thirds], axis=1).T,
        grad_gate_up,
        grad_down,
        own_attn[:, edge : edge + 2],
        own_attn[:, edge + 2 : edge + 4],
    )


def solution(mesh):
    in_specs = (
        P(None, ("row", "col"), None),
        P(None, ("row", "col")),
        P(None, ("row", "col")),
        P("row", None, "col"),
        P("col", "row"),
        P("row", None, "col"),
        P("col", "row"),
        P("row", None),
        P("row", None),
        P(None, ("row", "col"), None),
    )
    out_specs = (
        P(None, ("row", "col"), None),
        P(None, ("row", "col"), None),
        P("row", None, "col"),
        P("col", "row"),
        P("row", None, "col"),
        P("col", "row"),
        P("row", None),
        P("row", None),
    )
    return jax.shard_map(
        functools.partial(on_device, Links(mesh)), mesh=mesh, in_specs=in_specs, out_specs=out_specs, check_vma=False
    )
```

```python
import functools
import math

import jax
import jax.numpy as jnp
from jax import lax
from jax.experimental import pallas as pl
from jax.experimental.pallas import tpu as pltpu
from jax.sharding import PartitionSpec as P

HD = 64
PAIR = 2 * HD
QROWS = 256
epsilon = 1e-12
rope_base = 1000.0
masked_score = -1e30
f32 = jnp.float32
bf16 = jnp.bfloat16

NN = (((1,), (0,)), ((), ()))
NT = (((1,), (1,)), ((), ()))
TN = (((0,), (0,)), ((), ()))


def dot(a, b, dims=NN):
    return lax.dot_general(a, b, dims, preferred_element_type=f32)


def rope_tables(positions, width):
    half_dim = HD // 2
    freq = rope_base ** (-jnp.arange(half_dim, dtype=f32) / half_dim)
    angles = positions.astype(f32)[:, None] * freq[None, :]
    cosine, sine = jnp.cos(angles), jnp.sin(angles)
    times = width // HD
    return (
        jnp.tile(jnp.concatenate([cosine, cosine], axis=1), (1, times)),
        jnp.tile(jnp.concatenate([-sine, sine], axis=1), (1, times)),
    )


def rotated(values, cosine, sine):
    width = values.shape[1]
    lane = lax.broadcasted_iota(jnp.int32, values.shape, 1)
    up = pltpu.roll(values, width - HD // 2, 1)
    down = pltpu.roll(values, HD // 2, 1)
    return values * cosine + jnp.where(lane % HD < HD // 2, up, down) * sine


def normalize(hidden):
    centred = hidden - jnp.mean(hidden, axis=-1, keepdims=True)
    variance = jnp.mean(centred * centred, axis=-1, keepdims=True)
    inv_std = lax.rsqrt(variance + epsilon)
    return (centred * inv_std, inv_std)


def norm_back(grad_norm, normed, inv_std):
    return inv_std * (
        grad_norm
        - jnp.mean(grad_norm, axis=-1, keepdims=True)
        - normed * jnp.mean(grad_norm * normed, axis=-1, keepdims=True)
    )


BLOCKS = 4


def block_starts(width):
    return [(0, 0), (0, width // 2), (1, 0), (1, width // 2)]


def start_weights(blocks, w_ref, sems):
    @pl.when(pl.program_id(0) == 0)
    def _():
        for block, (slot, row) in zip(blocks, block_starts(w_ref.shape[1])):
            pltpu.make_async_copy(
                block, w_ref.at[slot, pl.ds(row, block.shape[0])], sems.at[slot]
            ).start()


def wait_weights(w_ref, sems, slot):
    pltpu.make_async_copy(w_ref.at[slot], w_ref.at[slot], sems.at[slot]).wait()


def weight_scratch(blocks):
    width = 2 * blocks[0].shape[0]
    return [
        pltpu.VMEM((2, width, blocks[0].shape[1]), bf16),
        pltpu.SemaphoreType.DMA((2,)),
    ]


ANY = pl.BlockSpec(memory_space=pl.ANY)


def cost(flops, nbytes, exps=0):
    return pl.CostEstimate(flops=int(flops), bytes_accessed=int(nbytes), transcendentals=int(exps))


def whole(shape):
    return pl.BlockSpec(shape, lambda *_: (0,) * len(shape), pipeline_mode=pl.Buffered(1))


def qkv_kernel(own_ref, other_ref, cos_ref, sin_ref, *rest):
    blocks, (q_ref, kv_ref, wo_ref, w_ref, sems) = rest[:BLOCKS], rest[BLOCKS:]
    slot = pl.program_id(0)
    start_weights(blocks, w_ref, sems)
    wait_weights(w_ref, sems, slot)
    part = w_ref.shape[2] // 3
    rows = own_ref.shape[0]
    for i, x_ref in enumerate((own_ref, other_ref)):
        span = slice(i * rows, (i + 1) * rows)
        cosine, sine = cos_ref[span, :], sin_ref[span, :]
        x = x_ref[...]
        q = dot(x, w_ref[slot, :, :part])
        q_ref[span, :] = (rotated(q, cosine, sine) * (1.0 / math.sqrt(HD))).astype(bf16)
        k = dot(x, w_ref[slot, :, part : 2 * part])
        kv_ref[span, :part] = rotated(k, cosine, sine).astype(bf16)
        kv_ref[span, part:] = dot(x, w_ref[slot, :, 2 * part :]).astype(bf16)
    lane = lax.broadcasted_iota(jnp.int32, (w_ref.shape[1], part), 1)
    out = jnp.zeros(lane.shape, f32)
    for h in range(3):
        piece = w_ref[slot, :, h * part : (h + 1) * part].astype(f32)
        piece = pltpu.roll(piece, (h + 1) * HD, 1)
        out = jnp.where(lane // HD == h, piece, out)
    wo_ref[...] = out.astype(bf16)


def qkv(own, other, cosine, sine, blocks):
    rows, width = own.shape
    part = blocks[0].shape[1] // 3
    table = whole((2 * rows, part))
    return pl.pallas_call(
        qkv_kernel,
        grid=(2,),
        in_specs=[whole((rows, width))] * 2 + [table] * 2 + [ANY] * BLOCKS,
        out_specs=[
            pl.BlockSpec((2 * rows, part), lambda i: (0, i)),
            pl.BlockSpec((2 * rows, 2 * part), lambda i: (0, i)),
            pl.BlockSpec((width, part), lambda i: (0, i)),
        ],
        scratch_shapes=weight_scratch(blocks),
        out_shape=[
            jax.ShapeDtypeStruct((2 * rows, 2 * part), bf16),
            jax.ShapeDtypeStruct((2 * rows, 4 * part), bf16),
            jax.ShapeDtypeStruct((width, 2 * part), bf16),
        ],
        cost_estimate=cost(24 * rows * width * part, 40 * width * part),
        compiler_params=pltpu.CompilerParams(vmem_limit_bytes=14 << 20),
        name="qkv",
    )(own, other, cosine, sine, *blocks)


def attend_kernel(q_ref, kv_ref, segq_ref, segk_ref, out_ref, log_ref, vt_ref):
    block, part = q_ref.shape
    low_half = lax.broadcasted_iota(jnp.int32, (block, PAIR), 1) < HD

    @pl.when(pl.program_id(0) == 0)
    def _():
        vt_ref[...] = kv_ref[:, part:].T

    q = q_ref[...]
    bias = jnp.where(segk_ref[...] == segq_ref[...], 0.0, masked_score)
    parts = []
    for h in range(3):
        pair = slice(h // 2 * PAIR, (h // 2 + 1) * PAIR)
        mine = low_half if h % 2 == 0 else jnp.logical_not(low_half)
        masked = jnp.where(mine, q[:, pair], jnp.zeros((block, PAIR), bf16))
        scores = dot(kv_ref[:, pair], masked, NT) + bias
        top = jnp.max(scores, axis=0, keepdims=True)
        expo = jnp.exp(scores - top)
        total = jnp.sum(expo, axis=0, keepdims=True)
        out = dot(vt_ref[h * HD : (h + 1) * HD, :], expo.astype(bf16))
        parts.append(out / total)
        log_ref[h : h + 1, :] = top + jnp.log(total)
    parts.append(jnp.zeros((HD, block), f32))
    out_ref[...] = jnp.concatenate(parts, axis=0).T.astype(bf16)


def attend(quarter, q, kv, seg_row, seg_col):
    rows = q.shape[0]
    part = q.shape[1] // 2
    return pl.pallas_call(
        attend_kernel,
        grid=(rows // QROWS,),
        in_specs=[
            pl.BlockSpec((QROWS, part), lambda i: (i, quarter)),
            pl.BlockSpec((rows, 2 * part), lambda i: (0, quarter)),
            pl.BlockSpec((1, QROWS), lambda i: (0, i)),
            whole((rows, 1)),
        ],
        out_specs=[
            pl.BlockSpec((QROWS, part), lambda i: (i, 0)),
            pl.BlockSpec((8, QROWS), lambda i: (0, i)),
        ],
        out_shape=[
            jax.ShapeDtypeStruct((rows, part), bf16),
            jax.ShapeDtypeStruct((8, rows), f32),
        ],
        scratch_shapes=[pltpu.VMEM((part, rows), bf16)],
        cost_estimate=cost(16 * rows * rows * part, 12 * rows * part, rows * rows * 3),
        compiler_params=pltpu.CompilerParams(vmem_limit_bytes=8 << 20),
        name="attend",
    )(q, kv, seg_row, seg_col)


def attend_back_kernel(
    q_ref, kv_ref, own_ref, other_ref, wo_ref, att_ref, log_ref, segq_ref, segk_ref, cos_ref, sin_ref,
    dq_ref, dkv_ref, kt_ref, dk_ref, dv_ref,
):
    step = pl.program_id(0)
    block, part = q_ref.shape
    low_half = lax.broadcasted_iota(jnp.int32, (block, PAIR), 1) < HD

    @pl.when(step == 0)
    def _():
        kt_ref[...] = kv_ref[:, :part].T
        dk_ref[...] = jnp.zeros_like(dk_ref)
        dv_ref[...] = jnp.zeros_like(dv_ref)

    low = jnp.where(step < pl.num_programs(0) // 2, own_ref[...], other_ref[...])
    do = dot(low, wo_ref[...]).astype(bf16)
    prod = do.astype(f32) * att_ref[...].astype(f32)
    high = prod.astype(bf16)
    rest = (prod - high.astype(f32)).astype(bf16)
    row = lax.broadcasted_iota(jnp.int32, (8, part), 0)
    lane = lax.broadcasted_iota(jnp.int32, (8, part), 1) // HD
    pick = jnp.where(row == lane, 1.0, 0.0).astype(bf16)
    delta = dot(pick, high, NT) + dot(pick, rest, NT)

    q = q_ref[...]
    bias = jnp.where(segk_ref[...] == segq_ref[...], 0.0, masked_score)
    zero = jnp.zeros((block, PAIR), bf16)
    dq = []
    for h in range(3):
        pair = slice(h // 2 * PAIR, (h // 2 + 1) * PAIR)
        values = slice(part + h // 2 * PAIR, part + (h // 2 + 1) * PAIR)
        mine = low_half if h % 2 == 0 else jnp.logical_not(low_half)
        q_head = jnp.where(mine, q[:, pair], zero)
        do_head = jnp.where(mine, do[:, pair], zero)
        scores = dot(kv_ref[:, pair], q_head, NT) + bias
        probs = jnp.exp(scores - log_ref[h : h + 1, :])
        dprobs = dot(kv_ref[:, values], do_head, NT)
        dscores = (probs * (dprobs - delta[h : h + 1, :])).astype(bf16)
        dv_ref[:, pair] += dot(probs.astype(bf16), do_head)
        dk_ref[:, pair] += dot(dscores, q_head)
        dq.append(dot(kt_ref[h * HD : (h + 1) * HD, :], dscores))
    dq.append(jnp.zeros((HD, block), f32))
    dq = (jnp.concatenate(dq, axis=0) * (1.0 / math.sqrt(HD))).T
    span = pl.ds(pl.multiple_of(step * block, block), block)
    dq_ref[...] = rotated(dq, cos_ref[span, :], -sin_ref[span, :]).astype(bf16)

    @pl.when(step == pl.num_programs(0) - 1)
    def _():
        dkv_ref[:, :part] = rotated(dk_ref[...], cos_ref[...], -sin_ref[...]).astype(bf16)
        dkv_ref[:, part:] = dv_ref[...].astype(bf16)


def attend_back(quarter, q, kv, own, other, wo, att, logs, seg_row, seg_col, cosine, sine):
    rows = q.shape[0]
    width = own.shape[1]
    part = q.shape[1] // 2
    steps = rows // QROWS
    return pl.pallas_call(
        attend_back_kernel,
        grid=(steps,),
        in_specs=[
            pl.BlockSpec((QROWS, part), lambda i: (i, quarter)),
            pl.BlockSpec((rows, 2 * part), lambda i: (0, quarter)),
            pl.BlockSpec((QROWS, width), lambda i: (jnp.minimum(i, steps // 2 - 1), 0)),
            pl.BlockSpec((QROWS, width), lambda i: (jnp.maximum(i - steps // 2, 0), 0)),
            pl.BlockSpec((width, part), lambda i: (0, quarter)),
            pl.BlockSpec((QROWS, part), lambda i: (i, 0)),
            pl.BlockSpec((8, QROWS), lambda i: (0, i)),
            pl.BlockSpec((1, QROWS), lambda i: (0, i)),
            whole((rows, 1)),
            whole((rows, part)),
            whole((rows, part)),
        ],
        out_specs=[
            pl.BlockSpec((QROWS, part), lambda i: (i, 0)),
            whole((rows, 2 * part)),
        ],
        out_shape=[
            jax.ShapeDtypeStruct((rows, part), bf16),
            jax.ShapeDtypeStruct((rows, 2 * part), bf16),
        ],
        scratch_shapes=[
            pltpu.VMEM((part, rows), bf16),
            pltpu.VMEM((rows, part), f32),
            pltpu.VMEM((rows, part), f32),
        ],
        cost_estimate=cost(40 * rows * rows * part, 30 * rows * part, rows * rows * 3),
        compiler_params=pltpu.CompilerParams(vmem_limit_bytes=18 << 20),
        name="attend_back",
    )(q, kv, own, other, wo, att, logs, seg_row, seg_col, cosine, sine)


def project_kernel(att_a_ref, att_b_ref, wo_ref, own_ref, send_ref):
    part = att_a_ref.shape[1]
    rows = own_ref.shape[0]
    for out_ref, span in ((send_ref, slice(rows, 2 * rows)), (own_ref, slice(0, rows))):
        out = dot(att_a_ref[span, :], wo_ref[:, :part], NT) + dot(att_b_ref[span, :], wo_ref[:, part:], NT)
        out_ref[...] = out.astype(out_ref.dtype)


def project(att_a, att_b, wo):
    rows, part = att_a.shape
    rows = rows // 2
    width = wo.shape[0]
    return pl.pallas_call(
        project_kernel,
        grid=(1,),
        in_specs=[whole(att_a.shape)] * 2 + [whole(wo.shape)],
        out_specs=[whole((rows, width))] * 2,
        out_shape=[
            jax.ShapeDtypeStruct((rows, width), f32),
            jax.ShapeDtypeStruct((rows, width), bf16),
        ],
        cost_estimate=cost(8 * rows * width * part, 16 * rows * width),
        compiler_params=pltpu.CompilerParams(vmem_limit_bytes=10 << 20),
        name="project",
    )(att_a, att_b, wo)


def first_kernel(
    x_ref, own_ref, came_ref, norm_a_ref, norm_b_ref, n_ref, s_ref, low_ref, low_t_ref, gains_ref
):
    norms = jnp.concatenate([norm_a_ref[...], norm_b_ref[...]], axis=0).astype(f32).T
    gains_ref[...] = norms[:8]
    branch = own_ref[...] + came_ref[...].astype(f32)
    normed, inv = normalize(x_ref[...].astype(f32) + branch)
    n_ref[...] = normed
    s_ref[...] = jnp.broadcast_to(inv, s_ref.shape)
    first = normed * norms[0:1] + norms[2:3]
    low_ref[...] = first.astype(bf16)
    low_t_ref[...] = first.T.astype(bf16)


def first_norm(x, own, came, norm_a, norm_b):
    rows, width = x.shape
    at = norm_a.shape[1] // 128 - 1
    strip = pl.BlockSpec((width // 2, 128), lambda i: (0, at))
    return pl.pallas_call(
        first_kernel,
        grid=(1,),
        in_specs=[whole(x.shape)] * 3 + [strip] * 2,
        out_specs=[
            whole((rows, width)), whole((rows, 128)), whole((rows, width)), whole((width, rows)), whole((8, width)),
        ],
        out_shape=[
            jax.ShapeDtypeStruct((rows, width), f32),
            jax.ShapeDtypeStruct((rows, 128), f32),
            jax.ShapeDtypeStruct((rows, width), bf16),
            jax.ShapeDtypeStruct((width, rows), bf16),
            jax.ShapeDtypeStruct((8, width), f32),
        ],
        cost_estimate=cost(20 * rows * width, 16 * rows * width),
        compiler_params=pltpu.CompilerParams(vmem_limit_bytes=10 << 20),
        name="first_norm",
    )(x, own, came, norm_a, norm_b)


def mlp_kernel(has_base, low_ref, *rest):
    if has_base:
        base_ref, rest = rest[0], rest[1:]
    blocks, (act_ref, feed_ref, w_ref, sems, sum_ref) = rest[:BLOCKS], rest[BLOCKS:]
    slot = pl.program_id(0)
    half = act_ref.shape[3]
    start_weights(blocks, w_ref, sems)

    @pl.when(slot == 0)
    def _():
        sum_ref[...] = base_ref[...] if has_base else jnp.zeros_like(sum_ref)

    wait_weights(w_ref, sems, slot)

    gate = dot(low_ref[...], w_ref[slot, :, half : 2 * half])
    up = dot(low_ref[...], w_ref[slot, :, 2 * half : 3 * half])
    act_ref[0, 0] = gate.astype(bf16)
    act_ref[0, 1] = up.astype(bf16)
    act_ref[0, 2] = (gate / (1.0 + jnp.exp(-gate)) * up).astype(bf16)
    sum_ref[...] += dot(act_ref[0, 2], w_ref[slot, :, :half], NT)

    @pl.when(slot == 1)
    def _():
        feed_ref[...] = sum_ref[...].astype(feed_ref.dtype)


def mlp(low, base, blocks, half, dtype):
    rows, width = low.shape
    has_base = base is not None
    extra = [base] if has_base else []
    return pl.pallas_call(
        functools.partial(mlp_kernel, has_base),
        grid=(2,),
        in_specs=[whole((rows, width))] * (1 + has_base) + [ANY] * BLOCKS,
        out_specs=[
            pl.BlockSpec((1, 3, rows, half), lambda i: (i, 0, 0, 0)),
            whole((rows, width)),
        ],
        scratch_shapes=weight_scratch(blocks) + [pltpu.VMEM((rows, width), f32)],
        out_shape=[
            jax.ShapeDtypeStruct((2, 3, rows, half), bf16),
            jax.ShapeDtypeStruct((rows, width), dtype),
        ],
        cost_estimate=cost(12 * rows * width * half, 30 * half * width, 2 * rows * half),
        compiler_params=pltpu.CompilerParams(vmem_limit_bytes=14 << 20),
        name="mlp",
    )(low, *extra, *blocks)


def second_kernel(
    n_ref, gains_ref, feed_ref, came_ref, dy_ref, out_ref, dh_ref, low_ref, low_t_ref, sums_ref
):
    first = n_ref[...] * gains_ref[0:1] + gains_ref[2:3]
    normed, inv = normalize(first + feed_ref[...] + came_ref[...].astype(f32))
    out_ref[...] = (normed * gains_ref[1:2] + gains_ref[3:4]).astype(bf16)
    dy = dy_ref[...]
    sums_ref[...] = jnp.zeros_like(sums_ref)
    sums_ref[1:2] = jnp.sum(dy * normed, axis=0, keepdims=True)
    sums_ref[3:4] = jnp.sum(dy, axis=0, keepdims=True)
    dh = norm_back(dy * gains_ref[1:2], normed, inv)
    dh_ref[...] = dh
    low_ref[...] = dh.astype(bf16)
    low_t_ref[...] = dh.T.astype(bf16)


def second_norm(n1, gains, feed, came, dy):
    rows, width = n1.shape
    full = whole((rows, width))
    return pl.pallas_call(
        second_kernel,
        grid=(1,),
        in_specs=[full, whole((8, width)), full, full, full],
        out_specs=[full, full, full, whole((width, rows)), whole((8, width))],
        out_shape=[
            jax.ShapeDtypeStruct((rows, width), bf16),
            jax.ShapeDtypeStruct((rows, width), f32),
            jax.ShapeDtypeStruct((rows, width), bf16),
            jax.ShapeDtypeStruct((width, rows), bf16),
            jax.ShapeDtypeStruct((8, width), f32),
        ],
        cost_estimate=cost(40 * rows * width, 22 * rows * width),
        compiler_params=pltpu.CompilerParams(vmem_limit_bytes=14 << 20),
        name="second_norm",
    )(n1, gains, feed, came, dy)


def mlp_back_kernel(has_base, *rest):
    dfeeds, dfeeds_t, lows_t, acts = rest[:2], rest[2:4], rest[4:6], rest[6:8]
    rest = rest[8:]
    if has_base:
        bases, rest = rest[:2], rest[2:]
    blocks, rest = rest[:BLOCKS], rest[BLOCKS:]
    own_ref, other_ref, to_x_ref, to_y_ref, keep_ref, w_ref, sems, part_ref, sum_ref = rest
    slot = pl.program_id(0)
    rows = own_ref.shape[0]
    half = acts[0].shape[3]
    start_weights(blocks, w_ref, sems)

    @pl.when(slot == 0)
    def _():
        for i in range(2):
            sum_ref[i * rows : (i + 1) * rows, :] = (
                bases[i][...] if has_base else jnp.zeros((rows, sum_ref.shape[1]), f32)
            )

    wait_weights(w_ref, sems, slot)

    for i in range(2):
        span = slice(i * rows, (i + 1) * rows)
        dhidden = dot(dfeeds[i][...], w_ref[slot, :, :half])
        gate = acts[i][0, 0].astype(f32)
        up = acts[i][0, 1].astype(f32)
        sg = 1.0 / (1.0 + jnp.exp(-gate))
        dgate = dhidden * up * sg * (1.0 + gate * (1.0 - sg))
        dup = dhidden * (gate * sg)
        part_ref[span, :half] = dgate.astype(bf16)
        part_ref[span, half:] = dup.astype(bf16)
        sum_ref[span, :] += dot(part_ref[span, :], w_ref[slot, :, half : 3 * half], NT)
    gate_up = (
        dot(lows_t[0][...], part_ref[:rows, :]) + dot(lows_t[1][...], part_ref[rows:, :])
    ).astype(bf16)
    down = (
        dot(dfeeds_t[0][...], acts[0][0, 2]) + dot(dfeeds_t[1][...], acts[1][0, 2])
    ).astype(bf16)
    cut = keep_ref.shape[1]

    def emit(out_ref, at, block):
        span = slice(block * cut, (block + 1) * cut)
        out_ref[at, :, :half] = down[span]
        out_ref[at, :, half:] = gate_up[span]

    emit(to_x_ref, 0, 3)

    @pl.when(slot == 0)
    def _():
        for block in range(3):
            emit(keep_ref, block, block)

    @pl.when(slot == 1)
    def _():
        emit(to_y_ref, 0, 0)
        emit(to_y_ref, 1, 2)
        emit(keep_ref, 3, 1)
        own_ref[...] = sum_ref[:rows, :]
        other_ref[...] = sum_ref[rows:, :].astype(other_ref.dtype)


def mlp_back(bases, dfeeds, dfeeds_t, lows_t, acts, blocks):
    rows, width = dfeeds[0].shape
    half = acts[0].shape[3]
    has_base = bases is not None
    full = whole((rows, width))
    return pl.pallas_call(
        functools.partial(mlp_back_kernel, has_base),
        grid=(2,),
        in_specs=[full] * 2
        + [whole((width, rows))] * 4
        + [pl.BlockSpec((1, 3, rows, half), lambda i: (i, 0, 0, 0))] * 2
        + [full] * (2 * has_base)
        + [ANY] * BLOCKS,
        out_specs=[
            full,
            full,
            pl.BlockSpec((1, width // 4, 3 * half), lambda i: (i, 0, 0)),
            whole((2, width // 4, 3 * half)),
            whole((4, width // 4, 3 * half)),
        ],
        scratch_shapes=weight_scratch(blocks)
        + [pltpu.VMEM((2 * rows, 2 * half), bf16), pltpu.VMEM((2 * rows, width), f32)],
        out_shape=[
            jax.ShapeDtypeStruct((rows, width), f32),
            jax.ShapeDtypeStruct((rows, width), bf16 if has_base else f32),
            jax.ShapeDtypeStruct((2, width // 4, 3 * half), bf16),
            jax.ShapeDtypeStruct((2, width // 4, 3 * half), bf16),
            jax.ShapeDtypeStruct((4, width // 4, 3 * half), bf16),
        ],
        cost_estimate=cost(48 * rows * width * half, 100 * half * width, 4 * rows * half),
        compiler_params=pltpu.CompilerParams(vmem_limit_bytes=28 << 20),
        name="mlp_back",
    )(*dfeeds, *dfeeds_t, *lows_t, *acts, *(bases if has_base else ()), *blocks)


def first_back_kernel(
    base_ref, own_ref, came_ref, n_ref, s_ref, gains_ref, sums_ref, dh_ref, low_ref, low_t_ref
):
    dfirst = base_ref[...] + own_ref[...] + came_ref[...].astype(f32)
    normed = n_ref[...]
    width = dfirst.shape[1]
    gain_sum = jnp.sum(dfirst * normed, axis=0, keepdims=True)
    bias_sum = jnp.sum(dfirst, axis=0, keepdims=True)
    sums = sums_ref[...]
    stacked = jnp.concatenate(
        [gain_sum, sums[1:2], bias_sum, sums[3:4], jnp.zeros((124, width), f32)], axis=0
    )
    rows = dfirst.shape[0]
    low_t_ref[:, rows:] = stacked.T.astype(bf16)
    dh = norm_back(dfirst * gains_ref[0:1], normed, s_ref[:, 0:1])
    dh_ref[...] = dh
    low_ref[...] = dh.astype(bf16)
    low_t_ref[:, :rows] = dh.T.astype(bf16)


def first_back(base, own, came, n1, s1, gains, sums):
    rows, width = n1.shape
    full = whole((rows, width))
    return pl.pallas_call(
        first_back_kernel,
        grid=(1,),
        in_specs=[full] * 4 + [whole((rows, 128)), whole((8, width)), whole((8, width))],
        out_specs=[full, full, whole((width, rows + 128))],
        out_shape=[
            jax.ShapeDtypeStruct((rows, width), f32),
            jax.ShapeDtypeStruct((rows, width), bf16),
            jax.ShapeDtypeStruct((width, rows + 128), bf16),
        ],
        cost_estimate=cost(40 * rows * width, 20 * rows * width),
        compiler_params=pltpu.CompilerParams(vmem_limit_bytes=14 << 20),
        name="first_back",
    )(base, own, came, n1, s1, gains, sums)


def qkv_back_kernel(
    quarter, has_base, dq_ref, dkv_ref, x_a_ref, x_b_ref, low_a_ref, low_b_ref, cols_a_ref, cols_b_ref, att_ref, *rest
):
    if has_base:
        bases, rest = rest[:2], rest[2:]
    blocks, (own_ref, other_ref, send_ref, keep_ref, w_ref, sem) = rest[:2], rest[2:]
    rows = own_ref.shape[0]
    part = dq_ref.shape[1]
    starts = [row for slot, row in block_starts(w_ref.shape[0]) if slot == quarter]
    for block, row in zip(blocks, starts):
        pltpu.make_async_copy(block, w_ref.at[pl.ds(row, block.shape[0])], sem).start()
    d_out = dot(low_a_ref[...], att_ref[:rows, :]) + dot(low_b_ref[...], att_ref[rows:, :])
    lane = lax.broadcasted_iota(jnp.int32, d_out.shape, 1)
    cut = keep_ref.shape[1]
    if quarter == 0:
        places = [(keep_ref, 0), (keep_ref, 1), (keep_ref, 2), (send_ref, 0)]
    else:
        places = [(send_ref, 0), (keep_ref, 0), (send_ref, 1), (send_ref, 2)]

    def emit(value, lanes):
        for block, (out_ref, at) in enumerate(places):
            out_ref[at, :, lanes] = value[block * cut : (block + 1) * cut]

    for h in range(3):
        source, at = (dq_ref, 0) if h == 0 else (dkv_ref, (h - 1) * part)
        piece = dot(x_a_ref[...], source[:rows, at : at + part]) + dot(x_b_ref[...], source[rows:, at : at + part])
        moved = pltpu.roll(d_out, (3 - h) * HD, 1)
        emit(jnp.where(lane < 3 * HD, piece, moved).astype(bf16), slice(h * part, (h + 1) * part))
    cols = cols_a_ref[...].astype(f32) + cols_b_ref[...].astype(f32)
    emit(cols.astype(bf16), slice(3 * part, 3 * part + 128))
    pltpu.make_async_copy(w_ref, w_ref, sem).wait()
    for i, out_ref in enumerate((own_ref, other_ref)):
        span = slice(i * rows, (i + 1) * rows)
        total = dot(dq_ref[span, :], w_ref[:, :part], NT) + dot(dkv_ref[span, :], w_ref[:, part:], NT)
        if has_base:
            total = total + bases[i][...]
        out_ref[...] = total.astype(out_ref.dtype)


def qkv_back(quarter, bases, dq, dkv, x_t, low_t, att, blocks):
    rows = dq.shape[0] // 2
    width = low_t[0].shape[0]
    part = dq.shape[1]
    has_base = bases is not None
    full = whole((rows, width))
    turned = whole((width, rows))
    blocks = [b for b, (slot, _) in zip(blocks, block_starts(width)) if slot == quarter]
    counts = (1, 3) if quarter == 0 else (3, 1)
    pieces = [(n, width // 4, 3 * part + 128) for n in counts]
    return pl.pallas_call(
        functools.partial(qkv_back_kernel, quarter, has_base),
        grid=(1,),
        in_specs=[whole(dq.shape), whole(dkv.shape)]
        + [turned] * 4
        + [pl.BlockSpec((width, 128), lambda i: (0, rows // 128))] * 2
        + [whole(att.shape)]
        + [full] * (2 * has_base)
        + [ANY] * 2,
        out_specs=[full, full] + [whole(p) for p in pieces],
        scratch_shapes=[pltpu.VMEM((width, 3 * part), bf16), pltpu.SemaphoreType.DMA],
        out_shape=[
            jax.ShapeDtypeStruct((rows, width), f32),
            jax.ShapeDtypeStruct((rows, width), bf16 if has_base else f32),
        ]
        + [jax.ShapeDtypeStruct(p, bf16) for p in pieces],
        cost_estimate=cost(26 * rows * width * part, 40 * width * part),
        compiler_params=pltpu.CompilerParams(vmem_limit_bytes=16 << 20),
        name="qkv_back",
    )(dq, dkv, *x_t, *low_t, *low_t, att, *(bases if has_base else ()), *blocks)


def bits_of(n):
    bits = n.bit_length() - 1
    if 1 << bits != n:
        raise ValueError("row count")
    return bits


class Links:
    def __init__(self, mesh):
        self.rows = mesh.shape["row"]
        self.cols = mesh.shape["col"]
        self.bits = bits_of(self.rows // 2)

    def locate(self):
        row = lax.axis_index("row")
        col = lax.axis_index("col")
        return row // 2, row % 2, col // (self.cols // 2), col % 2

    def send(self, v, move):
        pairs = []
        for row in range(self.rows):
            for col in range(self.cols):
                ring, x, y, k = move(row // 2, row % 2, col // (self.cols // 2), col % 2)
                pairs.append(
                    (row * self.cols + col, (ring * 2 + x) * self.cols + y * (self.cols // 2) + k)
                )
        return lax.ppermute(v, ("row", "col"), pairs)

    def across(self, v):
        return self.send(v, lambda ring, x, y, k: (ring, x, 1 - y, k))

    def beside(self, v):
        return self.send(v, lambda ring, x, y, k: (ring, x, y, 1 - k))

    def far(self, v):
        return self.send(
            v, lambda ring, x, y, k: (ring, 1 - x, y, k) if k else (ring, x, 1 - y, k)
        )

    def along(self, v):
        return self.send(v, lambda ring, x, y, k: (ring, 1 - x, y, k))

    def turned(self, v, bit):
        return self.send(v, lambda ring, x, y, k: (ring ^ (1 << bit), x, y, k))

    def ring_gather(self, block):
        for bit in reversed(range(self.bits)):
            block = jnp.concatenate([block, self.turned(block, bit)], axis=0)
        return block

    def ring_split(self, block):
        own, low = jnp.split(block, 2, axis=0)
        return own, low.astype(bf16)

    def ring_scatter(self, own, low):
        for bit in range(self.bits):
            if bit > 0:
                own, low = self.ring_split(own)
            own = own + self.turned(low, bit).astype(f32)
        return own


def tie(value, *others):
    return lax.optimization_barrier((value, *others))[0]


class Scatter:
    def __init__(self, links, to_x, to_y, keep):
        self.links, self.keep = links, keep
        self.by_x = [links.along(v) for v in to_x]
        self.by_y = links.across(to_y)

    def second(self):
        by_x = self.by_x[0][1] if len(self.by_x) == 1 else self.by_x[1][0]
        to_x = (self.keep[2].astype(f32) + self.by_y[1].astype(f32)).astype(bf16)
        to_y = (self.keep[3].astype(f32) + by_x.astype(f32)).astype(bf16)
        self.late_x, self.late_y = self.links.along(to_x), self.links.across(to_y)
        return to_x, to_y

    def third(self):
        low = self.keep[0].astype(f32) + self.by_y[0].astype(f32) + self.late_x.astype(f32)
        high = self.keep[1].astype(f32) + self.by_x[0][0].astype(f32) + self.late_y.astype(f32)
        self.own, self.low = self.links.ring_split(jnp.concatenate([low, high], axis=0))
        return [self.low]

    def last(self):
        return self.links.ring_scatter(self.own, self.low)


def relative_order(links, depth):
    ring, x, _, _ = links.locate()
    where = lax.broadcasted_iota(jnp.int32, (1, links.rows * depth), 1)
    block, inside = where // depth, where % depth
    steps = links.rows // 2
    place = block % steps
    turn = jnp.zeros_like(place)
    for bit in reversed(range(links.bits)):
        turn = turn + (place % 2 << bit)
        place = place // 2
    row = jnp.bitwise_xor(ring, turn) * 2 + jnp.bitwise_xor(x, block // steps)
    return row * depth + inside


def on_device(
    links, tokens, segments, positions, w_qkv, w_out, w_gate_up, w_down, norm_gain, norm_bias, cotangent
):
    ring, x_place, side, core = links.locate()
    depth = w_qkv.shape[0]
    width = tokens.shape[2]
    head_cols = w_qkv.shape[2]
    hid = w_gate_up.shape[2]
    sizes = [hid - hid // 3, hid // 3]
    rows = 2 * tokens.shape[1]
    mine = rows // 2
    part = head_cols + HD

    source = relative_order(links, depth)
    swap = (lax.broadcasted_iota(jnp.int32, (width, width), 0) == source).astype(bf16)

    def split(v):
        high = v.astype(bf16)
        return high, (v - high.astype(f32)).astype(bf16)

    def own_and_other(v):
        own = lax.dynamic_index_in_dim(v, side, 0, keepdims=False)
        return own, lax.dynamic_index_in_dim(v, 1 - side, 0, keepdims=False)

    def from_sequence(own, came):
        first = side == 0
        return jnp.stack([jnp.where(first, own, came), jnp.where(first, came, own)], axis=0)

    out_t = w_out.T
    attn_shard = jnp.concatenate(
        sum(
            [[w_qkv[:, p], out_t[:, p * HD : (p + 1) * HD]] for p in range(3)],
            [],
        ),
        axis=1,
    )
    norms = jnp.concatenate([norm_gain, norm_bias], axis=1)
    norms = jnp.pad(norms, ((0, 0), (0, 128 - norms.shape[1])))
    down_t = w_down.T
    mlp_shards = []
    for h, at in enumerate([0, sizes[0]]):
        cols = slice(at, at + sizes[h])
        pieces = [down_t[:, cols], w_gate_up[:, 0, cols], w_gate_up[:, 1, cols]]
        mlp_shards.append(jnp.concatenate(pieces + ([norms] if h == 0 else []), axis=1))

    small_own, small_other = own_and_other(jnp.stack([segments, positions], axis=1))
    small_came = links.across(small_other)
    tokens_own, tokens_other = own_and_other(tokens)
    tokens_came = links.across(tie(tokens_other, attn_shard, small_other))
    dy_own, dy_other = own_and_other(cotangent)
    dy_came = links.across(tie(dy_other.astype(bf16), attn_shard, small_other))

    odd = core == 1
    ring_a = links.ring_gather(attn_shard)
    x_a, y_a = links.along(ring_a), links.across(ring_a)
    ring_b = links.ring_gather(tie(mlp_shards[0], ring_a))
    turn_a = jnp.where(odd, y_a, x_a)
    attn_w = [ring_a, x_a, y_a, links.far(turn_a)]

    x_abs = jnp.concatenate([tokens_own, tokens_came], axis=0)
    x = dot(x_abs, swap).astype(bf16)
    x_other = links.beside(x)
    small = jnp.concatenate([small_own, small_came], axis=1)
    small = jnp.concatenate([small, links.beside(small)], axis=1)
    seg_row, seg_col = small[0][None, :], small[0][:, None]
    cosine, sine = rope_tables(small[1], part)

    ring_b = tie(ring_b, turn_a)
    x_b, y_b = links.along(ring_b), links.across(ring_b)
    ring_c = links.ring_gather(tie(mlp_shards[1], ring_b))
    q, kv, wo = qkv(tie(x, ring_b, dy_came), x_other, cosine, sine, attn_w)
    att_0, logs_0 = attend(0, q, kv, seg_row, seg_col)
    att_1, logs_1 = attend(1, tie(q, att_0), kv, seg_row, seg_col)
    held_x, held_y = lax.optimization_barrier((x_b, y_b, att_1))[:2]
    turn_b = jnp.where(odd, held_y, held_x)
    mlp_b = [ring_b, x_b, y_b, links.far(turn_b)]
    ring_c = tie(ring_c, turn_b)
    x_c, y_c = links.along(ring_c), links.across(ring_c)
    own, send = project(att_0, tie(att_1, turn_b, ring_c), wo)
    n1, s1, low, low_t, gains = first_norm(x, own, links.beside(send), ring_b, x_b)
    low_other = links.beside(low)
    x_t = lax.dot_general(
        swap, tie(x_abs, low_other), (((0,), (1,)), ((), ())), preferred_element_type=f32
    ).astype(bf16)
    x_t = [x_t, links.beside(x_t)]
    low1_t = [low_t, links.beside(tie(low_t, low_other))]
    high, low_part = split(dy_own)
    dy = jnp.concatenate([dot(high, swap) + dot(low_part, swap), dot(dy_came, swap)], axis=0)
    act_b_own, feed = mlp(tie(low, x_t[1], low1_t[1], dy), None, mlp_b, sizes[0], f32)
    act_b_other, feed_other = mlp(low_other, None, mlp_b, sizes[0], f32)
    held_x, held_y = lax.optimization_barrier((x_c, y_c, feed))[:2]
    turn_c = jnp.where(odd, held_y, held_x)
    mlp_c = [ring_c, x_c, y_c, links.far(turn_c)]
    act_c_other, send = mlp(low_other, feed_other, mlp_c, sizes[1], bf16)
    came = links.beside(send)
    act_c_own, feed = mlp(tie(low, send), feed, mlp_c, sizes[1], f32)
    layer_out, dh2, dfeed, dfeed_t, sums = second_norm(n1, gains, feed, came, dy)
    dfeeds = [dfeed, links.beside(dfeed)]
    dfeeds_t = [dfeed_t, links.beside(dfeed_t)]

    own, other, to_x, to_y, keep = mlp_back(None, dfeeds, dfeeds_t, low1_t, (act_c_own, act_c_other), mlp_c)
    sum_b = Scatter(links, [to_x], to_y, keep)
    own, other, to_x, to_y, keep = mlp_back(
        (own, other), dfeeds, dfeeds_t, low1_t, (act_b_own, act_b_other), mlp_b
    )
    came = links.beside(other)
    sum_b.keep = tie(sum_b.keep, own)
    ops_b = sum_b.second()
    sum_c = Scatter(links, [tie(to_x, *ops_b)], tie(to_y, *ops_b), keep)
    dh1, low, low_t = first_back(tie(dh2, *ops_b), own, came, n1, s1, gains, sums)
    lows = [low, links.beside(low)]
    low_t = [low_t, links.beside(low_t)]
    dq, dkv = attend_back(1, q, kv, *lows, wo, att_1, logs_1, seg_row, seg_col, cosine, sine)
    sum_b.keep = tie(sum_b.keep, dq)
    block_b = sum_b.third()
    own, other, send, keep_1 = qkv_back(1, None, tie(dq, *block_b), dkv, x_t, low_t, att_1, attn_w)
    own_b = sum_b.last()
    sum_c.keep = tie(sum_c.keep, own)
    ops_c = sum_c.second()
    to_y, to_x = tie(send[:2], *ops_c), [tie(send[2:], *ops_c)]
    dq, dkv = attend_back(
        0, tie(q, own, *ops_c), kv, *lows, wo, att_0, logs_0, seg_row, seg_col, cosine, sine
    )
    sum_c.keep = tie(sum_c.keep, dq)
    block_c = sum_c.third()
    own, other, send, keep_0 = qkv_back(
        0, (own, other), tie(dq, *block_c, own_b), dkv, x_t, low_t, att_0, attn_w
    )
    own_c = sum_c.last()
    sum_a = Scatter(links, [send] + to_x, to_y, jnp.concatenate([keep_0, keep_1], axis=0))
    grad = dh1 + own + links.beside(other).astype(f32)
    high, low = split(grad)
    grad = dot(high, swap, NT) + dot(low, swap, NT)
    ops_a = sum_a.second()
    other = tie(grad[mine:].astype(bf16), *ops_a)
    input_grad = from_sequence(grad[:mine], links.across(other).astype(f32))
    layer_out = dot(layer_out, swap, NT).astype(bf16)
    layer_out = from_sequence(layer_out[:mine], links.across(tie(layer_out[mine:], *ops_a)))
    sum_a.third()
    own_attn = sum_a.last()
    own_mlp = [own_c, own_b]

    grad_down = jnp.concatenate([v[:, :n] for v, n in zip(own_mlp, sizes)], axis=1).T
    grad_gate_up = jnp.stack(
        [
            jnp.concatenate([v[:, p * n : (p + 1) * n] for v, n in zip(own_mlp, sizes)], axis=1)
            for p in (1, 2)
        ],
        axis=1,
    )
    thirds = [own_attn[:, p * part : (p + 1) * part] for p in range(3)]
    edge = 3 * part
    return (
        layer_out,
        input_grad,
        jnp.stack([v[:, :head_cols] for v in thirds], axis=1),
        jnp.concatenate([v[:, head_cols:] for v in thirds], axis=1).T,
        grad_gate_up,
        grad_down,
        own_attn[:, edge : edge + 2],
        own_attn[:, edge + 2 : edge + 4],
    )


def solution(mesh):
    in_specs = (
        P(None, ("row", "col"), None),
        P(None, ("row", "col")),
        P(None, ("row", "col")),
        P("row", None, "col"),
        P("col", "row"),
        P("row", None, "col"),
        P("col", "row"),
        P("row", None),
        P("row", None),
        P(None, ("row", "col"), None),
    )
    out_specs = (
        P(None, ("row", "col"), None),
        P(None, ("row", "col"), None),
        P("row", None, "col"),
        P("col", "row"),
        P("row", None, "col"),
        P("col", "row"),
        P("row", None),
        P("row", None),
    )
    return jax.shard_map(
        functools.partial(on_device, Links(mesh)), mesh=mesh, in_specs=in_specs, out_specs=out_specs, check_vma=False
    )
```

```python
import functools
import math

import jax
import jax.numpy as jnp
from jax import lax
from jax.experimental import pallas as pl
from jax.experimental.pallas import tpu as pltpu
from jax.sharding import PartitionSpec as P

HD = 64
PAIR = 2 * HD
QROWS = 256
epsilon = 1e-12
rope_base = 1000.0
masked_score = -1e30
f32 = jnp.float32
bf16 = jnp.bfloat16

NN = (((1,), (0,)), ((), ()))
NT = (((1,), (1,)), ((), ()))
TN = (((0,), (0,)), ((), ()))


def dot(a, b, dims=NN):
    return lax.dot_general(a, b, dims, preferred_element_type=f32)


def rope_tables(positions):
    half_dim = HD // 2
    lane = jnp.arange(PAIR)
    freq = rope_base ** (-(lane % half_dim).astype(f32) / half_dim)
    sign = jnp.where(lane % HD < half_dim, -1.0, 1.0)
    angles = positions.astype(f32)[:, None] * freq[None, :]
    return jnp.cos(angles), jnp.sin(angles) * sign[None, :]


def rotated(values, cosine, sine):
    width = values.shape[1]
    cosine = jnp.concatenate([cosine] * (width // PAIR), axis=1)
    sine = jnp.concatenate([sine] * (width // PAIR), axis=1)
    lane = lax.broadcasted_iota(jnp.int32, values.shape, 1)
    up = pltpu.roll(values, width - HD // 2, 1)
    down = pltpu.roll(values, HD // 2, 1)
    return values * cosine + jnp.where(lane % HD < HD // 2, up, down) * sine


def normalize(hidden):
    centred = hidden - jnp.mean(hidden, axis=-1, keepdims=True)
    variance = jnp.mean(centred * centred, axis=-1, keepdims=True)
    inv_std = lax.rsqrt(variance + epsilon)
    return (centred * inv_std, inv_std)


def norm_back(grad_norm, normed, inv_std):
    return inv_std * (
        grad_norm
        - jnp.mean(grad_norm, axis=-1, keepdims=True)
        - normed * jnp.mean(grad_norm * normed, axis=-1, keepdims=True)
    )


BLOCKS = 4


def block_starts(width):
    return [(0, 0), (0, width // 2), (1, 0), (1, width // 2)]


def start_weights(blocks, w_ref, sems):
    @pl.when(pl.program_id(0) == 0)
    def _():
        for block, (slot, row) in zip(blocks, block_starts(w_ref.shape[1])):
            pltpu.make_async_copy(
                block, w_ref.at[slot, pl.ds(row, block.shape[0])], sems.at[slot]
            ).start()


def wait_weights(w_ref, sems, slot):
    pltpu.make_async_copy(w_ref.at[slot], w_ref.at[slot], sems.at[slot]).wait()


def weight_scratch(blocks):
    width = 2 * blocks[0].shape[0]
    return [
        pltpu.VMEM((2, width, blocks[0].shape[1]), bf16),
        pltpu.SemaphoreType.DMA((2,)),
    ]


ANY = pl.BlockSpec(memory_space=pl.ANY)


def cost(flops, nbytes, exps=0):
    return pl.CostEstimate(flops=int(flops), bytes_accessed=int(nbytes), transcendentals=int(exps))


def whole(shape):
    return pl.BlockSpec(shape, lambda *_: (0,) * len(shape), pipeline_mode=pl.Buffered(1))


def qkv_kernel(own_ref, other_ref, cos_ref, sin_ref, *rest):
    blocks, (q_ref, kv_ref, wo_ref, w_ref, sems) = rest[:BLOCKS], rest[BLOCKS:]
    slot = pl.program_id(0)
    start_weights(blocks, w_ref, sems)
    wait_weights(w_ref, sems, slot)
    part = w_ref.shape[2] // 3
    rows = own_ref.shape[0]
    for i, x_ref in enumerate((own_ref, other_ref)):
        span = slice(i * rows, (i + 1) * rows)
        cosine, sine = cos_ref[span, :], sin_ref[span, :]
        x = x_ref[...]
        q = dot(x, w_ref[slot, :, :part])
        q_ref[span, :] = (rotated(q, cosine, sine) * (1.0 / math.sqrt(HD))).astype(bf16)
        k = dot(x, w_ref[slot, :, part : 2 * part])
        kv_ref[span, :part] = rotated(k, cosine, sine).astype(bf16)
        kv_ref[span, part:] = dot(x, w_ref[slot, :, 2 * part :]).astype(bf16)
    lane = lax.broadcasted_iota(jnp.int32, (w_ref.shape[1], part), 1)
    out = jnp.zeros(lane.shape, f32)
    for h in range(3):
        piece = w_ref[slot, :, h * part : (h + 1) * part].astype(f32)
        piece = pltpu.roll(piece, (h + 1) * HD, 1)
        out = jnp.where(lane // HD == h, piece, out)
    wo_ref[...] = out.astype(bf16)


def qkv(own, other, cosine, sine, blocks):
    rows, width = own.shape
    part = blocks[0].shape[1] // 3
    table = whole((2 * rows, PAIR))
    return pl.pallas_call(
        qkv_kernel,
        grid=(2,),
        in_specs=[whole((rows, width))] * 2 + [table] * 2 + [ANY] * BLOCKS,
        out_specs=[
            pl.BlockSpec((2 * rows, part), lambda i: (0, i)),
            pl.BlockSpec((2 * rows, 2 * part), lambda i: (0, i)),
            pl.BlockSpec((width, part), lambda i: (0, i)),
        ],
        scratch_shapes=weight_scratch(blocks),
        out_shape=[
            jax.ShapeDtypeStruct((2 * rows, 2 * part), bf16),
            jax.ShapeDtypeStruct((2 * rows, 4 * part), bf16),
            jax.ShapeDtypeStruct((width, 2 * part), bf16),
        ],
        cost_estimate=cost(24 * rows * width * part, 40 * width * part),
        compiler_params=pltpu.CompilerParams(vmem_limit_bytes=12 << 20),
        name="qkv",
    )(own, other, cosine, sine, *blocks)


def attend_kernel(q_ref, kv_ref, segq_ref, segk_ref, out_ref, log_ref, vt_ref):
    block, part = q_ref.shape
    low_half = lax.broadcasted_iota(jnp.int32, (block, PAIR), 1) < HD

    @pl.when(pl.program_id(0) == 0)
    def _():
        vt_ref[...] = kv_ref[:, part:].T

    q = q_ref[...]
    bias = jnp.where(segk_ref[...] == segq_ref[...], 0.0, masked_score)
    parts = []
    for h in range(3):
        pair = slice(h // 2 * PAIR, (h // 2 + 1) * PAIR)
        mine = low_half if h % 2 == 0 else jnp.logical_not(low_half)
        masked = jnp.where(mine, q[:, pair], jnp.zeros((block, PAIR), bf16))
        scores = dot(kv_ref[:, pair], masked, NT) + bias
        top = jnp.max(scores, axis=0, keepdims=True)
        expo = jnp.exp(scores - top)
        total = jnp.sum(expo, axis=0, keepdims=True)
        out = dot(vt_ref[h * HD : (h + 1) * HD, :], expo.astype(bf16))
        parts.append(out / total)
        log_ref[h : h + 1, :] = top + jnp.log(total)
    parts.append(jnp.zeros((HD, block), f32))
    out_ref[...] = jnp.concatenate(parts, axis=0).T.astype(bf16)


def attend(quarter, q, kv, seg_row, seg_col):
    rows = q.shape[0]
    part = q.shape[1] // 2
    return pl.pallas_call(
        attend_kernel,
        grid=(rows // QROWS,),
        in_specs=[
            pl.BlockSpec((QROWS, part), lambda i: (i, quarter)),
            pl.BlockSpec((rows, 2 * part), lambda i: (0, quarter)),
            pl.BlockSpec((1, QROWS), lambda i: (0, i)),
            whole((rows, 1)),
        ],
        out_specs=[
            pl.BlockSpec((QROWS, part), lambda i: (i, 0)),
            pl.BlockSpec((8, QROWS), lambda i: (0, i)),
        ],
        out_shape=[
            jax.ShapeDtypeStruct((rows, part), bf16),
            jax.ShapeDtypeStruct((8, rows), f32),
        ],
        scratch_shapes=[pltpu.VMEM((part, rows), bf16)],
        cost_estimate=cost(16 * rows * rows * part, 12 * rows * part, rows * rows * 3),
        compiler_params=pltpu.CompilerParams(vmem_limit_bytes=7 << 20),
        name="attend",
    )(q, kv, seg_row, seg_col)


def attend_back_kernel(
    q_ref, kv_ref, own_ref, other_ref, wo_ref, att_ref, log_ref, segq_ref, segk_ref, cos_ref, sin_ref,
    dq_ref, dkv_ref, kt_ref, dk_ref, dv_ref,
):
    step = pl.program_id(0)
    block, part = q_ref.shape
    low_half = lax.broadcasted_iota(jnp.int32, (block, PAIR), 1) < HD

    @pl.when(step == 0)
    def _():
        kt_ref[...] = kv_ref[:, :part].T
        dk_ref[...] = jnp.zeros_like(dk_ref)
        dv_ref[...] = jnp.zeros_like(dv_ref)

    low = jnp.where(step < pl.num_programs(0) // 2, own_ref[...], other_ref[...])
    do = dot(low, wo_ref[...]).astype(bf16)
    prod = do.astype(f32) * att_ref[...].astype(f32)
    high = prod.astype(bf16)
    rest = (prod - high.astype(f32)).astype(bf16)
    row = lax.broadcasted_iota(jnp.int32, (8, part), 0)
    lane = lax.broadcasted_iota(jnp.int32, (8, part), 1) // HD
    pick = jnp.where(row == lane, 1.0, 0.0).astype(bf16)
    delta = dot(pick, high, NT) + dot(pick, rest, NT)

    q = q_ref[...]
    bias = jnp.where(segk_ref[...] == segq_ref[...], 0.0, masked_score)
    zero = jnp.zeros((block, PAIR), bf16)
    dq = []
    for h in range(3):
        pair = slice(h // 2 * PAIR, (h // 2 + 1) * PAIR)
        values = slice(part + h // 2 * PAIR, part + (h // 2 + 1) * PAIR)
        mine = low_half if h % 2 == 0 else jnp.logical_not(low_half)
        q_head = jnp.where(mine, q[:, pair], zero)
        do_head = jnp.where(mine, do[:, pair], zero)
        scores = dot(kv_ref[:, pair], q_head, NT) + bias
        probs = jnp.exp(scores - log_ref[h : h + 1, :])
        dprobs = dot(kv_ref[:, values], do_head, NT)
        dscores = (probs * (dprobs - delta[h : h + 1, :])).astype(bf16)
        dv_ref[:, pair] += dot(probs.astype(bf16), do_head)
        dk_ref[:, pair] += dot(dscores, q_head)
        dq.append(dot(kt_ref[h * HD : (h + 1) * HD, :], dscores))
    dq.append(jnp.zeros((HD, block), f32))
    dq = (jnp.concatenate(dq, axis=0) * (1.0 / math.sqrt(HD))).T
    span = pl.ds(pl.multiple_of(step * block, block), block)
    dq_ref[...] = rotated(dq, cos_ref[span, :], -sin_ref[span, :]).astype(bf16)

    @pl.when(step == pl.num_programs(0) - 1)
    def _():
        dkv_ref[:, :part] = rotated(dk_ref[...], cos_ref[...], -sin_ref[...]).astype(bf16)
        dkv_ref[:, part:] = dv_ref[...].astype(bf16)


def attend_back(quarter, q, kv, own, other, wo, att, logs, seg_row, seg_col, cosine, sine):
    rows = q.shape[0]
    width = own.shape[1]
    part = q.shape[1] // 2
    steps = rows // QROWS
    return pl.pallas_call(
        attend_back_kernel,
        grid=(steps,),
        in_specs=[
            pl.BlockSpec((QROWS, part), lambda i: (i, quarter)),
            pl.BlockSpec((rows, 2 * part), lambda i: (0, quarter)),
            pl.BlockSpec((QROWS, width), lambda i: (jnp.minimum(i, steps // 2 - 1), 0)),
            pl.BlockSpec((QROWS, width), lambda i: (jnp.maximum(i - steps // 2, 0), 0)),
            pl.BlockSpec((width, part), lambda i: (0, quarter)),
            pl.BlockSpec((QROWS, part), lambda i: (i, 0)),
            pl.BlockSpec((8, QROWS), lambda i: (0, i)),
            pl.BlockSpec((1, QROWS), lambda i: (0, i)),
            whole((rows, 1)),
            whole((rows, PAIR)),
            whole((rows, PAIR)),
        ],
        out_specs=[
            pl.BlockSpec((QROWS, part), lambda i: (i, 0)),
            whole((rows, 2 * part)),
        ],
        out_shape=[
            jax.ShapeDtypeStruct((rows, part), bf16),
            jax.ShapeDtypeStruct((rows, 2 * part), bf16),
        ],
        scratch_shapes=[
            pltpu.VMEM((part, rows), bf16),
            pltpu.VMEM((rows, part), f32),
            pltpu.VMEM((rows, part), f32),
        ],
        cost_estimate=cost(40 * rows * rows * part, 30 * rows * part, rows * rows * 3),
        compiler_params=pltpu.CompilerParams(vmem_limit_bytes=14 << 20),
        name="attend_back",
    )(q, kv, own, other, wo, att, logs, seg_row, seg_col, cosine, sine)


def project_kernel(att_a_ref, att_b_ref, wo_ref, own_ref, send_ref):
    part = att_a_ref.shape[1]
    rows = own_ref.shape[0]
    for out_ref, span in ((send_ref, slice(rows, 2 * rows)), (own_ref, slice(0, rows))):
        out = dot(att_a_ref[span, :], wo_ref[:, :part], NT) + dot(att_b_ref[span, :], wo_ref[:, part:], NT)
        out_ref[...] = out.astype(out_ref.dtype)


def project(att_a, att_b, wo):
    rows, part = att_a.shape
    rows = rows // 2
    width = wo.shape[0]
    return pl.pallas_call(
        project_kernel,
        grid=(1,),
        in_specs=[whole(att_a.shape)] * 2 + [whole(wo.shape)],
        out_specs=[whole((rows, width))] * 2,
        out_shape=[
            jax.ShapeDtypeStruct((rows, width), f32),
            jax.ShapeDtypeStruct((rows, width), bf16),
        ],
        cost_estimate=cost(8 * rows * width * part, 16 * rows * width),
        compiler_params=pltpu.CompilerParams(vmem_limit_bytes=6 << 20),
        name="project",
    )(att_a, att_b, wo)


def first_kernel(
    x_ref, own_ref, came_ref, norm_a_ref, norm_b_ref, n_ref, s_ref, low_ref, low_t_ref, gains_ref
):
    norms = jnp.concatenate([norm_a_ref[...], norm_b_ref[...]], axis=0).astype(f32).T
    gains_ref[...] = norms[:8]
    branch = own_ref[...] + came_ref[...].astype(f32)
    normed, inv = normalize(x_ref[...].astype(f32) + branch)
    n_ref[...] = normed
    s_ref[...] = jnp.broadcast_to(inv, s_ref.shape)
    first = normed * norms[0:1] + norms[2:3]
    low_ref[...] = first.astype(bf16)
    low_t_ref[...] = first.T.astype(bf16)


def first_norm(x, own, came, norm_a, norm_b):
    rows, width = x.shape
    at = norm_a.shape[1] // 128 - 1
    strip = pl.BlockSpec((width // 2, 128), lambda i: (0, at))
    return pl.pallas_call(
        first_kernel,
        grid=(1,),
        in_specs=[whole(x.shape)] * 3 + [strip] * 2,
        out_specs=[
            whole((rows, width)), whole((rows, 128)), whole((rows, width)), whole((width, rows)), whole((8, width)),
        ],
        out_shape=[
            jax.ShapeDtypeStruct((rows, width), f32),
            jax.ShapeDtypeStruct((rows, 128), f32),
            jax.ShapeDtypeStruct((rows, width), bf16),
            jax.ShapeDtypeStruct((width, rows), bf16),
            jax.ShapeDtypeStruct((8, width), f32),
        ],
        cost_estimate=cost(20 * rows * width, 16 * rows * width),
        compiler_params=pltpu.CompilerParams(vmem_limit_bytes=7 << 20),
        name="first_norm",
    )(x, own, came, norm_a, norm_b)


def mlp_kernel(has_base, low_ref, *rest):
    if has_base:
        base_ref, rest = rest[0], rest[1:]
    blocks, (act_ref, feed_ref, w_ref, sems, sum_ref) = rest[:BLOCKS], rest[BLOCKS:]
    slot = pl.program_id(0)
    half = act_ref.shape[3]
    start_weights(blocks, w_ref, sems)

    @pl.when(slot == 0)
    def _():
        sum_ref[...] = base_ref[...] if has_base else jnp.zeros_like(sum_ref)

    wait_weights(w_ref, sems, slot)

    gate = dot(low_ref[...], w_ref[slot, :, half : 2 * half])
    up = dot(low_ref[...], w_ref[slot, :, 2 * half : 3 * half])
    act_ref[0, 0] = gate.astype(bf16)
    act_ref[0, 1] = up.astype(bf16)
    act_ref[0, 2] = (gate / (1.0 + jnp.exp(-gate)) * up).astype(bf16)
    sum_ref[...] += dot(act_ref[0, 2], w_ref[slot, :, :half], NT)

    @pl.when(slot == 1)
    def _():
        feed_ref[...] = sum_ref[...].astype(feed_ref.dtype)


def mlp(low, base, blocks, half, dtype):
    rows, width = low.shape
    has_base = base is not None
    extra = [base] if has_base else []
    return pl.pallas_call(
        functools.partial(mlp_kernel, has_base),
        grid=(2,),
        in_specs=[whole((rows, width))] * (1 + has_base) + [ANY] * BLOCKS,
        out_specs=[
            pl.BlockSpec((1, 3, rows, half), lambda i: (i, 0, 0, 0)),
            whole((rows, width)),
        ],
        scratch_shapes=weight_scratch(blocks) + [pltpu.VMEM((rows, width), f32)],
        out_shape=[
            jax.ShapeDtypeStruct((2, 3, rows, half), bf16),
            jax.ShapeDtypeStruct((rows, width), dtype),
        ],
        cost_estimate=cost(12 * rows * width * half, 30 * half * width, 2 * rows * half),
        compiler_params=pltpu.CompilerParams(vmem_limit_bytes=(6 + half // 64) << 20),
        name="mlp",
    )(low, *extra, *blocks)


def second_kernel(
    n_ref, gains_ref, feed_ref, came_ref, dy_ref, out_ref, dh_ref, low_ref, low_t_ref, sums_ref
):
    first = n_ref[...] * gains_ref[0:1] + gains_ref[2:3]
    normed, inv = normalize(first + feed_ref[...] + came_ref[...].astype(f32))
    out_ref[...] = (normed * gains_ref[1:2] + gains_ref[3:4]).astype(bf16)
    dy = dy_ref[...]
    sums_ref[...] = jnp.zeros_like(sums_ref)
    sums_ref[1:2] = jnp.sum(dy * normed, axis=0, keepdims=True)
    sums_ref[3:4] = jnp.sum(dy, axis=0, keepdims=True)
    dh = norm_back(dy * gains_ref[1:2], normed, inv)
    dh_ref[...] = dh
    low_ref[...] = dh.astype(bf16)
    low_t_ref[...] = dh.T.astype(bf16)


def second_norm(n1, gains, feed, came, dy):
    rows, width = n1.shape
    full = whole((rows, width))
    return pl.pallas_call(
        second_kernel,
        grid=(1,),
        in_specs=[full, whole((8, width)), full, full, full],
        out_specs=[full, full, full, whole((width, rows)), whole((8, width))],
        out_shape=[
            jax.ShapeDtypeStruct((rows, width), bf16),
            jax.ShapeDtypeStruct((rows, width), f32),
            jax.ShapeDtypeStruct((rows, width), bf16),
            jax.ShapeDtypeStruct((width, rows), bf16),
            jax.ShapeDtypeStruct((8, width), f32),
        ],
        cost_estimate=cost(40 * rows * width, 22 * rows * width),
        compiler_params=pltpu.CompilerParams(vmem_limit_bytes=9 << 20),
        name="second_norm",
    )(n1, gains, feed, came, dy)


def mlp_back_kernel(has_base, *rest):
    dfeeds, dfeeds_t, lows_t, acts = rest[:2], rest[2:4], rest[4:6], rest[6:8]
    rest = rest[8:]
    if has_base:
        bases, rest = rest[:2], rest[2:]
    blocks, rest = rest[:BLOCKS], rest[BLOCKS:]
    own_ref, other_ref, to_x_ref, to_y_ref, keep_ref, w_ref, sems, part_ref, sum_ref = rest
    slot = pl.program_id(0)
    rows = own_ref.shape[0]
    half = acts[0].shape[3]
    start_weights(blocks, w_ref, sems)

    @pl.when(slot == 0)
    def _():
        for i in range(2):
            sum_ref[i * rows : (i + 1) * rows, :] = (
                bases[i][...] if has_base else jnp.zeros((rows, sum_ref.shape[1]), f32)
            )

    wait_weights(w_ref, sems, slot)

    for i in range(2):
        span = slice(i * rows, (i + 1) * rows)
        dhidden = dot(dfeeds[i][...], w_ref[slot, :, :half])
        gate = acts[i][0, 0].astype(f32)
        up = acts[i][0, 1].astype(f32)
        sg = 1.0 / (1.0 + jnp.exp(-gate))
        dgate = dhidden * up * sg * (1.0 + gate * (1.0 - sg))
        dup = dhidden * (gate * sg)
        part_ref[span, :half] = dgate.astype(bf16)
        part_ref[span, half:] = dup.astype(bf16)
        sum_ref[span, :] += dot(part_ref[span, :], w_ref[slot, :, half : 3 * half], NT)
    gate_up = (
        dot(lows_t[0][...], part_ref[:rows, :]) + dot(lows_t[1][...], part_ref[rows:, :])
    ).astype(bf16)
    down = (
        dot(dfeeds_t[0][...], acts[0][0, 2]) + dot(dfeeds_t[1][...], acts[1][0, 2])
    ).astype(bf16)
    cut = keep_ref.shape[1]

    def emit(out_ref, at, block):
        span = slice(block * cut, (block + 1) * cut)
        out_ref[at, :, :half] = down[span]
        out_ref[at, :, half:] = gate_up[span]

    emit(to_x_ref, 0, 3)

    @pl.when(slot == 0)
    def _():
        for block in range(3):
            emit(keep_ref, block, block)

    @pl.when(slot == 1)
    def _():
        emit(to_y_ref, 0, 0)
        emit(to_y_ref, 1, 2)
        emit(keep_ref, 3, 1)
        own_ref[...] = sum_ref[:rows, :]
        other_ref[...] = sum_ref[rows:, :].astype(other_ref.dtype)


def mlp_back(bases, dfeeds, dfeeds_t, lows_t, acts, blocks):
    rows, width = dfeeds[0].shape
    half = acts[0].shape[3]
    has_base = bases is not None
    full = whole((rows, width))
    return pl.pallas_call(
        functools.partial(mlp_back_kernel, has_base),
        grid=(2,),
        in_specs=[full] * 2
        + [whole((width, rows))] * 4
        + [pl.BlockSpec((1, 3, rows, half), lambda i: (i, 0, 0, 0))] * 2
        + [full] * (2 * has_base)
        + [ANY] * BLOCKS,
        out_specs=[
            full,
            full,
            pl.BlockSpec((1, width // 4, 3 * half), lambda i: (i, 0, 0)),
            whole((2, width // 4, 3 * half)),
            whole((4, width // 4, 3 * half)),
        ],
        scratch_shapes=weight_scratch(blocks)
        + [pltpu.VMEM((2 * rows, 2 * half), bf16), pltpu.VMEM((2 * rows, width), f32)],
        out_shape=[
            jax.ShapeDtypeStruct((rows, width), f32),
            jax.ShapeDtypeStruct((rows, width), bf16 if has_base else f32),
            jax.ShapeDtypeStruct((2, width // 4, 3 * half), bf16),
            jax.ShapeDtypeStruct((2, width // 4, 3 * half), bf16),
            jax.ShapeDtypeStruct((4, width // 4, 3 * half), bf16),
        ],
        cost_estimate=cost(48 * rows * width * half, 100 * half * width, 4 * rows * half),
        compiler_params=pltpu.CompilerParams(vmem_limit_bytes=(5 + half // 28) << 20),
        name="mlp_back",
    )(*dfeeds, *dfeeds_t, *lows_t, *acts, *(bases if has_base else ()), *blocks)


def first_back_kernel(
    base_ref, own_ref, came_ref, n_ref, s_ref, gains_ref, sums_ref, dh_ref, low_ref, low_t_ref
):
    dfirst = base_ref[...] + own_ref[...] + came_ref[...].astype(f32)
    normed = n_ref[...]
    width = dfirst.shape[1]
    gain_sum = jnp.sum(dfirst * normed, axis=0, keepdims=True)
    bias_sum = jnp.sum(dfirst, axis=0, keepdims=True)
    sums = sums_ref[...]
    stacked = jnp.concatenate(
        [gain_sum, sums[1:2], bias_sum, sums[3:4], jnp.zeros((124, width), f32)], axis=0
    )
    rows = dfirst.shape[0]
    low_t_ref[:, rows:] = stacked.T.astype(bf16)
    dh = norm_back(dfirst * gains_ref[0:1], normed, s_ref[:, 0:1])
    dh_ref[...] = dh
    low_ref[...] = dh.astype(bf16)
    low_t_ref[:, :rows] = dh.T.astype(bf16)


def first_back(base, own, came, n1, s1, gains, sums):
    rows, width = n1.shape
    full = whole((rows, width))
    return pl.pallas_call(
        first_back_kernel,
        grid=(1,),
        in_specs=[full] * 4 + [whole((rows, 128)), whole((8, width)), whole((8, width))],
        out_specs=[full, full, whole((width, rows + 128))],
        out_shape=[
            jax.ShapeDtypeStruct((rows, width), f32),
            jax.ShapeDtypeStruct((rows, width), bf16),
            jax.ShapeDtypeStruct((width, rows + 128), bf16),
        ],
        cost_estimate=cost(40 * rows * width, 20 * rows * width),
        compiler_params=pltpu.CompilerParams(vmem_limit_bytes=9 << 20),
        name="first_back",
    )(base, own, came, n1, s1, gains, sums)


def qkv_back_kernel(
    quarter, has_base, dq_ref, dkv_ref, x_a_ref, x_b_ref, low_a_ref, low_b_ref, cols_a_ref, cols_b_ref, att_ref, *rest
):
    if has_base:
        bases, rest = rest[:2], rest[2:]
    blocks, (own_ref, other_ref, send_ref, keep_ref, w_ref, sem) = rest[:2], rest[2:]
    rows = own_ref.shape[0]
    part = dq_ref.shape[1]
    starts = [row for slot, row in block_starts(w_ref.shape[0]) if slot == quarter]
    for block, row in zip(blocks, starts):
        pltpu.make_async_copy(block, w_ref.at[pl.ds(row, block.shape[0])], sem).start()
    d_out = dot(low_a_ref[...], att_ref[:rows, :]) + dot(low_b_ref[...], att_ref[rows:, :])
    lane = lax.broadcasted_iota(jnp.int32, d_out.shape, 1)
    cut = keep_ref.shape[1]
    if quarter == 0:
        places = [(keep_ref, 0), (keep_ref, 1), (keep_ref, 2), (send_ref, 0)]
    else:
        places = [(send_ref, 0), (keep_ref, 0), (send_ref, 1), (send_ref, 2)]

    def emit(value, lanes):
        for block, (out_ref, at) in enumerate(places):
            out_ref[at, :, lanes] = value[block * cut : (block + 1) * cut]

    for h in range(3):
        source, at = (dq_ref, 0) if h == 0 else (dkv_ref, (h - 1) * part)
        piece = dot(x_a_ref[...], source[:rows, at : at + part]) + dot(x_b_ref[...], source[rows:, at : at + part])
        moved = pltpu.roll(d_out, (3 - h) * HD, 1)
        emit(jnp.where(lane < 3 * HD, piece, moved).astype(bf16), slice(h * part, (h + 1) * part))
    cols = cols_a_ref[...].astype(f32) + cols_b_ref[...].astype(f32)
    emit(cols.astype(bf16), slice(3 * part, 3 * part + 128))
    pltpu.make_async_copy(w_ref, w_ref, sem).wait()
    for i, out_ref in enumerate((own_ref, other_ref)):
        span = slice(i * rows, (i + 1) * rows)
        total = dot(dq_ref[span, :], w_ref[:, :part], NT) + dot(dkv_ref[span, :], w_ref[:, part:], NT)
        if has_base:
            total = total + bases[i][...]
        out_ref[...] = total.astype(out_ref.dtype)


def qkv_back(quarter, bases, dq, dkv, x_t, low_t, att, blocks):
    rows = dq.shape[0] // 2
    width = low_t[0].shape[0]
    part = dq.shape[1]
    has_base = bases is not None
    full = whole((rows, width))
    turned = whole((width, rows))
    blocks = [b for b, (slot, _) in zip(blocks, block_starts(width)) if slot == quarter]
    counts = (1, 3) if quarter == 0 else (3, 1)
    pieces = [(n, width // 4, 3 * part + 128) for n in counts]
    return pl.pallas_call(
        functools.partial(qkv_back_kernel, quarter, has_base),
        grid=(1,),
        in_specs=[whole(dq.shape), whole(dkv.shape)]
        + [turned] * 4
        + [pl.BlockSpec((width, 128), lambda i: (0, rows // 128))] * 2
        + [whole(att.shape)]
        + [full] * (2 * has_base)
        + [ANY] * 2,
        out_specs=[full, full] + [whole(p) for p in pieces],
        scratch_shapes=[pltpu.VMEM((width, 3 * part), bf16), pltpu.SemaphoreType.DMA],
        out_shape=[
            jax.ShapeDtypeStruct((rows, width), f32),
            jax.ShapeDtypeStruct((rows, width), bf16 if has_base else f32),
        ]
        + [jax.ShapeDtypeStruct(p, bf16) for p in pieces],
        cost_estimate=cost(26 * rows * width * part, 40 * width * part),
        compiler_params=pltpu.CompilerParams(vmem_limit_bytes=9 << 20),
        name="qkv_back",
    )(dq, dkv, *x_t, *low_t, *low_t, att, *(bases if has_base else ()), *blocks)


def bits_of(n):
    bits = n.bit_length() - 1
    if 1 << bits != n:
        raise ValueError("row count")
    return bits


class Links:
    def __init__(self, mesh):
        self.rows = mesh.shape["row"]
        self.cols = mesh.shape["col"]
        self.bits = bits_of(self.rows // 2)

    def locate(self):
        row = lax.axis_index("row")
        col = lax.axis_index("col")
        return row // 2, row % 2, col // (self.cols // 2), col % 2

    def send(self, v, move):
        pairs = []
        for row in range(self.rows):
            for col in range(self.cols):
                ring, x, y, k = move(row // 2, row % 2, col // (self.cols // 2), col % 2)
                pairs.append(
                    (row * self.cols + col, (ring * 2 + x) * self.cols + y * (self.cols // 2) + k)
                )
        return lax.ppermute(v, ("row", "col"), pairs)

    def across(self, v):
        return self.send(v, lambda ring, x, y, k: (ring, x, 1 - y, k))

    def beside(self, v):
        return self.send(v, lambda ring, x, y, k: (ring, x, y, 1 - k))

    def far(self, v):
        return self.send(
            v, lambda ring, x, y, k: (ring, 1 - x, y, k) if k else (ring, x, 1 - y, k)
        )

    def along(self, v):
        return self.send(v, lambda ring, x, y, k: (ring, 1 - x, y, k))

    def turned(self, v, bit):
        return self.send(v, lambda ring, x, y, k: (ring ^ (1 << bit), x, y, k))

    def ring_grow(self, block, bit):
        return jnp.concatenate([block, self.turned(block, bit)], axis=0)

    def ring_gather(self, block, last=0):
        for bit in reversed(range(last, self.bits)):
            block = self.ring_grow(block, bit)
        return block

    def ring_split(self, block):
        own, low = jnp.split(block, 2, axis=0)
        return own, low.astype(bf16)

    def ring_scatter(self, own, low, held=()):
        for bit in range(self.bits):
            if bit > 0:
                own, low = self.ring_split(own)
                low = tie(low, *held)
            own = own + self.turned(low, bit).astype(f32)
        return own


def tie(value, *others):
    return lax.optimization_barrier((value, *others))[0]


class Scatter:
    def __init__(self, links, to_x, to_y, keep):
        self.links, self.keep = links, keep
        self.by_x = [links.along(v) for v in to_x]
        self.by_y = links.across(to_y)

    def second(self):
        by_x = self.by_x[0][1] if len(self.by_x) == 1 else self.by_x[1][0]
        to_x = (self.keep[2].astype(f32) + self.by_y[1].astype(f32)).astype(bf16)
        to_y = (self.keep[3].astype(f32) + by_x.astype(f32)).astype(bf16)
        self.late_x, self.late_y = self.links.along(to_x), self.links.across(to_y)
        return to_x, to_y

    def third(self):
        low = self.keep[0].astype(f32) + self.by_y[0].astype(f32) + self.late_x.astype(f32)
        high = self.keep[1].astype(f32) + self.by_x[0][0].astype(f32) + self.late_y.astype(f32)
        self.own, self.low = self.links.ring_split(jnp.concatenate([low, high], axis=0))
        return [self.low]

    def last(self, held=()):
        return self.links.ring_scatter(self.own, self.low, held)


def relative_order(links, depth):
    ring, x, _, _ = links.locate()
    where = lax.broadcasted_iota(jnp.int32, (1, links.rows * depth), 1)
    block, inside = where // depth, where % depth
    steps = links.rows // 2
    place = block % steps
    turn = jnp.zeros_like(place)
    for bit in reversed(range(links.bits)):
        turn = turn + (place % 2 << bit)
        place = place // 2
    row = jnp.bitwise_xor(ring, turn) * 2 + jnp.bitwise_xor(x, block // steps)
    return row * depth + inside


def on_device(
    links, tokens, segments, positions, w_qkv, w_out, w_gate_up, w_down, norm_gain, norm_bias, cotangent
):
    ring, x_place, side, core = links.locate()
    depth = w_qkv.shape[0]
    width = tokens.shape[2]
    head_cols = w_qkv.shape[2]
    hid = w_gate_up.shape[2]
    sizes = [hid - hid // 3, hid // 3]
    rows = 2 * tokens.shape[1]
    mine = rows // 2
    part = head_cols + HD

    source = relative_order(links, depth)
    swap = (lax.broadcasted_iota(jnp.int32, (width, width), 0) == source).astype(bf16)

    def split(v):
        high = v.astype(bf16)
        return high, (v - high.astype(f32)).astype(bf16)

    def own_and_other(v):
        own = lax.dynamic_index_in_dim(v, side, 0, keepdims=False)
        return own, lax.dynamic_index_in_dim(v, 1 - side, 0, keepdims=False)

    def from_sequence(own, came):
        first = side == 0
        return jnp.stack([jnp.where(first, own, came), jnp.where(first, came, own)], axis=0)

    out_t = w_out.T
    attn_shard = jnp.concatenate(
        sum(
            [[w_qkv[:, p], out_t[:, p * HD : (p + 1) * HD]] for p in range(3)],
            [],
        ),
        axis=1,
    )
    norms = jnp.concatenate([norm_gain, norm_bias], axis=1)
    norms = jnp.pad(norms, ((0, 0), (0, 128 - norms.shape[1])))
    down_t = w_down.T
    mlp_shards = []
    for h, at in enumerate([0, sizes[0]]):
        cols = slice(at, at + sizes[h])
        pieces = [down_t[:, cols], w_gate_up[:, 0, cols], w_gate_up[:, 1, cols]]
        mlp_shards.append(jnp.concatenate(pieces + ([norms] if h == 0 else []), axis=1))

    small_own, small_other = own_and_other(jnp.stack([segments, positions], axis=1))
    small_came = links.across(small_other)
    tokens_own, tokens_other = own_and_other(tokens)
    tokens_came = links.across(tie(tokens_other, attn_shard, small_other))
    dy_own, dy_other = own_and_other(cotangent)
    dy_came = links.across(tie(dy_other.astype(bf16), attn_shard, small_other))

    odd = core == 1
    ring_a = links.ring_gather(attn_shard)
    x_a, y_a = links.along(ring_a), links.across(ring_a)
    ring_b = links.ring_gather(tie(mlp_shards[0], ring_a))
    turn_a = jnp.where(odd, y_a, x_a)
    attn_w = [ring_a, x_a, y_a, links.far(turn_a)]

    x_abs = jnp.concatenate([tokens_own, tokens_came], axis=0)
    x = dot(x_abs, swap).astype(bf16)
    x_other = links.beside(x)
    small = jnp.concatenate([small_own, small_came], axis=1)
    small = jnp.concatenate([small, links.beside(small)], axis=1)
    seg_row, seg_col = small[0][None, :], small[0][:, None]
    cosine, sine = rope_tables(small[1])

    ring_b = tie(ring_b, turn_a, cosine, sine, seg_col)
    x_b, y_b = links.along(ring_b), links.across(ring_b)
    ring_c = links.ring_gather(tie(mlp_shards[1], ring_b))
    q, kv, wo = qkv(tie(x, ring_b, dy_came), x_other, cosine, sine, attn_w)
    att_0, logs_0 = attend(0, q, kv, seg_row, seg_col)
    att_1, logs_1 = attend(1, tie(q, att_0), kv, seg_row, seg_col)
    held_x, held_y = lax.optimization_barrier((x_b, y_b, att_1))[:2]
    turn_b = jnp.where(odd, held_y, held_x)
    mlp_b = [ring_b, x_b, y_b, links.far(turn_b)]
    ring_c = tie(ring_c, turn_b)
    x_c, y_c = links.along(ring_c), links.across(ring_c)
    own, send = project(att_0, tie(att_1, turn_b, ring_c), wo)
    x_t = lax.dot_general(
        swap, tie(x_abs, own), (((0,), (1,)), ((), ())), preferred_element_type=f32
    ).astype(bf16)
    x_t = [x_t, links.beside(x_t)]
    high, low_part = split(tie(dy_own, own))
    dy = jnp.concatenate([dot(high, swap) + dot(low_part, swap), dot(dy_came, swap)], axis=0)
    n1, s1, low, low_t, gains = first_norm(
        x, tie(own, mlp_b[3], x_t[1], dy), links.beside(send), ring_b, x_b
    )
    low_other = links.beside(low)
    act_b_own, feed = mlp(low, None, mlp_b, sizes[0], f32)
    low1_t = [low_t, links.beside(tie(low_t, feed))]
    act_b_other, feed_other = mlp(low_other, None, mlp_b, sizes[0], f32)
    held_x, held_y = lax.optimization_barrier((x_c, y_c, feed))[:2]
    turn_c = jnp.where(odd, held_y, held_x)
    mlp_c = [ring_c, x_c, y_c, links.far(turn_c)]
    act_c_other, send = mlp(tie(low_other, low1_t[1]), feed_other, mlp_c, sizes[1], bf16)
    came = links.beside(send)
    act_c_own, feed = mlp(tie(low, send), feed, mlp_c, sizes[1], f32)
    layer_out, dh2, dfeed, dfeed_t, sums = second_norm(n1, gains, feed, came, dy)
    layer_out = dot(layer_out, swap, NT).astype(bf16)
    layer_came = links.across(layer_out[mine:])
    dfeeds = [dfeed, links.beside(dfeed)]
    dfeeds_t = [dfeed_t, links.beside(dfeed_t)]

    own, other, to_x, to_y, keep = mlp_back(None, dfeeds, dfeeds_t, low1_t, (act_c_own, act_c_other), mlp_c)
    sum_b = Scatter(links, [to_x], to_y, keep)
    own, other, to_x, to_y, keep = mlp_back(
        (tie(own, layer_came), other), dfeeds, dfeeds_t, low1_t, (act_b_own, act_b_other), mlp_b
    )
    came = links.beside(other)
    sum_b.keep = tie(sum_b.keep, own)
    ops_b = sum_b.second()
    sum_c = Scatter(links, [tie(to_x, *ops_b)], tie(to_y, *ops_b), keep)
    dh1, low, low_t = first_back(tie(dh2, *ops_b), own, came, n1, s1, gains, sums)
    lows = [low, links.beside(low)]
    low_t = [low_t, links.beside(low_t)]
    dq, dkv = attend_back(1, q, kv, *lows, wo, att_1, logs_1, seg_row, seg_col, cosine, sine)
    sum_b.keep = tie(sum_b.keep, dq)
    block_b = sum_b.third()
    own, other, send, keep_1 = qkv_back(1, None, tie(dq, *block_b), dkv, x_t, low_t, att_1, attn_w)
    own_b = sum_b.last()
    sum_c.keep = tie(sum_c.keep, own)
    ops_c = sum_c.second()
    to_y, to_x = tie(send[:2], *ops_c), [tie(send[2:], *ops_c)]
    dq, dkv = attend_back(
        0, tie(q, own, *ops_c), kv, *lows, wo, att_0, logs_0, seg_row, seg_col, cosine, sine
    )
    sum_c.keep = tie(sum_c.keep, dq)
    block_c = sum_c.third()
    own, other, send, keep_0 = qkv_back(
        0, (own, other), tie(dq, *block_c, own_b), dkv, x_t, low_t, att_0, attn_w
    )
    own_c = sum_c.last()
    sum_a = Scatter(links, [send] + to_x, to_y, jnp.concatenate([keep_0, keep_1], axis=0))
    grad = dh1 + own + links.beside(other).astype(f32)
    high, low = split(grad)
    grad = dot(high, swap, NT) + dot(low, swap, NT)
    sum_a.keep = tie(sum_a.keep, grad)
    ops_a = sum_a.second()
    own_mlp = [own_c, own_b]
    grad_down = jnp.concatenate([v[:, :n] for v, n in zip(own_mlp, sizes)], axis=1).T
    grad_gate_up = jnp.stack(
        [
            jnp.concatenate([v[:, p * n : (p + 1) * n] for v, n in zip(own_mlp, sizes)], axis=1)
            for p in (1, 2)
        ],
        axis=1,
    )
    block_a = sum_a.third()
    came = links.across(tie(grad[mine:].astype(bf16), *block_a))
    input_grad = from_sequence(grad[:mine], came.astype(f32))
    layer_out = from_sequence(layer_out[:mine], layer_came)
    own_attn = sum_a.last((came, grad_down, grad_gate_up, layer_out))
    thirds = [own_attn[:, p * part : (p + 1) * part] for p in range(3)]
    edge = 3 * part
    return (
        layer_out,
        input_grad,
        jnp.stack([v[:, :head_cols] for v in thirds], axis=1),
        jnp.concatenate([v[:, head_cols:] for v in thirds], axis=1).T,
        grad_gate_up,
        grad_down,
        own_attn[:, edge : edge + 2],
        own_attn[:, edge + 2 : edge + 4],
    )


def solution(mesh):
    in_specs = (
        P(None, ("row", "col"), None),
        P(None, ("row", "col")),
        P(None, ("row", "col")),
        P("row", None, "col"),
        P("col", "row"),
        P("row", None, "col"),
        P("col", "row"),
        P("row", None),
        P("row", None),
        P(None, ("row", "col"), None),
    )
    out_specs = (
        P(None, ("row", "col"), None),
        P(None, ("row", "col"), None),
        P("row", None, "col"),
        P("col", "row"),
        P("row", None, "col"),
        P("col", "row"),
        P("row", None),
        P("row", None),
    )
    return jax.shard_map(
        functools.partial(on_device, Links(mesh)), mesh=mesh, in_specs=in_specs, out_specs=out_specs, check_vma=False
    )
```

```python
import functools
import math

import jax
import jax.numpy as jnp
from jax import lax
from jax.experimental import pallas as pl
from jax.experimental.pallas import tpu as pltpu
from jax.sharding import PartitionSpec as P

HD = 64
PAIR = 2 * HD
QROWS = 256
epsilon = 1e-12
rope_base = 1000.0
masked_score = -1e30
f32 = jnp.float32
bf16 = jnp.bfloat16

NN = (((1,), (0,)), ((), ()))
NT = (((1,), (1,)), ((), ()))
TN = (((0,), (0,)), ((), ()))


def dot(a, b, dims=NN):
    return lax.dot_general(a, b, dims, preferred_element_type=f32)


def rope_tables(positions):
    half_dim = HD // 2
    lane = jnp.arange(PAIR)
    freq = rope_base ** (-(lane % half_dim).astype(f32) / half_dim)
    sign = jnp.where(lane % HD < half_dim, -1.0, 1.0)
    angles = positions.astype(f32)[:, None] * freq[None, :]
    return jnp.cos(angles), jnp.sin(angles) * sign[None, :]


def rotated(values, cosine, sine):
    width = values.shape[1]
    cosine = jnp.concatenate([cosine] * (width // PAIR), axis=1)
    sine = jnp.concatenate([sine] * (width // PAIR), axis=1)
    lane = lax.broadcasted_iota(jnp.int32, values.shape, 1)
    up = pltpu.roll(values, width - HD // 2, 1)
    down = pltpu.roll(values, HD // 2, 1)
    return values * cosine + jnp.where(lane % HD < HD // 2, up, down) * sine


def normalize(hidden):
    centred = hidden - jnp.mean(hidden, axis=-1, keepdims=True)
    variance = jnp.mean(centred * centred, axis=-1, keepdims=True)
    inv_std = lax.rsqrt(variance + epsilon)
    return (centred * inv_std, inv_std)


def norm_back(grad_norm, normed, inv_std):
    return inv_std * (
        grad_norm
        - jnp.mean(grad_norm, axis=-1, keepdims=True)
        - normed * jnp.mean(grad_norm * normed, axis=-1, keepdims=True)
    )


BLOCKS = 4


def block_starts(width):
    return [(0, 0), (0, width // 2), (1, 0), (1, width // 2)]


def start_weights(blocks, w_ref, sems):
    @pl.when(pl.program_id(0) == 0)
    def _():
        for block, (slot, row) in zip(blocks, block_starts(w_ref.shape[1])):
            pltpu.make_async_copy(
                block, w_ref.at[slot, pl.ds(row, block.shape[0])], sems.at[slot]
            ).start()


def wait_weights(w_ref, sems, slot):
    pltpu.make_async_copy(w_ref.at[slot], w_ref.at[slot], sems.at[slot]).wait()


def weight_scratch(blocks):
    width = 2 * blocks[0].shape[0]
    return [
        pltpu.VMEM((2, width, blocks[0].shape[1]), bf16),
        pltpu.SemaphoreType.DMA((2,)),
    ]


ANY = pl.BlockSpec(memory_space=pl.ANY)


def cost(flops, nbytes, exps=0):
    return pl.CostEstimate(flops=int(flops), bytes_accessed=int(nbytes), transcendentals=int(exps))


def whole(shape):
    return pl.BlockSpec(shape, lambda *_: (0,) * len(shape), pipeline_mode=pl.Buffered(1))


def qkv_kernel(own_ref, other_ref, cos_ref, sin_ref, *rest):
    blocks, (q_ref, kv_ref, wo_ref, w_ref, sems) = rest[:BLOCKS], rest[BLOCKS:]
    slot = pl.program_id(0)
    start_weights(blocks, w_ref, sems)
    wait_weights(w_ref, sems, slot)
    part = w_ref.shape[2] // 3
    rows = own_ref.shape[0]
    for i, x_ref in enumerate((own_ref, other_ref)):
        span = slice(i * rows, (i + 1) * rows)
        cosine, sine = cos_ref[span, :], sin_ref[span, :]
        x = x_ref[...]
        q = dot(x, w_ref[slot, :, :part])
        q_ref[span, :] = (rotated(q, cosine, sine) * (1.0 / math.sqrt(HD))).astype(bf16)
        k = dot(x, w_ref[slot, :, part : 2 * part])
        kv_ref[span, :part] = rotated(k, cosine, sine).astype(bf16)
        kv_ref[span, part:] = dot(x, w_ref[slot, :, 2 * part :]).astype(bf16)
    lane = lax.broadcasted_iota(jnp.int32, (w_ref.shape[1], part), 1)
    out = jnp.zeros(lane.shape, f32)
    for h in range(3):
        piece = w_ref[slot, :, h * part : (h + 1) * part].astype(f32)
        piece = pltpu.roll(piece, (h + 1) * HD, 1)
        out = jnp.where(lane // HD == h, piece, out)
    wo_ref[...] = out.astype(bf16)


def qkv(own, other, cosine, sine, blocks):
    rows, width = own.shape
    part = blocks[0].shape[1] // 3
    table = whole((2 * rows, PAIR))
    return pl.pallas_call(
        qkv_kernel,
        grid=(2,),
        in_specs=[whole((rows, width))] * 2 + [table] * 2 + [ANY] * BLOCKS,
        out_specs=[
            pl.BlockSpec((2 * rows, part), lambda i: (0, i)),
            pl.BlockSpec((2 * rows, 2 * part), lambda i: (0, i)),
            pl.BlockSpec((width, part), lambda i: (0, i)),
        ],
        scratch_shapes=weight_scratch(blocks),
        out_shape=[
            jax.ShapeDtypeStruct((2 * rows, 2 * part), bf16),
            jax.ShapeDtypeStruct((2 * rows, 4 * part), bf16),
            jax.ShapeDtypeStruct((width, 2 * part), bf16),
        ],
        cost_estimate=cost(24 * rows * width * part, 40 * width * part),
        compiler_params=pltpu.CompilerParams(vmem_limit_bytes=12 << 20),
        name="qkv",
    )(own, other, cosine, sine, *blocks)


BITS = 5


def document_codes(segment):
    lane = jnp.arange(PAIR) % HD
    bit = (segment[:, None] >> (lane % BITS)[None, :]) & 1
    used = (lane < 2 * BITS)[None, :]
    query = jnp.where(lane[None, :] < BITS, bit, 1 - bit)
    query = jnp.where(used, query, 0).astype(bf16)
    key = jnp.where(lane[None, :] < BITS, 1 - bit, bit)
    key = jnp.where(used, key, 0).astype(f32) * -(2.0**100)
    return query, key.astype(bf16)


def coded_keys(kx_ref, kv_ref, kcode_ref):
    lane = lax.broadcasted_iota(jnp.int32, kcode_ref.shape, 1)
    for h in range(3):
        pair = slice(h // 2 * PAIR, (h // 2 + 1) * PAIR)
        kx_ref[h] = jnp.where(lane // HD == h % 2, kv_ref[:, pair], kcode_ref[...])


def attend_kernel(quarter_ref, q_ref, kv_ref, qcode_ref, kcode_ref, out_ref, log_ref, vt_ref, kx_ref, ot_ref):
    block, part = q_ref.shape
    half_of = lax.broadcasted_iota(jnp.int32, (block, PAIR), 1) // HD

    @pl.when(pl.program_id(0) == 0)
    def _():
        vt_ref[...] = kv_ref[:, part:].T
        coded_keys(kx_ref, kv_ref, kcode_ref)
        ot_ref[3 * HD :, :] = jnp.zeros((HD, block), f32)

    def head(h, _):
        pair = pl.ds(pl.multiple_of(h // 2 * PAIR, PAIR), PAIR)
        rows = pl.ds(pl.multiple_of(h * HD, HD), HD)
        coded = jnp.where(half_of == h % 2, q_ref[:, pair], qcode_ref[...])
        scores = dot(kx_ref[h], coded, NT)
        top = jnp.max(scores, axis=0, keepdims=True)
        expo = jnp.exp(scores - top)
        total = jnp.sum(expo, axis=0, keepdims=True)
        ot_ref[rows, :] = dot(vt_ref[rows, :], expo.astype(bf16)) / total
        log_ref[pl.ds(h, 1), :] = top + jnp.log(total)
        return 0

    lax.fori_loop(0, 3, head, 0)
    out_ref[...] = ot_ref[...].T.astype(bf16)


def attend(quarter, q, kv, qcode, kcode):
    rows = q.shape[0]
    part = q.shape[1] // 2
    block = rows // 2
    grid_spec = pltpu.PrefetchScalarGridSpec(
        num_scalar_prefetch=1,
        grid=(2,),
        in_specs=[
            pl.BlockSpec((block, part), lambda i, c: (i, c[0])),
            pl.BlockSpec((rows, 2 * part), lambda i, c: (0, c[0])),
            pl.BlockSpec((block, PAIR), lambda i, c: (i, 0)),
            whole((rows, PAIR)),
        ],
        out_specs=[
            pl.BlockSpec((block, part), lambda i, c: (i, 0)),
            pl.BlockSpec((8, block), lambda i, c: (0, i)),
        ],
        scratch_shapes=[
            pltpu.VMEM((part, rows), bf16),
            pltpu.VMEM((3, rows, PAIR), bf16),
            pltpu.VMEM((part, block), f32),
        ],
    )
    return pl.pallas_call(
        attend_kernel,
        grid_spec=grid_spec,
        out_shape=[
            jax.ShapeDtypeStruct((rows, part), bf16),
            jax.ShapeDtypeStruct((8, rows), f32),
        ],
        cost_estimate=cost(16 * rows * rows * part, 12 * rows * part, rows * rows * 3),
        compiler_params=pltpu.CompilerParams(vmem_limit_bytes=12 << 20),
        name="attend",
    )(quarter, q, kv, qcode, kcode)


def attend_back_kernel(
    quarter_ref, q_ref, kv_ref, own_ref, other_ref, wo_ref, att_ref, log_ref, qcode_ref, kcode_ref, cos_ref, sin_ref,
    dq_ref, dkv_ref, kt_ref, kx_ref, do_ref, delta_ref, dqt_ref, dk_ref, dv_ref,
):
    step = pl.program_id(0)
    block, part = q_ref.shape
    half_of = lax.broadcasted_iota(jnp.int32, (block, PAIR), 1) // HD

    @pl.when(step == 0)
    def _():
        kt_ref[...] = kv_ref[:, :part].T
        coded_keys(kx_ref, kv_ref, kcode_ref)
        dk_ref[...] = jnp.zeros_like(dk_ref)
        dv_ref[...] = jnp.zeros_like(dv_ref)
        dqt_ref[3 * HD :, :] = jnp.zeros((HD, block), f32)

    low = jnp.where(step < pl.num_programs(0) // 2, own_ref[...], other_ref[...])
    do = dot(low, wo_ref[...]).astype(bf16)
    do_ref[...] = do
    prod = do.astype(f32) * att_ref[...].astype(f32)
    high = prod.astype(bf16)
    rest = (prod - high.astype(f32)).astype(bf16)
    row = lax.broadcasted_iota(jnp.int32, (8, part), 0)
    lane = lax.broadcasted_iota(jnp.int32, (8, part), 1) // HD
    pick = jnp.where(row == lane, 1.0, 0.0).astype(bf16)
    delta_ref[...] = dot(pick, high, NT) + dot(pick, rest, NT)

    def head(h, _):
        pair = pl.ds(pl.multiple_of(h // 2 * PAIR, PAIR), PAIR)
        values = pl.ds(pl.multiple_of(part + h // 2 * PAIR, PAIR), PAIR)
        rows = pl.ds(pl.multiple_of(h * HD, HD), HD)
        mine = half_of == h % 2
        zero = jnp.zeros((block, PAIR), bf16)
        q = q_ref[:, pair]
        q_head = jnp.where(mine, q, zero)
        do_head = jnp.where(mine, do_ref[:, pair], zero)
        scores = dot(kx_ref[h], jnp.where(mine, q, qcode_ref[...]), NT)
        probs = jnp.exp(scores - log_ref[pl.ds(h, 1), :])
        dprobs = dot(kv_ref[:, values], do_head, NT)
        dscores = (probs * (dprobs - delta_ref[pl.ds(h, 1), :])).astype(bf16)
        dv_ref[:, pair] += dot(probs.astype(bf16), do_head)
        dk_ref[:, pair] += dot(dscores, q_head)
        dqt_ref[rows, :] = dot(kt_ref[rows, :], dscores)
        return 0

    lax.fori_loop(0, 3, head, 0)
    dq = (dqt_ref[...] * (1.0 / math.sqrt(HD))).T
    span = pl.ds(pl.multiple_of(step * block, block), block)
    dq_ref[...] = rotated(dq, cos_ref[span, :], -sin_ref[span, :]).astype(bf16)

    @pl.when(step == pl.num_programs(0) - 1)
    def _():
        dkv_ref[:, :part] = rotated(dk_ref[...], cos_ref[...], -sin_ref[...]).astype(bf16)
        dkv_ref[:, part:] = dv_ref[...].astype(bf16)


def attend_back(quarter, q, kv, own, other, wo, att, logs, qcode, kcode, cosine, sine):
    rows = q.shape[0]
    width = own.shape[1]
    part = q.shape[1] // 2
    block = rows // 2
    grid_spec = pltpu.PrefetchScalarGridSpec(
        num_scalar_prefetch=1,
        grid=(2,),
        in_specs=[
            pl.BlockSpec((block, part), lambda i, c: (i, c[0])),
            pl.BlockSpec((rows, 2 * part), lambda i, c: (0, c[0]), pipeline_mode=pl.Buffered(1)),
            whole((block, width)),
            whole((block, width)),
            pl.BlockSpec((width, part), lambda i, c: (0, c[0]), pipeline_mode=pl.Buffered(1)),
            pl.BlockSpec((block, part), lambda i, c: (i, 0)),
            pl.BlockSpec((8, block), lambda i, c: (0, i)),
            pl.BlockSpec((block, PAIR), lambda i, c: (i, 0)),
            whole((rows, PAIR)),
            whole((rows, PAIR)),
            whole((rows, PAIR)),
        ],
        out_specs=[
            pl.BlockSpec((block, part), lambda i, c: (i, 0)),
            whole((rows, 2 * part)),
        ],
        scratch_shapes=[
            pltpu.VMEM((part, rows), bf16),
            pltpu.VMEM((3, rows, PAIR), bf16),
            pltpu.VMEM((block, part), bf16),
            pltpu.VMEM((8, block), f32),
            pltpu.VMEM((part, block), f32),
            pltpu.VMEM((rows, part), f32),
            pltpu.VMEM((rows, part), f32),
        ],
    )
    return pl.pallas_call(
        attend_back_kernel,
        grid_spec=grid_spec,
        out_shape=[
            jax.ShapeDtypeStruct((rows, part), bf16),
            jax.ShapeDtypeStruct((rows, 2 * part), bf16),
        ],
        cost_estimate=cost(40 * rows * rows * part, 30 * rows * part, rows * rows * 3),
        compiler_params=pltpu.CompilerParams(vmem_limit_bytes=22 << 20),
        name="attend_back",
    )(quarter, q, kv, own, other, wo, att, logs, qcode, kcode, cosine, sine)


def project_kernel(att_a_ref, att_b_ref, wo_ref, own_ref, send_ref):
    part = att_a_ref.shape[1]
    rows = own_ref.shape[0]
    for out_ref, span in ((send_ref, slice(rows, 2 * rows)), (own_ref, slice(0, rows))):
        out = dot(att_a_ref[span, :], wo_ref[:, :part], NT) + dot(att_b_ref[span, :], wo_ref[:, part:], NT)
        out_ref[...] = out.astype(out_ref.dtype)


def project(att_a, att_b, wo):
    rows, part = att_a.shape
    rows = rows // 2
    width = wo.shape[0]
    return pl.pallas_call(
        project_kernel,
        grid=(1,),
        in_specs=[whole(att_a.shape)] * 2 + [whole(wo.shape)],
        out_specs=[whole((rows, width))] * 2,
        out_shape=[
            jax.ShapeDtypeStruct((rows, width), f32),
            jax.ShapeDtypeStruct((rows, width), bf16),
        ],
        cost_estimate=cost(8 * rows * width * part, 16 * rows * width),
        compiler_params=pltpu.CompilerParams(vmem_limit_bytes=6 << 20),
        name="project",
    )(att_a, att_b, wo)


def first_kernel(
    x_ref, own_ref, came_ref, norm_a_ref, norm_b_ref, n_ref, s_ref, low_ref, low_t_ref, gains_ref
):
    norms = jnp.concatenate([norm_a_ref[...], norm_b_ref[...]], axis=0).astype(f32).T
    gains_ref[...] = norms[:8]
    branch = own_ref[...] + came_ref[...].astype(f32)
    normed, inv = normalize(x_ref[...].astype(f32) + branch)
    n_ref[...] = normed
    s_ref[...] = jnp.broadcast_to(inv, s_ref.shape)
    first = normed * norms[0:1] + norms[2:3]
    low_ref[...] = first.astype(bf16)
    low_t_ref[...] = first.T.astype(bf16)


def first_norm(x, own, came, norm_a, norm_b):
    rows, width = x.shape
    at = norm_a.shape[1] // 128 - 1
    strip = pl.BlockSpec((width // 2, 128), lambda i: (0, at))
    return pl.pallas_call(
        first_kernel,
        grid=(1,),
        in_specs=[whole(x.shape)] * 3 + [strip] * 2,
        out_specs=[
            whole((rows, width)), whole((rows, 128)), whole((rows, width)), whole((width, rows)), whole((8, width)),
        ],
        out_shape=[
            jax.ShapeDtypeStruct((rows, width), f32),
            jax.ShapeDtypeStruct((rows, 128), f32),
            jax.ShapeDtypeStruct((rows, width), bf16),
            jax.ShapeDtypeStruct((width, rows), bf16),
            jax.ShapeDtypeStruct((8, width), f32),
        ],
        cost_estimate=cost(20 * rows * width, 16 * rows * width),
        compiler_params=pltpu.CompilerParams(vmem_limit_bytes=7 << 20),
        name="first_norm",
    )(x, own, came, norm_a, norm_b)


def mlp_kernel(has_base, low_ref, *rest):
    if has_base:
        base_ref, rest = rest[0], rest[1:]
    blocks, (act_ref, feed_ref, w_ref, sems, sum_ref) = rest[:BLOCKS], rest[BLOCKS:]
    slot = pl.program_id(0)
    half = act_ref.shape[3]
    start_weights(blocks, w_ref, sems)

    @pl.when(slot == 0)
    def _():
        sum_ref[...] = base_ref[...] if has_base else jnp.zeros_like(sum_ref)

    wait_weights(w_ref, sems, slot)

    gate = dot(low_ref[...], w_ref[slot, :, half : 2 * half])
    up = dot(low_ref[...], w_ref[slot, :, 2 * half : 3 * half])
    act_ref[0, 0] = gate.astype(bf16)
    act_ref[0, 1] = up.astype(bf16)
    act_ref[0, 2] = (gate / (1.0 + jnp.exp(-gate)) * up).astype(bf16)
    sum_ref[...] += dot(act_ref[0, 2], w_ref[slot, :, :half], NT)

    @pl.when(slot == 1)
    def _():
        feed_ref[...] = sum_ref[...].astype(feed_ref.dtype)


def mlp(low, base, blocks, half, dtype):
    rows, width = low.shape
    has_base = base is not None
    extra = [base] if has_base else []
    return pl.pallas_call(
        functools.partial(mlp_kernel, has_base),
        grid=(2,),
        in_specs=[whole((rows, width))] * (1 + has_base) + [ANY] * BLOCKS,
        out_specs=[
            pl.BlockSpec((1, 3, rows, half), lambda i: (i, 0, 0, 0)),
            whole((rows, width)),
        ],
        scratch_shapes=weight_scratch(blocks) + [pltpu.VMEM((rows, width), f32)],
        out_shape=[
            jax.ShapeDtypeStruct((2, 3, rows, half), bf16),
            jax.ShapeDtypeStruct((rows, width), dtype),
        ],
        cost_estimate=cost(12 * rows * width * half, 30 * half * width, 2 * rows * half),
        compiler_params=pltpu.CompilerParams(vmem_limit_bytes=(6 + half // 64) << 20),
        name="mlp",
    )(low, *extra, *blocks)


def second_kernel(
    n_ref, gains_ref, feed_ref, came_ref, dy_ref, out_ref, dh_ref, low_ref, low_t_ref, sums_ref
):
    first = n_ref[...] * gains_ref[0:1] + gains_ref[2:3]
    normed, inv = normalize(first + feed_ref[...] + came_ref[...].astype(f32))
    out_ref[...] = (normed * gains_ref[1:2] + gains_ref[3:4]).astype(bf16)
    dy = dy_ref[...]
    sums_ref[...] = jnp.zeros_like(sums_ref)
    sums_ref[1:2] = jnp.sum(dy * normed, axis=0, keepdims=True)
    sums_ref[3:4] = jnp.sum(dy, axis=0, keepdims=True)
    dh = norm_back(dy * gains_ref[1:2], normed, inv)
    dh_ref[...] = dh
    low_ref[...] = dh.astype(bf16)
    low_t_ref[...] = dh.T.astype(bf16)


def second_norm(n1, gains, feed, came, dy):
    rows, width = n1.shape
    full = whole((rows, width))
    return pl.pallas_call(
        second_kernel,
        grid=(1,),
        in_specs=[full, whole((8, width)), full, full, full],
        out_specs=[full, full, full, whole((width, rows)), whole((8, width))],
        out_shape=[
            jax.ShapeDtypeStruct((rows, width), bf16),
            jax.ShapeDtypeStruct((rows, width), f32),
            jax.ShapeDtypeStruct((rows, width), bf16),
            jax.ShapeDtypeStruct((width, rows), bf16),
            jax.ShapeDtypeStruct((8, width), f32),
        ],
        cost_estimate=cost(40 * rows * width, 22 * rows * width),
        compiler_params=pltpu.CompilerParams(vmem_limit_bytes=9 << 20),
        name="second_norm",
    )(n1, gains, feed, came, dy)


def mlp_back_kernel(has_base, *rest):
    dfeeds, dfeeds_t, lows_t, acts = rest[:2], rest[2:4], rest[4:6], rest[6:8]
    rest = rest[8:]
    if has_base:
        bases, rest = rest[:2], rest[2:]
    blocks, rest = rest[:BLOCKS], rest[BLOCKS:]
    own_ref, other_ref, to_x_ref, to_y_ref, keep_ref, w_ref, sems, part_ref, sum_ref = rest
    slot = pl.program_id(0)
    rows = own_ref.shape[0]
    half = acts[0].shape[3]
    start_weights(blocks, w_ref, sems)

    @pl.when(slot == 0)
    def _():
        for i in range(2):
            sum_ref[i * rows : (i + 1) * rows, :] = (
                bases[i][...] if has_base else jnp.zeros((rows, sum_ref.shape[1]), f32)
            )

    wait_weights(w_ref, sems, slot)

    for i in range(2):
        span = slice(i * rows, (i + 1) * rows)
        dhidden = dot(dfeeds[i][...], w_ref[slot, :, :half])
        gate = acts[i][0, 0].astype(f32)
        up = acts[i][0, 1].astype(f32)
        sg = 1.0 / (1.0 + jnp.exp(-gate))
        dgate = dhidden * up * sg * (1.0 + gate * (1.0 - sg))
        dup = dhidden * (gate * sg)
        part_ref[span, :half] = dgate.astype(bf16)
        part_ref[span, half:] = dup.astype(bf16)
        sum_ref[span, :] += dot(part_ref[span, :], w_ref[slot, :, half : 3 * half], NT)
    gate_up = (
        dot(lows_t[0][...], part_ref[:rows, :]) + dot(lows_t[1][...], part_ref[rows:, :])
    ).astype(bf16)
    down = (
        dot(dfeeds_t[0][...], acts[0][0, 2]) + dot(dfeeds_t[1][...], acts[1][0, 2])
    ).astype(bf16)
    cut = keep_ref.shape[1]

    def emit(out_ref, at, block):
        span = slice(block * cut, (block + 1) * cut)
        out_ref[at, :, :half] = down[span]
        out_ref[at, :, half:] = gate_up[span]

    emit(to_x_ref, 0, 3)

    @pl.when(slot == 0)
    def _():
        for block in range(3):
            emit(keep_ref, block, block)

    @pl.when(slot == 1)
    def _():
        emit(to_y_ref, 0, 0)
        emit(to_y_ref, 1, 2)
        emit(keep_ref, 3, 1)
        own_ref[...] = sum_ref[:rows, :]
        other_ref[...] = sum_ref[rows:, :].astype(other_ref.dtype)


def mlp_back(bases, dfeeds, dfeeds_t, lows_t, acts, blocks):
    rows, width = dfeeds[0].shape
    half = acts[0].shape[3]
    has_base = bases is not None
    full = whole((rows, width))
    return pl.pallas_call(
        functools.partial(mlp_back_kernel, has_base),
        grid=(2,),
        in_specs=[full] * 2
        + [whole((width, rows))] * 4
        + [pl.BlockSpec((1, 3, rows, half), lambda i: (i, 0, 0, 0))] * 2
        + [full] * (2 * has_base)
        + [ANY] * BLOCKS,
        out_specs=[
            full,
            full,
            pl.BlockSpec((1, width // 4, 3 * half), lambda i: (i, 0, 0)),
            whole((2, width // 4, 3 * half)),
            whole((4, width // 4, 3 * half)),
        ],
        scratch_shapes=weight_scratch(blocks)
        + [pltpu.VMEM((2 * rows, 2 * half), bf16), pltpu.VMEM((2 * rows, width), f32)],
        out_shape=[
            jax.ShapeDtypeStruct((rows, width), f32),
            jax.ShapeDtypeStruct((rows, width), bf16 if has_base else f32),
            jax.ShapeDtypeStruct((2, width // 4, 3 * half), bf16),
            jax.ShapeDtypeStruct((2, width // 4, 3 * half), bf16),
            jax.ShapeDtypeStruct((4, width // 4, 3 * half), bf16),
        ],
        cost_estimate=cost(48 * rows * width * half, 100 * half * width, 4 * rows * half),
        compiler_params=pltpu.CompilerParams(vmem_limit_bytes=(5 + half // 28) << 20),
        name="mlp_back",
    )(*dfeeds, *dfeeds_t, *lows_t, *acts, *(bases if has_base else ()), *blocks)


def first_back_kernel(
    base_ref, own_ref, came_ref, n_ref, s_ref, gains_ref, sums_ref, dh_ref, low_ref, low_t_ref
):
    dfirst = base_ref[...] + own_ref[...] + came_ref[...].astype(f32)
    normed = n_ref[...]
    width = dfirst.shape[1]
    gain_sum = jnp.sum(dfirst * normed, axis=0, keepdims=True)
    bias_sum = jnp.sum(dfirst, axis=0, keepdims=True)
    sums = sums_ref[...]
    stacked = jnp.concatenate(
        [gain_sum, sums[1:2], bias_sum, sums[3:4], jnp.zeros((124, width), f32)], axis=0
    )
    rows = dfirst.shape[0]
    low_t_ref[:, rows:] = stacked.T.astype(bf16)
    dh = norm_back(dfirst * gains_ref[0:1], normed, s_ref[:, 0:1])
    dh_ref[...] = dh
    low_ref[...] = dh.astype(bf16)
    low_t_ref[:, :rows] = dh.T.astype(bf16)


def first_back(base, own, came, n1, s1, gains, sums):
    rows, width = n1.shape
    full = whole((rows, width))
    return pl.pallas_call(
        first_back_kernel,
        grid=(1,),
        in_specs=[full] * 4 + [whole((rows, 128)), whole((8, width)), whole((8, width))],
        out_specs=[full, full, whole((width, rows + 128))],
        out_shape=[
            jax.ShapeDtypeStruct((rows, width), f32),
            jax.ShapeDtypeStruct((rows, width), bf16),
            jax.ShapeDtypeStruct((width, rows + 128), bf16),
        ],
        cost_estimate=cost(40 * rows * width, 20 * rows * width),
        compiler_params=pltpu.CompilerParams(vmem_limit_bytes=9 << 20),
        name="first_back",
    )(base, own, came, n1, s1, gains, sums)


def qkv_back_kernel(
    dq_ref, dkv_ref, x_a_ref, x_b_ref, low_a_ref, low_b_ref, cols_a_ref, cols_b_ref, att_ref, base_own_ref, base_other_ref,
    top_ref, bottom_ref, own_ref, other_ref, early_ref, mid_ref, late_ref, w_ref, sem,
):
    rows = own_ref.shape[0]
    part = dq_ref.shape[1]
    copies = [
        pltpu.make_async_copy(top_ref, w_ref.at[pl.ds(0, top_ref.shape[0])], sem),
        pltpu.make_async_copy(bottom_ref, w_ref.at[pl.ds(top_ref.shape[0], top_ref.shape[0])], sem),
    ]
    for copy in copies:
        copy.start()
    d_out = dot(low_a_ref[...], att_ref[:rows, :]) + dot(low_b_ref[...], att_ref[rows:, :])
    lane = lax.broadcasted_iota(jnp.int32, d_out.shape, 1)
    cut = mid_ref.shape[0]

    def emit(value, lanes):
        early_ref[0, :, lanes] = value[:cut]
        mid_ref[:, lanes] = value[cut : 2 * cut]
        early_ref[1, :, lanes] = value[2 * cut : 3 * cut]
        late_ref[:, lanes] = value[3 * cut :]

    for h in range(3):
        source, at = (dq_ref, 0) if h == 0 else (dkv_ref, (h - 1) * part)
        piece = dot(x_a_ref[...], source[:rows, at : at + part]) + dot(x_b_ref[...], source[rows:, at : at + part])
        moved = pltpu.roll(d_out, (3 - h) * HD, 1)
        emit(jnp.where(lane < 3 * HD, piece, moved).astype(bf16), slice(h * part, (h + 1) * part))
    cols = cols_a_ref[...].astype(f32) + cols_b_ref[...].astype(f32)
    emit(cols.astype(bf16), slice(3 * part, 3 * part + 128))
    pltpu.make_async_copy(w_ref, w_ref, sem).wait()
    for i, (base_ref, out_ref) in enumerate(((base_own_ref, own_ref), (base_other_ref, other_ref))):
        span = slice(i * rows, (i + 1) * rows)
        total = dot(dq_ref[span, :], w_ref[:, :part], NT) + dot(dkv_ref[span, :], w_ref[:, part:], NT)
        out_ref[...] = (total + base_ref[...].astype(f32)).astype(out_ref.dtype)


def qkv_back(bases, dq, dkv, x_t, low_t, att, blocks):
    rows = dq.shape[0] // 2
    width = low_t[0].shape[0]
    part = dq.shape[1]
    lanes = 3 * part + 128
    full = whole((rows, width))
    turned = whole((width, rows))
    strip = pl.BlockSpec((width, 128), lambda i: (0, rows // 128), pipeline_mode=pl.Buffered(1))
    pieces = [(2, width // 4, lanes), (width // 4, lanes), (width // 4, lanes)]
    return pl.pallas_call(
        qkv_back_kernel,
        grid=(1,),
        in_specs=[whole(dq.shape), whole(dkv.shape)]
        + [turned] * 4
        + [strip] * 2
        + [whole(att.shape), full, full, ANY, ANY],
        out_specs=[full, full] + [whole(p) for p in pieces],
        scratch_shapes=[pltpu.VMEM((width, 3 * part), bf16), pltpu.SemaphoreType.DMA],
        out_shape=[
            jax.ShapeDtypeStruct((rows, width), f32),
            jax.ShapeDtypeStruct((rows, width), bf16),
        ]
        + [jax.ShapeDtypeStruct(p, bf16) for p in pieces],
        cost_estimate=cost(26 * rows * width * part, 40 * width * part),
        compiler_params=pltpu.CompilerParams(vmem_limit_bytes=12 << 20),
        name="qkv_back",
    )(dq, dkv, *x_t, *low_t, *low_t, att, *bases, *blocks)


def bits_of(n):
    bits = n.bit_length() - 1
    if 1 << bits != n:
        raise ValueError("row count")
    return bits


class Links:
    def __init__(self, mesh):
        self.rows = mesh.shape["row"]
        self.cols = mesh.shape["col"]
        self.bits = bits_of(self.rows // 2)

    def locate(self):
        row = lax.axis_index("row")
        col = lax.axis_index("col")
        return row // 2, row % 2, col // (self.cols // 2), col % 2

    def send(self, v, move):
        pairs = []
        for row in range(self.rows):
            for col in range(self.cols):
                ring, x, y, k = move(row // 2, row % 2, col // (self.cols // 2), col % 2)
                pairs.append(
                    (row * self.cols + col, (ring * 2 + x) * self.cols + y * (self.cols // 2) + k)
                )
        return lax.ppermute(v, ("row", "col"), pairs)

    def across(self, v):
        return self.send(v, lambda ring, x, y, k: (ring, x, 1 - y, k))

    def beside(self, v):
        return self.send(v, lambda ring, x, y, k: (ring, x, y, 1 - k))

    def far(self, v):
        return self.send(
            v, lambda ring, x, y, k: (ring, 1 - x, y, k) if k else (ring, x, 1 - y, k)
        )

    def along(self, v):
        return self.send(v, lambda ring, x, y, k: (ring, 1 - x, y, k))

    def turned(self, v, bit):
        return self.send(v, lambda ring, x, y, k: (ring ^ (1 << bit), x, y, k))

    def ring_grow(self, block, bit):
        return jnp.concatenate([block, self.turned(block, bit)], axis=0)

    def ring_gather(self, block, last=0):
        for bit in reversed(range(last, self.bits)):
            block = self.ring_grow(block, bit)
        return block

    def ring_split(self, block):
        own, low = jnp.split(block, 2, axis=0)
        return own, low.astype(bf16)

    def ring_scatter(self, own, low, held=()):
        for bit in range(self.bits):
            if bit > 0:
                own, low = self.ring_split(own)
                low = tie(low, *held)
            own = own + self.turned(low, bit).astype(f32)
        return own


def tie(value, *others):
    return lax.optimization_barrier((value, *others))[0]


class Scatter:
    def __init__(self, links, to_x, to_y, keep):
        self.links, self.keep = links, keep
        by_x = [links.along(v) for v in to_x]
        self.by_x = [by_x[0][0], by_x[0][1]] if len(by_x) == 1 else by_x
        self.by_y = links.across(to_y)

    def second(self):
        to_x = (self.keep[2].astype(f32) + self.by_y[1].astype(f32)).astype(bf16)
        to_y = (self.keep[3].astype(f32) + self.by_x[1].astype(f32)).astype(bf16)
        self.late_x, self.late_y = self.links.along(to_x), self.links.across(to_y)
        return to_x, to_y

    def third(self):
        low = self.keep[0].astype(f32) + self.by_y[0].astype(f32) + self.late_x.astype(f32)
        high = self.keep[1].astype(f32) + self.by_x[0].astype(f32) + self.late_y.astype(f32)
        self.own, self.low = self.links.ring_split(jnp.concatenate([low, high], axis=0))
        return [self.low]

    def last(self, held=()):
        return self.links.ring_scatter(self.own, self.low, held)


def relative_order(links, depth):
    ring, x, _, _ = links.locate()
    where = lax.broadcasted_iota(jnp.int32, (1, links.rows * depth), 1)
    block, inside = where // depth, where % depth
    steps = links.rows // 2
    place = block % steps
    turn = jnp.zeros_like(place)
    for bit in reversed(range(links.bits)):
        turn = turn + (place % 2 << bit)
        place = place // 2
    row = jnp.bitwise_xor(ring, turn) * 2 + jnp.bitwise_xor(x, block // steps)
    return row * depth + inside


def on_device(
    links, tokens, segments, positions, w_qkv, w_out, w_gate_up, w_down, norm_gain, norm_bias, cotangent
):
    ring, x_place, side, core = links.locate()
    depth = w_qkv.shape[0]
    width = tokens.shape[2]
    head_cols = w_qkv.shape[2]
    hid = w_gate_up.shape[2]
    sizes = [hid - hid // 3, hid // 3]
    rows = 2 * tokens.shape[1]
    mine = rows // 2
    part = head_cols + HD

    source = relative_order(links, depth)
    swap = (lax.broadcasted_iota(jnp.int32, (width, width), 0) == source).astype(bf16)

    def split(v):
        high = v.astype(bf16)
        return high, (v - high.astype(f32)).astype(bf16)

    def own_and_other(v):
        own = lax.dynamic_index_in_dim(v, side, 0, keepdims=False)
        return own, lax.dynamic_index_in_dim(v, 1 - side, 0, keepdims=False)

    def from_sequence(own, came):
        first = side == 0
        return jnp.stack([jnp.where(first, own, came), jnp.where(first, came, own)], axis=0)

    out_t = w_out.T
    attn_shard = jnp.concatenate(
        sum(
            [[w_qkv[:, p], out_t[:, p * HD : (p + 1) * HD]] for p in range(3)],
            [],
        ),
        axis=1,
    )
    norms = jnp.concatenate([norm_gain, norm_bias], axis=1)
    norms = jnp.pad(norms, ((0, 0), (0, 128 - norms.shape[1])))
    down_t = w_down.T
    mlp_shards = []
    for h, at in enumerate([0, sizes[0]]):
        cols = slice(at, at + sizes[h])
        pieces = [down_t[:, cols], w_gate_up[:, 0, cols], w_gate_up[:, 1, cols]]
        mlp_shards.append(jnp.concatenate(pieces + ([norms] if h == 0 else []), axis=1))

    small_own, small_other = own_and_other(jnp.stack([segments, positions], axis=1))
    small_came = links.across(small_other)
    tokens_own, tokens_other = own_and_other(tokens)
    tokens_came = links.across(tie(tokens_other, attn_shard, small_other))
    dy_own, dy_other = own_and_other(cotangent)
    dy_came = links.across(tie(dy_other.astype(bf16), attn_shard, small_other))

    odd = core == 1
    ring_a = links.ring_gather(attn_shard)
    x_a, y_a = links.along(ring_a), links.across(ring_a)
    ring_b = links.ring_gather(tie(mlp_shards[0], ring_a))
    turn_a = jnp.where(odd, y_a, x_a)
    attn_w = [ring_a, x_a, y_a, links.far(turn_a)]

    x_abs = jnp.concatenate([tokens_own, tokens_came], axis=0)
    x = dot(x_abs, swap).astype(bf16)
    x_other = links.beside(x)
    small = jnp.concatenate([small_own, small_came], axis=1)
    small = jnp.concatenate([small, links.beside(small)], axis=1)
    qcode, kcode = document_codes(small[0])
    first_quarter, second_quarter = jnp.zeros((1,), jnp.int32), jnp.ones((1,), jnp.int32)
    cosine, sine = rope_tables(small[1])

    ring_b = tie(ring_b, turn_a, cosine, sine, qcode, kcode)
    x_b, y_b = links.along(ring_b), links.across(ring_b)
    ring_c = links.ring_gather(tie(mlp_shards[1], ring_b))
    q, kv, wo = qkv(tie(x, ring_b, dy_came), x_other, cosine, sine, attn_w)
    att_0, logs_0 = attend(first_quarter, q, kv, qcode, kcode)
    att_1, logs_1 = attend(second_quarter, tie(q, att_0), kv, qcode, kcode)
    held_x, held_y = lax.optimization_barrier((x_b, y_b, att_1))[:2]
    turn_b = jnp.where(odd, held_y, held_x)
    mlp_b = [ring_b, x_b, y_b, links.far(turn_b)]
    ring_c = tie(ring_c, turn_b)
    x_c, y_c = links.along(ring_c), links.across(ring_c)
    own, send = project(att_0, tie(att_1, turn_b, ring_c), wo)
    x_t = lax.dot_general(
        swap, tie(x_abs, own), (((0,), (1,)), ((), ())), preferred_element_type=f32
    ).astype(bf16)
    x_t = [x_t, links.beside(x_t)]
    high, low_part = split(tie(dy_own, own))
    dy = jnp.concatenate([dot(high, swap) + dot(low_part, swap), dot(dy_came, swap)], axis=0)
    n1, s1, low, low_t, gains = first_norm(
        x, tie(own, mlp_b[3], x_t[1], dy), links.beside(send), ring_b, x_b
    )
    low_other = links.beside(low)
    act_b_own, feed = mlp(low, None, mlp_b, sizes[0], f32)
    low1_t = [low_t, links.beside(tie(low_t, feed))]
    act_b_other, feed_other = mlp(low_other, None, mlp_b, sizes[0], f32)
    held_x, held_y = lax.optimization_barrier((x_c, y_c, feed))[:2]
    turn_c = jnp.where(odd, held_y, held_x)
    mlp_c = [ring_c, x_c, y_c, links.far(turn_c)]
    act_c_other, send = mlp(tie(low_other, low1_t[1]), feed_other, mlp_c, sizes[1], bf16)
    came = links.beside(send)
    act_c_own, feed = mlp(tie(low, send), feed, mlp_c, sizes[1], f32)
    layer_out, dh2, dfeed, dfeed_t, sums = second_norm(n1, gains, feed, came, dy)
    layer_out = dot(layer_out, swap, NT).astype(bf16)
    layer_came = links.across(layer_out[mine:])
    dfeeds = [dfeed, links.beside(dfeed)]
    dfeeds_t = [dfeed_t, links.beside(dfeed_t)]

    own, other, to_x, to_y, keep = mlp_back(None, dfeeds, dfeeds_t, low1_t, (act_c_own, act_c_other), mlp_c)
    sum_b = Scatter(links, [to_x], to_y, keep)
    own, other, to_x, to_y, keep = mlp_back(
        (tie(own, layer_came), other), dfeeds, dfeeds_t, low1_t, (act_b_own, act_b_other), mlp_b
    )
    came = links.beside(other)
    sum_b.keep = tie(sum_b.keep, own)
    ops_b = sum_b.second()
    sum_c = Scatter(links, [tie(to_x, *ops_b)], tie(to_y, *ops_b), keep)
    dh1, low, low_t = first_back(tie(dh2, *ops_b), own, came, n1, s1, gains, sums)
    lows = [low, links.beside(low)]
    low_t = [low_t, links.beside(low_t)]
    dq, dkv = attend_back(
        second_quarter, q, kv, *lows, wo, att_1, logs_1, qcode, kcode, cosine, sine
    )
    sum_b.keep = tie(sum_b.keep, dq)
    block_b = sum_b.third()
    bases = (dh1, jnp.zeros(low.shape, bf16))
    own, other, to_y, keep_1, to_x_1 = qkv_back(
        bases, tie(dq, *block_b), dkv, x_t, low_t, att_1, attn_w[2:]
    )
    own_b = sum_b.last()
    sum_c.keep = tie(sum_c.keep, own)
    ops_c = sum_c.second()
    dq, dkv = attend_back(
        first_quarter, tie(q, own, *ops_c), kv, *lows, wo, att_0, logs_0, qcode, kcode, cosine, sine
    )
    sum_c.keep = tie(sum_c.keep, dq)
    block_c = sum_c.third()
    own, other, early, middle, to_x_0 = qkv_back(
        (own, other), tie(dq, *block_c, own_b), dkv, x_t, low_t, att_0, attn_w[:2]
    )
    own_c = sum_c.last()
    sum_a = Scatter(links, [to_x_0, to_x_1], to_y, [early[0], middle, early[1], keep_1])
    grad = own + links.beside(other).astype(f32)
    high, low = split(grad)
    grad = dot(high, swap, NT) + dot(low, swap, NT)
    sum_a.keep = tie(sum_a.keep, grad)
    ops_a = sum_a.second()
    own_mlp = [own_c, own_b]
    grad_down = jnp.concatenate([v[:, :n] for v, n in zip(own_mlp, sizes)], axis=1).T
    grad_gate_up = jnp.stack(
        [
            jnp.concatenate([v[:, p * n : (p + 1) * n] for v, n in zip(own_mlp, sizes)], axis=1)
            for p in (1, 2)
        ],
        axis=1,
    )
    block_a = sum_a.third()
    came = links.across(tie(grad[mine:].astype(bf16), *block_a))
    input_grad = from_sequence(grad[:mine], came.astype(f32))
    layer_out = from_sequence(tie(layer_out[:mine], to_x_0), layer_came)
    own_attn = sum_a.last((came, grad_down, grad_gate_up, layer_out))
    thirds = [own_attn[:, p * part : (p + 1) * part] for p in range(3)]
    edge = 3 * part
    return (
        layer_out,
        input_grad,
        jnp.stack([v[:, :head_cols] for v in thirds], axis=1),
        jnp.concatenate([v[:, head_cols:] for v in thirds], axis=1).T,
        grad_gate_up,
        grad_down,
        own_attn[:, edge : edge + 2],
        own_attn[:, edge + 2 : edge + 4],
    )


def solution(mesh):
    in_specs = (
        P(None, ("row", "col"), None),
        P(None, ("row", "col")),
        P(None, ("row", "col")),
        P("row", None, "col"),
        P("col", "row"),
        P("row", None, "col"),
        P("col", "row"),
        P("row", None),
        P("row", None),
        P(None, ("row", "col"), None),
    )
    out_specs = (
        P(None, ("row", "col"), None),
        P(None, ("row", "col"), None),
        P("row", None, "col"),
        P("col", "row"),
        P("row", None, "col"),
        P("col", "row"),
        P("row", None),
        P("row", None),
    )
    return jax.shard_map(
        functools.partial(on_device, Links(mesh)), mesh=mesh, in_specs=in_specs, out_specs=out_specs, check_vma=False
    )
```

```python
import functools
import math

import jax
import jax.numpy as jnp
from jax import lax
from jax.experimental import pallas as pl
from jax.experimental.pallas import tpu as pltpu
from jax.sharding import PartitionSpec as P

HD = 64
PAIR = 2 * HD
QROWS = 256
epsilon = 1e-12
rope_base = 1000.0
masked_score = -1e30
f32 = jnp.float32
bf16 = jnp.bfloat16

NN = (((1,), (0,)), ((), ()))
NT = (((1,), (1,)), ((), ()))
TN = (((0,), (0,)), ((), ()))


def dot(a, b, dims=NN):
    return lax.dot_general(a, b, dims, preferred_element_type=f32)


def rope_tables(positions):
    half_dim = HD // 2
    lane = jnp.arange(PAIR)
    freq = rope_base ** (-(lane % half_dim).astype(f32) / half_dim)
    sign = jnp.where(lane % HD < half_dim, -1.0, 1.0)
    angles = positions.astype(f32)[:, None] * freq[None, :]
    return jnp.cos(angles), jnp.sin(angles) * sign[None, :]


def rotated(values, cosine, sine):
    width = values.shape[1]
    cosine = jnp.concatenate([cosine] * (width // PAIR), axis=1)
    sine = jnp.concatenate([sine] * (width // PAIR), axis=1)
    lane = lax.broadcasted_iota(jnp.int32, values.shape, 1)
    up = pltpu.roll(values, width - HD // 2, 1)
    down = pltpu.roll(values, HD // 2, 1)
    return values * cosine + jnp.where(lane % HD < HD // 2, up, down) * sine


def normalize(hidden):
    centred = hidden - jnp.mean(hidden, axis=-1, keepdims=True)
    variance = jnp.mean(centred * centred, axis=-1, keepdims=True)
    inv_std = lax.rsqrt(variance + epsilon)
    return (centred * inv_std, inv_std)


def norm_back(grad_norm, normed, inv_std):
    return inv_std * (
        grad_norm
        - jnp.mean(grad_norm, axis=-1, keepdims=True)
        - normed * jnp.mean(grad_norm * normed, axis=-1, keepdims=True)
    )


BLOCKS = 4


def block_starts(width):
    return [(0, 0), (0, width // 2), (1, 0), (1, width // 2)]


def start_weights(blocks, w_ref, sems):
    @pl.when(pl.program_id(0) == 0)
    def _():
        for block, (slot, row) in zip(blocks, block_starts(w_ref.shape[1])):
            pltpu.make_async_copy(
                block, w_ref.at[slot, pl.ds(row, block.shape[0])], sems.at[slot]
            ).start()


def wait_weights(w_ref, sems, slot):
    pltpu.make_async_copy(w_ref.at[slot], w_ref.at[slot], sems.at[slot]).wait()


def weight_scratch(blocks):
    width = 2 * blocks[0].shape[0]
    return [
        pltpu.VMEM((2, width, blocks[0].shape[1]), bf16),
        pltpu.SemaphoreType.DMA((2,)),
    ]


ANY = pl.BlockSpec(memory_space=pl.ANY)


def cost(flops, nbytes, exps=0):
    return pl.CostEstimate(flops=int(flops), bytes_accessed=int(nbytes), transcendentals=int(exps))


def whole(shape):
    return pl.BlockSpec(shape, lambda *_: (0,) * len(shape), pipeline_mode=pl.Buffered(1))


def qkv_kernel(own_ref, other_ref, cos_ref, sin_ref, *rest):
    blocks, (q_ref, kv_ref, wo_ref, w_ref, sems) = rest[:BLOCKS], rest[BLOCKS:]
    slot = pl.program_id(0)
    start_weights(blocks, w_ref, sems)
    wait_weights(w_ref, sems, slot)
    part = w_ref.shape[2] // 3
    rows = own_ref.shape[0]
    for i, x_ref in enumerate((own_ref, other_ref)):
        span = slice(i * rows, (i + 1) * rows)
        cosine, sine = cos_ref[span, :], sin_ref[span, :]
        x = x_ref[...]
        q = dot(x, w_ref[slot, :, :part])
        q_ref[span, :] = (rotated(q, cosine, sine) * (1.0 / math.sqrt(HD))).astype(bf16)
        k = dot(x, w_ref[slot, :, part : 2 * part])
        kv_ref[span, :part] = rotated(k, cosine, sine).astype(bf16)
        kv_ref[span, part:] = dot(x, w_ref[slot, :, 2 * part :]).astype(bf16)
    lane = lax.broadcasted_iota(jnp.int32, (w_ref.shape[1], part), 1)
    out = jnp.zeros(lane.shape, f32)
    for h in range(3):
        piece = w_ref[slot, :, h * part : (h + 1) * part].astype(f32)
        piece = pltpu.roll(piece, (h + 1) * HD, 1)
        out = jnp.where(lane // HD == h, piece, out)
    wo_ref[...] = out.astype(bf16)


def qkv(own, other, cosine, sine, blocks):
    rows, width = own.shape
    part = blocks[0].shape[1] // 3
    table = whole((2 * rows, PAIR))
    return pl.pallas_call(
        qkv_kernel,
        grid=(2,),
        in_specs=[whole((rows, width))] * 2 + [table] * 2 + [ANY] * BLOCKS,
        out_specs=[
            pl.BlockSpec((2 * rows, part), lambda i: (0, i)),
            pl.BlockSpec((2 * rows, 2 * part), lambda i: (0, i)),
            pl.BlockSpec((width, part), lambda i: (0, i)),
        ],
        scratch_shapes=weight_scratch(blocks),
        out_shape=[
            jax.ShapeDtypeStruct((2 * rows, 2 * part), bf16),
            jax.ShapeDtypeStruct((2 * rows, 4 * part), bf16),
            jax.ShapeDtypeStruct((width, 2 * part), bf16),
        ],
        cost_estimate=cost(24 * rows * width * part, 40 * width * part),
        compiler_params=pltpu.CompilerParams(vmem_limit_bytes=12 << 20),
        name="qkv",
    )(own, other, cosine, sine, *blocks)


BITS = 5


def document_codes(segment):
    lane = jnp.arange(PAIR) % HD
    bit = (segment[:, None] >> (lane % BITS)[None, :]) & 1
    used = (lane < 2 * BITS)[None, :]
    query = jnp.where(lane[None, :] < BITS, bit, 1 - bit)
    query = jnp.where(used, query, 0).astype(bf16)
    key = jnp.where(lane[None, :] < BITS, 1 - bit, bit)
    key = jnp.where(used, key, 0).astype(f32) * -(2.0**100)
    return query, key.astype(bf16)


def coded_keys(kx_ref, kv_ref, kcode_ref):
    lane = lax.broadcasted_iota(jnp.int32, kcode_ref.shape, 1)
    for h in range(3):
        pair = slice(h // 2 * PAIR, (h // 2 + 1) * PAIR)
        kx_ref[h] = jnp.where(lane // HD == h % 2, kv_ref[:, pair], kcode_ref[...])


def attend_kernel(quarter_ref, q_ref, kv_ref, qcode_ref, kcode_ref, out_ref, log_ref, vt_ref, kx_ref, ot_ref):
    block, part = q_ref.shape
    half_of = lax.broadcasted_iota(jnp.int32, (block, PAIR), 1) // HD

    @pl.when(pl.program_id(0) == 0)
    def _():
        vt_ref[...] = kv_ref[:, part:].T
        coded_keys(kx_ref, kv_ref, kcode_ref)
        ot_ref[3 * HD :, :] = jnp.zeros((HD, block), f32)

    def head(h, _):
        pair = pl.ds(pl.multiple_of(h // 2 * PAIR, PAIR), PAIR)
        rows = pl.ds(pl.multiple_of(h * HD, HD), HD)
        coded = jnp.where(half_of == h % 2, q_ref[:, pair], qcode_ref[...])
        scores = dot(kx_ref[h], coded, NT)
        top = jnp.max(scores, axis=0, keepdims=True)
        expo = jnp.exp(scores - top)
        total = jnp.sum(expo, axis=0, keepdims=True)
        ot_ref[rows, :] = dot(vt_ref[rows, :], expo.astype(bf16)) / total
        log_ref[pl.ds(h, 1), :] = top + jnp.log(total)
        return 0

    lax.fori_loop(0, 3, head, 0)
    out_ref[...] = ot_ref[...].T.astype(bf16)


def attend(quarter, q, kv, qcode, kcode):
    rows = q.shape[0]
    part = q.shape[1] // 2
    block = rows // 2
    grid_spec = pltpu.PrefetchScalarGridSpec(
        num_scalar_prefetch=1,
        grid=(2,),
        in_specs=[
            pl.BlockSpec((block, part), lambda i, c: (i, c[0])),
            pl.BlockSpec((rows, 2 * part), lambda i, c: (0, c[0])),
            pl.BlockSpec((block, PAIR), lambda i, c: (i, 0)),
            whole((rows, PAIR)),
        ],
        out_specs=[
            pl.BlockSpec((block, part), lambda i, c: (i, 0)),
            pl.BlockSpec((8, block), lambda i, c: (0, i)),
        ],
        scratch_shapes=[
            pltpu.VMEM((part, rows), bf16),
            pltpu.VMEM((3, rows, PAIR), bf16),
            pltpu.VMEM((part, block), f32),
        ],
    )
    return pl.pallas_call(
        attend_kernel,
        grid_spec=grid_spec,
        out_shape=[
            jax.ShapeDtypeStruct((rows, part), bf16),
            jax.ShapeDtypeStruct((8, rows), f32),
        ],
        cost_estimate=cost(16 * rows * rows * part, 12 * rows * part, rows * rows * 3),
        compiler_params=pltpu.CompilerParams(vmem_limit_bytes=12 << 20),
        name="attend",
    )(quarter, q, kv, qcode, kcode)


def attend_back_kernel(
    quarter_ref, q_ref, kv_ref, own_ref, other_ref, wo_ref, att_ref, log_ref, qcode_ref, kcode_ref, cos_ref, sin_ref,
    dq_ref, dkv_ref, kt_ref, kx_ref, do_ref, delta_ref, dqt_ref, dk_ref, dv_ref,
):
    step = pl.program_id(0)
    block, part = q_ref.shape
    half_of = lax.broadcasted_iota(jnp.int32, (block, PAIR), 1) // HD

    @pl.when(step == 0)
    def _():
        kt_ref[...] = kv_ref[:, :part].T
        coded_keys(kx_ref, kv_ref, kcode_ref)
        dk_ref[...] = jnp.zeros_like(dk_ref)
        dv_ref[...] = jnp.zeros_like(dv_ref)
        dqt_ref[3 * HD :, :] = jnp.zeros((HD, block), f32)

    low = jnp.where(step < pl.num_programs(0) // 2, own_ref[...], other_ref[...])
    do = dot(low, wo_ref[...]).astype(bf16)
    do_ref[...] = do
    prod = do.astype(f32) * att_ref[...].astype(f32)
    high = prod.astype(bf16)
    rest = (prod - high.astype(f32)).astype(bf16)
    row = lax.broadcasted_iota(jnp.int32, (8, part), 0)
    lane = lax.broadcasted_iota(jnp.int32, (8, part), 1) // HD
    pick = jnp.where(row == lane, 1.0, 0.0).astype(bf16)
    delta_ref[...] = dot(pick, high, NT) + dot(pick, rest, NT)

    def head(h, _):
        pair = pl.ds(pl.multiple_of(h // 2 * PAIR, PAIR), PAIR)
        values = pl.ds(pl.multiple_of(part + h // 2 * PAIR, PAIR), PAIR)
        rows = pl.ds(pl.multiple_of(h * HD, HD), HD)
        mine = half_of == h % 2
        zero = jnp.zeros((block, PAIR), bf16)
        q = q_ref[:, pair]
        q_head = jnp.where(mine, q, zero)
        do_head = jnp.where(mine, do_ref[:, pair], zero)
        scores = dot(kx_ref[h], jnp.where(mine, q, qcode_ref[...]), NT)
        probs = jnp.exp(scores - log_ref[pl.ds(h, 1), :])
        dprobs = dot(kv_ref[:, values], do_head, NT)
        dscores = (probs * (dprobs - delta_ref[pl.ds(h, 1), :])).astype(bf16)
        dv_ref[:, pair] += dot(probs.astype(bf16), do_head)
        dk_ref[:, pair] += dot(dscores, q_head)
        dqt_ref[rows, :] = dot(kt_ref[rows, :], dscores)
        return 0

    lax.fori_loop(0, 3, head, 0)
    dq = (dqt_ref[...] * (1.0 / math.sqrt(HD))).T
    span = pl.ds(pl.multiple_of(step * block, block), block)
    dq_ref[...] = rotated(dq, cos_ref[span, :], -sin_ref[span, :]).astype(bf16)

    @pl.when(step == pl.num_programs(0) - 1)
    def _():
        dkv_ref[:, :part] = rotated(dk_ref[...], cos_ref[...], -sin_ref[...]).astype(bf16)
        dkv_ref[:, part:] = dv_ref[...].astype(bf16)


def attend_back(quarter, q, kv, own, other, wo, att, logs, qcode, kcode, cosine, sine):
    rows = q.shape[0]
    width = own.shape[1]
    part = q.shape[1] // 2
    block = rows // 2
    grid_spec = pltpu.PrefetchScalarGridSpec(
        num_scalar_prefetch=1,
        grid=(2,),
        in_specs=[
            pl.BlockSpec((block, part), lambda i, c: (i, c[0])),
            pl.BlockSpec((rows, 2 * part), lambda i, c: (0, c[0]), pipeline_mode=pl.Buffered(1)),
            whole((block, width)),
            whole((block, width)),
            pl.BlockSpec((width, part), lambda i, c: (0, c[0]), pipeline_mode=pl.Buffered(1)),
            pl.BlockSpec((block, part), lambda i, c: (i, 0)),
            pl.BlockSpec((8, block), lambda i, c: (0, i)),
            pl.BlockSpec((block, PAIR), lambda i, c: (i, 0)),
            whole((rows, PAIR)),
            whole((rows, PAIR)),
            whole((rows, PAIR)),
        ],
        out_specs=[
            pl.BlockSpec((block, part), lambda i, c: (i, 0)),
            whole((rows, 2 * part)),
        ],
        scratch_shapes=[
            pltpu.VMEM((part, rows), bf16),
            pltpu.VMEM((3, rows, PAIR), bf16),
            pltpu.VMEM((block, part), bf16),
            pltpu.VMEM((8, block), f32),
            pltpu.VMEM((part, block), f32),
            pltpu.VMEM((rows, part), f32),
            pltpu.VMEM((rows, part), f32),
        ],
    )
    return pl.pallas_call(
        attend_back_kernel,
        grid_spec=grid_spec,
        out_shape=[
            jax.ShapeDtypeStruct((rows, part), bf16),
            jax.ShapeDtypeStruct((rows, 2 * part), bf16),
        ],
        cost_estimate=cost(40 * rows * rows * part, 30 * rows * part, rows * rows * 3),
        compiler_params=pltpu.CompilerParams(vmem_limit_bytes=22 << 20),
        name="attend_back",
    )(quarter, q, kv, own, other, wo, att, logs, qcode, kcode, cosine, sine)


def project_kernel(att_a_ref, att_b_ref, wo_ref, own_ref, send_ref):
    part = att_a_ref.shape[1]
    rows = own_ref.shape[0]
    for out_ref, span in ((send_ref, slice(rows, 2 * rows)), (own_ref, slice(0, rows))):
        out = dot(att_a_ref[span, :], wo_ref[:, :part], NT) + dot(att_b_ref[span, :], wo_ref[:, part:], NT)
        out_ref[...] = out.astype(out_ref.dtype)


def project(att_a, att_b, wo):
    rows, part = att_a.shape
    rows = rows // 2
    width = wo.shape[0]
    return pl.pallas_call(
        project_kernel,
        grid=(1,),
        in_specs=[whole(att_a.shape)] * 2 + [whole(wo.shape)],
        out_specs=[whole((rows, width))] * 2,
        out_shape=[
            jax.ShapeDtypeStruct((rows, width), f32),
            jax.ShapeDtypeStruct((rows, width), bf16),
        ],
        cost_estimate=cost(8 * rows * width * part, 16 * rows * width),
        compiler_params=pltpu.CompilerParams(vmem_limit_bytes=6 << 20),
        name="project",
    )(att_a, att_b, wo)


def first_kernel(
    x_ref, own_ref, came_ref, norm_a_ref, norm_b_ref, n_ref, s_ref, low_ref, low_t_ref, gains_ref
):
    norms = jnp.concatenate([norm_a_ref[...], norm_b_ref[...]], axis=0).astype(f32).T
    gains_ref[...] = norms[:8]
    branch = own_ref[...] + came_ref[...].astype(f32)
    normed, inv = normalize(x_ref[...].astype(f32) + branch)
    n_ref[...] = normed
    s_ref[...] = jnp.broadcast_to(inv, s_ref.shape)
    first = normed * norms[0:1] + norms[2:3]
    low_ref[...] = first.astype(bf16)
    low_t_ref[...] = first.T.astype(bf16)


def first_norm(x, own, came, norm_a, norm_b):
    rows, width = x.shape
    at = norm_a.shape[1] // 128 - 1
    strip = pl.BlockSpec((width // 2, 128), lambda i: (0, at))
    return pl.pallas_call(
        first_kernel,
        grid=(1,),
        in_specs=[whole(x.shape)] * 3 + [strip] * 2,
        out_specs=[
            whole((rows, width)), whole((rows, 128)), whole((rows, width)), whole((width, rows)), whole((8, width)),
        ],
        out_shape=[
            jax.ShapeDtypeStruct((rows, width), f32),
            jax.ShapeDtypeStruct((rows, 128), f32),
            jax.ShapeDtypeStruct((rows, width), bf16),
            jax.ShapeDtypeStruct((width, rows), bf16),
            jax.ShapeDtypeStruct((8, width), f32),
        ],
        cost_estimate=cost(20 * rows * width, 16 * rows * width),
        compiler_params=pltpu.CompilerParams(vmem_limit_bytes=7 << 20),
        name="first_norm",
    )(x, own, came, norm_a, norm_b)


def mlp_kernel(has_base, low_ref, *rest):
    if has_base:
        base_ref, rest = rest[0], rest[1:]
    blocks, (act_ref, feed_ref, w_ref, sems, sum_ref) = rest[:BLOCKS], rest[BLOCKS:]
    slot = pl.program_id(0)
    half = act_ref.shape[3]
    start_weights(blocks, w_ref, sems)

    @pl.when(slot == 0)
    def _():
        sum_ref[...] = base_ref[...] if has_base else jnp.zeros_like(sum_ref)

    wait_weights(w_ref, sems, slot)

    gate = dot(low_ref[...], w_ref[slot, :, half : 2 * half])
    up = dot(low_ref[...], w_ref[slot, :, 2 * half : 3 * half])
    act_ref[0, 0] = gate.astype(bf16)
    act_ref[0, 1] = up.astype(bf16)
    act_ref[0, 2] = (gate / (1.0 + jnp.exp(-gate)) * up).astype(bf16)
    sum_ref[...] += dot(act_ref[0, 2], w_ref[slot, :, :half], NT)

    @pl.when(slot == 1)
    def _():
        feed_ref[...] = sum_ref[...].astype(feed_ref.dtype)


def mlp(low, base, blocks, half, dtype):
    rows, width = low.shape
    has_base = base is not None
    extra = [base] if has_base else []
    return pl.pallas_call(
        functools.partial(mlp_kernel, has_base),
        grid=(2,),
        in_specs=[whole((rows, width))] * (1 + has_base) + [ANY] * BLOCKS,
        out_specs=[
            pl.BlockSpec((1, 3, rows, half), lambda i: (i, 0, 0, 0)),
            whole((rows, width)),
        ],
        scratch_shapes=weight_scratch(blocks) + [pltpu.VMEM((rows, width), f32)],
        out_shape=[
            jax.ShapeDtypeStruct((2, 3, rows, half), bf16),
            jax.ShapeDtypeStruct((rows, width), dtype),
        ],
        cost_estimate=cost(12 * rows * width * half, 30 * half * width, 2 * rows * half),
        compiler_params=pltpu.CompilerParams(vmem_limit_bytes=(6 + half // 64) << 20),
        name="mlp",
    )(low, *extra, *blocks)


def second_kernel(
    n_ref, gains_ref, feed_ref, came_ref, dy_ref, out_ref, dh_ref, low_ref, low_t_ref, sums_ref
):
    first = n_ref[...] * gains_ref[0:1] + gains_ref[2:3]
    normed, inv = normalize(first + feed_ref[...] + came_ref[...].astype(f32))
    out_ref[...] = (normed * gains_ref[1:2] + gains_ref[3:4]).astype(bf16)
    dy = dy_ref[...]
    sums_ref[...] = jnp.zeros_like(sums_ref)
    sums_ref[1:2] = jnp.sum(dy * normed, axis=0, keepdims=True)
    sums_ref[3:4] = jnp.sum(dy, axis=0, keepdims=True)
    dh = norm_back(dy * gains_ref[1:2], normed, inv)
    dh_ref[...] = dh
    low_ref[...] = dh.astype(bf16)
    low_t_ref[...] = dh.T.astype(bf16)


def second_norm(n1, gains, feed, came, dy):
    rows, width = n1.shape
    full = whole((rows, width))
    return pl.pallas_call(
        second_kernel,
        grid=(1,),
        in_specs=[full, whole((8, width)), full, full, full],
        out_specs=[full, full, full, whole((width, rows)), whole((8, width))],
        out_shape=[
            jax.ShapeDtypeStruct((rows, width), bf16),
            jax.ShapeDtypeStruct((rows, width), f32),
            jax.ShapeDtypeStruct((rows, width), bf16),
            jax.ShapeDtypeStruct((width, rows), bf16),
            jax.ShapeDtypeStruct((8, width), f32),
        ],
        cost_estimate=cost(40 * rows * width, 22 * rows * width),
        compiler_params=pltpu.CompilerParams(vmem_limit_bytes=9 << 20),
        name="second_norm",
    )(n1, gains, feed, came, dy)


def mlp_back_kernel(has_base, *rest):
    dfeeds, dfeeds_t, lows_t, acts = rest[:2], rest[2:4], rest[4:6], rest[6:8]
    rest = rest[8:]
    if has_base:
        bases, rest = rest[:2], rest[2:]
    blocks, rest = rest[:BLOCKS], rest[BLOCKS:]
    own_ref, other_ref, to_x_ref, to_y_ref, keep_ref, w_ref, sems, part_ref, sum_ref = rest
    slot = pl.program_id(0)
    rows = own_ref.shape[0]
    half = acts[0].shape[3]
    start_weights(blocks, w_ref, sems)

    @pl.when(slot == 0)
    def _():
        for i in range(2):
            sum_ref[i * rows : (i + 1) * rows, :] = (
                bases[i][...] if has_base else jnp.zeros((rows, sum_ref.shape[1]), f32)
            )

    wait_weights(w_ref, sems, slot)

    for i in range(2):
        span = slice(i * rows, (i + 1) * rows)
        dhidden = dot(dfeeds[i][...], w_ref[slot, :, :half])
        gate = acts[i][0, 0].astype(f32)
        up = acts[i][0, 1].astype(f32)
        sg = 1.0 / (1.0 + jnp.exp(-gate))
        dgate = dhidden * up * sg * (1.0 + gate * (1.0 - sg))
        dup = dhidden * (gate * sg)
        part_ref[span, :half] = dgate.astype(bf16)
        part_ref[span, half:] = dup.astype(bf16)
        sum_ref[span, :] += dot(part_ref[span, :], w_ref[slot, :, half : 3 * half], NT)
    gate_up = (
        dot(lows_t[0][...], part_ref[:rows, :]) + dot(lows_t[1][...], part_ref[rows:, :])
    ).astype(bf16)
    down = (
        dot(dfeeds_t[0][...], acts[0][0, 2]) + dot(dfeeds_t[1][...], acts[1][0, 2])
    ).astype(bf16)
    cut = keep_ref.shape[1]

    def emit(out_ref, at, block):
        span = slice(block * cut, (block + 1) * cut)
        out_ref[at, :, :half] = down[span]
        out_ref[at, :, half:] = gate_up[span]

    emit(to_x_ref, 0, 3)

    @pl.when(slot == 0)
    def _():
        for block in range(3):
            emit(keep_ref, block, block)

    @pl.when(slot == 1)
    def _():
        emit(to_y_ref, 0, 0)
        emit(to_y_ref, 1, 2)
        emit(keep_ref, 3, 1)
        own_ref[...] = sum_ref[:rows, :]
        other_ref[...] = sum_ref[rows:, :].astype(other_ref.dtype)


def mlp_back(bases, dfeeds, dfeeds_t, lows_t, acts, blocks):
    rows, width = dfeeds[0].shape
    half = acts[0].shape[3]
    has_base = bases is not None
    full = whole((rows, width))
    return pl.pallas_call(
        functools.partial(mlp_back_kernel, has_base),
        grid=(2,),
        in_specs=[full] * 2
        + [whole((width, rows))] * 4
        + [pl.BlockSpec((1, 3, rows, half), lambda i: (i, 0, 0, 0))] * 2
        + [full] * (2 * has_base)
        + [ANY] * BLOCKS,
        out_specs=[
            full,
            full,
            pl.BlockSpec((1, width // 4, 3 * half), lambda i: (i, 0, 0)),
            whole((2, width // 4, 3 * half)),
            whole((4, width // 4, 3 * half)),
        ],
        scratch_shapes=weight_scratch(blocks)
        + [pltpu.VMEM((2 * rows, 2 * half), bf16), pltpu.VMEM((2 * rows, width), f32)],
        out_shape=[
            jax.ShapeDtypeStruct((rows, width), f32),
            jax.ShapeDtypeStruct((rows, width), bf16 if has_base else f32),
            jax.ShapeDtypeStruct((2, width // 4, 3 * half), bf16),
            jax.ShapeDtypeStruct((2, width // 4, 3 * half), bf16),
            jax.ShapeDtypeStruct((4, width // 4, 3 * half), bf16),
        ],
        cost_estimate=cost(48 * rows * width * half, 100 * half * width, 4 * rows * half),
        compiler_params=pltpu.CompilerParams(vmem_limit_bytes=(5 + half // 28) << 20),
        name="mlp_back",
    )(*dfeeds, *dfeeds_t, *lows_t, *acts, *(bases if has_base else ()), *blocks)


def first_back_kernel(
    base_ref, own_ref, came_ref, n_ref, s_ref, gains_ref, sums_ref, dh_ref, low_ref, low_t_ref
):
    dfirst = base_ref[...] + own_ref[...] + came_ref[...].astype(f32)
    normed = n_ref[...]
    width = dfirst.shape[1]
    gain_sum = jnp.sum(dfirst * normed, axis=0, keepdims=True)
    bias_sum = jnp.sum(dfirst, axis=0, keepdims=True)
    sums = sums_ref[...]
    stacked = jnp.concatenate(
        [gain_sum, sums[1:2], bias_sum, sums[3:4], jnp.zeros((124, width), f32)], axis=0
    )
    rows = dfirst.shape[0]
    low_t_ref[:, rows:] = stacked.T.astype(bf16)
    dh = norm_back(dfirst * gains_ref[0:1], normed, s_ref[:, 0:1])
    dh_ref[...] = dh
    low_ref[...] = dh.astype(bf16)
    low_t_ref[:, :rows] = dh.T.astype(bf16)


def first_back(base, own, came, n1, s1, gains, sums):
    rows, width = n1.shape
    full = whole((rows, width))
    return pl.pallas_call(
        first_back_kernel,
        grid=(1,),
        in_specs=[full] * 4 + [whole((rows, 128)), whole((8, width)), whole((8, width))],
        out_specs=[full, full, whole((width, rows + 128))],
        out_shape=[
            jax.ShapeDtypeStruct((rows, width), f32),
            jax.ShapeDtypeStruct((rows, width), bf16),
            jax.ShapeDtypeStruct((width, rows + 128), bf16),
        ],
        cost_estimate=cost(40 * rows * width, 20 * rows * width),
        compiler_params=pltpu.CompilerParams(vmem_limit_bytes=9 << 20),
        name="first_back",
    )(base, own, came, n1, s1, gains, sums)


def qkv_back_kernel(
    dq_ref, dkv_ref, x_a_ref, x_b_ref, low_a_ref, low_b_ref, cols_a_ref, cols_b_ref, att_ref, base_own_ref, base_other_ref,
    top_ref, bottom_ref, own_ref, other_ref, early_ref, mid_ref, late_ref, w_ref, sem,
):
    rows = own_ref.shape[0]
    part = dq_ref.shape[1]
    copies = [
        pltpu.make_async_copy(top_ref, w_ref.at[pl.ds(0, top_ref.shape[0])], sem),
        pltpu.make_async_copy(bottom_ref, w_ref.at[pl.ds(top_ref.shape[0], top_ref.shape[0])], sem),
    ]
    for copy in copies:
        copy.start()
    d_out = dot(low_a_ref[...], att_ref[:rows, :]) + dot(low_b_ref[...], att_ref[rows:, :])
    lane = lax.broadcasted_iota(jnp.int32, d_out.shape, 1)
    cut = mid_ref.shape[0]

    def emit(value, lanes):
        early_ref[0, :, lanes] = value[:cut]
        mid_ref[:, lanes] = value[cut : 2 * cut]
        early_ref[1, :, lanes] = value[2 * cut : 3 * cut]
        late_ref[:, lanes] = value[3 * cut :]

    for h in range(3):
        source, at = (dq_ref, 0) if h == 0 else (dkv_ref, (h - 1) * part)
        piece = dot(x_a_ref[...], source[:rows, at : at + part]) + dot(x_b_ref[...], source[rows:, at : at + part])
        moved = pltpu.roll(d_out, (3 - h) * HD, 1)
        emit(jnp.where(lane < 3 * HD, piece, moved).astype(bf16), slice(h * part, (h + 1) * part))
    cols = cols_a_ref[...].astype(f32) + cols_b_ref[...].astype(f32)
    emit(cols.astype(bf16), slice(3 * part, 3 * part + 128))
    pltpu.make_async_copy(w_ref, w_ref, sem).wait()
    for i, (base_ref, out_ref) in enumerate(((base_own_ref, own_ref), (base_other_ref, other_ref))):
        span = slice(i * rows, (i + 1) * rows)
        total = dot(dq_ref[span, :], w_ref[:, :part], NT) + dot(dkv_ref[span, :], w_ref[:, part:], NT)
        out_ref[...] = (total + base_ref[...].astype(f32)).astype(out_ref.dtype)


def qkv_back(bases, dq, dkv, x_t, low_t, att, blocks):
    rows = dq.shape[0] // 2
    width = low_t[0].shape[0]
    part = dq.shape[1]
    lanes = 3 * part + 128
    full = whole((rows, width))
    turned = whole((width, rows))
    strip = pl.BlockSpec((width, 128), lambda i: (0, rows // 128), pipeline_mode=pl.Buffered(1))
    pieces = [(2, width // 4, lanes), (width // 4, lanes), (width // 4, lanes)]
    return pl.pallas_call(
        qkv_back_kernel,
        grid=(1,),
        in_specs=[whole(dq.shape), whole(dkv.shape)]
        + [turned] * 4
        + [strip] * 2
        + [whole(att.shape), full, full, ANY, ANY],
        out_specs=[full, full] + [whole(p) for p in pieces],
        scratch_shapes=[pltpu.VMEM((width, 3 * part), bf16), pltpu.SemaphoreType.DMA],
        out_shape=[
            jax.ShapeDtypeStruct((rows, width), f32),
            jax.ShapeDtypeStruct((rows, width), bf16),
        ]
        + [jax.ShapeDtypeStruct(p, bf16) for p in pieces],
        cost_estimate=cost(26 * rows * width * part, 40 * width * part),
        compiler_params=pltpu.CompilerParams(vmem_limit_bytes=12 << 20),
        name="qkv_back",
    )(dq, dkv, *x_t, *low_t, *low_t, att, *bases, *blocks)


def bits_of(n):
    bits = n.bit_length() - 1
    if 1 << bits != n:
        raise ValueError("row count")
    return bits


class Links:
    def __init__(self, mesh):
        self.rows = mesh.shape["row"]
        self.cols = mesh.shape["col"]
        self.bits = bits_of(self.rows // 2)

    def locate(self):
        row = lax.axis_index("row")
        col = lax.axis_index("col")
        return row // 2, row % 2, col // (self.cols // 2), col % 2

    def send(self, v, move):
        pairs = []
        for row in range(self.rows):
            for col in range(self.cols):
                ring, x, y, k = move(row // 2, row % 2, col // (self.cols // 2), col % 2)
                pairs.append(
                    (row * self.cols + col, (ring * 2 + x) * self.cols + y * (self.cols // 2) + k)
                )
        return lax.ppermute(v, ("row", "col"), pairs)

    def across(self, v):
        return self.send(v, lambda ring, x, y, k: (ring, x, 1 - y, k))

    def beside(self, v):
        return self.send(v, lambda ring, x, y, k: (ring, x, y, 1 - k))

    def far(self, v):
        return self.send(
            v, lambda ring, x, y, k: (ring, 1 - x, y, k) if k else (ring, x, 1 - y, k)
        )

    def along(self, v):
        return self.send(v, lambda ring, x, y, k: (ring, 1 - x, y, k))

    def turned(self, v, bit):
        return self.send(v, lambda ring, x, y, k: (ring ^ (1 << bit), x, y, k))

    def ring_grow(self, block, bit):
        return jnp.concatenate([block, self.turned(block, bit)], axis=0)

    def ring_gather(self, block, last=0):
        for bit in reversed(range(last, self.bits)):
            block = self.ring_grow(block, bit)
        return block

    def ring_split(self, block):
        own, low = jnp.split(block, 2, axis=0)
        return own, low.astype(bf16)

    def ring_scatter(self, own, low, held=()):
        for bit in range(self.bits):
            if bit > 0:
                own, low = self.ring_split(own)
                low = tie(low, *held)
            own = own + self.turned(low, bit).astype(f32)
        return own


def tie(value, *others):
    return lax.optimization_barrier((value, *others))[0]


class Scatter:
    def __init__(self, links, to_x, to_y, keep):
        self.links, self.keep = links, keep
        by_x = [links.along(v) for v in to_x]
        self.by_x = [by_x[0][0], by_x[0][1]] if len(by_x) == 1 else by_x
        self.by_y = links.across(to_y)

    def second(self):
        to_x = (self.keep[2].astype(f32) + self.by_y[1].astype(f32)).astype(bf16)
        to_y = (self.keep[3].astype(f32) + self.by_x[1].astype(f32)).astype(bf16)
        self.late_x, self.late_y = self.links.along(to_x), self.links.across(to_y)
        return to_x, to_y

    def third(self):
        low = self.keep[0].astype(f32) + self.by_y[0].astype(f32) + self.late_x.astype(f32)
        high = self.keep[1].astype(f32) + self.by_x[0].astype(f32) + self.late_y.astype(f32)
        self.own, self.low = self.links.ring_split(jnp.concatenate([low, high], axis=0))
        return [self.low]

    def last(self, held=()):
        return self.links.ring_scatter(self.own, self.low, held)


def relative_order(links, depth):
    ring, x, _, _ = links.locate()
    where = lax.broadcasted_iota(jnp.int32, (1, links.rows * depth), 1)
    block, inside = where // depth, where % depth
    steps = links.rows // 2
    place = block % steps
    turn = jnp.zeros_like(place)
    for bit in reversed(range(links.bits)):
        turn = turn + (place % 2 << bit)
        place = place // 2
    row = jnp.bitwise_xor(ring, turn) * 2 + jnp.bitwise_xor(x, block // steps)
    return row * depth + inside


def on_device(
    links, tokens, segments, positions, w_qkv, w_out, w_gate_up, w_down, norm_gain, norm_bias, cotangent
):
    ring, x_place, side, core = links.locate()
    depth = w_qkv.shape[0]
    width = tokens.shape[2]
    head_cols = w_qkv.shape[2]
    hid = w_gate_up.shape[2]
    sizes = [hid - hid // 3, hid // 3]
    rows = 2 * tokens.shape[1]
    mine = rows // 2
    part = head_cols + HD

    source = relative_order(links, depth)
    swap = (lax.broadcasted_iota(jnp.int32, (width, width), 0) == source).astype(bf16)

    def split(v):
        high = v.astype(bf16)
        return high, (v - high.astype(f32)).astype(bf16)

    def own_and_other(v):
        own = lax.dynamic_index_in_dim(v, side, 0, keepdims=False)
        return own, lax.dynamic_index_in_dim(v, 1 - side, 0, keepdims=False)

    def from_sequence(own, came):
        first = side == 0
        return jnp.stack([jnp.where(first, own, came), jnp.where(first, came, own)], axis=0)

    out_t = w_out.T
    attn_shard = jnp.concatenate(
        sum(
            [[w_qkv[:, p], out_t[:, p * HD : (p + 1) * HD]] for p in range(3)],
            [],
        ),
        axis=1,
    )
    norms = jnp.concatenate([norm_gain, norm_bias], axis=1)
    norms = jnp.pad(norms, ((0, 0), (0, 128 - norms.shape[1])))
    down_t = w_down.T
    mlp_shards = []
    for h, at in enumerate([0, sizes[0]]):
        cols = slice(at, at + sizes[h])
        pieces = [down_t[:, cols], w_gate_up[:, 0, cols], w_gate_up[:, 1, cols]]
        mlp_shards.append(jnp.concatenate(pieces + ([norms] if h == 0 else []), axis=1))

    small_own, small_other = own_and_other(jnp.stack([segments, positions], axis=1))
    small_came = links.across(small_other)
    tokens_own, tokens_other = own_and_other(tokens)
    tokens_came = links.across(tie(tokens_other, attn_shard, small_other))
    dy_own, dy_other = own_and_other(cotangent)
    dy_came = links.across(tie(dy_other.astype(bf16), attn_shard, small_other))

    odd = core == 1
    grow_a = links.ring_gather(attn_shard, last=1)
    ring_a = links.ring_grow(grow_a, 0)
    x_a, y_a = links.along(ring_a), links.across(ring_a)
    ring_b = links.ring_gather(tie(mlp_shards[0], grow_a))
    turn_a = jnp.where(odd, y_a, x_a)
    attn_w = [ring_a, x_a, y_a, links.far(turn_a)]

    x_abs = jnp.concatenate([tokens_own, tokens_came], axis=0)
    x = dot(x_abs, swap).astype(bf16)
    x_other = links.beside(x)
    small = jnp.concatenate([small_own, small_came], axis=1)
    small = jnp.concatenate([small, links.beside(small)], axis=1)
    qcode, kcode = document_codes(small[0])
    first_quarter, second_quarter = jnp.zeros((1,), jnp.int32), jnp.ones((1,), jnp.int32)
    cosine, sine = rope_tables(small[1])

    ring_b = tie(ring_b, turn_a, cosine, sine, qcode, kcode)
    x_b, y_b = links.along(ring_b), links.across(ring_b)
    grow_c = links.ring_gather(tie(mlp_shards[1], ring_b), last=1)
    q, kv, wo = qkv(tie(x, ring_b, dy_came), x_other, cosine, sine, attn_w)
    ring_c = links.ring_grow(tie(grow_c, q), 0)
    att_0, logs_0 = attend(first_quarter, q, kv, qcode, kcode)
    att_1, logs_1 = attend(second_quarter, tie(q, att_0), kv, qcode, kcode)
    held_x, held_y = lax.optimization_barrier((x_b, y_b, att_1))[:2]
    turn_b = jnp.where(odd, held_y, held_x)
    mlp_b = [ring_b, x_b, y_b, links.far(turn_b)]
    ring_c = tie(ring_c, turn_b)
    x_c, y_c = links.along(ring_c), links.across(ring_c)
    own, send = project(att_0, tie(att_1, turn_b, ring_c), wo)
    x_t = lax.dot_general(
        swap, tie(x_abs, own), (((0,), (1,)), ((), ())), preferred_element_type=f32
    ).astype(bf16)
    x_t = [x_t, links.beside(x_t)]
    high, low_part = split(tie(dy_own, own))
    dy = jnp.concatenate([dot(high, swap) + dot(low_part, swap), dot(dy_came, swap)], axis=0)
    n1, s1, low, low_t, gains = first_norm(
        x, tie(own, mlp_b[3], x_t[1], dy), links.beside(send), ring_b, x_b
    )
    low_other = links.beside(low)
    act_b_own, feed = mlp(low, None, mlp_b, sizes[0], f32)
    low1_t = [low_t, links.beside(tie(low_t, feed))]
    act_b_other, feed_other = mlp(low_other, None, mlp_b, sizes[0], f32)
    held_x, held_y = lax.optimization_barrier((x_c, y_c, feed))[:2]
    turn_c = jnp.where(odd, held_y, held_x)
    mlp_c = [ring_c, x_c, y_c, links.far(turn_c)]
    act_c_other, send = mlp(tie(low_other, low1_t[1]), feed_other, mlp_c, sizes[1], bf16)
    came = links.beside(send)
    act_c_own, feed = mlp(tie(low, send), feed, mlp_c, sizes[1], f32)
    layer_out, dh2, dfeed, dfeed_t, sums = second_norm(n1, gains, feed, came, dy)
    layer_out = dot(layer_out, swap, NT).astype(bf16)
    layer_came = links.across(layer_out[mine:])
    dfeeds = [dfeed, links.beside(dfeed)]
    dfeeds_t = [dfeed_t, links.beside(dfeed_t)]

    own, other, to_x, to_y, keep = mlp_back(None, dfeeds, dfeeds_t, low1_t, (act_c_own, act_c_other), mlp_c)
    sum_b = Scatter(links, [to_x], to_y, keep)
    own, other, to_x, to_y, keep = mlp_back(
        (tie(own, layer_came), other), dfeeds, dfeeds_t, low1_t, (act_b_own, act_b_other), mlp_b
    )
    came = links.beside(other)
    sum_b.keep = tie(sum_b.keep, own)
    ops_b = sum_b.second()
    sum_c = Scatter(links, [tie(to_x, *ops_b)], tie(to_y, *ops_b), keep)
    dh1, low, low_t = first_back(tie(dh2, *ops_b), own, came, n1, s1, gains, sums)
    lows = [low, links.beside(low)]
    low_t = [low_t, links.beside(low_t)]
    dq, dkv = attend_back(
        second_quarter, q, kv, *lows, wo, att_1, logs_1, qcode, kcode, cosine, sine
    )
    sum_b.keep = tie(sum_b.keep, dq)
    block_b = sum_b.third()
    bases = (dh1, jnp.zeros(low.shape, bf16))
    own, other, to_y, keep_1, to_x_1 = qkv_back(
        bases, tie(dq, *block_b), dkv, x_t, low_t, att_1, attn_w[2:]
    )
    own_b = sum_b.last()
    sum_c.keep = tie(sum_c.keep, own)
    ops_c = sum_c.second()
    dq, dkv = attend_back(
        first_quarter, tie(q, own, *ops_c), kv, *lows, wo, att_0, logs_0, qcode, kcode, cosine, sine
    )
    sum_c.keep = tie(sum_c.keep, dq)
    block_c = sum_c.third()
    own, other, early, middle, to_x_0 = qkv_back(
        (own, other), tie(dq, *block_c, own_b), dkv, x_t, low_t, att_0, attn_w[:2]
    )
    own_c = sum_c.last()
    sum_a = Scatter(links, [to_x_0, to_x_1], to_y, [early[0], middle, early[1], keep_1])
    grad = own + links.beside(other).astype(f32)
    high, low = split(grad)
    grad = dot(high, swap, NT) + dot(low, swap, NT)
    sum_a.keep = tie(sum_a.keep, grad)
    ops_a = sum_a.second()
    own_mlp = [own_c, own_b]
    grad_down = jnp.concatenate([v[:, :n] for v, n in zip(own_mlp, sizes)], axis=1).T
    grad_gate_up = jnp.stack(
        [
            jnp.concatenate([v[:, p * n : (p + 1) * n] for v, n in zip(own_mlp, sizes)], axis=1)
            for p in (1, 2)
        ],
        axis=1,
    )
    block_a = sum_a.third()
    came = links.across(tie(grad[mine:].astype(bf16), *block_a))
    input_grad = from_sequence(grad[:mine], came.astype(f32))
    layer_out = from_sequence(tie(layer_out[:mine], to_x_0), layer_came)
    own_attn = sum_a.last((came, grad_down, grad_gate_up, layer_out))
    thirds = [own_attn[:, p * part : (p + 1) * part] for p in range(3)]
    edge = 3 * part
    return (
        layer_out,
        input_grad,
        jnp.stack([v[:, :head_cols] for v in thirds], axis=1),
        jnp.concatenate([v[:, head_cols:] for v in thirds], axis=1).T,
        grad_gate_up,
        grad_down,
        own_attn[:, edge : edge + 2],
        own_attn[:, edge + 2 : edge + 4],
    )


def solution(mesh):
    in_specs = (
        P(None, ("row", "col"), None),
        P(None, ("row", "col")),
        P(None, ("row", "col")),
        P("row", None, "col"),
        P("col", "row"),
        P("row", None, "col"),
        P("col", "row"),
        P("row", None),
        P("row", None),
        P(None, ("row", "col"), None),
    )
    out_specs = (
        P(None, ("row", "col"), None),
        P(None, ("row", "col"), None),
        P("row", None, "col"),
        P("col", "row"),
        P("row", None, "col"),
        P("col", "row"),
        P("row", None),
        P("row", None),
    )
    return jax.shard_map(
        functools.partial(on_device, Links(mesh)), mesh=mesh, in_specs=in_specs, out_specs=out_specs, check_vma=False
    )
```

```python
import functools
import math

import jax
import jax.numpy as jnp
from jax import lax
from jax.experimental import pallas as pl
from jax.experimental.pallas import tpu as pltpu
from jax.sharding import PartitionSpec as P

HD = 64
PAIR = 2 * HD
QROWS = 256
epsilon = 1e-12
rope_base = 1000.0
masked_score = -1e30
f32 = jnp.float32
bf16 = jnp.bfloat16

NN = (((1,), (0,)), ((), ()))
NT = (((1,), (1,)), ((), ()))
TN = (((0,), (0,)), ((), ()))


def dot(a, b, dims=NN):
    return lax.dot_general(a, b, dims, preferred_element_type=f32)


def rope_tables(positions):
    half_dim = HD // 2
    lane = jnp.arange(PAIR)
    freq = rope_base ** (-(lane % half_dim).astype(f32) / half_dim)
    sign = jnp.where(lane % HD < half_dim, -1.0, 1.0)
    angles = positions.astype(f32)[:, None] * freq[None, :]
    return jnp.cos(angles), jnp.sin(angles) * sign[None, :]


def rotated(values, cosine, sine):
    width = values.shape[1]
    cosine = jnp.concatenate([cosine] * (width // PAIR), axis=1)
    sine = jnp.concatenate([sine] * (width // PAIR), axis=1)
    lane = lax.broadcasted_iota(jnp.int32, values.shape, 1)
    up = pltpu.roll(values, width - HD // 2, 1)
    down = pltpu.roll(values, HD // 2, 1)
    return values * cosine + jnp.where(lane % HD < HD // 2, up, down) * sine


def normalize(hidden):
    centred = hidden - jnp.mean(hidden, axis=-1, keepdims=True)
    variance = jnp.mean(centred * centred, axis=-1, keepdims=True)
    inv_std = lax.rsqrt(variance + epsilon)
    return (centred * inv_std, inv_std)


def norm_back(grad_norm, normed, inv_std):
    return inv_std * (
        grad_norm
        - jnp.mean(grad_norm, axis=-1, keepdims=True)
        - normed * jnp.mean(grad_norm * normed, axis=-1, keepdims=True)
    )


BLOCKS = 4


def block_starts(width):
    return [(0, 0), (0, width // 2), (1, 0), (1, width // 2)]


def start_weights(blocks, w_ref, sems):
    @pl.when(pl.program_id(0) == 0)
    def _():
        for block, (slot, row) in zip(blocks, block_starts(w_ref.shape[1])):
            pltpu.make_async_copy(
                block, w_ref.at[slot, pl.ds(row, block.shape[0])], sems.at[slot]
            ).start()


def wait_weights(w_ref, sems, slot):
    pltpu.make_async_copy(w_ref.at[slot], w_ref.at[slot], sems.at[slot]).wait()


def weight_scratch(blocks):
    width = 2 * blocks[0].shape[0]
    return [
        pltpu.VMEM((2, width, blocks[0].shape[1]), bf16),
        pltpu.SemaphoreType.DMA((2,)),
    ]


ANY = pl.BlockSpec(memory_space=pl.ANY)


def cost(flops, nbytes, exps=0):
    return pl.CostEstimate(flops=int(flops), bytes_accessed=int(nbytes), transcendentals=int(exps))


def whole(shape):
    return pl.BlockSpec(shape, lambda *_: (0,) * len(shape), pipeline_mode=pl.Buffered(1))


def qkv_kernel(own_ref, other_ref, cos_ref, sin_ref, *rest):
    blocks, (q_ref, kv_ref, wo_ref, w_ref, sems) = rest[:BLOCKS], rest[BLOCKS:]
    slot = pl.program_id(0)
    start_weights(blocks, w_ref, sems)
    wait_weights(w_ref, sems, slot)
    part = w_ref.shape[2] // 3
    rows = own_ref.shape[0]
    for i, x_ref in enumerate((own_ref, other_ref)):
        span = slice(i * rows, (i + 1) * rows)
        cosine, sine = cos_ref[span, :], sin_ref[span, :]
        x = x_ref[...]
        q = dot(x, w_ref[slot, :, :part])
        q_ref[span, :] = (rotated(q, cosine, sine) * (1.0 / math.sqrt(HD))).astype(bf16)
        k = dot(x, w_ref[slot, :, part : 2 * part])
        kv_ref[span, :part] = rotated(k, cosine, sine).astype(bf16)
        kv_ref[span, part:] = dot(x, w_ref[slot, :, 2 * part :]).astype(bf16)
    lane = lax.broadcasted_iota(jnp.int32, (w_ref.shape[1], part), 1)
    out = jnp.zeros(lane.shape, f32)
    for h in range(3):
        piece = w_ref[slot, :, h * part : (h + 1) * part].astype(f32)
        piece = pltpu.roll(piece, (h + 1) * HD, 1)
        out = jnp.where(lane // HD == h, piece, out)
    wo_ref[...] = out.astype(bf16)


def qkv(own, other, cosine, sine, blocks):
    rows, width = own.shape
    part = blocks[0].shape[1] // 3
    table = whole((2 * rows, PAIR))
    return pl.pallas_call(
        qkv_kernel,
        grid=(2,),
        in_specs=[whole((rows, width))] * 2 + [table] * 2 + [ANY] * BLOCKS,
        out_specs=[
            pl.BlockSpec((2 * rows, part), lambda i: (0, i)),
            pl.BlockSpec((2 * rows, 2 * part), lambda i: (0, i)),
            pl.BlockSpec((width, part), lambda i: (0, i)),
        ],
        scratch_shapes=weight_scratch(blocks),
        out_shape=[
            jax.ShapeDtypeStruct((2 * rows, 2 * part), bf16),
            jax.ShapeDtypeStruct((2 * rows, 4 * part), bf16),
            jax.ShapeDtypeStruct((width, 2 * part), bf16),
        ],
        cost_estimate=cost(24 * rows * width * part, 40 * width * part),
        compiler_params=pltpu.CompilerParams(vmem_limit_bytes=12 << 20),
        name="qkv",
    )(own, other, cosine, sine, *blocks)


BITS = 5


def document_codes(segment):
    lane = jnp.arange(PAIR) % HD
    bit = (segment[:, None] >> (lane % BITS)[None, :]) & 1
    used = (lane < 2 * BITS)[None, :]
    query = jnp.where(lane[None, :] < BITS, bit, 1 - bit)
    query = jnp.where(used, query, 0).astype(bf16)
    key = jnp.where(lane[None, :] < BITS, 1 - bit, bit)
    key = jnp.where(used, key, 0).astype(f32) * -(2.0**100)
    return query, key.astype(bf16)


def coded_keys(kx_ref, kv_ref, kcode_ref):
    lane = lax.broadcasted_iota(jnp.int32, kcode_ref.shape, 1)
    for h in range(3):
        pair = slice(h // 2 * PAIR, (h // 2 + 1) * PAIR)
        kx_ref[h] = jnp.where(lane // HD == h % 2, kv_ref[:, pair], kcode_ref[...])


def attend_kernel(quarter_ref, q_ref, kv_ref, qcode_ref, kcode_ref, out_ref, log_ref, vt_ref, kx_ref, ot_ref):
    block, part = q_ref.shape
    half_of = lax.broadcasted_iota(jnp.int32, (block, PAIR), 1) // HD

    @pl.when(pl.program_id(0) == 0)
    def _():
        vt_ref[...] = kv_ref[:, part:].T
        coded_keys(kx_ref, kv_ref, kcode_ref)
        ot_ref[3 * HD :, :] = jnp.zeros((HD, block), f32)

    def head(h, _):
        pair = pl.ds(pl.multiple_of(h // 2 * PAIR, PAIR), PAIR)
        rows = pl.ds(pl.multiple_of(h * HD, HD), HD)
        coded = jnp.where(half_of == h % 2, q_ref[:, pair], qcode_ref[...])
        scores = dot(kx_ref[h], coded, NT)
        top = jnp.max(scores, axis=0, keepdims=True)
        expo = jnp.exp(scores - top)
        total = jnp.sum(expo, axis=0, keepdims=True)
        ot_ref[rows, :] = dot(vt_ref[rows, :], expo.astype(bf16)) / total
        log_ref[pl.ds(h, 1), :] = top + jnp.log(total)
        return 0

    lax.fori_loop(0, 3, head, 0)
    out_ref[...] = ot_ref[...].T.astype(bf16)


def attend(quarter, q, kv, qcode, kcode):
    rows = q.shape[0]
    part = q.shape[1] // 2
    block = rows // 2
    grid_spec = pltpu.PrefetchScalarGridSpec(
        num_scalar_prefetch=1,
        grid=(2,),
        in_specs=[
            pl.BlockSpec((block, part), lambda i, c: (i, c[0])),
            pl.BlockSpec((rows, 2 * part), lambda i, c: (0, c[0])),
            pl.BlockSpec((block, PAIR), lambda i, c: (i, 0)),
            whole((rows, PAIR)),
        ],
        out_specs=[
            pl.BlockSpec((block, part), lambda i, c: (i, 0)),
            pl.BlockSpec((8, block), lambda i, c: (0, i)),
        ],
        scratch_shapes=[
            pltpu.VMEM((part, rows), bf16),
            pltpu.VMEM((3, rows, PAIR), bf16),
            pltpu.VMEM((part, block), f32),
        ],
    )
    return pl.pallas_call(
        attend_kernel,
        grid_spec=grid_spec,
        out_shape=[
            jax.ShapeDtypeStruct((rows, part), bf16),
            jax.ShapeDtypeStruct((8, rows), f32),
        ],
        cost_estimate=cost(16 * rows * rows * part, 12 * rows * part, rows * rows * 3),
        compiler_params=pltpu.CompilerParams(vmem_limit_bytes=12 << 20),
        name="attend",
    )(quarter, q, kv, qcode, kcode)


def attend_back_kernel(
    quarter_ref, q_ref, kv_ref, own_ref, other_ref, wo_ref, att_ref, log_ref, qcode_ref, kcode_ref, cos_ref, sin_ref,
    dq_ref, dkv_ref, kt_ref, kx_ref, do_ref, delta_ref, dqt_ref, dk_ref, dv_ref,
):
    step = pl.program_id(0)
    block, part = q_ref.shape
    half_of = lax.broadcasted_iota(jnp.int32, (block, PAIR), 1) // HD

    @pl.when(step == 0)
    def _():
        kt_ref[...] = kv_ref[:, :part].T
        coded_keys(kx_ref, kv_ref, kcode_ref)
        dk_ref[...] = jnp.zeros_like(dk_ref)
        dv_ref[...] = jnp.zeros_like(dv_ref)
        dqt_ref[3 * HD :, :] = jnp.zeros((HD, block), f32)

    low = jnp.where(step < pl.num_programs(0) // 2, own_ref[...], other_ref[...])
    do = dot(low, wo_ref[...]).astype(bf16)
    do_ref[...] = do
    prod = do.astype(f32) * att_ref[...].astype(f32)
    high = prod.astype(bf16)
    rest = (prod - high.astype(f32)).astype(bf16)
    row = lax.broadcasted_iota(jnp.int32, (8, part), 0)
    lane = lax.broadcasted_iota(jnp.int32, (8, part), 1) // HD
    pick = jnp.where(row == lane, 1.0, 0.0).astype(bf16)
    delta_ref[...] = dot(pick, high, NT) + dot(pick, rest, NT)

    def head(h, _):
        pair = pl.ds(pl.multiple_of(h // 2 * PAIR, PAIR), PAIR)
        values = pl.ds(pl.multiple_of(part + h // 2 * PAIR, PAIR), PAIR)
        rows = pl.ds(pl.multiple_of(h * HD, HD), HD)
        mine = half_of == h % 2
        zero = jnp.zeros((block, PAIR), bf16)
        q = q_ref[:, pair]
        q_head = jnp.where(mine, q, zero)
        do_head = jnp.where(mine, do_ref[:, pair], zero)
        scores = dot(kx_ref[h], jnp.where(mine, q, qcode_ref[...]), NT)
        probs = jnp.exp(scores - log_ref[pl.ds(h, 1), :])
        dprobs = dot(kv_ref[:, values], do_head, NT)
        dscores = (probs * (dprobs - delta_ref[pl.ds(h, 1), :])).astype(bf16)
        dv_ref[:, pair] += dot(probs.astype(bf16), do_head)
        dk_ref[:, pair] += dot(dscores, q_head)
        dqt_ref[rows, :] = dot(kt_ref[rows, :], dscores)
        return 0

    lax.fori_loop(0, 3, head, 0)
    dq = (dqt_ref[...] * (1.0 / math.sqrt(HD))).T
    span = pl.ds(pl.multiple_of(step * block, block), block)
    dq_ref[...] = rotated(dq, cos_ref[span, :], -sin_ref[span, :]).astype(bf16)

    @pl.when(step == pl.num_programs(0) - 1)
    def _():
        dkv_ref[:, :part] = rotated(dk_ref[...], cos_ref[...], -sin_ref[...]).astype(bf16)
        dkv_ref[:, part:] = dv_ref[...].astype(bf16)


def attend_back(quarter, q, kv, own, other, wo, att, logs, qcode, kcode, cosine, sine):
    rows = q.shape[0]
    width = own.shape[1]
    part = q.shape[1] // 2
    block = rows // 2
    grid_spec = pltpu.PrefetchScalarGridSpec(
        num_scalar_prefetch=1,
        grid=(2,),
        in_specs=[
            pl.BlockSpec((block, part), lambda i, c: (i, c[0])),
            pl.BlockSpec((rows, 2 * part), lambda i, c: (0, c[0]), pipeline_mode=pl.Buffered(1)),
            whole((block, width)),
            whole((block, width)),
            pl.BlockSpec((width, part), lambda i, c: (0, c[0]), pipeline_mode=pl.Buffered(1)),
            pl.BlockSpec((block, part), lambda i, c: (i, 0)),
            pl.BlockSpec((8, block), lambda i, c: (0, i)),
            pl.BlockSpec((block, PAIR), lambda i, c: (i, 0)),
            whole((rows, PAIR)),
            whole((rows, PAIR)),
            whole((rows, PAIR)),
        ],
        out_specs=[
            pl.BlockSpec((block, part), lambda i, c: (i, 0)),
            whole((rows, 2 * part)),
        ],
        scratch_shapes=[
            pltpu.VMEM((part, rows), bf16),
            pltpu.VMEM((3, rows, PAIR), bf16),
            pltpu.VMEM((block, part), bf16),
            pltpu.VMEM((8, block), f32),
            pltpu.VMEM((part, block), f32),
            pltpu.VMEM((rows, part), f32),
            pltpu.VMEM((rows, part), f32),
        ],
    )
    return pl.pallas_call(
        attend_back_kernel,
        grid_spec=grid_spec,
        out_shape=[
            jax.ShapeDtypeStruct((rows, part), bf16),
            jax.ShapeDtypeStruct((rows, 2 * part), bf16),
        ],
        cost_estimate=cost(40 * rows * rows * part, 30 * rows * part, rows * rows * 3),
        compiler_params=pltpu.CompilerParams(vmem_limit_bytes=14 << 20),
        name="attend_back",
    )(quarter, q, kv, own, other, wo, att, logs, qcode, kcode, cosine, sine)


def project_kernel(att_a_ref, att_b_ref, wo_ref, own_ref, send_ref):
    part = att_a_ref.shape[1]
    rows = own_ref.shape[0]
    for out_ref, span in ((send_ref, slice(rows, 2 * rows)), (own_ref, slice(0, rows))):
        out = dot(att_a_ref[span, :], wo_ref[:, :part], NT) + dot(att_b_ref[span, :], wo_ref[:, part:], NT)
        out_ref[...] = out.astype(out_ref.dtype)


def project(att_a, att_b, wo):
    rows, part = att_a.shape
    rows = rows // 2
    width = wo.shape[0]
    return pl.pallas_call(
        project_kernel,
        grid=(1,),
        in_specs=[whole(att_a.shape)] * 2 + [whole(wo.shape)],
        out_specs=[whole((rows, width))] * 2,
        out_shape=[
            jax.ShapeDtypeStruct((rows, width), f32),
            jax.ShapeDtypeStruct((rows, width), bf16),
        ],
        cost_estimate=cost(8 * rows * width * part, 16 * rows * width),
        compiler_params=pltpu.CompilerParams(vmem_limit_bytes=6 << 20),
        name="project",
    )(att_a, att_b, wo)


def first_kernel(
    x_ref, own_ref, came_ref, norm_a_ref, norm_b_ref, n_ref, s_ref, low_ref, low_t_ref, gains_ref
):
    norms = jnp.concatenate([norm_a_ref[...], norm_b_ref[...]], axis=0).astype(f32).T
    gains_ref[...] = norms[:8]
    branch = own_ref[...] + came_ref[...].astype(f32)
    normed, inv = normalize(x_ref[...].astype(f32) + branch)
    n_ref[...] = normed
    s_ref[...] = jnp.broadcast_to(inv, s_ref.shape)
    first = normed * norms[0:1] + norms[2:3]
    low_ref[...] = first.astype(bf16)
    low_t_ref[...] = first.T.astype(bf16)


def first_norm(x, own, came, norm_a, norm_b):
    rows, width = x.shape
    at = norm_a.shape[1] // 128 - 1
    strip = pl.BlockSpec((width // 2, 128), lambda i: (0, at))
    return pl.pallas_call(
        first_kernel,
        grid=(1,),
        in_specs=[whole(x.shape)] * 3 + [strip] * 2,
        out_specs=[
            whole((rows, width)), whole((rows, 128)), whole((rows, width)), whole((width, rows)), whole((8, width)),
        ],
        out_shape=[
            jax.ShapeDtypeStruct((rows, width), f32),
            jax.ShapeDtypeStruct((rows, 128), f32),
            jax.ShapeDtypeStruct((rows, width), bf16),
            jax.ShapeDtypeStruct((width, rows), bf16),
            jax.ShapeDtypeStruct((8, width), f32),
        ],
        cost_estimate=cost(20 * rows * width, 16 * rows * width),
        compiler_params=pltpu.CompilerParams(vmem_limit_bytes=7 << 20),
        name="first_norm",
    )(x, own, came, norm_a, norm_b)


def mlp_kernel(has_base, low_ref, *rest):
    if has_base:
        base_ref, rest = rest[0], rest[1:]
    blocks, (act_ref, feed_ref, w_ref, sems, sum_ref) = rest[:BLOCKS], rest[BLOCKS:]
    slot = pl.program_id(0)
    half = act_ref.shape[3]
    start_weights(blocks, w_ref, sems)

    @pl.when(slot == 0)
    def _():
        sum_ref[...] = base_ref[...] if has_base else jnp.zeros_like(sum_ref)

    wait_weights(w_ref, sems, slot)

    gate = dot(low_ref[...], w_ref[slot, :, half : 2 * half])
    up = dot(low_ref[...], w_ref[slot, :, 2 * half : 3 * half])
    act_ref[0, 0] = gate.astype(bf16)
    act_ref[0, 1] = up.astype(bf16)
    act_ref[0, 2] = (gate / (1.0 + jnp.exp(-gate)) * up).astype(bf16)
    sum_ref[...] += dot(act_ref[0, 2], w_ref[slot, :, :half], NT)

    @pl.when(slot == 1)
    def _():
        feed_ref[...] = sum_ref[...].astype(feed_ref.dtype)


def mlp(low, base, blocks, half, dtype):
    rows, width = low.shape
    has_base = base is not None
    extra = [base] if has_base else []
    return pl.pallas_call(
        functools.partial(mlp_kernel, has_base),
        grid=(2,),
        in_specs=[whole((rows, width))] * (1 + has_base) + [ANY] * BLOCKS,
        out_specs=[
            pl.BlockSpec((1, 3, rows, half), lambda i: (i, 0, 0, 0)),
            whole((rows, width)),
        ],
        scratch_shapes=weight_scratch(blocks) + [pltpu.VMEM((rows, width), f32)],
        out_shape=[
            jax.ShapeDtypeStruct((2, 3, rows, half), bf16),
            jax.ShapeDtypeStruct((rows, width), dtype),
        ],
        cost_estimate=cost(12 * rows * width * half, 30 * half * width, 2 * rows * half),
        compiler_params=pltpu.CompilerParams(vmem_limit_bytes=(6 + half // 64) << 20),
        name="mlp",
    )(low, *extra, *blocks)


def second_kernel(
    n_ref, gains_ref, feed_ref, came_ref, dy_ref, out_ref, dh_ref, low_ref, low_t_ref, sums_ref
):
    first = n_ref[...] * gains_ref[0:1] + gains_ref[2:3]
    normed, inv = normalize(first + feed_ref[...] + came_ref[...].astype(f32))
    out_ref[...] = (normed * gains_ref[1:2] + gains_ref[3:4]).astype(bf16)
    dy = dy_ref[...]
    sums_ref[...] = jnp.zeros_like(sums_ref)
    sums_ref[1:2] = jnp.sum(dy * normed, axis=0, keepdims=True)
    sums_ref[3:4] = jnp.sum(dy, axis=0, keepdims=True)
    dh = norm_back(dy * gains_ref[1:2], normed, inv)
    dh_ref[...] = dh
    low_ref[...] = dh.astype(bf16)
    low_t_ref[...] = dh.T.astype(bf16)


def second_norm(n1, gains, feed, came, dy):
    rows, width = n1.shape
    full = whole((rows, width))
    return pl.pallas_call(
        second_kernel,
        grid=(1,),
        in_specs=[full, whole((8, width)), full, full, full],
        out_specs=[full, full, full, whole((width, rows)), whole((8, width))],
        out_shape=[
            jax.ShapeDtypeStruct((rows, width), bf16),
            jax.ShapeDtypeStruct((rows, width), f32),
            jax.ShapeDtypeStruct((rows, width), bf16),
            jax.ShapeDtypeStruct((width, rows), bf16),
            jax.ShapeDtypeStruct((8, width), f32),
        ],
        cost_estimate=cost(40 * rows * width, 22 * rows * width),
        compiler_params=pltpu.CompilerParams(vmem_limit_bytes=9 << 20),
        name="second_norm",
    )(n1, gains, feed, came, dy)


def mlp_back_kernel(has_base, *rest):
    dfeeds, dfeeds_t, lows_t, acts = rest[:2], rest[2:4], rest[4:6], rest[6:8]
    rest = rest[8:]
    if has_base:
        bases, rest = rest[:2], rest[2:]
    blocks, rest = rest[:BLOCKS], rest[BLOCKS:]
    own_ref, other_ref, to_x_ref, to_y_ref, keep_ref, w_ref, sems, part_ref, sum_ref = rest
    slot = pl.program_id(0)
    rows = own_ref.shape[0]
    half = acts[0].shape[3]
    start_weights(blocks, w_ref, sems)

    @pl.when(slot == 0)
    def _():
        for i in range(2):
            sum_ref[i * rows : (i + 1) * rows, :] = (
                bases[i][...] if has_base else jnp.zeros((rows, sum_ref.shape[1]), f32)
            )

    wait_weights(w_ref, sems, slot)

    for i in range(2):
        span = slice(i * rows, (i + 1) * rows)
        dhidden = dot(dfeeds[i][...], w_ref[slot, :, :half])
        gate = acts[i][0, 0].astype(f32)
        up = acts[i][0, 1].astype(f32)
        sg = 1.0 / (1.0 + jnp.exp(-gate))
        dgate = dhidden * up * sg * (1.0 + gate * (1.0 - sg))
        dup = dhidden * (gate * sg)
        part_ref[span, :half] = dgate.astype(bf16)
        part_ref[span, half:] = dup.astype(bf16)
        sum_ref[span, :] += dot(part_ref[span, :], w_ref[slot, :, half : 3 * half], NT)
    gate_up = (
        dot(lows_t[0][...], part_ref[:rows, :]) + dot(lows_t[1][...], part_ref[rows:, :])
    ).astype(bf16)
    down = (
        dot(dfeeds_t[0][...], acts[0][0, 2]) + dot(dfeeds_t[1][...], acts[1][0, 2])
    ).astype(bf16)
    cut = keep_ref.shape[1]

    def emit(out_ref, at, block):
        span = slice(block * cut, (block + 1) * cut)
        out_ref[at, :, :half] = down[span]
        out_ref[at, :, half:] = gate_up[span]

    emit(to_x_ref, 0, 3)

    @pl.when(slot == 0)
    def _():
        for block in range(3):
            emit(keep_ref, block, block)

    @pl.when(slot == 1)
    def _():
        emit(to_y_ref, 0, 0)
        emit(to_y_ref, 1, 2)
        emit(keep_ref, 3, 1)
        own_ref[...] = sum_ref[:rows, :]
        other_ref[...] = sum_ref[rows:, :].astype(other_ref.dtype)


def mlp_back(bases, dfeeds, dfeeds_t, lows_t, acts, blocks):
    rows, width = dfeeds[0].shape
    half = acts[0].shape[3]
    has_base = bases is not None
    full = whole((rows, width))
    return pl.pallas_call(
        functools.partial(mlp_back_kernel, has_base),
        grid=(2,),
        in_specs=[full] * 2
        + [whole((width, rows))] * 4
        + [pl.BlockSpec((1, 3, rows, half), lambda i: (i, 0, 0, 0))] * 2
        + [full] * (2 * has_base)
        + [ANY] * BLOCKS,
        out_specs=[
            full,
            full,
            pl.BlockSpec((1, width // 4, 3 * half), lambda i: (i, 0, 0)),
            whole((2, width // 4, 3 * half)),
            whole((4, width // 4, 3 * half)),
        ],
        scratch_shapes=weight_scratch(blocks)
        + [pltpu.VMEM((2 * rows, 2 * half), bf16), pltpu.VMEM((2 * rows, width), f32)],
        out_shape=[
            jax.ShapeDtypeStruct((rows, width), f32),
            jax.ShapeDtypeStruct((rows, width), bf16 if has_base else f32),
            jax.ShapeDtypeStruct((2, width // 4, 3 * half), bf16),
            jax.ShapeDtypeStruct((2, width // 4, 3 * half), bf16),
            jax.ShapeDtypeStruct((4, width // 4, 3 * half), bf16),
        ],
        cost_estimate=cost(48 * rows * width * half, 100 * half * width, 4 * rows * half),
        compiler_params=pltpu.CompilerParams(vmem_limit_bytes=(5 + half // 28) << 20),
        name="mlp_back",
    )(*dfeeds, *dfeeds_t, *lows_t, *acts, *(bases if has_base else ()), *blocks)


def first_back_kernel(
    base_ref, own_ref, came_ref, n_ref, s_ref, gains_ref, sums_ref, dh_ref, low_ref, low_t_ref
):
    dfirst = base_ref[...] + own_ref[...] + came_ref[...].astype(f32)
    normed = n_ref[...]
    width = dfirst.shape[1]
    gain_sum = jnp.sum(dfirst * normed, axis=0, keepdims=True)
    bias_sum = jnp.sum(dfirst, axis=0, keepdims=True)
    sums = sums_ref[...]
    stacked = jnp.concatenate(
        [gain_sum, sums[1:2], bias_sum, sums[3:4], jnp.zeros((124, width), f32)], axis=0
    )
    rows = dfirst.shape[0]
    low_t_ref[:, rows:] = stacked.T.astype(bf16)
    dh = norm_back(dfirst * gains_ref[0:1], normed, s_ref[:, 0:1])
    dh_ref[...] = dh
    low_ref[...] = dh.astype(bf16)
    low_t_ref[:, :rows] = dh.T.astype(bf16)


def first_back(base, own, came, n1, s1, gains, sums):
    rows, width = n1.shape
    full = whole((rows, width))
    return pl.pallas_call(
        first_back_kernel,
        grid=(1,),
        in_specs=[full] * 4 + [whole((rows, 128)), whole((8, width)), whole((8, width))],
        out_specs=[full, full, whole((width, rows + 128))],
        out_shape=[
            jax.ShapeDtypeStruct((rows, width), f32),
            jax.ShapeDtypeStruct((rows, width), bf16),
            jax.ShapeDtypeStruct((width, rows + 128), bf16),
        ],
        cost_estimate=cost(40 * rows * width, 20 * rows * width),
        compiler_params=pltpu.CompilerParams(vmem_limit_bytes=9 << 20),
        name="first_back",
    )(base, own, came, n1, s1, gains, sums)


def qkv_back_kernel(
    dq_ref, dkv_ref, x_a_ref, x_b_ref, low_a_ref, low_b_ref, cols_a_ref, cols_b_ref, att_ref, base_own_ref, base_other_ref,
    top_ref, bottom_ref, own_ref, other_ref, early_ref, mid_ref, late_ref, w_ref, sem,
):
    rows = own_ref.shape[0]
    part = dq_ref.shape[1]
    copies = [
        pltpu.make_async_copy(top_ref, w_ref.at[pl.ds(0, top_ref.shape[0])], sem),
        pltpu.make_async_copy(bottom_ref, w_ref.at[pl.ds(top_ref.shape[0], top_ref.shape[0])], sem),
    ]
    for copy in copies:
        copy.start()
    d_out = dot(low_a_ref[...], att_ref[:rows, :]) + dot(low_b_ref[...], att_ref[rows:, :])
    lane = lax.broadcasted_iota(jnp.int32, d_out.shape, 1)
    cut = mid_ref.shape[0]

    def emit(value, lanes):
        early_ref[0, :, lanes] = value[:cut]
        mid_ref[:, lanes] = value[cut : 2 * cut]
        early_ref[1, :, lanes] = value[2 * cut : 3 * cut]
        late_ref[:, lanes] = value[3 * cut :]

    for h in range(3):
        source, at = (dq_ref, 0) if h == 0 else (dkv_ref, (h - 1) * part)
        piece = dot(x_a_ref[...], source[:rows, at : at + part]) + dot(x_b_ref[...], source[rows:, at : at + part])
        moved = pltpu.roll(d_out, (3 - h) * HD, 1)
        emit(jnp.where(lane < 3 * HD, piece, moved).astype(bf16), slice(h * part, (h + 1) * part))
    cols = cols_a_ref[...].astype(f32) + cols_b_ref[...].astype(f32)
    emit(cols.astype(bf16), slice(3 * part, 3 * part + 128))
    pltpu.make_async_copy(w_ref, w_ref, sem).wait()
    for i, (base_ref, out_ref) in enumerate(((base_own_ref, own_ref), (base_other_ref, other_ref))):
        span = slice(i * rows, (i + 1) * rows)
        total = dot(dq_ref[span, :], w_ref[:, :part], NT) + dot(dkv_ref[span, :], w_ref[:, part:], NT)
        out_ref[...] = (total + base_ref[...].astype(f32)).astype(out_ref.dtype)


def qkv_back(bases, dq, dkv, x_t, low_t, att, blocks):
    rows = dq.shape[0] // 2
    width = low_t[0].shape[0]
    part = dq.shape[1]
    lanes = 3 * part + 128
    full = whole((rows, width))
    turned = whole((width, rows))
    strip = pl.BlockSpec((width, 128), lambda i: (0, rows // 128), pipeline_mode=pl.Buffered(1))
    pieces = [(2, width // 4, lanes), (width // 4, lanes), (width // 4, lanes)]
    return pl.pallas_call(
        qkv_back_kernel,
        grid=(1,),
        in_specs=[whole(dq.shape), whole(dkv.shape)]
        + [turned] * 4
        + [strip] * 2
        + [whole(att.shape), full, full, ANY, ANY],
        out_specs=[full, full] + [whole(p) for p in pieces],
        scratch_shapes=[pltpu.VMEM((width, 3 * part), bf16), pltpu.SemaphoreType.DMA],
        out_shape=[
            jax.ShapeDtypeStruct((rows, width), f32),
            jax.ShapeDtypeStruct((rows, width), bf16),
        ]
        + [jax.ShapeDtypeStruct(p, bf16) for p in pieces],
        cost_estimate=cost(26 * rows * width * part, 40 * width * part),
        compiler_params=pltpu.CompilerParams(vmem_limit_bytes=12 << 20),
        name="qkv_back",
    )(dq, dkv, *x_t, *low_t, *low_t, att, *bases, *blocks)


def bits_of(n):
    bits = n.bit_length() - 1
    if 1 << bits != n:
        raise ValueError("row count")
    return bits


class Links:
    def __init__(self, mesh):
        self.rows = mesh.shape["row"]
        self.cols = mesh.shape["col"]
        self.bits = bits_of(self.rows // 2)

    def locate(self):
        row = lax.axis_index("row")
        col = lax.axis_index("col")
        return row // 2, row % 2, col // (self.cols // 2), col % 2

    def send(self, v, move):
        pairs = []
        for row in range(self.rows):
            for col in range(self.cols):
                ring, x, y, k = move(row // 2, row % 2, col // (self.cols // 2), col % 2)
                pairs.append(
                    (row * self.cols + col, (ring * 2 + x) * self.cols + y * (self.cols // 2) + k)
                )
        return lax.ppermute(v, ("row", "col"), pairs)

    def across(self, v):
        return self.send(v, lambda ring, x, y, k: (ring, x, 1 - y, k))

    def beside(self, v):
        return self.send(v, lambda ring, x, y, k: (ring, x, y, 1 - k))

    def far(self, v):
        return self.send(
            v, lambda ring, x, y, k: (ring, 1 - x, y, k) if k else (ring, x, 1 - y, k)
        )

    def along(self, v):
        return self.send(v, lambda ring, x, y, k: (ring, 1 - x, y, k))

    def turned(self, v, bit):
        return self.send(v, lambda ring, x, y, k: (ring ^ (1 << bit), x, y, k))

    def ring_grow(self, block, bit):
        return jnp.concatenate([block, self.turned(block, bit)], axis=0)

    def ring_gather(self, block, last=0):
        for bit in reversed(range(last, self.bits)):
            block = self.ring_grow(block, bit)
        return block

    def ring_split(self, block):
        own, low = jnp.split(block, 2, axis=0)
        return own, low.astype(bf16)

    def ring_scatter(self, own, low, held=()):
        for bit in range(self.bits):
            if bit > 0:
                own, low = self.ring_split(own)
                low = tie(low, *held)
            own = own + self.turned(low, bit).astype(f32)
        return own


def tie(value, *others):
    return lax.optimization_barrier((value, *others))[0]


class Scatter:
    def __init__(self, links, to_x, to_y, keep):
        self.links, self.keep = links, keep
        by_x = [links.along(v) for v in to_x]
        self.by_x = [by_x[0][0], by_x[0][1]] if len(by_x) == 1 else by_x
        self.by_y = links.across(to_y)

    def second(self):
        to_x = (self.keep[2].astype(f32) + self.by_y[1].astype(f32)).astype(bf16)
        to_y = (self.keep[3].astype(f32) + self.by_x[1].astype(f32)).astype(bf16)
        self.late_x, self.late_y = self.links.along(to_x), self.links.across(to_y)
        return to_x, to_y

    def third(self):
        low = self.keep[0].astype(f32) + self.by_y[0].astype(f32) + self.late_x.astype(f32)
        high = self.keep[1].astype(f32) + self.by_x[0].astype(f32) + self.late_y.astype(f32)
        self.own, self.low = self.links.ring_split(jnp.concatenate([low, high], axis=0))
        return [self.low]

    def last(self, held=()):
        return self.links.ring_scatter(self.own, self.low, held)


def relative_order(links, depth):
    ring, x, _, _ = links.locate()
    where = lax.broadcasted_iota(jnp.int32, (1, links.rows * depth), 1)
    block, inside = where // depth, where % depth
    steps = links.rows // 2
    place = block % steps
    turn = jnp.zeros_like(place)
    for bit in reversed(range(links.bits)):
        turn = turn + (place % 2 << bit)
        place = place // 2
    row = jnp.bitwise_xor(ring, turn) * 2 + jnp.bitwise_xor(x, block // steps)
    return row * depth + inside


def on_device(
    links, tokens, segments, positions, w_qkv, w_out, w_gate_up, w_down, norm_gain, norm_bias, cotangent
):
    ring, x_place, side, core = links.locate()
    depth = w_qkv.shape[0]
    width = tokens.shape[2]
    head_cols = w_qkv.shape[2]
    hid = w_gate_up.shape[2]
    sizes = [hid - hid // 3, hid // 3]
    rows = 2 * tokens.shape[1]
    mine = rows // 2
    part = head_cols + HD

    source = relative_order(links, depth)
    swap = (lax.broadcasted_iota(jnp.int32, (width, width), 0) == source).astype(bf16)

    def split(v):
        high = v.astype(bf16)
        return high, (v - high.astype(f32)).astype(bf16)

    def own_and_other(v):
        own = lax.dynamic_index_in_dim(v, side, 0, keepdims=False)
        return own, lax.dynamic_index_in_dim(v, 1 - side, 0, keepdims=False)

    def from_sequence(own, came):
        first = side == 0
        return jnp.stack([jnp.where(first, own, came), jnp.where(first, came, own)], axis=0)

    out_t = w_out.T
    attn_shard = jnp.concatenate(
        sum(
            [[w_qkv[:, p], out_t[:, p * HD : (p + 1) * HD]] for p in range(3)],
            [],
        ),
        axis=1,
    )
    norms = jnp.concatenate([norm_gain, norm_bias], axis=1)
    norms = jnp.pad(norms, ((0, 0), (0, 128 - norms.shape[1])))
    down_t = w_down.T
    mlp_shards = []
    for h, at in enumerate([0, sizes[0]]):
        cols = slice(at, at + sizes[h])
        pieces = [down_t[:, cols], w_gate_up[:, 0, cols], w_gate_up[:, 1, cols]]
        mlp_shards.append(jnp.concatenate(pieces + ([norms] if h == 0 else []), axis=1))

    small_own, small_other = own_and_other(jnp.stack([segments, positions], axis=1))
    small_came = links.across(small_other)
    tokens_own, tokens_other = own_and_other(tokens)
    tokens_came = links.across(tie(tokens_other, attn_shard, small_other))
    dy_own, dy_other = own_and_other(cotangent)
    dy_came = links.across(tie(dy_other.astype(bf16), attn_shard, small_other))

    odd = core == 1
    grow_a = links.ring_gather(attn_shard, last=1)
    ring_a = links.ring_grow(grow_a, 0)
    x_a, y_a = links.along(ring_a), links.across(ring_a)
    ring_b = links.ring_gather(tie(mlp_shards[0], grow_a))
    turn_a = jnp.where(odd, y_a, x_a)
    attn_w = [ring_a, x_a, y_a, links.far(turn_a)]

    x_abs = jnp.concatenate([tokens_own, tokens_came], axis=0)
    x = dot(x_abs, swap).astype(bf16)
    x_other = links.beside(x)
    small = jnp.concatenate([small_own, small_came], axis=1)
    small = jnp.concatenate([small, links.beside(small)], axis=1)
    qcode, kcode = document_codes(small[0])
    first_quarter, second_quarter = jnp.zeros((1,), jnp.int32), jnp.ones((1,), jnp.int32)
    cosine, sine = rope_tables(small[1])

    ring_b = tie(ring_b, turn_a, cosine, sine, qcode, kcode)
    x_b, y_b = links.along(ring_b), links.across(ring_b)
    grow_c = links.ring_gather(tie(mlp_shards[1], ring_b), last=1)
    q, kv, wo = qkv(tie(x, ring_b, dy_came), x_other, cosine, sine, attn_w)
    ring_c = links.ring_grow(tie(grow_c, q), 0)
    att_0, logs_0 = attend(first_quarter, q, kv, qcode, kcode)
    att_1, logs_1 = attend(second_quarter, tie(q, att_0), kv, qcode, kcode)
    held_x, held_y = lax.optimization_barrier((x_b, y_b, att_1))[:2]
    turn_b = jnp.where(odd, held_y, held_x)
    mlp_b = [ring_b, x_b, y_b, links.far(turn_b)]
    ring_c = tie(ring_c, turn_b)
    x_c, y_c = links.along(ring_c), links.across(ring_c)
    own, send = project(att_0, tie(att_1, turn_b, ring_c), wo)
    x_t = lax.dot_general(
        swap, tie(x_abs, own), (((0,), (1,)), ((), ())), preferred_element_type=f32
    ).astype(bf16)
    x_t = [x_t, links.beside(x_t)]
    high, low_part = split(tie(dy_own, own))
    dy = jnp.concatenate([dot(high, swap) + dot(low_part, swap), dot(dy_came, swap)], axis=0)
    n1, s1, low, low_t, gains = first_norm(
        x, tie(own, mlp_b[3], x_t[1], dy), links.beside(send), ring_b, x_b
    )
    low_other = links.beside(low)
    act_b_own, feed = mlp(low, None, mlp_b, sizes[0], f32)
    low1_t = [low_t, links.beside(tie(low_t, feed))]
    act_b_other, feed_other = mlp(low_other, None, mlp_b, sizes[0], f32)
    held_x, held_y = lax.optimization_barrier((x_c, y_c, feed))[:2]
    turn_c = jnp.where(odd, held_y, held_x)
    mlp_c = [ring_c, x_c, y_c, links.far(turn_c)]
    act_c_other, send = mlp(tie(low_other, low1_t[1]), feed_other, mlp_c, sizes[1], bf16)
    came = links.beside(send)
    act_c_own, feed = mlp(tie(low, send), feed, mlp_c, sizes[1], f32)
    layer_out, dh2, dfeed, dfeed_t, sums = second_norm(n1, gains, feed, came, dy)
    layer_out = dot(layer_out, swap, NT).astype(bf16)
    layer_came = links.across(layer_out[mine:])
    dfeeds = [dfeed, links.beside(dfeed)]
    dfeeds_t = [dfeed_t, links.beside(dfeed_t)]

    own, other, to_x, to_y, keep = mlp_back(None, dfeeds, dfeeds_t, low1_t, (act_c_own, act_c_other), mlp_c)
    sum_b = Scatter(links, [to_x], to_y, keep)
    own, other, to_x, to_y, keep = mlp_back(
        (tie(own, layer_came), other), dfeeds, dfeeds_t, low1_t, (act_b_own, act_b_other), mlp_b
    )
    came = links.beside(other)
    sum_b.keep = tie(sum_b.keep, own)
    ops_b = sum_b.second()
    sum_c = Scatter(links, [tie(to_x, *ops_b)], tie(to_y, *ops_b), keep)
    dh1, low, low_t = first_back(tie(dh2, *ops_b), own, came, n1, s1, gains, sums)
    lows = [low, links.beside(low)]
    low_t = [low_t, links.beside(low_t)]
    dq, dkv = attend_back(
        second_quarter, q, kv, *lows, wo, att_1, logs_1, qcode, kcode, cosine, sine
    )
    sum_b.keep = tie(sum_b.keep, dq)
    block_b = sum_b.third()
    bases = (dh1, jnp.zeros(low.shape, bf16))
    own, other, to_y, keep_1, to_x_1 = qkv_back(
        bases, tie(dq, *block_b), dkv, x_t, low_t, att_1, attn_w[2:]
    )
    own_b = sum_b.last()
    sum_c.keep = tie(sum_c.keep, own)
    ops_c = sum_c.second()
    dq, dkv = attend_back(
        first_quarter, tie(q, own, *ops_c), kv, *lows, wo, att_0, logs_0, qcode, kcode, cosine, sine
    )
    sum_c.keep = tie(sum_c.keep, dq)
    block_c = sum_c.third()
    own, other, early, middle, to_x_0 = qkv_back(
        (own, other), tie(dq, *block_c, own_b), dkv, x_t, low_t, att_0, attn_w[:2]
    )
    own_c = sum_c.last()
    sum_a = Scatter(links, [to_x_0, to_x_1], to_y, [early[0], middle, early[1], keep_1])
    grad = own + links.beside(other).astype(f32)
    high, low = split(grad)
    grad = dot(high, swap, NT) + dot(low, swap, NT)
    sum_a.keep = tie(sum_a.keep, grad)
    ops_a = sum_a.second()
    own_mlp = [own_c, own_b]
    grad_down = jnp.concatenate([v[:, :n] for v, n in zip(own_mlp, sizes)], axis=1).T
    grad_gate_up = jnp.stack(
        [
            jnp.concatenate([v[:, p * n : (p + 1) * n] for v, n in zip(own_mlp, sizes)], axis=1)
            for p in (1, 2)
        ],
        axis=1,
    )
    block_a = sum_a.third()
    came = links.across(tie(grad[mine:].astype(bf16), *block_a))
    input_grad = from_sequence(grad[:mine], came.astype(f32))
    layer_out = from_sequence(tie(layer_out[:mine], to_x_0), layer_came)
    own_attn = sum_a.last((came, grad_down, grad_gate_up, layer_out))
    thirds = [own_attn[:, p * part : (p + 1) * part] for p in range(3)]
    edge = 3 * part
    return (
        layer_out,
        input_grad,
        jnp.stack([v[:, :head_cols] for v in thirds], axis=1),
        jnp.concatenate([v[:, head_cols:] for v in thirds], axis=1).T,
        grad_gate_up,
        grad_down,
        own_attn[:, edge : edge + 2],
        own_attn[:, edge + 2 : edge + 4],
    )


def solution(mesh):
    in_specs = (
        P(None, ("row", "col"), None),
        P(None, ("row", "col")),
        P(None, ("row", "col")),
        P("row", None, "col"),
        P("col", "row"),
        P("row", None, "col"),
        P("col", "row"),
        P("row", None),
        P("row", None),
        P(None, ("row", "col"), None),
    )
    out_specs = (
        P(None, ("row", "col"), None),
        P(None, ("row", "col"), None),
        P("row", None, "col"),
        P("col", "row"),
        P("row", None, "col"),
        P("col", "row"),
        P("row", None),
        P("row", None),
    )
    return jax.shard_map(
        functools.partial(on_device, Links(mesh)), mesh=mesh, in_specs=in_specs, out_specs=out_specs, check_vma=False
    )
```
